32 devices in a mesh: dp: 4 (over y, core), context: 2 (over x), tensor: 4 (over z).
Axes of the slice: x: 2, y: 2, z: 4, core: 2. Of those that a mesh axis runs over, the one named last changes fastest.
Arguments:
- prompt_x: bfloat16 [4096, 2560], P(('dp', 'context')), may hold values from -6 to 6
- cont_x: bfloat16 [4096, 2560], P(('dp', 'context')), may hold values from -6 to 6
- prompt_len: int32 [4], P('dp'), may hold values from 513 to 1024
- cont_seg: int32 [8, 512], P(('dp', 'context')), may hold values from 0 to 3, never falling along the last dimension, each value on 1 to 256 neighbouring positions
- attn_gain: bfloat16 [2560], P(('dp', 'context')), may hold values from 0.5 to 1.5
- q_weight: bfloat16 [2560, 2560], P(('dp', 'context'), 'tensor'), may hold values from -0.125 to 0.125
- key_matrix: bfloat16 [2560, 640], P(('dp', 'context'), 'tensor'), may hold values from -0.125 to 0.125
- value_matrix: bfloat16 [2560, 640], P(('dp', 'context'), 'tensor'), may hold values from -0.125 to 0.125
- o_weight: bfloat16 [2560, 2560], P(('dp', 'context'), 'tensor'), may hold values from -1 to 1
- mlp_gain: bfloat16 [2560], P(('dp', 'context')), may hold values from 0.5 to 1.5
- gate_weight: bfloat16 [2560, 6912], P(('dp', 'context'), 'tensor'), may hold values from -0.125 to 0.125
- up_weight: bfloat16 [2560, 6912], P(('dp', 'context'), 'tensor'), may hold values from -0.125 to 0.125
- down_weight: bfloat16 [2560, 6912], P(('dp', 'context'), 'tensor'), may hold values from -0.078125 to 0.078125
- prompt_cot: bfloat16 [4096, 2560], P(('dp', 'context')), may hold values from -6 to 6
- cont_cot: bfloat16 [4096, 2560], P(('dp', 'context')), may hold values from -6 to 6
Outputs:
- prompt_out: bfloat16 [4096, 2560], P(('dp', 'context'))
- cont_out: bfloat16 [4096, 2560], P(('dp', 'context'))
- prompt_grad: float32 [4096, 2560], P(('dp', 'context'))
- cont_grad: float32 [4096, 2560], P(('dp', 'context'))
- attn_gain_grad: float32 [2560], P(('dp', 'context'))
- q_grad: float32 [2560, 2560], P(('dp', 'context'), 'tensor')
- k_grad: float32 [2560, 640], P(('dp', 'context'), 'tensor')
- v_grad: float32 [2560, 640], P(('dp', 'context'), 'tensor')
- o_grad: float32 [2560, 2560], P(('dp', 'context'), 'tensor')
- mlp_gain_grad: float32 [2560], P(('dp', 'context'))
- gate_grad: float32 [2560, 6912], P(('dp', 'context'), 'tensor')
- up_grad: float32 [2560, 6912], P(('dp', 'context'), 'tensor')
- down_grad: float32 [2560, 6912], P(('dp', 'context'), 'tensor')
The draws below stay inside these ranges and needn't reach their ends.
Inputs may be any that keep to these rules, and one draw needn't show every extreme that they name: `cont_seg`: in each row, continuation numbers never fall; each of the 4 continuations has 1 to 256 tokens, and one has exactly 256.
All inputs are finite; a program needn't handle non-finite values.
Results may differ from the reference program's by a relative error of at most 0.017.
Values may be sent and summed in bfloat16 or wider, within the bound.
A program may use at most 384 MiB of HBM per device.

```python
import math
import jax
import jax.numpy as jnp
import numpy as np
from jax import lax

MODEL_WIDTH = 2560
QUERY_HEADS = 32
KEY_VALUE_HEADS = 8
HEAD_SIZE = 80
FF = 6912
PROMPT = 1024
CONT_LEN = 256
CONT_DEV = 512
SEGS = 4
PROMPT_DEV = 512
PTOKENS = 4096
CTOKENS = 4096
CROWS = 8
N_DP = 4
N_CONTEXT = 2


def place_ends(drawn, own_key, low, high):
    extent = drawn.shape
    spot = [jax.random.randint(jax.random.fold_in(own_key, axis), (), 0, extent[axis]) for axis in range(len(extent))]
    drawn = drawn.at[tuple(spot)].set(low)
    longest = extent.index(max(extent))
    spot[longest] = (spot[longest] + 1) % extent[longest]
    return drawn.at[tuple(spot)].set(high)


def raised(values, key, source, target, blocks, factor):
    def block_of(dim):
        return (jnp.arange(values.shape[dim]) // (values.shape[dim] // blocks)).reshape((-1,) + (1,) * (values.ndim - 1 - dim))

    first = jax.random.permutation(key, blocks)[block_of(target)]
    far = (block_of(target) + blocks // 2) % blocks
    return jnp.where((block_of(source) == first) | (block_of(source) == far), factor * values, values)


def block_scale(own_key, shape, shards, low, high):
    def one(axis_at, blocks):
        heights = jax.random.uniform(jax.random.fold_in(jax.random.fold_in(own_key, 6), axis_at), (blocks,), jnp.float32, low / len(shards), high / len(shards))
        return jnp.repeat(jnp.exp(heights), shape[axis_at] // blocks).reshape((-1,) + (1,) * (len(shape) - axis_at - 1))

    loudness = one(*shards[0])
    for cut in shards[1:]:
        loudness = loudness * one(*cut)
    return loudness


def length_profile(number_of, total, limit, skew):
    portions = [(1 << 20) // math.isqrt(rank ** skew) + 1 for rank in range(2, number_of + 1)]
    spare, holding = total - limit - (number_of - 1), [1] * (number_of - 1)
    while spare > 0:
        candidates = [i for i in range(number_of - 1) if holding[i] < limit]
        pool, budget = sum([portions[i] for i in candidates]), spare
        for i in candidates:
            more = min(limit - holding[i], max(1, budget * portions[i] // pool), spare)
            holding[i] = holding[i] + more
            spare = spare - more
    return np.array([limit] + holding)


def uneven(rng, count, total, reach, slope):
    if count == 2:
        one = jax.random.randint(rng, (), max(1, total - reach), min(reach, total - 1) + 1)
        return jnp.stack([one, total - one])
    tallies = jnp.asarray(length_profile(count, total, reach, slope), jnp.int32)
    couples = (count - 1) // 2
    donor, sink = tallies[1:1 + 2 * couples:2], tallies[2:2 + 2 * couples:2]
    margin = jnp.minimum(donor - 1, reach - sink)
    shifted = jax.random.randint(jax.random.fold_in(rng, 1), (couples,), 0, 1 << 20) % (margin + 1)
    tallies = tallies.at[1:1 + 2 * couples:2].set(donor - shifted).at[2:2 + 2 * couples:2].set(sink + shifted)
    return tallies[jax.random.permutation(jax.random.fold_in(rng, 2), count)]


def normal_values(stream_key, dims, spread, limit, cuts=(), kind=jnp.bfloat16):
    drawn = jax.random.normal(stream_key, dims, jnp.float32) * spread
    if len(cuts) > 0:
        drawn = block_scale(stream_key, dims, cuts, -0.22, 0.18) * drawn
    return jnp.clip(drawn, min=-limit, max=limit).astype(kind)


def gaussian_with(key, extent, spread, most, cuts, heavy, held_as=jnp.bfloat16):
    entries = spread * jax.random.normal(key, extent, jnp.float32)
    if cuts:
        entries = entries * block_scale(key, extent, cuts, -0.22, 0.18)
    return jnp.clip(raised(entries, jax.random.fold_in(key, 3), *heavy), -most, most).astype(held_as)


def setup_inputs(seed: int = 0) -> dict:
    streams_of = jax.random.split(jax.random.key(seed), 16)
    prompt_x = normal_values(streams_of[0], (PTOKENS, MODEL_WIDTH), 1.0, 6.0, ((0, 8),))
    cont_x = normal_values(streams_of[1], (CTOKENS, MODEL_WIDTH), 1.0, 6.0, ((0, 8),))
    prompt_len = place_ends(jax.random.randint(streams_of[2], (N_DP,), PROMPT - PROMPT_DEV + 1, PROMPT + 1), jax.random.fold_in(streams_of[2], 1), PROMPT - PROMPT_DEV + 1, PROMPT).astype(jnp.int32)
    cont_seg = jax.vmap(lambda own: jnp.searchsorted(jnp.cumsum(uneven(own, SEGS, CONT_DEV, CONT_LEN, 1)), jnp.arange(CONT_DEV), side="right"))(jax.random.split(streams_of[3], CROWS)).reshape((CROWS, CONT_DEV)).astype(jnp.int32)
    attn_gain = jnp.clip(1.0 + 0.1 * jax.random.normal(streams_of[4], (MODEL_WIDTH,), jnp.float32), 0.5, 1.5).astype(jnp.bfloat16)
    q_weight = normal_values(streams_of[5], (MODEL_WIDTH, QUERY_HEADS * HEAD_SIZE), MODEL_WIDTH ** -0.5, 0.125, ((0, 8), (1, 4)))
    key_matrix = normal_values(streams_of[6], (MODEL_WIDTH, KEY_VALUE_HEADS * HEAD_SIZE), MODEL_WIDTH ** -0.5, 0.125, ((0, 8), (1, 4)))
    value_matrix = normal_values(streams_of[7], (MODEL_WIDTH, KEY_VALUE_HEADS * HEAD_SIZE), MODEL_WIDTH ** -0.5, 0.125, ((0, 8), (1, 4)))
    o_weight = normal_values(streams_of[8], (MODEL_WIDTH, QUERY_HEADS * HEAD_SIZE), (QUERY_HEADS * HEAD_SIZE // 64) ** -0.5, 1.0, ((0, 8), (1, 4)))
    mlp_gain = jnp.clip(1.0 + 0.1 * jax.random.normal(streams_of[9], (MODEL_WIDTH,), jnp.float32), 0.5, 1.5).astype(jnp.bfloat16)
    gate_weight = normal_values(streams_of[10], (MODEL_WIDTH, FF), MODEL_WIDTH ** -0.5, 0.125, ((0, 8), (1, 4)))
    up_weight = normal_values(streams_of[11], (MODEL_WIDTH, FF), MODEL_WIDTH ** -0.5, 0.125, ((0, 8), (1, 4)))
    down_weight = normal_values(streams_of[12], (MODEL_WIDTH, FF), FF ** -0.5, 0.078125, ((0, 8), (1, 4)))
    prompt_cot = normal_values(streams_of[13], (PTOKENS, MODEL_WIDTH), 1.0, 6.0, ((0, 8),))
    cont_cot = gaussian_with(streams_of[14], (CTOKENS, MODEL_WIDTH), 1.0, 6.0, ((0, 8),), (0, 1, 8, 2.0))
    return dict(prompt_x=prompt_x, cont_x=cont_x, prompt_len=prompt_len, cont_seg=cont_seg, attn_gain=attn_gain, q_weight=q_weight, key_matrix=key_matrix, value_matrix=value_matrix, o_weight=o_weight, mlp_gain=mlp_gain, gate_weight=gate_weight, up_weight=up_weight, down_weight=down_weight, prompt_cot=prompt_cot, cont_cot=cont_cot)


EPS = 1e-05
THETA = 10000.0
PRECISE = lax.Precision.HIGHEST

@jax.custom_vjp
def lowered_inputs(v):
    return lax.optimization_barrier(v.astype(jnp.bfloat16)).astype(jnp.float32)

@jax.custom_vjp
def lowered_backward(v):
    return v

def low_keep(v):
    return (lowered_inputs(v), None)

def low_pass(kept, grad):
    return (grad,)

def back_keep(v):
    return (v, None)

def back_low(kept, grad):
    return (lowered_inputs(grad),)
lowered_inputs.defvjp(low_keep, low_pass)
lowered_backward.defvjp(back_keep, back_low)

def normalize(values):
    return values * lax.rsqrt(lax.optimization_barrier(jnp.mean(values * values, axis=-1, keepdims=True)) + EPS)

def rotate(values, cosine, sine_table):
    half_dim = values.shape[-1] // 2
    first_half = values[..., :half_dim]
    second_half = values[..., half_dim:]
    return jnp.concatenate([first_half * cosine - second_half * sine_table, second_half * cosine + first_half * sine_table], axis=-1)

def matrix_product(left_side, right_side):
    return jnp.dot(left_side, right_side, preferred_element_type=jnp.float32, precision=PRECISE)

def group_layer(params, prompt_part, cont_part, length, segment_rows):
    attn_gain, q_weight, key_matrix, value_matrix, o_weight, mlp_gain, gate_weight, up_weight, down_weight = params
    tokens = jnp.concatenate([prompt_part, cont_part], axis=0)
    count_of_tokens = tokens.shape[0]
    blocks, block_rows = segment_rows.shape
    local_index = jnp.arange(block_rows, dtype=jnp.int32)
    earlier = lax.optimization_barrier(jnp.sum((segment_rows[:, None, :] < segment_rows[:, :, None]).astype(jnp.int32), axis=2))
    offset = local_index[None, :] - earlier
    label_cont = (segment_rows + jnp.arange(blocks, dtype=jnp.int32)[:, None] * block_rows).reshape(-1)
    cont_pos = (length + offset).reshape(-1)
    position = jnp.concatenate([jnp.arange(PROMPT, dtype=jnp.int32), cont_pos])
    index_all = jnp.arange(count_of_tokens, dtype=jnp.int32)
    is_prompt = index_all < PROMPT
    label_all = jnp.concatenate([jnp.full((PROMPT,), -1, jnp.int32), label_cont.astype(jnp.int32)])

    def block_mask(row_index):
        query_prompt = row_index[:, None] < PROMPT
        causal = index_all[None, :] <= row_index[:, None]
        from_prompt = jnp.where(query_prompt, causal, index_all[None, :] < length) & is_prompt[None, :]
        same = (label_all[row_index][:, None] == label_all[None, :]) & causal & jnp.logical_not(query_prompt)
        return from_prompt | same
    unit_one = normalize(tokens)
    first_normed = lowered_inputs(unit_one * attn_gain)
    query_proj = lowered_backward(matrix_product(first_normed, q_weight)).reshape(count_of_tokens, QUERY_HEADS, HEAD_SIZE)
    key_projected = lowered_backward(matrix_product(first_normed, key_matrix)).reshape(count_of_tokens, KEY_VALUE_HEADS, HEAD_SIZE)
    value_projected = lowered_inputs(lowered_backward(matrix_product(first_normed, value_matrix))).reshape(count_of_tokens, KEY_VALUE_HEADS, HEAD_SIZE)
    inv_freq = THETA ** (-jnp.arange(HEAD_SIZE // 2, dtype=jnp.float32) * 2.0 / HEAD_SIZE)
    angle_table = position.astype(jnp.float32)[:, None] * inv_freq[None, :]
    cosine = jnp.cos(angle_table)[:, None, :]
    sine_table = jnp.sin(angle_table)[:, None, :]
    query_rot = lowered_inputs(rotate(query_proj, cosine, sine_table))
    key_rot = lowered_inputs(rotate(key_projected, cosine, sine_table))
    heads_per_group = QUERY_HEADS // KEY_VALUE_HEADS
    score_scale = HEAD_SIZE ** (-0.5)

    def attend(block_args):
        row_index, query_tile_rows = block_args
        grouped_queries = query_tile_rows.reshape(-1, KEY_VALUE_HEADS, heads_per_group, HEAD_SIZE)
        raw_scores = jnp.einsum('qngd,knd->ngqk', grouped_queries, key_rot, precision=PRECISE) * score_scale
        raw_scores = lowered_backward(raw_scores)
        masked = jnp.where(block_mask(row_index)[None, None], raw_scores, -1e+30)
        log_total = jax.nn.logsumexp(masked, axis=-1, keepdims=True)
        weights = lowered_inputs(jnp.exp(masked - log_total))
        block_out = jnp.einsum('ngqk,knd->qngd', weights, value_projected, precision=PRECISE)
        return block_out.reshape(-1, QUERY_HEADS * HEAD_SIZE)
    query_rows = math.gcd(count_of_tokens, 512)
    block_count = count_of_tokens // query_rows
    attended = lax.map(jax.checkpoint(attend), (index_all.reshape(block_count, query_rows), query_rot.reshape(block_count, query_rows, QUERY_HEADS, HEAD_SIZE)))
    attended = lowered_inputs(lowered_backward(attended.reshape(count_of_tokens, QUERY_HEADS * HEAD_SIZE)))
    middle = tokens + lowered_backward(matrix_product(attended, o_weight.T))
    unit_two = normalize(middle)
    normed_two = lowered_inputs(unit_two * mlp_gain)
    gate_value = lowered_backward(matrix_product(normed_two, gate_weight))
    up_value = lowered_backward(matrix_product(normed_two, up_weight))
    hidden = lowered_inputs(jax.nn.silu(gate_value) * up_value)
    return middle + lowered_backward(matrix_product(hidden, down_weight.T))

def reference(prompt_x, cont_x, prompt_len, cont_seg, attn_gain, q_weight, key_matrix, value_matrix, o_weight, mlp_gain, gate_weight, up_weight, down_weight, prompt_cot, cont_cot):
    params = tuple((weight.astype(jnp.float32) for weight in (attn_gain, q_weight, key_matrix, value_matrix, o_weight, mlp_gain, gate_weight, up_weight, down_weight)))
    prompt_in = prompt_x.astype(jnp.float32).reshape(N_DP, PROMPT, MODEL_WIDTH)
    cont_in = cont_x.astype(jnp.float32).reshape(N_DP, N_CONTEXT * CONT_DEV, MODEL_WIDTH)
    segments = cont_seg.reshape(N_DP, N_CONTEXT, CONT_DEV)

    def forward(weights_all, prompt_all, cont_all):

        def run_group(group_args):
            prompt_part, cont_part, length, segment_rows = group_args
            result = jax.checkpoint(group_layer)(weights_all, prompt_part, cont_part, length, segment_rows)
            return (result[:PROMPT], result[PROMPT:])
        return lax.map(run_group, (prompt_all, cont_all, prompt_len, segments))
    (prompt_out, cont_out), pullback = jax.vjp(forward, params, prompt_in, cont_in)
    cot_prompt = prompt_cot.astype(jnp.float32).reshape(N_DP, PROMPT, MODEL_WIDTH)
    cot_cont = cont_cot.astype(jnp.float32).reshape(N_DP, N_CONTEXT * CONT_DEV, MODEL_WIDTH)
    weight_grads, prompt_grad, cont_grad = pullback((cot_prompt, cot_cont))
    return (prompt_out.reshape(-1, MODEL_WIDTH).astype(jnp.bfloat16), cont_out.reshape(-1, MODEL_WIDTH).astype(jnp.bfloat16), prompt_grad.reshape(-1, MODEL_WIDTH), cont_grad.reshape(-1, MODEL_WIDTH), weight_grads[0], weight_grads[1], weight_grads[2], weight_grads[3], weight_grads[4], weight_grads[5], weight_grads[6], weight_grads[7], weight_grads[8])
```

```python
import jax
import jax.numpy as jnp
from jax import lax
from jax.sharding import PartitionSpec as P

HEAD_SIZE = 80


EPS = 1e-05
THETA = 10000.0
NEGATIVE = -1e30


def normalize(values):
    inverse = lax.rsqrt(jnp.mean(values * values, axis=-1, keepdims=True) + EPS)
    return (values * inverse, inverse)


def norm_back(grad_unit, unit_rows, inverse):
    inner_sum = jnp.mean(grad_unit * unit_rows, axis=-1, keepdims=True)
    return inverse * (grad_unit - unit_rows * inner_sum)


def rotate(values, cosine, sine_table, direction):
    half_dim = values.shape[-1] // 2
    first_half = values[..., :half_dim]
    second_half = values[..., half_dim:]
    return jnp.concatenate(
        [
            first_half * cosine - direction * second_half * sine_table,
            second_half * cosine + direction * first_half * sine_table,
        ],
        axis=-1,
    )


def contract_last(left_side, right_side):
    return lax.dot_general(
        left_side, right_side, (((1,), (1,)), ((), ())), preferred_element_type=jnp.float32
    )


def contract_first(left_side, right_side):
    return lax.dot_general(
        left_side, right_side, (((0,), (0,)), ((), ())), preferred_element_type=jnp.float32
    )


def per_device(
    prompt_x,
    cont_x,
    prompt_len,
    cont_seg,
    attn_gain,
    q_weight,
    key_matrix,
    value_matrix,
    o_weight,
    mlp_gain,
    gate_weight,
    up_weight,
    down_weight,
    prompt_cot,
    cont_cot,
):
    head_dim = HEAD_SIZE
    prompt_rows = prompt_x.shape[0]
    cont_rows = cont_x.shape[0]
    row_count = prompt_rows + cont_rows
    prompt_total = prompt_rows * lax.axis_size("context")
    q_cols = q_weight.shape[1]
    kv_cols = key_matrix.shape[1]
    attn_cols = 2 * q_cols + 2 * kv_cols
    pad_cols = -(attn_cols + 2) % 128
    packed = jnp.concatenate(
        [
            o_weight,
            q_weight,
            key_matrix,
            value_matrix,
            attn_gain[:, None],
            mlp_gain[:, None],
            jnp.zeros((q_weight.shape[0], pad_cols), jnp.bfloat16),
        ],
        axis=1,
    )
    packed_full = lax.all_gather(packed, ("dp", "context"), axis=0, tiled=True)
    gain_one = packed_full[:, attn_cols].astype(jnp.float32)
    gain_two = packed_full[:, attn_cols + 1].astype(jnp.float32)
    wo_full = packed_full[:, :q_cols]
    wq_full = packed_full[:, q_cols : 2 * q_cols]
    wqkv_full = packed_full[:, q_cols:attn_cols]
    wk_full = packed_full[:, 2 * q_cols : 2 * q_cols + kv_cols]
    q_heads = wq_full.shape[1] // head_dim
    kv_heads = wk_full.shape[1] // head_dim
    heads_per_group = q_heads // kv_heads
    score_scale = head_dim ** (-0.5)
    context_pos = lax.axis_index("context")
    prompt_pos = context_pos * prompt_rows + jnp.arange(prompt_rows, dtype=jnp.int32)
    segment = cont_seg[0]
    earlier = jnp.sum((segment[None, :] < segment[:, None]).astype(jnp.int32), axis=1)
    local_index = jnp.arange(cont_rows, dtype=jnp.int32)
    length = prompt_len[0]
    cont_pos = length + local_index - earlier
    position = jnp.concatenate([prompt_pos, cont_pos]).astype(jnp.float32)
    half_dim = head_dim // 2
    inv_freq = THETA ** (-jnp.arange(half_dim, dtype=jnp.float32) * 2.0 / head_dim)
    angle_table = position[:, None] * inv_freq[None, :]
    cosine = jnp.cos(angle_table)[:, None, :]
    sine_table = jnp.sin(angle_table)[:, None, :]
    key_index = jnp.arange(prompt_total, dtype=jnp.int32)
    prompt_mask = jnp.concatenate(
        [key_index[None, :] <= prompt_pos[:, None], jnp.zeros((prompt_rows, cont_rows), jnp.bool_)],
        axis=1,
    )
    own_mask = (segment[None, :] == segment[:, None]) & (
        local_index[None, :] <= local_index[:, None]
    )
    reach_mask = jnp.broadcast_to(key_index[None, :] < length, (cont_rows, prompt_total))
    cont_mask = jnp.concatenate([reach_mask, own_mask], axis=1)
    allowed = jnp.concatenate([prompt_mask, cont_mask], axis=0)
    inputs = jnp.concatenate([prompt_x, cont_x], axis=0).astype(jnp.float32)
    unit_one, inv_one = normalize(inputs)
    first_normed = (unit_one * gain_one).astype(jnp.bfloat16)
    qkv = jnp.dot(first_normed, wqkv_full, preferred_element_type=jnp.float32)
    query_proj = qkv[:, :q_cols].reshape(row_count, q_heads, head_dim)
    key_projected = qkv[:, q_cols : q_cols + kv_cols].reshape(row_count, kv_heads, head_dim)
    value_projected = qkv[:, q_cols + kv_cols :]
    query_rot = rotate(query_proj, cosine, sine_table, 1.0).astype(jnp.bfloat16)
    key_rot = (
        rotate(key_projected, cosine, sine_table, 1.0)
        .astype(jnp.bfloat16)
        .reshape(row_count, kv_heads * head_dim)
    )
    value_rot = value_projected.astype(jnp.bfloat16)
    prompt_kv = lax.all_gather(
        jnp.concatenate([key_rot[:prompt_rows], value_rot[:prompt_rows]], axis=1),
        "context",
        axis=0,
        tiled=True,
    )
    prompt_keys, prompt_values = prompt_kv[:, :kv_cols], prompt_kv[:, kv_cols:]
    all_keys = jnp.concatenate([prompt_keys, key_rot[prompt_rows:]], axis=0).reshape(
        -1, kv_heads, head_dim
    )
    all_values = jnp.concatenate([prompt_values, value_rot[prompt_rows:]], axis=0).reshape(
        -1, kv_heads, head_dim
    )

    def scores_of(head_index):
        grouped_queries = query_rot[
            :, head_index * heads_per_group : (head_index + 1) * heads_per_group, :
        ]
        raw_scores = (
            jnp.einsum(
                "rgd,kd->grk",
                grouped_queries,
                all_keys[:, head_index, :],
                preferred_element_type=jnp.float32,
            )
            * score_scale
        )
        return (grouped_queries, jnp.where(allowed[None], raw_scores, NEGATIVE))

    head_outputs = []
    log_totals = []
    for head_index in range(kv_heads):
        grouped_queries, masked = scores_of(head_index)
        log_total = jax.nn.logsumexp(masked, axis=-1)
        weights = jnp.exp(masked - log_total[..., None]).astype(jnp.bfloat16)
        head_outputs.append(
            jnp.einsum(
                "grk,kd->rgd",
                weights,
                all_values[:, head_index, :],
                preferred_element_type=jnp.float32,
            )
        )
        log_totals.append(log_total)
    attn_out = (
        jnp.concatenate(head_outputs, axis=1)
        .reshape(row_count, q_heads * head_dim)
        .astype(jnp.bfloat16)
    )
    attn_sum = lax.psum(contract_last(attn_out, wo_full).astype(jnp.bfloat16), "tensor")
    middle = inputs + attn_sum.astype(jnp.float32)
    mlp_set = (
        None,
        lax.all_gather(gate_weight, ("dp", "context"), axis=0, tiled=True),
        lax.all_gather(up_weight, ("dp", "context"), axis=0, tiled=True),
        lax.all_gather(down_weight, ("dp", "context"), axis=0, tiled=True),
    )
    unit_two, inv_two = normalize(middle)
    normed_two = (unit_two * gain_two).astype(jnp.bfloat16)
    gate_value = jnp.dot(normed_two, mlp_set[1], preferred_element_type=jnp.float32)
    up_value = jnp.dot(normed_two, mlp_set[2], preferred_element_type=jnp.float32)
    sigmoid_gate = jax.nn.sigmoid(gate_value)
    silu_gate = gate_value * sigmoid_gate
    hidden = (silu_gate * up_value).astype(jnp.bfloat16)
    mlp_sum = lax.psum(contract_last(hidden, mlp_set[3]).astype(jnp.bfloat16), "tensor")
    result = middle + mlp_sum.astype(jnp.float32)
    back_mlp = mlp_set
    grad_out = jnp.concatenate([prompt_cot, cont_cot], axis=0)
    grad_hidden = jnp.dot(grad_out, back_mlp[3], preferred_element_type=jnp.float32)
    grad_down = contract_first(grad_out, hidden)
    grad_gate = (
        grad_hidden * up_value * sigmoid_gate * (1.0 + gate_value * (1.0 - sigmoid_gate))
    ).astype(jnp.bfloat16)
    grad_up = (grad_hidden * silu_gate).astype(jnp.bfloat16)
    grad_wg = contract_first(normed_two, grad_gate)
    grad_wu = contract_first(normed_two, grad_up)
    back_two = contract_last(grad_gate, back_mlp[1]) + contract_last(grad_up, back_mlp[2])
    back_two = lax.psum(back_two.astype(jnp.bfloat16), "tensor").astype(jnp.float32)
    grad_middle = grad_out.astype(jnp.float32) + norm_back(back_two * gain_two, unit_two, inv_two)
    grad_middle_b = grad_middle.astype(jnp.bfloat16)
    grad_attended = (
        jnp.dot(grad_middle_b, wo_full, preferred_element_type=jnp.float32)
        .astype(jnp.bfloat16)
        .reshape(row_count, q_heads, head_dim)
    )
    grad_wo = contract_first(grad_middle_b, attn_out)
    query_grads = []
    key_grads = []
    value_grads = []
    for head_index in range(kv_heads):
        grouped_queries, masked = scores_of(head_index)
        weights = jnp.exp(masked - log_totals[head_index][..., None])
        grad_head = grad_attended[
            :, head_index * heads_per_group : (head_index + 1) * heads_per_group, :
        ]
        grad_weights = jnp.einsum(
            "rgd,kd->grk",
            grad_head,
            all_values[:, head_index, :],
            preferred_element_type=jnp.float32,
        )
        inner_sum = jnp.sum(weights * grad_weights, axis=-1, keepdims=True)
        grad_scores = (weights * (grad_weights - inner_sum)).astype(jnp.bfloat16)
        query_grads.append(
            jnp.einsum(
                "grk,kd->rgd",
                grad_scores,
                all_keys[:, head_index, :],
                preferred_element_type=jnp.float32,
            )
            * score_scale
        )
        key_grads.append(
            jnp.einsum(
                "grk,rgd->kd", grad_scores, grouped_queries, preferred_element_type=jnp.float32
            )
            * score_scale
        )
        value_grads.append(
            jnp.einsum(
                "grk,rgd->kd",
                weights.astype(jnp.bfloat16),
                grad_head,
                preferred_element_type=jnp.float32,
            )
        )
    grad_query = jnp.concatenate(query_grads, axis=1)
    grad_key_all = jnp.stack(key_grads, axis=1).reshape(-1, kv_heads * head_dim)
    grad_value_all = jnp.stack(value_grads, axis=1).reshape(-1, kv_heads * head_dim)
    own_kv = lax.psum_scatter(
        jnp.concatenate([grad_key_all[:prompt_total], grad_value_all[:prompt_total]], axis=1),
        "context",
        scatter_dimension=0,
        tiled=True,
    )
    own_key, own_value = own_kv[:, :kv_cols], own_kv[:, kv_cols:]
    grad_key = jnp.concatenate([own_key, grad_key_all[prompt_total:]], axis=0).reshape(
        row_count, kv_heads, head_dim
    )
    grad_value = jnp.concatenate([own_value, grad_value_all[prompt_total:]], axis=0).astype(
        jnp.bfloat16
    )
    grad_query_b = (
        rotate(grad_query, cosine, sine_table, -1.0)
        .reshape(row_count, q_heads * head_dim)
        .astype(jnp.bfloat16)
    )
    grad_key_b = (
        rotate(grad_key, cosine, sine_table, -1.0)
        .reshape(row_count, kv_heads * head_dim)
        .astype(jnp.bfloat16)
    )
    grad_qkv = jnp.concatenate([grad_query_b, grad_key_b, grad_value], axis=1)
    grad_attn = jnp.concatenate([grad_wo, contract_first(first_normed, grad_qkv)], axis=1)
    back_one = contract_last(grad_qkv, wqkv_full).astype(jnp.bfloat16)
    back_one, mlp_sum = lax.optimization_barrier((back_one, mlp_sum))
    result = middle + mlp_sum.astype(jnp.float32)
    back_one = lax.psum(back_one, "tensor").astype(jnp.float32)
    grad_inputs = grad_middle + norm_back(back_one * gain_one, unit_one, inv_one)
    data = ("dp", "context")

    def scatter(values):
        return lax.psum_scatter(
            values.astype(jnp.bfloat16), data, scatter_dimension=0, tiled=True
        ).astype(jnp.float32)

    down_own = scatter(grad_down)
    gate_own = scatter(grad_wg)
    up_own = scatter(grad_wu)
    attn_own = scatter(grad_attn)
    o_own = attn_own[:, :q_cols]
    q_own = attn_own[:, q_cols : 2 * q_cols]
    k_own = attn_own[:, 2 * q_cols : 2 * q_cols + kv_cols]
    v_own = attn_own[:, 2 * q_cols + kv_cols :]

    def row_dot(weight, grad):
        return jnp.sum(weight.astype(jnp.float32) * grad, axis=1)

    gain_rows = jnp.stack(
        [
            (row_dot(q_weight, q_own) + row_dot(key_matrix, k_own) + row_dot(value_matrix, v_own))
            / attn_gain.astype(jnp.float32),
            (row_dot(gate_weight, gate_own) + row_dot(up_weight, up_own))
            / mlp_gain.astype(jnp.float32),
        ]
    )
    gain_rows = lax.psum(gain_rows, "tensor")
    owned = (gain_rows[0], q_own, k_own, v_own, o_own, gain_rows[1], gate_own, up_own, down_own)
    return (
        result[:prompt_rows].astype(jnp.bfloat16),
        result[prompt_rows:].astype(jnp.bfloat16),
        grad_inputs[:prompt_rows],
        grad_inputs[prompt_rows:],
        owned[0],
        owned[1],
        owned[2],
        owned[3],
        owned[4],
        owned[5],
        owned[6],
        owned[7],
        owned[8],
    )


def solution(mesh):
    in_specs = (
        P(("dp", "context"), None),
        P(("dp", "context"), None),
        P("dp"),
        P(("dp", "context"), None),
        P(("dp", "context")),
        P(("dp", "context"), "tensor"),
        P(("dp", "context"), "tensor"),
        P(("dp", "context"), "tensor"),
        P(("dp", "context"), "tensor"),
        P(("dp", "context")),
        P(("dp", "context"), "tensor"),
        P(("dp", "context"), "tensor"),
        P(("dp", "context"), "tensor"),
        P(("dp", "context"), None),
        P(("dp", "context"), None),
    )
    out_specs = (
        P(("dp", "context"), None),
        P(("dp", "context"), None),
        P(("dp", "context"), None),
        P(("dp", "context"), None),
        P(("dp", "context")),
        P(("dp", "context"), "tensor"),
        P(("dp", "context"), "tensor"),
        P(("dp", "context"), "tensor"),
        P(("dp", "context"), "tensor"),
        P(("dp", "context")),
        P(("dp", "context"), "tensor"),
        P(("dp", "context"), "tensor"),
        P(("dp", "context"), "tensor"),
    )
    return jax.shard_map(
        per_device, mesh=mesh, in_specs=in_specs, out_specs=out_specs, check_vma=False
    )
```

```python
import functools
import math

import jax
import jax.numpy as jnp
from jax import lax
from jax.experimental import pallas as pl
from jax.experimental.pallas import tpu as pltpu
from jax.sharding import PartitionSpec as P

HEAD_SIZE = 80


EPS = 1e-05
THETA = 10000.0
NEGATIVE = -1e30
LOG2E = math.log2(math.e)
MESH = pl.DeviceIdType.MESH
AXIS = "tensor"


def line_kernel(blocks, part_ref, out_ref, recv, both, s_up, s_mid, s_dn, r_up, r_mid, r_dn):
    me = lax.axis_index(AXIS)
    n = lax.axis_size(AXIS)
    half = n // 2
    outer = (me == 0) | (me == n - 1)
    mate = jnp.where(me < half, 1 - me, 2 * n - 3 - me)
    across = n - 1 - me
    rows = part_ref.shape[0] // blocks
    barrier = pltpu.get_barrier_semaphore()

    def sl(b):
        return pl.ds(pl.multiple_of(b * rows, rows), rows)

    def up(b):
        return pltpu.make_async_remote_copy(
            part_ref.at[sl(b)], recv.at[sl(b)], s_up.at[b], r_up.at[b],
            device_id={AXIS: mate}, device_id_type=MESH)

    def mid(b):
        return pltpu.make_async_remote_copy(
            both.at[sl(b)], out_ref.at[sl(b)], s_mid.at[b], r_mid.at[b],
            device_id={AXIS: across}, device_id_type=MESH)

    def down(b):
        return pltpu.make_async_remote_copy(
            out_ref.at[sl(b)], out_ref.at[sl(b)], s_dn.at[b], r_dn.at[b],
            device_id={AXIS: mate}, device_id_type=MESH)

    @pl.when(outer)
    def _():
        pl.semaphore_signal(barrier, inc=1, device_id={AXIS: mate}, device_id_type=MESH)
        pl.semaphore_wait(barrier, 1)

        @pl.loop(0, blocks)
        def _(b):
            up(b).start()

        @pl.loop(0, blocks)
        def _(b):
            down(b).wait_recv()
            up(b).wait_send()

    @pl.when(jnp.logical_not(outer))
    def _():
        pl.semaphore_signal(barrier, inc=1, device_id={AXIS: mate}, device_id_type=MESH)
        pl.semaphore_signal(barrier, inc=1, device_id={AXIS: across}, device_id_type=MESH)
        pl.semaphore_wait(barrier, 2)

        @pl.loop(0, blocks + 1)
        def _(t):
            @pl.when(t < blocks)
            def _():
                up(t).wait_recv()
                both[sl(t), :] = (part_ref[sl(t), :].astype(jnp.float32) + recv[sl(t), :].astype(jnp.float32)).astype(jnp.bfloat16)
                mid(t).start()

            @pl.when(t >= 1)
            def _():
                b = t - 1
                mid(b).wait_recv()
                out_ref[sl(b), :] = (both[sl(b), :].astype(jnp.float32) + out_ref[sl(b), :].astype(jnp.float32)).astype(jnp.bfloat16)
                down(b).start()

        @pl.loop(0, blocks)
        def _(b):
            mid(b).wait_send()
            down(b).wait_send()


def line_sum(part, cid):
    shape = part.shape
    blocks = shape[0] // 32
    return pl.pallas_call(
        functools.partial(line_kernel, blocks),
        out_shape=jax.ShapeDtypeStruct(shape, jnp.bfloat16),
        in_specs=[pl.BlockSpec(memory_space=pltpu.VMEM)],
        out_specs=pl.BlockSpec(memory_space=pltpu.VMEM),
        scratch_shapes=[pltpu.VMEM(shape, jnp.bfloat16)] * 2
        + [pltpu.SemaphoreType.DMA((blocks,))] * 6,
        compiler_params=pltpu.CompilerParams(collective_id=cid, has_side_effects=True, vmem_limit_bytes=40 << 20
        ),
        cost_estimate=pl.CostEstimate(
            flops=120_000_000_000, bytes_accessed=4 * part.size, transcendentals=0
        ),
    )(part)


def normalize(values):
    inverse = lax.rsqrt(jnp.mean(values * values, axis=-1, keepdims=True) + EPS)
    return (values * inverse, inverse)


def norm_back(grad_unit, unit_rows, inverse):
    inner_sum = jnp.mean(grad_unit * unit_rows, axis=-1, keepdims=True)
    return inverse * (grad_unit - unit_rows * inner_sum)


def contract_last(left_side, right_side):
    return lax.dot_general(
        left_side, right_side, (((1,), (1,)), ((), ())), preferred_element_type=jnp.float32
    )


def contract_first(left_side, right_side):
    return lax.dot_general(
        left_side, right_side, (((0,), (0,)), ((), ())), preferred_element_type=jnp.float32
    )


def rope_kernel(q_heads, kv_heads, dim, x_ref, w_ref, gain_ref, cos_ref, sin_ref, normed_ref, qt_ref, kvt_ref):
    rows = x_ref[...].astype(jnp.float32)
    inverse = lax.rsqrt(jnp.mean(rows * rows, axis=-1, keepdims=True) + EPS)
    normed = (rows * inverse * gain_ref[...]).astype(jnp.bfloat16)
    normed_ref[...] = normed
    flat = jnp.dot(normed, w_ref[...], preferred_element_type=jnp.float32).T
    cosine, sine = cos_ref[...], sin_ref[...]
    half = dim // 2
    for head in range(q_heads + kv_heads):
        first = flat[head * dim : head * dim + half]
        second = flat[head * dim + half : (head + 1) * dim]
        turned = jnp.concatenate(
            [first * cosine - second * sine, second * cosine + first * sine], axis=0
        ).astype(jnp.bfloat16)
        if head < q_heads:
            qt_ref[head * dim : (head + 1) * dim, :] = turned
        else:
            at = (head - q_heads) * dim
            kvt_ref[at : at + dim, :] = turned
    at = (q_heads + kv_heads) * dim
    kvt_ref[kv_heads * dim :, :] = flat[at : at + kv_heads * dim].astype(jnp.bfloat16)


def project_rope(x, packed_full, gain, cos_t, sin_t, q_heads, kv_heads):
    rows, width = x.shape
    dim = HEAD_SIZE
    step = math.gcd(rows, 256)
    cols = (q_heads + 2 * kv_heads) * dim
    cols_wide = cols + -cols % 128
    by_row = lambda i: (i, 0)
    by_col = lambda i: (0, i)
    fixed = lambda i: (0, 0)
    return pl.pallas_call(
        functools.partial(rope_kernel, q_heads, kv_heads, dim),
        grid=(rows // step,),
        in_specs=[
            pl.BlockSpec((step, width), by_row),
            pl.BlockSpec((width, cols_wide), fixed, pipeline_mode=pl.Buffered(1)),
            pl.BlockSpec((1, width), fixed),
            pl.BlockSpec((dim // 2, step), by_col),
            pl.BlockSpec((dim // 2, step), by_col),
        ],
        out_specs=[
            pl.BlockSpec((step, width), by_row),
            pl.BlockSpec((q_heads * dim, step), by_col),
            pl.BlockSpec((2 * kv_heads * dim, step), by_col),
        ],
        out_shape=[
            jax.ShapeDtypeStruct((rows, width), jnp.bfloat16),
            jax.ShapeDtypeStruct((q_heads * dim, rows), jnp.bfloat16),
            jax.ShapeDtypeStruct((2 * kv_heads * dim, rows), jnp.bfloat16),
        ],
        compiler_params=pltpu.CompilerParams(vmem_limit_bytes=48 << 20),
        cost_estimate=pl.CostEstimate(
            flops=2 * rows * width * cols_wide,
            bytes_accessed=4 * x.size + 2 * width * cols_wide,
            transcendentals=0,
        ),
    )(x, packed_full, gain, cos_t, sin_t)


def greet(axis, count):
    me = lax.axis_index(axis)
    barrier = pltpu.get_barrier_semaphore()
    for k in range(1, count):
        peer = lax.rem(me + k, count)
        pl.semaphore_signal(barrier, inc=1, device_id={axis: peer}, device_id_type=MESH)
    pl.semaphore_wait(barrier, count - 1)


def gather_kernel(count, own_ref, all_ref, send, recv, local):
    me = lax.axis_index("context")
    keep = pltpu.make_async_copy(own_ref, all_ref.at[me], local)
    keep.start()
    greet("context", count)
    copies = []
    for k in range(1, count):
        peer = lax.rem(me + k, count)
        copy = pltpu.make_async_remote_copy(
            own_ref,
            all_ref.at[me],
            send.at[k],
            recv.at[k],
            device_id={"context": peer},
            device_id_type=MESH,
        )
        copy.start()
        copies.append(copy)
    keep.wait()
    for copy in copies:
        copy.wait()


def context_gather(own, cid):
    count = lax.axis_size("context")
    return pl.pallas_call(
        functools.partial(gather_kernel, count),
        out_shape=jax.ShapeDtypeStruct((count, *own.shape), own.dtype),
        in_specs=[pl.BlockSpec(memory_space=pltpu.VMEM)],
        out_specs=pl.BlockSpec(memory_space=pltpu.VMEM),
        scratch_shapes=[
            pltpu.SemaphoreType.DMA((count,)),
            pltpu.SemaphoreType.DMA((count,)),
            pltpu.SemaphoreType.DMA,
        ],
        compiler_params=pltpu.CompilerParams(collective_id=cid, has_side_effects=True),
        cost_estimate=pl.CostEstimate(flops=0, bytes_accessed=8 << 20, transcendentals=0),
    )(own)


def scatter_kernel(count, kv_dim, dim, part_ref, own_ref, cos_ref, sin_ref, rows_ref, got, send, recv):
    me = lax.axis_index("context")
    greet("context", count)
    copies = []
    for k in range(1, count):
        peer = lax.rem(me + k, count)
        copy = pltpu.make_async_remote_copy(
            part_ref.at[peer],
            got.at[k],
            send.at[k],
            recv.at[k],
            device_id={"context": peer},
            device_id_type=MESH,
        )
        copy.start()
        copies.append(copy)
    prompt_rows = part_ref.shape[2]
    cosine, sine = cos_ref[...], sin_ref[...]
    half = dim // 2

    def finish(flat, cosine, sine):
        pieces = []
        for at in range(0, kv_dim, dim):
            first, second = flat[at : at + half], flat[at + half : at + dim]
            pieces += [first * cosine + second * sine, second * cosine - first * sine]
        pieces.append(flat[kv_dim:])
        return jnp.concatenate(pieces, axis=0).T.astype(jnp.bfloat16)

    rows_ref[prompt_rows:, :] = finish(own_ref[...], cosine[:, prompt_rows:], sine[:, prompt_rows:])
    total = part_ref[me].astype(jnp.float32)
    for k in range(1, count):
        copies[k - 1].wait()
        total += got[k].astype(jnp.float32)
    rows_ref[:prompt_rows, :] = finish(total, cosine[:, :prompt_rows], sine[:, :prompt_rows])


def context_scatter(part, own, cos_t, sin_t, cid):
    count, kv2, prompt_rows = part.shape
    rows = prompt_rows + own.shape[1]
    return pl.pallas_call(
        functools.partial(scatter_kernel, count, kv2 // 2, HEAD_SIZE),
        out_shape=jax.ShapeDtypeStruct((rows, kv2), jnp.bfloat16),
        in_specs=[pl.BlockSpec(memory_space=pltpu.VMEM)] * 4,
        out_specs=pl.BlockSpec(memory_space=pltpu.VMEM),
        scratch_shapes=[
            pltpu.VMEM(part.shape, part.dtype),
            pltpu.SemaphoreType.DMA((count,)),
            pltpu.SemaphoreType.DMA((count,)),
        ],
        compiler_params=pltpu.CompilerParams(collective_id=cid, has_side_effects=True),
        cost_estimate=pl.CostEstimate(flops=0, bytes_accessed=8 << 20, transcendentals=0),
    )(part, own, cos_t, sin_t)


def attend_shape(prompt_all, kvt_cont):
    count, kv2, prompt_rows = prompt_all.shape
    cont_rows = kvt_cont.shape[1]
    chunk = math.gcd(math.gcd(prompt_rows, cont_rows), 256)
    return count, kv2, prompt_rows, cont_rows, chunk


def fill_keys(first, chunk, dim, kv_heads, all_ref, cont_ref, rows_of, chunks_ref):
    count, _, prompt_rows = all_ref.shape
    per = prompt_rows // chunk
    total = count * per + cont_ref.shape[1] // chunk
    for c in range(total):
        if c < count * per:
            block = all_ref[c // per, :, (c % per) * chunk : (c % per + 1) * chunk]
        else:
            at = (c - count * per) * chunk
            block = cont_ref[:, at : at + chunk]
        chunks_ref[c] = block
        for n, target in enumerate(rows_of):
            for g in range(kv_heads):
                at = (n * kv_heads + g) * dim
                target[g, c * chunk : (c + 1) * chunk, :] = (
                    block[at : at + dim].astype(jnp.float32).T.astype(jnp.bfloat16)
                )


def trip_count(len_ref, tile, chunk, i, prompt_rows, count):
    me = lax.axis_index("context")
    prompt_tiles = prompt_rows // tile
    own = me * prompt_rows + (i + 1) * tile
    return i < prompt_tiles, (own + chunk - 1) // chunk, (len_ref[0] + chunk - 1) // chunk, (
        (i - prompt_tiles + 1) * tile + chunk - 1
    ) // chunk


def attend_kernel(
    shape, dim, kv_heads, per, tile, len_ref, q_ref, all_ref, cont_ref, bias_ref, out_ref, lse_ref, keys, chunks
):
    count, prompt_rows, chunk = shape
    i = pl.program_id(0)

    @pl.when(i == 0)
    def _():
        fill_keys(i, chunk, dim, kv_heads, all_ref, cont_ref, [keys], chunks)

    is_prompt, n_prompt, n_len, n_own = trip_count(len_ref, tile, chunk, i, prompt_rows, count)
    base = count * prompt_rows // chunk
    wide = per * tile
    factor = dim ** (-0.5) * LOG2E
    outs, sums = [], []
    for g in range(kv_heads):
        q = jnp.concatenate(
            [q_ref[(g * per + h) * dim : (g * per + h + 1) * dim, :] for h in range(per)], axis=1
        )

        def body(c, state):
            top, total, acc = state
            s = jnp.dot(
                keys[g, pl.ds(pl.multiple_of(c * chunk, chunk), chunk), :],
                q,
                preferred_element_type=jnp.float32,
            )
            b = bias_ref[pl.ds(pl.multiple_of(c * chunk, chunk), chunk), :]
            t = s * factor + jnp.concatenate([b] * per, axis=1)
            new = jnp.maximum(top, jnp.max(t, axis=0, keepdims=True))
            p = jnp.exp2(t - new)
            scale = jnp.exp2(top - new)
            total = total * scale + jnp.sum(p, axis=0, keepdims=True)
            v = chunks[c, (kv_heads + g) * dim : (kv_heads + g + 1) * dim, :]
            acc = acc * scale + jnp.dot(
                v, p.astype(jnp.bfloat16), preferred_element_type=jnp.float32
            )
            return new, total, acc

        start = (
            jnp.full((1, wide), NEGATIVE, jnp.float32),
            jnp.zeros((1, wide), jnp.float32),
            jnp.zeros((dim, wide), jnp.float32),
        )
        state = lax.fori_loop(0, jnp.where(is_prompt, n_prompt, n_len), body, start)
        top, total, acc = lax.fori_loop(base, base + jnp.where(is_prompt, 0, n_own), body, state)
        acc = acc / total
        top = top + jnp.log2(total)
        outs += [acc[:, h * tile : (h + 1) * tile] for h in range(per)]
        sums += [top[:, h * tile : (h + 1) * tile] for h in range(per)]
    out_ref[...] = jnp.concatenate(outs, axis=0).T.astype(jnp.bfloat16)
    lse_ref[...] = jnp.concatenate(sums, axis=0)


def attend(length, q_t, prompt_all, kvt_cont, bias, q_heads, kv_heads):
    dim = HEAD_SIZE
    count, kv2, prompt_rows, cont_rows, chunk = attend_shape(prompt_all, kvt_cont)
    rows = q_t.shape[1]
    keys_all = bias.shape[0]
    tile = 128
    whole = pl.BlockSpec(memory_space=pltpu.VMEM)
    by_col = lambda i, _: (0, i)
    return pl.pallas_call(
        functools.partial(
            attend_kernel, (count, prompt_rows, chunk), dim, kv_heads, q_heads // kv_heads, tile
        ),
        grid_spec=pltpu.PrefetchScalarGridSpec(
            num_scalar_prefetch=1,
            grid=(rows // tile,),
            in_specs=[
                pl.BlockSpec((q_t.shape[0], tile), by_col),
                whole,
                whole,
                pl.BlockSpec((keys_all, tile), by_col),
            ],
            out_specs=[
                pl.BlockSpec((tile, q_t.shape[0]), lambda i, _: (i, 0)),
                pl.BlockSpec((q_heads, tile), by_col),
            ],
            scratch_shapes=[
                pltpu.VMEM((kv_heads, keys_all, dim), jnp.bfloat16),
                pltpu.VMEM((keys_all // chunk, kv2, chunk), jnp.bfloat16),
            ],
        ),
        out_shape=[
            jax.ShapeDtypeStruct((rows, q_t.shape[0]), jnp.bfloat16),
            jax.ShapeDtypeStruct((q_heads, rows), jnp.float32),
        ],
        compiler_params=pltpu.CompilerParams(vmem_limit_bytes=40 << 20),
        cost_estimate=pl.CostEstimate(
            flops=20_000_000_000, bytes_accessed=4 * bias.size, transcendentals=0
        ),
    )(length, q_t, prompt_all, kvt_cont, bias)


def attend_back_kernel(
    shape,
    dim,
    kv_heads,
    per,
    tile,
    len_ref,
    q_ref,
    all_ref,
    cont_ref,
    bias_ref,
    out_ref,
    lse_ref,
    grad_ref,
    cos_ref,
    sin_ref,
    gq_ref,
    part_ref,
    own_ref,
    keys,
    values,
    chunks,
    gk,
    gv,
):
    count, prompt_rows, chunk = shape
    i = pl.program_id(0)

    @pl.when(i == 0)
    def _():
        fill_keys(i, chunk, dim, kv_heads, all_ref, cont_ref, [keys, values], chunks)
        gk[...] = jnp.zeros_like(gk)
        gv[...] = jnp.zeros_like(gv)

    is_prompt, n_prompt, n_len, n_own = trip_count(len_ref, tile, chunk, i, prompt_rows, count)
    base = count * prompt_rows // chunk
    root = dim ** (-0.5)
    factor = root * LOG2E
    grad_t = grad_ref[...].astype(jnp.float32).T
    prod = grad_t * out_ref[...].astype(jnp.float32).T
    grad_t = grad_t.astype(jnp.bfloat16)
    cosine, sine = cos_ref[...], sin_ref[...]
    half = dim // 2
    pieces = []
    for g in range(kv_heads):
        heads = [g * per + h for h in range(per)]
        q = jnp.concatenate([q_ref[h * dim : (h + 1) * dim, :] for h in heads], axis=1)
        go = jnp.concatenate([grad_t[h * dim : (h + 1) * dim] for h in heads], axis=1)
        inner = jnp.concatenate(
            [jnp.sum(prod[h * dim : (h + 1) * dim], axis=0, keepdims=True) for h in heads], axis=1
        )
        lse = jnp.concatenate([lse_ref[h : h + 1, :] for h in heads], axis=1)

        def body(c, acc):
            at = pl.ds(pl.multiple_of(c * chunk, chunk), chunk)
            s = jnp.dot(keys[g, at, :], q, preferred_element_type=jnp.float32)
            b = bias_ref[at, :]
            p = jnp.exp2(s * factor + (jnp.concatenate([b] * per, axis=1) - lse))
            dp = jnp.dot(values[g, at, :], go, preferred_element_type=jnp.float32)
            ds = (p * (dp - inner)).astype(jnp.bfloat16)
            gv[g, at, :] += contract_last(p.astype(jnp.bfloat16), go)
            gk[g, at, :] += contract_last(ds, q)
            k_t = chunks[c, g * dim : (g + 1) * dim, :]
            return acc + jnp.dot(k_t, ds, preferred_element_type=jnp.float32)

        acc = jnp.zeros((dim, per * tile), jnp.float32)
        acc = lax.fori_loop(0, jnp.where(is_prompt, n_prompt, n_len), body, acc)
        acc = lax.fori_loop(base, base + jnp.where(is_prompt, 0, n_own), body, acc)
        acc = acc * root
        for h in range(per):
            first = acc[:half, h * tile : (h + 1) * tile]
            second = acc[half:, h * tile : (h + 1) * tile]
            pieces += [first * cosine + second * sine, second * cosine - first * sine]
    gq_ref[...] = jnp.concatenate(pieces, axis=0).T.astype(jnp.bfloat16)

    @pl.when(i == pl.num_programs(0) - 1)
    def _():
        for g in range(kv_heads):
            for n, (acc, scale) in enumerate(((gk, root), (gv, 1.0))):
                at = (n * kv_heads + g) * dim
                for c in range(count):
                    rows = acc[g, c * prompt_rows : (c + 1) * prompt_rows, :]
                    part_ref[c, at : at + dim, :] = (rows * scale).T.astype(jnp.bfloat16)
                own_ref[at : at + dim, :] = (acc[g, count * prompt_rows :, :] * scale).T


def attend_back(
    length, q_t, prompt_all, kvt_cont, bias, attended, lse, grad, cos_t, sin_t, q_heads, kv_heads
):
    dim = HEAD_SIZE
    count, kv2, prompt_rows, cont_rows, chunk = attend_shape(prompt_all, kvt_cont)
    rows = q_t.shape[1]
    keys_all = bias.shape[0]
    tile = 128
    whole = pl.BlockSpec(memory_space=pltpu.VMEM)
    by_col = lambda i, _: (0, i)
    by_row = lambda i, _: (i, 0)
    return pl.pallas_call(
        functools.partial(
            attend_back_kernel, (count, prompt_rows, chunk), dim, kv_heads, q_heads // kv_heads, tile
        ),
        grid_spec=pltpu.PrefetchScalarGridSpec(
            num_scalar_prefetch=1,
            grid=(rows // tile,),
            in_specs=[
                pl.BlockSpec((q_t.shape[0], tile), by_col),
                whole,
                whole,
                pl.BlockSpec((keys_all, tile), by_col),
                pl.BlockSpec((tile, q_t.shape[0]), by_row),
                pl.BlockSpec((q_heads, tile), by_col),
                pl.BlockSpec((tile, q_t.shape[0]), by_row),
                pl.BlockSpec((dim // 2, tile), by_col),
                pl.BlockSpec((dim // 2, tile), by_col),
            ],
            out_specs=[
                pl.BlockSpec((tile, q_t.shape[0]), by_row),
                pl.BlockSpec((count, kv2, prompt_rows), lambda i, _: (0, 0, 0)),
                pl.BlockSpec((kv2, cont_rows), lambda i, _: (0, 0)),
            ],
            scratch_shapes=[
                pltpu.VMEM((kv_heads, keys_all, dim), jnp.bfloat16),
                pltpu.VMEM((kv_heads, keys_all, dim), jnp.bfloat16),
                pltpu.VMEM((keys_all // chunk, kv2, chunk), jnp.bfloat16),
                pltpu.VMEM((kv_heads, keys_all, dim), jnp.float32),
                pltpu.VMEM((kv_heads, keys_all, dim), jnp.float32),
            ],
        ),
        out_shape=[
            jax.ShapeDtypeStruct((rows, q_t.shape[0]), jnp.bfloat16),
            jax.ShapeDtypeStruct((count, kv2, prompt_rows), jnp.bfloat16),
            jax.ShapeDtypeStruct((kv2, cont_rows), jnp.float32),
        ],
        compiler_params=pltpu.CompilerParams(vmem_limit_bytes=48 << 20),
        cost_estimate=pl.CostEstimate(
            flops=40_000_000_000, bytes_accessed=4 * bias.size, transcendentals=0
        ),
    )(length, q_t, prompt_all, kvt_cont, bias, attended, lse, grad, cos_t, sin_t)


def per_device(
    prompt_x,
    cont_x,
    prompt_len,
    cont_seg,
    attn_gain,
    q_weight,
    key_matrix,
    value_matrix,
    o_weight,
    mlp_gain,
    gate_weight,
    up_weight,
    down_weight,
    prompt_cot,
    cont_cot,
):
    head_dim = HEAD_SIZE
    data = ("dp", "context")
    prompt_rows = prompt_x.shape[0]
    cont_rows = cont_x.shape[0]
    prompt_total = prompt_rows * lax.axis_size("context")
    q_cols = q_weight.shape[1]
    kv_cols = key_matrix.shape[1]
    q_heads = q_cols // head_dim
    kv_heads = kv_cols // head_dim
    qkv_cols = q_cols + 2 * kv_cols
    qkv_wide = qkv_cols + 2 + -(qkv_cols + 2) % 128
    hidden_cols = gate_weight.shape[1]
    wide = hidden_cols + -hidden_cols % 256
    packed = jnp.concatenate(
        [
            q_weight,
            key_matrix,
            value_matrix,
            attn_gain[:, None],
            mlp_gain[:, None],
            jnp.zeros((q_weight.shape[0], qkv_wide - qkv_cols - 2), jnp.bfloat16),
            o_weight,
        ],
        axis=1,
    )
    packed_full = lax.all_gather(packed, data, axis=0, tiled=True)
    fill = ((0, 0), (0, wide - hidden_cols))
    mlp_full = lax.all_gather(
        jnp.concatenate(
            [jnp.pad(w, fill) for w in (down_weight, gate_weight, up_weight)], axis=1
        ),
        data,
        axis=0,
        tiled=True,
    )
    wd_full = mlp_full[:, :wide]
    wg_full = mlp_full[:, wide : 2 * wide]
    wu_full = mlp_full[:, 2 * wide :]
    gain_one = packed_full[:, qkv_cols].astype(jnp.float32)[None, :]
    gain_two = packed_full[:, qkv_cols + 1].astype(jnp.float32)[None, :]
    wo_full = packed_full[:, qkv_wide:]
    wqkv_full = packed_full[:, :qkv_cols]
    context_pos = lax.axis_index("context")
    prompt_pos = context_pos * prompt_rows + jnp.arange(prompt_rows, dtype=jnp.int32)
    segment = cont_seg[0]
    earlier = jnp.sum((segment[None, :] < segment[:, None]).astype(jnp.int32), axis=1)
    local_index = jnp.arange(cont_rows, dtype=jnp.int32)
    length = prompt_len[0]
    cont_pos = length + local_index - earlier
    position = jnp.concatenate([prompt_pos, cont_pos]).astype(jnp.float32)
    inv_freq = THETA ** (-jnp.arange(head_dim // 2, dtype=jnp.float32) * 2.0 / head_dim)
    angle_table = inv_freq[:, None] * position[None, :]
    cosine = jnp.cos(angle_table)
    sine_table = jnp.sin(angle_table)
    key_index = jnp.arange(prompt_total, dtype=jnp.int32)
    prompt_mask = jnp.concatenate(
        [key_index[:, None] <= prompt_pos[None, :], jnp.zeros((cont_rows, prompt_rows), jnp.bool_)],
        axis=0,
    )
    own_mask = (segment[:, None] == segment[None, :]) & (
        local_index[:, None] <= local_index[None, :]
    )
    reach_mask = jnp.broadcast_to(key_index[:, None] < length, (prompt_total, cont_rows))
    allowed = jnp.concatenate(
        [prompt_mask, jnp.concatenate([reach_mask, own_mask], axis=0)], axis=1
    )
    bias = jnp.where(allowed, 0.0, NEGATIVE)
    x_all = jnp.concatenate([prompt_x, cont_x], axis=0)
    first_normed, q_t, kv_t = project_rope(
        x_all, packed_full, gain_one, cosine, sine_table, q_heads, kv_heads
    )
    prompt_all = context_gather(kv_t[:, :prompt_rows], 4)
    cont_kv = kv_t[:, prompt_rows:]
    attn_out, lse = attend(prompt_len, q_t, prompt_all, cont_kv, bias, q_heads, kv_heads)
    attn_sum = line_sum(contract_last(attn_out, wo_full).astype(jnp.bfloat16), 0)
    inputs = x_all.astype(jnp.float32)
    middle = inputs + attn_sum.astype(jnp.float32)
    unit_two, inv_two = normalize(middle)
    normed_two = (unit_two * gain_two).astype(jnp.bfloat16)
    gate_value = jnp.dot(normed_two, wg_full, preferred_element_type=jnp.float32)
    up_value = jnp.dot(normed_two, wu_full, preferred_element_type=jnp.float32)
    sigmoid_gate = jax.nn.sigmoid(gate_value)
    silu_gate = gate_value * sigmoid_gate
    hidden = (silu_gate * up_value).astype(jnp.bfloat16)
    mlp_part = contract_last(hidden, wd_full).astype(jnp.bfloat16)
    grad_out = jnp.concatenate([prompt_cot, cont_cot], axis=0)
    grad_hidden = jnp.dot(grad_out, wd_full, preferred_element_type=jnp.float32)
    grad_gate = (
        grad_hidden * up_value * sigmoid_gate * (1.0 + gate_value * (1.0 - sigmoid_gate))
    ).astype(jnp.bfloat16)
    grad_up = (grad_hidden * silu_gate).astype(jnp.bfloat16)
    grad_down = contract_first(grad_out, hidden).astype(jnp.bfloat16)
    grad_wg = contract_first(normed_two, grad_gate).astype(jnp.bfloat16)
    grad_wu = contract_first(normed_two, grad_up).astype(jnp.bfloat16)
    back_two = contract_last(grad_gate, wg_full) + contract_last(grad_up, wu_full)
    back_two = back_two.astype(jnp.bfloat16)
    back_two, grad_down, grad_wg, grad_wu = lax.optimization_barrier(
        (back_two, grad_down, grad_wg, grad_wu)
    )
    def scatter(values):
        return lax.psum_scatter(values, data, scatter_dimension=0, tiled=True).astype(jnp.float32)

    back_two = line_sum(back_two, 1)
    down_own = scatter(grad_down)
    back_two, mlp_part, down_own = lax.optimization_barrier((back_two, mlp_part, down_own))
    mlp_sum = line_sum(mlp_part, 3)
    gate_own = scatter(grad_wg)
    back_two, mlp_sum, gate_own = lax.optimization_barrier((back_two, mlp_sum, gate_own))
    result = middle + mlp_sum.astype(jnp.float32)
    back_two = back_two.astype(jnp.float32)
    grad_middle = grad_out.astype(jnp.float32) + norm_back(back_two * gain_two, unit_two, inv_two)
    grad_middle_b = grad_middle.astype(jnp.bfloat16)
    grad_attended = jnp.dot(grad_middle_b, wo_full, preferred_element_type=jnp.float32).astype(
        jnp.bfloat16
    )
    grad_wo = contract_first(grad_middle_b, attn_out).astype(jnp.bfloat16)
    grad_q, part_kv, own_kv = attend_back(
        prompt_len,
        q_t,
        prompt_all,
        cont_kv,
        bias,
        attn_out,
        lse,
        grad_attended,
        cosine,
        sine_table,
        q_heads,
        kv_heads,
    )
    grad_kv = context_scatter(part_kv, own_kv, cosine, sine_table, 5)
    grad_qkv = jnp.concatenate([grad_q, grad_kv], axis=1)
    grad_attn = jnp.concatenate(
        [grad_wo, contract_first(first_normed, grad_qkv).astype(jnp.bfloat16)], axis=1
    )
    back_one = contract_last(grad_qkv, wqkv_full).astype(jnp.bfloat16)
    up_own = scatter(grad_wu)
    back_one, grad_attn, up_own = lax.optimization_barrier((back_one, grad_attn, up_own))
    back_one = line_sum(back_one, 2).astype(jnp.float32)
    unit_one, inv_one = normalize(inputs)
    grad_inputs = grad_middle + norm_back(back_one * gain_one, unit_one, inv_one)

    down_own = down_own[:, :hidden_cols]
    gate_own = gate_own[:, :hidden_cols]
    up_own = up_own[:, :hidden_cols]
    attn_own = scatter(grad_attn)
    o_own = attn_own[:, :q_cols]
    q_own = attn_own[:, q_cols : 2 * q_cols]
    k_own = attn_own[:, 2 * q_cols : 2 * q_cols + kv_cols]
    v_own = attn_own[:, 2 * q_cols + kv_cols :]

    def row_dot(weight, grad):
        return jnp.sum(weight.astype(jnp.float32) * grad, axis=1)

    gain_rows = jnp.stack(
        [
            (row_dot(q_weight, q_own) + row_dot(key_matrix, k_own) + row_dot(value_matrix, v_own))
            / attn_gain.astype(jnp.float32),
            (row_dot(gate_weight, gate_own) + row_dot(up_weight, up_own))
            / mlp_gain.astype(jnp.float32),
        ]
    )
    gain_rows = lax.psum(gain_rows, "tensor")
    owned = (gain_rows[0], q_own, k_own, v_own, o_own, gain_rows[1], gate_own, up_own, down_own)
    return (
        result[:prompt_rows].astype(jnp.bfloat16),
        result[prompt_rows:].astype(jnp.bfloat16),
        grad_inputs[:prompt_rows],
        grad_inputs[prompt_rows:],
        *owned,
    )


def solution(mesh):
    in_specs = (
        P(("dp", "context"), None),
        P(("dp", "context"), None),
        P("dp"),
        P(("dp", "context"), None),
        P(("dp", "context")),
        P(("dp", "context"), "tensor"),
        P(("dp", "context"), "tensor"),
        P(("dp", "context"), "tensor"),
        P(("dp", "context"), "tensor"),
        P(("dp", "context")),
        P(("dp", "context"), "tensor"),
        P(("dp", "context"), "tensor"),
        P(("dp", "context"), "tensor"),
        P(("dp", "context"), None),
        P(("dp", "context"), None),
    )
    out_specs = (
        P(("dp", "context"), None),
        P(("dp", "context"), None),
        P(("dp", "context"), None),
        P(("dp", "context"), None),
        P(("dp", "context")),
        P(("dp", "context"), "tensor"),
        P(("dp", "context"), "tensor"),
        P(("dp", "context"), "tensor"),
        P(("dp", "context"), "tensor"),
        P(("dp", "context")),
        P(("dp", "context"), "tensor"),
        P(("dp", "context"), "tensor"),
        P(("dp", "context"), "tensor"),
    )
    return jax.shard_map(
        per_device, mesh=mesh, in_specs=in_specs, out_specs=out_specs, check_vma=False
    )
```

```python
import functools
import math

import jax
import jax.numpy as jnp
from jax import lax
from jax.experimental import pallas as pl
from jax.experimental.pallas import tpu as pltpu
from jax.sharding import PartitionSpec as P

HEAD_SIZE = 80


EPS = 1e-05
THETA = 10000.0
NEGATIVE = -1e30
LOG2E = math.log2(math.e)
MESH = pl.DeviceIdType.MESH
AXIS = "tensor"
LAG = 3
SIZE = 256


def normalize(values):
    inverse = lax.rsqrt(jnp.mean(values * values, axis=-1, keepdims=True) + EPS)
    return (values * inverse, inverse)


def norm_back(grad_unit, unit_rows, inverse):
    inner_sum = jnp.mean(grad_unit * unit_rows, axis=-1, keepdims=True)
    return inverse * (grad_unit - unit_rows * inner_sum)


def contract_last(left_side, right_side):
    return lax.dot_general(
        left_side, right_side, (((1,), (1,)), ((), ())), preferred_element_type=jnp.float32
    )


def contract_first(left_side, right_side):
    return lax.dot_general(
        left_side, right_side, (((0,), (0,)), ((), ())), preferred_element_type=jnp.float32
    )


def rope_kernel(q_heads, kv_heads, dim, x_ref, w_ref, gain_ref, cos_ref, sin_ref, normed_ref, qt_ref, kvt_ref):
    rows = x_ref[...].astype(jnp.float32)
    inverse = lax.rsqrt(jnp.mean(rows * rows, axis=-1, keepdims=True) + EPS)
    normed = (rows * inverse * gain_ref[...]).astype(jnp.bfloat16)
    normed_ref[...] = normed
    flat = jnp.dot(normed, w_ref[...], preferred_element_type=jnp.float32).T
    cosine, sine = cos_ref[...], sin_ref[...]
    half = dim // 2
    for head in range(q_heads + kv_heads):
        first = flat[head * dim : head * dim + half]
        second = flat[head * dim + half : (head + 1) * dim]
        turned = jnp.concatenate(
            [first * cosine - second * sine, second * cosine + first * sine], axis=0
        ).astype(jnp.bfloat16)
        if head < q_heads:
            qt_ref[head * dim : (head + 1) * dim, :] = turned
        else:
            at = (head - q_heads) * dim
            kvt_ref[at : at + dim, :] = turned
    at = (q_heads + kv_heads) * dim
    kvt_ref[kv_heads * dim :, :] = flat[at : at + kv_heads * dim].astype(jnp.bfloat16)


def project_rope(x, packed_full, gain, cos_t, sin_t, q_heads, kv_heads):
    rows, width = x.shape
    dim = HEAD_SIZE
    step = math.gcd(rows, 256)
    cols = (q_heads + 2 * kv_heads) * dim
    cols_wide = cols + -cols % 128
    by_row = lambda i: (i, 0)
    by_col = lambda i: (0, i)
    fixed = lambda i: (0, 0)
    return pl.pallas_call(
        functools.partial(rope_kernel, q_heads, kv_heads, dim),
        grid=(rows // step,),
        in_specs=[
            pl.BlockSpec((step, width), by_row),
            pl.BlockSpec((width, cols_wide), fixed, pipeline_mode=pl.Buffered(1)),
            pl.BlockSpec((1, width), fixed),
            pl.BlockSpec((dim // 2, step), by_col),
            pl.BlockSpec((dim // 2, step), by_col),
        ],
        out_specs=[
            pl.BlockSpec((step, width), by_row),
            pl.BlockSpec((q_heads * dim, step), by_col),
            pl.BlockSpec((2 * kv_heads * dim, step), by_col),
        ],
        out_shape=[
            jax.ShapeDtypeStruct((rows, width), jnp.bfloat16),
            jax.ShapeDtypeStruct((q_heads * dim, rows), jnp.bfloat16),
            jax.ShapeDtypeStruct((2 * kv_heads * dim, rows), jnp.bfloat16),
        ],
        compiler_params=pltpu.CompilerParams(vmem_limit_bytes=48 << 20),
        cost_estimate=pl.CostEstimate(
            flops=2 * rows * width * cols_wide,
            bytes_accessed=4 * x.size + 2 * width * cols_wide,
            transcendentals=0,
        ),
    )(x, packed_full, gain, cos_t, sin_t)


def greet(axis, count):
    me = lax.axis_index(axis)
    barrier = pltpu.get_barrier_semaphore()
    for k in range(1, count):
        peer = lax.rem(me + k, count)
        pl.semaphore_signal(barrier, inc=1, device_id={axis: peer}, device_id_type=MESH)
    pl.semaphore_wait(barrier, count - 1)


def gather_kernel(count, own_ref, all_ref, send, recv, local):
    me = lax.axis_index("context")
    keep = pltpu.make_async_copy(own_ref, all_ref.at[me], local)
    keep.start()
    greet("context", count)
    copies = []
    for k in range(1, count):
        peer = lax.rem(me + k, count)
        copy = pltpu.make_async_remote_copy(
            own_ref,
            all_ref.at[me],
            send.at[k],
            recv.at[k],
            device_id={"context": peer},
            device_id_type=MESH,
        )
        copy.start()
        copies.append(copy)
    keep.wait()
    for copy in copies:
        copy.wait()


def context_gather(own, cid):
    count = lax.axis_size("context")
    return pl.pallas_call(
        functools.partial(gather_kernel, count),
        out_shape=jax.ShapeDtypeStruct((count, *own.shape), own.dtype),
        in_specs=[pl.BlockSpec(memory_space=pltpu.VMEM)],
        out_specs=pl.BlockSpec(memory_space=pltpu.VMEM),
        scratch_shapes=[
            pltpu.SemaphoreType.DMA((count,)),
            pltpu.SemaphoreType.DMA((count,)),
            pltpu.SemaphoreType.DMA,
        ],
        compiler_params=pltpu.CompilerParams(collective_id=cid, has_side_effects=True),
        cost_estimate=pl.CostEstimate(flops=0, bytes_accessed=8 << 20, transcendentals=0),
    )(own)


def scatter_kernel(count, kv_dim, dim, part_ref, own_ref, cos_ref, sin_ref, rows_ref, got, send, recv):
    me = lax.axis_index("context")
    greet("context", count)
    copies = []
    for k in range(1, count):
        peer = lax.rem(me + k, count)
        copy = pltpu.make_async_remote_copy(
            part_ref.at[peer],
            got.at[k],
            send.at[k],
            recv.at[k],
            device_id={"context": peer},
            device_id_type=MESH,
        )
        copy.start()
        copies.append(copy)
    prompt_rows = part_ref.shape[2]
    cosine, sine = cos_ref[...], sin_ref[...]
    half = dim // 2

    def finish(flat, cosine, sine):
        pieces = []
        for at in range(0, kv_dim, dim):
            first, second = flat[at : at + half], flat[at + half : at + dim]
            pieces += [first * cosine + second * sine, second * cosine - first * sine]
        pieces.append(flat[kv_dim:])
        return jnp.concatenate(pieces, axis=0).T.astype(jnp.bfloat16)

    rows_ref[prompt_rows:, :] = finish(own_ref[...], cosine[:, prompt_rows:], sine[:, prompt_rows:])
    total = part_ref[me].astype(jnp.float32)
    for k in range(1, count):
        copies[k - 1].wait()
        total += got[k].astype(jnp.float32)
    rows_ref[:prompt_rows, :] = finish(total, cosine[:, :prompt_rows], sine[:, :prompt_rows])


def context_scatter(part, own, cos_t, sin_t, cid):
    count, kv2, prompt_rows = part.shape
    rows = prompt_rows + own.shape[1]
    return pl.pallas_call(
        functools.partial(scatter_kernel, count, kv2 // 2, HEAD_SIZE),
        out_shape=jax.ShapeDtypeStruct((rows, kv2), jnp.bfloat16),
        in_specs=[pl.BlockSpec(memory_space=pltpu.VMEM)] * 4,
        out_specs=pl.BlockSpec(memory_space=pltpu.VMEM),
        scratch_shapes=[
            pltpu.VMEM(part.shape, part.dtype),
            pltpu.SemaphoreType.DMA((count,)),
            pltpu.SemaphoreType.DMA((count,)),
        ],
        compiler_params=pltpu.CompilerParams(collective_id=cid, has_side_effects=True),
        cost_estimate=pl.CostEstimate(flops=0, bytes_accessed=8 << 20, transcendentals=0),
    )(part, own, cos_t, sin_t)


def attend_shape(prompt_all, kvt_cont):
    count, kv2, prompt_rows = prompt_all.shape
    cont_rows = kvt_cont.shape[1]
    chunk = math.gcd(math.gcd(prompt_rows, cont_rows), 256)
    return count, kv2, prompt_rows, cont_rows, chunk


def fill_keys(first, chunk, dim, kv_heads, all_ref, cont_ref, rows_of, chunks_ref):
    count, _, prompt_rows = all_ref.shape
    per = prompt_rows // chunk
    total = count * per + cont_ref.shape[1] // chunk
    for c in range(total):
        if c < count * per:
            block = all_ref[c // per, :, (c % per) * chunk : (c % per + 1) * chunk]
        else:
            at = (c - count * per) * chunk
            block = cont_ref[:, at : at + chunk]
        chunks_ref[c] = block
        for n, target in enumerate(rows_of):
            for g in range(kv_heads):
                at = (n * kv_heads + g) * dim
                target[g, c * chunk : (c + 1) * chunk, :] = (
                    block[at : at + dim].astype(jnp.float32).T.astype(jnp.bfloat16)
                )


def trip_count(len_ref, tile, chunk, i, prompt_rows, count):
    me = lax.axis_index("context")
    prompt_tiles = prompt_rows // tile
    own = me * prompt_rows + (i + 1) * tile
    return i < prompt_tiles, (own + chunk - 1) // chunk, (len_ref[0] + chunk - 1) // chunk, (
        (i - prompt_tiles + 1) * tile + chunk - 1
    ) // chunk


def attend_kernel(
    shape, dim, kv_heads, per, tile, len_ref, q_ref, all_ref, cont_ref, bias_ref, out_ref, lse_ref, keys, chunks
):
    count, prompt_rows, chunk = shape
    i = pl.program_id(0)

    @pl.when(i == 0)
    def _():
        fill_keys(i, chunk, dim, kv_heads, all_ref, cont_ref, [keys], chunks)

    is_prompt, n_prompt, n_len, n_own = trip_count(len_ref, tile, chunk, i, prompt_rows, count)
    base = count * prompt_rows // chunk
    wide = per * tile
    factor = dim ** (-0.5) * LOG2E
    outs, sums = [], []
    for g in range(kv_heads):
        q = jnp.concatenate(
            [q_ref[(g * per + h) * dim : (g * per + h + 1) * dim, :] for h in range(per)], axis=1
        )

        def body(c, state):
            top, total, acc = state
            s = jnp.dot(
                keys[g, pl.ds(pl.multiple_of(c * chunk, chunk), chunk), :],
                q,
                preferred_element_type=jnp.float32,
            )
            b = bias_ref[pl.ds(pl.multiple_of(c * chunk, chunk), chunk), :]
            t = s * factor + jnp.concatenate([b] * per, axis=1)
            new = jnp.maximum(top, jnp.max(t, axis=0, keepdims=True))
            p = jnp.exp2(t - new)
            scale = jnp.exp2(top - new)
            total = total * scale + jnp.sum(p, axis=0, keepdims=True)
            v = chunks[c, (kv_heads + g) * dim : (kv_heads + g + 1) * dim, :]
            acc = acc * scale + jnp.dot(
                v, p.astype(jnp.bfloat16), preferred_element_type=jnp.float32
            )
            return new, total, acc

        start = (
            jnp.full((1, wide), NEGATIVE, jnp.float32),
            jnp.zeros((1, wide), jnp.float32),
            jnp.zeros((dim, wide), jnp.float32),
        )
        state = lax.fori_loop(0, jnp.where(is_prompt, n_prompt, n_len), body, start)
        top, total, acc = lax.fori_loop(base, base + jnp.where(is_prompt, 0, n_own), body, state)
        acc = acc / total
        top = top + jnp.log2(total)
        outs += [acc[:, h * tile : (h + 1) * tile] for h in range(per)]
        sums += [top[:, h * tile : (h + 1) * tile] for h in range(per)]
    out_ref[...] = jnp.concatenate(outs, axis=0).T.astype(jnp.bfloat16)
    lse_ref[...] = jnp.concatenate(sums, axis=0)


def attend(length, q_t, prompt_all, kvt_cont, bias, q_heads, kv_heads):
    dim = HEAD_SIZE
    count, kv2, prompt_rows, cont_rows, chunk = attend_shape(prompt_all, kvt_cont)
    rows = q_t.shape[1]
    keys_all = bias.shape[0]
    tile = 128
    whole = pl.BlockSpec(memory_space=pltpu.VMEM)
    by_col = lambda i, _: (0, i)
    return pl.pallas_call(
        functools.partial(
            attend_kernel, (count, prompt_rows, chunk), dim, kv_heads, q_heads // kv_heads, tile
        ),
        grid_spec=pltpu.PrefetchScalarGridSpec(
            num_scalar_prefetch=1,
            grid=(rows // tile,),
            in_specs=[
                pl.BlockSpec((q_t.shape[0], tile), by_col),
                whole,
                whole,
                pl.BlockSpec((keys_all, tile), by_col),
            ],
            out_specs=[
                pl.BlockSpec((tile, q_t.shape[0]), lambda i, _: (i, 0)),
                pl.BlockSpec((q_heads, tile), by_col),
            ],
            scratch_shapes=[
                pltpu.VMEM((kv_heads, keys_all, dim), jnp.bfloat16),
                pltpu.VMEM((keys_all // chunk, kv2, chunk), jnp.bfloat16),
            ],
        ),
        out_shape=[
            jax.ShapeDtypeStruct((rows, q_t.shape[0]), jnp.bfloat16),
            jax.ShapeDtypeStruct((q_heads, rows), jnp.float32),
        ],
        compiler_params=pltpu.CompilerParams(vmem_limit_bytes=40 << 20),
        cost_estimate=pl.CostEstimate(
            flops=20_000_000_000, bytes_accessed=4 * bias.size, transcendentals=0
        ),
    )(length, q_t, prompt_all, kvt_cont, bias)


class Line:
    def __init__(self, part, recv, out, sink, sems, sink_sems):
        self.part, self.recv, self.out, self.sink = part, recv, out, sink
        self.per = sink.shape[0] // out.shape[1]
        self.sems, self.sink_sems = sems, sink_sems
        self.blocks = out.shape[0]
        me, n = lax.axis_index(AXIS), lax.axis_size(AXIS)
        self.outer = (me == 0) | (me == n - 1)
        self.inner = jnp.logical_not(self.outer)
        self.mate = jnp.where(me < n // 2, 1 - me, 2 * n - 3 - me)
        self.across = n - 1 - me

    def copy(self, k, source, target, peer, b):
        return pltpu.make_async_remote_copy(
            source.at[b],
            target.at[b],
            self.sems.at[2 * k, b],
            self.sems.at[2 * k + 1, b],
            device_id={AXIS: peer},
            device_id_type=MESH,
        )

    def up(self, b):
        return self.copy(0, self.part, self.recv, self.mate, b)

    def mid(self, b):
        return self.copy(1, self.part, self.out, self.across, b)

    def down(self, b):
        return self.copy(2, self.out, self.out, self.mate, b)

    def keep(self, b):
        _, rows, cols = self.out.shape
        at = (
            pl.ds(pl.multiple_of(lax.rem(b, self.per) * rows, rows), rows),
            pl.ds(pl.multiple_of(lax.div(b, self.per) * cols, cols), cols),
        )
        return pltpu.make_async_copy(self.out.at[b], self.sink.at[at], self.sink_sems.at[b])

    def greet(self):
        barrier = pltpu.get_barrier_semaphore()
        pl.semaphore_signal(barrier, inc=1, device_id={AXIS: self.mate}, device_id_type=MESH)

        @pl.when(self.inner)
        def _():
            pl.semaphore_signal(barrier, inc=1, device_id={AXIS: self.across}, device_id_type=MESH)
            pl.semaphore_wait(barrier, 2)

        @pl.when(self.outer)
        def _():
            pl.semaphore_wait(barrier, 1)

    def start(self, first, count):
        @pl.when(self.outer)
        def _():
            @pl.loop(0, count)
            def _(k):
                self.up(first + k).start()

    def step(self, t):
        @pl.when(self.inner & (t < self.blocks))
        def _():
            self.up(t).wait_recv()
            self.part[t] = (
                self.part[t].astype(jnp.float32) + self.recv[t].astype(jnp.float32)
            ).astype(jnp.bfloat16)
            self.mid(t).start()

        @pl.when(self.inner & (t >= LAG) & (t < self.blocks + LAG))
        def _():
            b = t - LAG
            self.mid(b).wait()
            self.out[b] = (
                self.part[b].astype(jnp.float32) + self.out[b].astype(jnp.float32)
            ).astype(jnp.bfloat16)
            self.down(b).start()
            self.keep(b).start()

    def drain(self):
        for k in range(LAG):
            self.step(self.blocks + k)

        @pl.when(self.outer)
        def _():
            @pl.loop(0, self.blocks)
            def _(b):
                self.down(b).wait_recv()
                self.keep(b).start()
                self.up(b).wait_send()

        @pl.when(self.inner)
        def _():
            @pl.loop(0, self.blocks)
            def _(b):
                self.down(b).wait_send()

        @pl.loop(0, self.blocks)
        def _(b):
            self.keep(b).wait()


def line_scratch(shape):
    return [pltpu.VMEM(shape, jnp.bfloat16)] * 3 + [
        pltpu.SemaphoreType.DMA((6, shape[0])),
        pltpu.SemaphoreType.DMA((shape[0],)),
    ]


def feed_back_kernel(
    cut,
    gate_ref,
    up_ref,
    hidden_ref,
    wd_ref,
    wg_ref,
    wu_ref,
    cot_ref,
    normed_ref,
    grads_ref,
    mlp_ref,
    sum_ref,
    part,
    recv,
    out,
    sems,
    sink_sems,
):
    n = pl.program_id(0)
    rows, wide = gate_ref.shape
    per = rows // cut
    line = Line(part, recv, out, sum_ref, sems, sink_sems)

    back = contract_last(gate_ref[...], wg_ref[...]) + contract_last(up_ref[...], wu_ref[...])
    back = back.astype(jnp.bfloat16)
    for r in range(per):
        part[n * per + r] = back[r * cut : (r + 1) * cut]

    @pl.when(n == 0)
    def _():
        line.greet()

    line.start(n * per, per)

    def steps(low, high):
        for r in range(low, high):
            line.step(n * per + r)

    grads_ref[:, :wide] = contract_first(cot_ref[...], hidden_ref[...]).astype(jnp.bfloat16)
    steps(0, per // 4)
    grads_ref[:, wide : 2 * wide] = contract_first(normed_ref[...], gate_ref[...]).astype(
        jnp.bfloat16
    )
    steps(per // 4, per // 2)
    grads_ref[:, 2 * wide :] = contract_first(normed_ref[...], up_ref[...]).astype(jnp.bfloat16)
    steps(per // 2, per - per // 4)
    mlp_ref[0] = contract_last(hidden_ref[...], wd_ref[...]).astype(jnp.bfloat16)
    steps(per - per // 4, per)

    @pl.when(n == pl.num_programs(0) - 1)
    def _():
        line.drain()


def feed_back(grad_gate, grad_up, hidden, mlp_full, cot, normed, cid):
    rows, wide = hidden.shape
    width = cot.shape[1]
    size = SIZE
    cut = math.gcd(rows, size)
    tiles = width // size
    blocks = (tiles * rows // cut, cut, size)
    whole = pl.BlockSpec(memory_space=pltpu.VMEM)
    return pl.pallas_call(
        functools.partial(feed_back_kernel, cut),
        grid=(tiles,),
        in_specs=[whole] * 3
        + [pl.BlockSpec((size, wide), lambda n, k=k: (n, k)) for k in range(3)]
        + [pl.BlockSpec((rows, size), lambda n: (0, n))] * 2,
        out_specs=[
            pl.BlockSpec((size, 3 * wide), lambda n: (n, 0)),
            pl.BlockSpec((1, rows, size), lambda n: (n, 0, 0)),
            pl.BlockSpec(memory_space=pl.ANY),
        ],
        out_shape=[
            jax.ShapeDtypeStruct((width, 3 * wide), jnp.bfloat16),
            jax.ShapeDtypeStruct((tiles, rows, size), jnp.bfloat16),
            jax.ShapeDtypeStruct((rows, width), jnp.bfloat16),
        ],
        scratch_shapes=line_scratch(blocks),
        compiler_params=pltpu.CompilerParams(
            collective_id=cid, has_side_effects=True, vmem_limit_bytes=58 << 20
        ),
        cost_estimate=pl.CostEstimate(
            flops=12 * rows * wide * width, bytes_accessed=200 << 20, transcendentals=0
        ),
    )(grad_gate, grad_up, hidden, mlp_full, mlp_full, mlp_full, cot, normed)


def window_kernel(
    shape,
    dim,
    kv_heads,
    per,
    tile,
    q_ref,
    all_ref,
    cont_ref,
    bias_ref,
    out_ref,
    lse_ref,
    back_ref,
    cot_ref,
    x_ref,
    attn_ref,
    gain_ref,
    wo_ref,
    cos_ref,
    sin_ref,
    mlp_ref,
    gq_ref,
    part_ref,
    own_ref,
    gm_ref,
    go_ref,
    sum_ref,
    keys,
    values,
    chunks,
    gk,
    gv,
    go,
    part,
    recv,
    out,
    sems,
    sink_sems,
):
    count, prompt_rows, chunk = shape
    i = pl.program_id(0)
    line = Line(part, recv, out, sum_ref, sems, sink_sems)
    slots = line.blocks // pl.num_programs(0)
    spots = 2 + kv_heads

    def step(k):
        for s in range(k * slots // spots, (k + 1) * slots // spots):
            line.step(i * slots + s)

    @pl.when(i == 0)
    def _():
        load = pltpu.make_async_copy(mlp_ref, part, sink_sems.at[0])
        load.start()
        fill_keys(i, chunk, dim, kv_heads, all_ref, cont_ref, [keys, values], chunks)
        gk[...] = jnp.zeros_like(gk)
        gv[...] = jnp.zeros_like(gv)
        go[...] = jnp.zeros_like(go)
        line.greet()
        load.wait()
        line.start(0, line.blocks)

    middle = x_ref[...].astype(jnp.float32) + attn_ref[...].astype(jnp.float32)
    inverse = lax.rsqrt(jnp.mean(middle * middle, axis=-1, keepdims=True) + EPS)
    unit = middle * inverse
    grad_unit = back_ref[...].astype(jnp.float32) * gain_ref[...]
    grad_middle = cot_ref[...].astype(jnp.float32) + norm_back(grad_unit, unit, inverse)
    gm_ref[...] = grad_middle
    grad_b = grad_middle.astype(jnp.bfloat16)
    step(0)
    grad_t = (
        jnp.dot(grad_b, wo_ref[...], preferred_element_type=jnp.float32).astype(jnp.bfloat16)
    ).astype(jnp.float32).T
    go[...] += contract_first(grad_b, out_ref[...])
    step(1)

    me = lax.axis_index("context")
    prompt_tiles = prompt_rows // tile
    is_prompt = i < prompt_tiles
    base = count * prompt_rows // chunk
    n_prompt = (me * prompt_rows + (i + 1) * tile + chunk - 1) // chunk
    n_own = ((i - prompt_tiles + 1) * tile + chunk - 1) // chunk
    root = dim ** (-0.5)
    factor = root * LOG2E
    prod = grad_t * out_ref[...].astype(jnp.float32).T
    grad_t = grad_t.astype(jnp.bfloat16)
    cosine, sine = cos_ref[...], sin_ref[...]
    half = dim // 2
    pieces = []
    for g in range(kv_heads):
        heads = [g * per + h for h in range(per)]
        q = jnp.concatenate([q_ref[h * dim : (h + 1) * dim, :] for h in heads], axis=1)
        grad = jnp.concatenate([grad_t[h * dim : (h + 1) * dim] for h in heads], axis=1)
        inner = jnp.concatenate(
            [jnp.sum(prod[h * dim : (h + 1) * dim], axis=0, keepdims=True) for h in heads], axis=1
        )
        lse = jnp.concatenate([lse_ref[h : h + 1, :] for h in heads], axis=1)

        def body(c, acc):
            at = pl.ds(pl.multiple_of(c * chunk, chunk), chunk)
            s = jnp.dot(keys[g, at, :], q, preferred_element_type=jnp.float32)
            b = bias_ref[at, :]
            p = jnp.exp2(s * factor + (jnp.concatenate([b] * per, axis=1) - lse))
            dp = jnp.dot(values[g, at, :], grad, preferred_element_type=jnp.float32)
            ds = (p * (dp - inner)).astype(jnp.bfloat16)
            gv[g, at, :] += contract_last(p.astype(jnp.bfloat16), grad)
            gk[g, at, :] += contract_last(ds, q)
            k_t = chunks[c, g * dim : (g + 1) * dim, :]
            return acc + jnp.dot(k_t, ds, preferred_element_type=jnp.float32)

        acc = jnp.zeros((dim, per * tile), jnp.float32)
        acc = lax.fori_loop(0, jnp.where(is_prompt, n_prompt, base), body, acc)
        acc = lax.fori_loop(base, base + jnp.where(is_prompt, 0, n_own), body, acc)
        acc = acc * root
        for h in range(per):
            first = acc[:half, h * tile : (h + 1) * tile]
            second = acc[half:, h * tile : (h + 1) * tile]
            pieces += [first * cosine + second * sine, second * cosine - first * sine]
        step(2 + g)
    gq_ref[...] = jnp.concatenate(pieces, axis=0).T.astype(jnp.bfloat16)

    @pl.when(i == pl.num_programs(0) - 1)
    def _():
        for g in range(kv_heads):
            for n, (acc, scale) in enumerate(((gk, root), (gv, 1.0))):
                at = (n * kv_heads + g) * dim
                for c in range(count):
                    rows = acc[g, c * prompt_rows : (c + 1) * prompt_rows, :]
                    part_ref[c, at : at + dim, :] = (rows * scale).T.astype(jnp.bfloat16)
                own_ref[at : at + dim, :] = (acc[g, count * prompt_rows :, :] * scale).T
        go_ref[...] = go[...].astype(jnp.bfloat16)
        line.drain()


def window(
    q_t,
    prompt_all,
    kvt_cont,
    bias,
    attended,
    lse,
    back,
    cot,
    x,
    attn_sum,
    gain,
    wo,
    cos_t,
    sin_t,
    mlp_part,
    q_heads,
    kv_heads,
    cid,
):
    dim = HEAD_SIZE
    count, kv2, prompt_rows, cont_rows, chunk = attend_shape(prompt_all, kvt_cont)
    rows, width = cot.shape
    q_cols = q_heads * dim
    keys_all = bias.shape[0]
    tile = 128
    whole = pl.BlockSpec(memory_space=pltpu.VMEM)
    anywhere = pl.BlockSpec(memory_space=pl.ANY)
    by_col = lambda i: (0, i)
    by_row = lambda i: (i, 0)
    fixed = lambda i: (0, 0)
    return pl.pallas_call(
        functools.partial(
            window_kernel, (count, prompt_rows, chunk), dim, kv_heads, q_heads // kv_heads, tile
        ),
        grid=(rows // tile,),
        in_specs=[
            pl.BlockSpec((q_cols, tile), by_col),
            whole,
            whole,
            pl.BlockSpec((keys_all, tile), by_col),
            pl.BlockSpec((tile, q_cols), by_row),
            pl.BlockSpec((q_heads, tile), by_col),
            pl.BlockSpec((tile, width), by_row),
            pl.BlockSpec((tile, width), by_row),
            pl.BlockSpec((tile, width), by_row),
            pl.BlockSpec((tile, width), by_row),
            pl.BlockSpec((1, width), fixed),
            whole,
            pl.BlockSpec((dim // 2, tile), by_col),
            pl.BlockSpec((dim // 2, tile), by_col),
            anywhere,
        ],
        out_specs=[
            pl.BlockSpec((tile, q_cols), by_row),
            pl.BlockSpec((count, kv2, prompt_rows), lambda i: (0, 0, 0)),
            pl.BlockSpec((kv2, cont_rows), fixed),
            pl.BlockSpec((tile, width), by_row),
            pl.BlockSpec((width, q_cols), fixed),
            anywhere,
        ],
        out_shape=[
            jax.ShapeDtypeStruct((rows, q_cols), jnp.bfloat16),
            jax.ShapeDtypeStruct((count, kv2, prompt_rows), jnp.bfloat16),
            jax.ShapeDtypeStruct((kv2, cont_rows), jnp.float32),
            jax.ShapeDtypeStruct((rows, width), jnp.float32),
            jax.ShapeDtypeStruct((width, q_cols), jnp.bfloat16),
            jax.ShapeDtypeStruct((rows, width), jnp.bfloat16),
        ],
        scratch_shapes=[
            pltpu.VMEM((kv_heads, keys_all, dim), jnp.bfloat16),
            pltpu.VMEM((kv_heads, keys_all, dim), jnp.bfloat16),
            pltpu.VMEM((keys_all // chunk, kv2, chunk), jnp.bfloat16),
            pltpu.VMEM((kv_heads, keys_all, dim), jnp.float32),
            pltpu.VMEM((kv_heads, keys_all, dim), jnp.float32),
            pltpu.VMEM((width, q_cols), jnp.float32),
            *line_scratch(mlp_part.shape),
        ],
        compiler_params=pltpu.CompilerParams(
            collective_id=cid, has_side_effects=True, vmem_limit_bytes=58 << 20
        ),
        cost_estimate=pl.CostEstimate(
            flops=100_000_000_000, bytes_accessed=200 << 20, transcendentals=0
        ),
    )(
        q_t, prompt_all, kvt_cont, bias, attended, lse, back, cot, x, attn_sum, gain, wo, cos_t, sin_t, mlp_part
    )


def product_kernel(cut, spans, lhs_refs, w_ref, sum_ref, part, recv, out, sems, sink_sems):
    n = pl.program_id(0)
    per = sum_ref.shape[0] // cut
    line = Line(part, recv, out, sum_ref, sems, sink_sems)
    term = sum(
        contract_last(ref[...], w_ref[:, low:high]) for ref, (low, high) in zip(lhs_refs, spans)
    ).astype(jnp.bfloat16)
    for r in range(per):
        part[n * per + r] = term[r * cut : (r + 1) * cut]

    @pl.when(n == 0)
    def _():
        line.greet()

    line.start(n * per, per)
    for r in range(per):
        line.step(n * per + r)

    @pl.when(n == pl.num_programs(0) - 1)
    def _():
        line.drain()


def product_sum(lhs, spans, weights, cid):
    rows = lhs[0].shape[0]
    width, cols = weights.shape
    cut = math.gcd(rows, SIZE)
    tiles = width // SIZE
    blocks = (tiles * rows // cut, cut, SIZE)

    def body(*refs):
        product_kernel(cut, spans, refs[: len(lhs)], *refs[len(lhs) :])

    return pl.pallas_call(
        body,
        grid=(tiles,),
        in_specs=[pl.BlockSpec(memory_space=pltpu.VMEM)] * len(lhs)
        + [pl.BlockSpec((SIZE, cols), lambda n: (n, 0))],
        out_specs=pl.BlockSpec(memory_space=pl.ANY),
        out_shape=jax.ShapeDtypeStruct((rows, width), jnp.bfloat16),
        scratch_shapes=line_scratch(blocks),
        compiler_params=pltpu.CompilerParams(
            collective_id=cid, has_side_effects=True, vmem_limit_bytes=40 << 20
        ),
        cost_estimate=pl.CostEstimate(
            flops=120_000_000_000, bytes_accessed=40 << 20, transcendentals=0
        ),
    )(*lhs, weights)


def feed_kernel(
    x_ref,
    attn_ref,
    gain_ref,
    cot_ref,
    wd_ref,
    wg_ref,
    wu_ref,
    normed_ref,
    hidden_ref,
    gate_grad_ref,
    up_grad_ref,
):
    @pl.when(pl.program_id(0) == 0)
    def _():
        @pl.loop(0, x_ref.shape[0] // 64)
        def _(r):
            at = pl.ds(pl.multiple_of(r * 64, 64), 64)
            middle = x_ref[at, :].astype(jnp.float32) + attn_ref[at, :].astype(jnp.float32)
            unit, _ = normalize(middle)
            normed_ref[at, :] = (unit * gain_ref[...]).astype(jnp.bfloat16)

    gate = jnp.dot(normed_ref[...], wg_ref[...], preferred_element_type=jnp.float32)
    up = jnp.dot(normed_ref[...], wu_ref[...], preferred_element_type=jnp.float32)
    grad_hidden = jnp.dot(cot_ref[...], wd_ref[...], preferred_element_type=jnp.float32)
    sigmoid = 1.0 / (1.0 + jnp.exp(-gate))
    silu = gate * sigmoid
    hidden_ref[...] = (silu * up).astype(jnp.bfloat16)
    gate_grad_ref[...] = (grad_hidden * up * sigmoid * (1.0 + gate * (1.0 - sigmoid))).astype(
        jnp.bfloat16
    )
    up_grad_ref[...] = (grad_hidden * silu).astype(jnp.bfloat16)


def feed(x, attn_sum, gain, cot, mlp_full):
    rows, width = x.shape
    wide = mlp_full.shape[1] // 3
    tiles = wide // SIZE
    whole = pl.BlockSpec(memory_space=pltpu.VMEM)
    tile = pl.BlockSpec((rows, SIZE), lambda n: (0, n))
    return pl.pallas_call(
        feed_kernel,
        grid=(tiles,),
        in_specs=[whole] * 4
        + [pl.BlockSpec((width, SIZE), lambda n, k=k: (0, k * tiles + n)) for k in range(3)],
        out_specs=[
            pl.BlockSpec((rows, width), lambda n: (0, 0), pipeline_mode=pl.Buffered(1)),
            tile,
            tile,
            tile,
        ],
        out_shape=[jax.ShapeDtypeStruct((rows, width), jnp.bfloat16)]
        + [jax.ShapeDtypeStruct((rows, wide), jnp.bfloat16)] * 3,
        compiler_params=pltpu.CompilerParams(vmem_limit_bytes=58 << 20),
        cost_estimate=pl.CostEstimate(
            flops=6 * rows * width * wide, bytes_accessed=60 << 20, transcendentals=rows * wide
        ),
    )(x, attn_sum, gain, cot, mlp_full, mlp_full, mlp_full)


def attn_grads_kernel(normed_ref, q_ref, kv_ref, o_ref, out_ref):
    q_cols, kv_cols = q_ref.shape[1], kv_ref.shape[1]
    out_ref[:, :q_cols] = o_ref[...]
    out_ref[:, q_cols : 2 * q_cols] = contract_first(normed_ref[...], q_ref[...]).astype(
        jnp.bfloat16
    )
    out_ref[:, 2 * q_cols :] = contract_first(normed_ref[...], kv_ref[...]).astype(jnp.bfloat16)


def attn_grads(normed, grad_q, grad_kv, grad_o):
    rows, width = normed.shape
    q_cols, kv_cols = grad_q.shape[1], grad_kv.shape[1]
    whole = pl.BlockSpec(memory_space=pltpu.VMEM)
    return pl.pallas_call(
        attn_grads_kernel,
        grid=(width // SIZE,),
        in_specs=[
            pl.BlockSpec((rows, SIZE), lambda n: (0, n)),
            whole,
            whole,
            pl.BlockSpec((SIZE, q_cols), lambda n: (n, 0)),
        ],
        out_specs=pl.BlockSpec((SIZE, 2 * q_cols + kv_cols), lambda n: (n, 0)),
        out_shape=jax.ShapeDtypeStruct((width, 2 * q_cols + kv_cols), jnp.bfloat16),
        compiler_params=pltpu.CompilerParams(vmem_limit_bytes=40 << 20),
        cost_estimate=pl.CostEstimate(
            flops=1_000_000_000, bytes_accessed=10 << 20, transcendentals=0
        ),
    )(normed, grad_q, grad_kv, grad_o)


def finish_kernel(
    prompt_tiles, x_ref, attn_ref, mlp_ref, gm_ref, back_ref, gain_ref, po_ref, co_ref, pg_ref, cg_ref
):
    i = pl.program_id(0)
    x = x_ref[...].astype(jnp.float32)
    result = (x + attn_ref[...].astype(jnp.float32)) + mlp_ref[...].astype(jnp.float32)
    result = result.astype(jnp.bfloat16)
    unit, inverse = normalize(x)
    grad = gm_ref[...] + norm_back(back_ref[...].astype(jnp.float32) * gain_ref[...], unit, inverse)

    @pl.when(i < prompt_tiles)
    def _():
        po_ref[...] = result
        pg_ref[...] = grad

    @pl.when(i >= prompt_tiles)
    def _():
        co_ref[...] = result
        cg_ref[...] = grad


def finish(x, attn_sum, mlp_sum, grad_middle, back, gain, prompt_rows):
    rows, width = x.shape
    tile = 128
    prompt_tiles = prompt_rows // tile
    every = pl.BlockSpec((tile, width), lambda i: (i, 0))
    first = pl.BlockSpec((tile, width), lambda i: (jnp.minimum(i, prompt_tiles - 1), 0))
    second = pl.BlockSpec((tile, width), lambda i: (jnp.maximum(i - prompt_tiles, 0), 0))
    shapes = [(prompt_rows, width), (rows - prompt_rows, width)]
    return pl.pallas_call(
        functools.partial(finish_kernel, prompt_tiles),
        grid=(rows // tile,),
        in_specs=[every] * 5 + [pl.BlockSpec((1, width), lambda i: (0, 0))],
        out_specs=[first, second, first, second],
        out_shape=[jax.ShapeDtypeStruct(shape, jnp.bfloat16) for shape in shapes]
        + [jax.ShapeDtypeStruct(shape, jnp.float32) for shape in shapes],
        compiler_params=pltpu.CompilerParams(vmem_limit_bytes=40 << 20),
        cost_estimate=pl.CostEstimate(
            flops=20 * x.size, bytes_accessed=20 * x.size, transcendentals=0
        ),
    )(x, attn_sum, mlp_sum, grad_middle, back, gain)


def per_device(
    prompt_x,
    cont_x,
    prompt_len,
    cont_seg,
    attn_gain,
    q_weight,
    key_matrix,
    value_matrix,
    o_weight,
    mlp_gain,
    gate_weight,
    up_weight,
    down_weight,
    prompt_cot,
    cont_cot,
):
    head_dim = HEAD_SIZE
    data = ("dp", "context")
    prompt_rows = prompt_x.shape[0]
    cont_rows = cont_x.shape[0]
    prompt_total = prompt_rows * lax.axis_size("context")
    q_cols = q_weight.shape[1]
    kv_cols = key_matrix.shape[1]
    q_heads = q_cols // head_dim
    kv_heads = kv_cols // head_dim
    qkv_cols = q_cols + 2 * kv_cols
    qkv_wide = qkv_cols + 2 + -(qkv_cols + 2) % 128
    hidden_cols = gate_weight.shape[1]
    wide = hidden_cols + -hidden_cols % 256
    packed = jnp.concatenate(
        [
            q_weight,
            key_matrix,
            value_matrix,
            attn_gain[:, None],
            mlp_gain[:, None],
            jnp.zeros((q_weight.shape[0], qkv_wide - qkv_cols - 2), jnp.bfloat16),
            o_weight,
        ],
        axis=1,
    )
    packed_full = lax.all_gather(packed, data, axis=0, tiled=True)
    gain_one = packed_full[:, qkv_cols].astype(jnp.float32)[None, :]
    gain_two = packed_full[:, qkv_cols + 1].astype(jnp.float32)[None, :]
    wo_full = packed_full[:, qkv_wide:]
    context_pos = lax.axis_index("context")
    prompt_pos = context_pos * prompt_rows + jnp.arange(prompt_rows, dtype=jnp.int32)
    segment = cont_seg[0]
    earlier = jnp.sum((segment[None, :] < segment[:, None]).astype(jnp.int32), axis=1)
    local_index = jnp.arange(cont_rows, dtype=jnp.int32)
    length = prompt_len[0]
    cont_pos = length + local_index - earlier
    position = jnp.concatenate([prompt_pos, cont_pos]).astype(jnp.float32)
    inv_freq = THETA ** (-jnp.arange(head_dim // 2, dtype=jnp.float32) * 2.0 / head_dim)
    angle_table = inv_freq[:, None] * position[None, :]
    cosine = jnp.cos(angle_table)
    sine_table = jnp.sin(angle_table)
    key_index = jnp.arange(prompt_total, dtype=jnp.int32)
    prompt_mask = jnp.concatenate(
        [key_index[:, None] <= prompt_pos[None, :], jnp.zeros((cont_rows, prompt_rows), jnp.bool_)],
        axis=0,
    )
    own_mask = (segment[:, None] == segment[None, :]) & (
        local_index[:, None] <= local_index[None, :]
    )
    reach_mask = jnp.broadcast_to(key_index[:, None] < length, (prompt_total, cont_rows))
    allowed = jnp.concatenate(
        [prompt_mask, jnp.concatenate([reach_mask, own_mask], axis=0)], axis=1
    )
    bias = jnp.where(allowed, 0.0, NEGATIVE)
    x_all = jnp.concatenate([prompt_x, cont_x], axis=0)
    first_normed, q_t, kv_t = project_rope(
        x_all, packed_full, gain_one, cosine, sine_table, q_heads, kv_heads
    )
    prompt_all = context_gather(kv_t[:, :prompt_rows], 4)
    prompt_all, *mlp_shards = lax.optimization_barrier(
        (prompt_all, down_weight, gate_weight, up_weight)
    )
    fill = ((0, 0), (0, wide - hidden_cols))
    mlp_full = lax.all_gather(
        jnp.concatenate(
            [jnp.pad(w, fill) for w in mlp_shards], axis=1
        ),
        data,
        axis=0,
        tiled=True,
    )
    cont_kv = kv_t[:, prompt_rows:]
    attn_out, lse = attend(prompt_len, q_t, prompt_all, cont_kv, bias, q_heads, kv_heads)
    attn_sum = product_sum([attn_out], [(qkv_wide, qkv_wide + q_cols)], packed_full, 0)
    grad_out = jnp.concatenate([prompt_cot, cont_cot], axis=0)
    normed_two, hidden, grad_gate, grad_up = feed(x_all, attn_sum, gain_two, grad_out, mlp_full)
    mlp_grads, mlp_part, back_two = feed_back(
        grad_gate, grad_up, hidden, mlp_full, grad_out, normed_two, 1
    )

    def scatter(values):
        return lax.psum_scatter(values, data, scatter_dimension=0, tiled=True).astype(jnp.float32)

    cut = math.gcd(prompt_rows + cont_rows, SIZE)
    grad_q, part_kv, own_kv, grad_middle, grad_wo, mlp_sum = window(
        q_t,
        prompt_all,
        cont_kv,
        bias,
        attn_out,
        lse,
        back_two,
        grad_out,
        x_all,
        attn_sum,
        gain_two,
        wo_full,
        cosine,
        sine_table,
        mlp_part.reshape(-1, cut, SIZE),
        q_heads,
        kv_heads,
        3,
    )
    grad_kv = context_scatter(part_kv, own_kv, cosine, sine_table, 5)
    grad_attn = attn_grads(first_normed, grad_q, grad_kv, grad_wo)
    mlp_own = scatter(mlp_grads)
    grad_q, grad_attn, mlp_own = lax.optimization_barrier((grad_q, grad_attn, mlp_own))
    back_one = product_sum(
        [grad_q, grad_kv], [(0, q_cols), (q_cols, qkv_cols)], packed_full, 2
    )
    outs = finish(x_all, attn_sum, mlp_sum, grad_middle, back_one, gain_one, prompt_rows)
    down_own = mlp_own[:, :hidden_cols]
    gate_own = mlp_own[:, wide : wide + hidden_cols]
    up_own = mlp_own[:, 2 * wide : 2 * wide + hidden_cols]
    attn_own = scatter(grad_attn)
    o_own = attn_own[:, :q_cols]
    q_own = attn_own[:, q_cols : 2 * q_cols]
    k_own = attn_own[:, 2 * q_cols : 2 * q_cols + kv_cols]
    v_own = attn_own[:, 2 * q_cols + kv_cols :]

    def row_dot(weight, grad):
        return jnp.sum(weight.astype(jnp.float32) * grad, axis=1)

    gain_rows = jnp.stack(
        [
            (row_dot(q_weight, q_own) + row_dot(key_matrix, k_own) + row_dot(value_matrix, v_own))
            / attn_gain.astype(jnp.float32),
            (row_dot(gate_weight, gate_own) + row_dot(up_weight, up_own))
            / mlp_gain.astype(jnp.float32),
        ]
    )
    gain_rows = lax.psum(gain_rows, "tensor")
    owned = (gain_rows[0], q_own, k_own, v_own, o_own, gain_rows[1], gate_own, up_own, down_own)
    return (*outs, *owned)


def solution(mesh):
    in_specs = (
        P(("dp", "context"), None),
        P(("dp", "context"), None),
        P("dp"),
        P(("dp", "context"), None),
        P(("dp", "context")),
        P(("dp", "context"), "tensor"),
        P(("dp", "context"), "tensor"),
        P(("dp", "context"), "tensor"),
        P(("dp", "context"), "tensor"),
        P(("dp", "context")),
        P(("dp", "context"), "tensor"),
        P(("dp", "context"), "tensor"),
        P(("dp", "context"), "tensor"),
        P(("dp", "context"), None),
        P(("dp", "context"), None),
    )
    out_specs = (
        P(("dp", "context"), None),
        P(("dp", "context"), None),
        P(("dp", "context"), None),
        P(("dp", "context"), None),
        P(("dp", "context")),
        P(("dp", "context"), "tensor"),
        P(("dp", "context"), "tensor"),
        P(("dp", "context"), "tensor"),
        P(("dp", "context"), "tensor"),
        P(("dp", "context")),
        P(("dp", "context"), "tensor"),
        P(("dp", "context"), "tensor"),
        P(("dp", "context"), "tensor"),
    )
    return jax.shard_map(
        per_device, mesh=mesh, in_specs=in_specs, out_specs=out_specs, check_vma=False
    )
```

```python
import functools
import math

import jax
import jax.numpy as jnp
from jax import lax
from jax.experimental import pallas as pl
from jax.experimental.pallas import tpu as pltpu
from jax.sharding import PartitionSpec as P

HEAD_SIZE = 80


EPS = 1e-05
THETA = 10000.0
NEGATIVE = -1e30
LOG2E = math.log2(math.e)
MESH = pl.DeviceIdType.MESH
AXIS = "tensor"
LAG = 3
SIZE = 256
SLOTS = 3


def normalize(values):
    inverse = lax.rsqrt(jnp.mean(values * values, axis=-1, keepdims=True) + EPS)
    return (values * inverse, inverse)


def norm_back(grad_unit, unit_rows, inverse):
    inner_sum = jnp.mean(grad_unit * unit_rows, axis=-1, keepdims=True)
    return inverse * (grad_unit - unit_rows * inner_sum)


def contract_last(left_side, right_side):
    return lax.dot_general(
        left_side, right_side, (((1,), (1,)), ((), ())), preferred_element_type=jnp.float32
    )


def contract_first(left_side, right_side):
    return lax.dot_general(
        left_side, right_side, (((0,), (0,)), ((), ())), preferred_element_type=jnp.float32
    )


def rope_kernel(q_heads, kv_heads, dim, x_ref, w_ref, gain_ref, cos_ref, sin_ref, normed_ref, qt_ref, kvt_ref):
    rows = x_ref[...].astype(jnp.float32)
    inverse = lax.rsqrt(jnp.mean(rows * rows, axis=-1, keepdims=True) + EPS)
    normed = (rows * inverse * gain_ref[...]).astype(jnp.bfloat16)
    normed_ref[...] = normed
    flat = jnp.dot(
        normed, w_ref[:, q_heads * dim :], preferred_element_type=jnp.float32
    ).T
    cosine, sine = cos_ref[...], sin_ref[...]
    half = dim // 2
    for head in range(q_heads + kv_heads):
        first = flat[head * dim : head * dim + half]
        second = flat[head * dim + half : (head + 1) * dim]
        turned = jnp.concatenate(
            [first * cosine - second * sine, second * cosine + first * sine], axis=0
        ).astype(jnp.bfloat16)
        if head < q_heads:
            qt_ref[head * dim : (head + 1) * dim, :] = turned
        else:
            at = (head - q_heads) * dim
            kvt_ref[at : at + dim, :] = turned
    at = (q_heads + kv_heads) * dim
    kvt_ref[kv_heads * dim :, :] = flat[at : at + kv_heads * dim].astype(jnp.bfloat16)


def project_rope(x, packed_full, gain, cos_t, sin_t, q_heads, kv_heads):
    rows, width = x.shape
    dim = HEAD_SIZE
    step = math.gcd(rows, 256)
    cols_wide = packed_full.shape[1]
    by_row = lambda i: (i, 0)
    by_col = lambda i: (0, i)
    fixed = lambda i: (0, 0)
    return pl.pallas_call(
        functools.partial(rope_kernel, q_heads, kv_heads, dim),
        grid=(rows // step,),
        in_specs=[
            pl.BlockSpec((step, width), by_row),
            pl.BlockSpec(packed_full.shape, fixed, pipeline_mode=pl.Buffered(1)),
            pl.BlockSpec((1, width), fixed),
            pl.BlockSpec((dim // 2, step), by_col),
            pl.BlockSpec((dim // 2, step), by_col),
        ],
        out_specs=[
            pl.BlockSpec((step, width), by_row),
            pl.BlockSpec((q_heads * dim, step), by_col),
            pl.BlockSpec((2 * kv_heads * dim, step), by_col),
        ],
        out_shape=[
            jax.ShapeDtypeStruct((rows, width), jnp.bfloat16),
            jax.ShapeDtypeStruct((q_heads * dim, rows), jnp.bfloat16),
            jax.ShapeDtypeStruct((2 * kv_heads * dim, rows), jnp.bfloat16),
        ],
        compiler_params=pltpu.CompilerParams(vmem_limit_bytes=48 << 20),
        cost_estimate=pl.CostEstimate(
            flops=2 * rows * width * cols_wide,
            bytes_accessed=4 * x.size + 2 * width * cols_wide,
            transcendentals=0,
        ),
    )(x, packed_full, gain, cos_t, sin_t)


def greet(axis, count):
    me = lax.axis_index(axis)
    barrier = pltpu.get_barrier_semaphore()
    for k in range(1, count):
        peer = lax.rem(me + k, count)
        pl.semaphore_signal(barrier, inc=1, device_id={axis: peer}, device_id_type=MESH)
    pl.semaphore_wait(barrier, count - 1)


def gather_kernel(count, own_ref, all_ref, send, recv, local):
    me = lax.axis_index("context")
    keep = pltpu.make_async_copy(own_ref, all_ref.at[me], local)
    keep.start()
    greet("context", count)
    copies = []
    for k in range(1, count):
        peer = lax.rem(me + k, count)
        copy = pltpu.make_async_remote_copy(
            own_ref,
            all_ref.at[me],
            send.at[k],
            recv.at[k],
            device_id={"context": peer},
            device_id_type=MESH,
        )
        copy.start()
        copies.append(copy)
    keep.wait()
    for copy in copies:
        copy.wait()


def context_gather(own, cid):
    count = lax.axis_size("context")
    return pl.pallas_call(
        functools.partial(gather_kernel, count),
        out_shape=jax.ShapeDtypeStruct((count, *own.shape), own.dtype),
        in_specs=[pl.BlockSpec(memory_space=pltpu.VMEM)],
        out_specs=pl.BlockSpec(memory_space=pltpu.VMEM),
        scratch_shapes=[
            pltpu.SemaphoreType.DMA((count,)),
            pltpu.SemaphoreType.DMA((count,)),
            pltpu.SemaphoreType.DMA,
        ],
        compiler_params=pltpu.CompilerParams(collective_id=cid, has_side_effects=True),
        cost_estimate=pl.CostEstimate(flops=0, bytes_accessed=8 << 20, transcendentals=0),
    )(own)


def attend_shape(prompt_all, kvt_cont):
    count, kv2, prompt_rows = prompt_all.shape
    cont_rows = kvt_cont.shape[1]
    chunk = math.gcd(math.gcd(prompt_rows, cont_rows), 256)
    return count, kv2, prompt_rows, cont_rows, chunk


def total_kernel(count, part_ref, out_ref, got, send, recv):
    greet(AXIS, count)
    me = lax.axis_index(AXIS)
    copies = []
    for k in range(1, count):
        peer = lax.rem(me + k, count)
        copy = pltpu.make_async_remote_copy(
            part_ref,
            got.at[me],
            send.at[k],
            recv.at[k],
            device_id={AXIS: peer},
            device_id_type=MESH,
        )
        copy.start()
        copies.append(copy)
    got[me] = part_ref[...]
    for copy in copies:
        copy.wait()
    total = got[0]
    for k in range(1, count):
        total += got[k]
    out_ref[...] = total


def tensor_total(part, cid):
    count = lax.axis_size(AXIS)
    return pl.pallas_call(
        functools.partial(total_kernel, count),
        out_shape=jax.ShapeDtypeStruct(part.shape, part.dtype),
        in_specs=[pl.BlockSpec(memory_space=pltpu.VMEM)],
        out_specs=pl.BlockSpec(memory_space=pltpu.VMEM),
        scratch_shapes=[
            pltpu.VMEM((count, *part.shape), part.dtype),
            pltpu.SemaphoreType.DMA((count,)),
            pltpu.SemaphoreType.DMA((count,)),
        ],
        compiler_params=pltpu.CompilerParams(collective_id=cid, has_side_effects=True),
        cost_estimate=pl.CostEstimate(flops=0, bytes_accessed=4 << 20, transcendentals=0),
    )(part)


def fill_keys(chunk, dim, kv_heads, all_ref, cont_ref, rows_of, chunks_ref):
    count, _, prompt_rows = all_ref.shape
    per = prompt_rows // chunk
    total = count * per + cont_ref.shape[1] // chunk
    for c in range(total):
        if c < count * per:
            block = all_ref[c // per, :, (c % per) * chunk : (c % per + 1) * chunk]
        else:
            at = (c - count * per) * chunk
            block = cont_ref[:, at : at + chunk]
        chunks_ref[c] = block
        for n, target in enumerate(rows_of):
            for g in range(kv_heads):
                at = (n * kv_heads + g) * dim
                target[g, c * chunk : (c + 1) * chunk, :] = (
                    block[at : at + dim].astype(jnp.float32).T.astype(jnp.bfloat16)
                )


def trip_count(tile, chunk, i, prompt_rows, count):
    me = lax.axis_index("context")
    prompt_tiles = prompt_rows // tile
    n_prompt = lax.div(me * prompt_rows + (i + 1) * tile + chunk - 1, chunk)
    n_own = lax.div((i - prompt_tiles + 1) * tile + chunk - 1, chunk)
    return i < prompt_tiles, n_prompt, count * prompt_rows // chunk, n_own


class Line:
    def __init__(self, part, recv, out, sink, sems, sink_sems):
        self.part, self.recv, self.out, self.sink = part, recv, out, sink
        self.per = sink.shape[0] // out.shape[1]
        self.sems, self.sink_sems = sems, sink_sems
        self.blocks = out.shape[0]
        me, n = lax.axis_index(AXIS), lax.axis_size(AXIS)
        self.outer = (me == 0) | (me == n - 1)
        self.inner = jnp.logical_not(self.outer)
        self.mate = jnp.where(me < n // 2, 1 - me, 2 * n - 3 - me)
        self.across = n - 1 - me

    def copy(self, k, source, target, peer, b):
        return pltpu.make_async_remote_copy(
            source.at[b],
            target.at[b],
            self.sems.at[2 * k, b],
            self.sems.at[2 * k + 1, b],
            device_id={AXIS: peer},
            device_id_type=MESH,
        )

    def up(self, b):
        return self.copy(0, self.part, self.recv, self.mate, b)

    def mid(self, b):
        return self.copy(1, self.part, self.out, self.across, b)

    def down(self, b):
        return self.copy(2, self.out, self.out, self.mate, b)

    def keep(self, b):
        _, rows, cols = self.out.shape
        at = (
            pl.ds(pl.multiple_of(lax.rem(b, self.per) * rows, rows), rows),
            pl.ds(pl.multiple_of(lax.div(b, self.per) * cols, cols), cols),
        )
        return pltpu.make_async_copy(self.out.at[b], self.sink.at[at], self.sink_sems.at[b])

    def greet(self, axis=None, count=1):
        barrier = pltpu.get_barrier_semaphore()
        pl.semaphore_signal(barrier, inc=1, device_id={AXIS: self.mate}, device_id_type=MESH)
        for k in range(1, count):
            peer = lax.rem(lax.axis_index(axis) + k, count)
            pl.semaphore_signal(barrier, inc=1, device_id={axis: peer}, device_id_type=MESH)

        @pl.when(self.inner)
        def _():
            pl.semaphore_signal(barrier, inc=1, device_id={AXIS: self.across}, device_id_type=MESH)
            pl.semaphore_wait(barrier, 1 + count)

        @pl.when(self.outer)
        def _():
            pl.semaphore_wait(barrier, count)

    def start(self, first, count):
        @pl.when(self.outer)
        def _():
            @pl.loop(0, count)
            def _(k):
                self.up(first + k).start()

    def step(self, t):
        @pl.when(self.inner & (t >= 0) & (t < self.blocks))
        def _():
            self.up(t).wait_recv()
            self.part[t] = (
                self.part[t].astype(jnp.float32) + self.recv[t].astype(jnp.float32)
            ).astype(jnp.bfloat16)
            self.mid(t).start()

        @pl.when(self.inner & (t >= LAG) & (t < self.blocks + LAG))
        def _():
            b = t - LAG
            self.mid(b).wait()
            self.out[b] = (
                self.part[b].astype(jnp.float32) + self.out[b].astype(jnp.float32)
            ).astype(jnp.bfloat16)
            self.down(b).start()
            self.keep(b).start()

    def drain(self):
        for k in range(LAG):
            self.step(self.blocks + k)

        @pl.when(self.outer)
        def _():
            @pl.loop(0, self.blocks)
            def _(b):
                self.down(b).wait_recv()
                self.keep(b).start()
                self.up(b).wait_send()

        @pl.when(self.inner)
        def _():
            @pl.loop(0, self.blocks)
            def _(b):
                self.down(b).wait_send()

        @pl.loop(0, self.blocks)
        def _(b):
            self.keep(b).wait()


def line_scratch(shape):
    return [pltpu.VMEM(shape, jnp.bfloat16)] * 3 + [
        pltpu.SemaphoreType.DMA((6, shape[0])),
        pltpu.SemaphoreType.DMA((shape[0],)),
    ]


def attend_kernel(
    shape,
    dim,
    kv_heads,
    per,
    tile,
    cut,
    q_ref,
    all_ref,
    cont_ref,
    bias_ref,
    wo_ref,
    out_ref,
    lse_ref,
    sum_ref,
    keys,
    chunks,
    part,
    recv,
    out,
    sems,
    sink_sems,
):
    count, prompt_rows, chunk = shape
    i = pl.program_id(0)
    line = Line(part, recv, out, sum_ref, sems, sink_sems)
    blocks = tile // cut

    @pl.when(i == 0)
    def _():
        fill_keys(chunk, dim, kv_heads, all_ref, cont_ref, [keys], chunks)
        line.greet()

    is_prompt, n_prompt, base, n_own = trip_count(tile, chunk, i, prompt_rows, count)
    wide = per * tile
    factor = dim ** (-0.5) * LOG2E
    outs, sums = [], []
    for g in range(kv_heads):
        q = jnp.concatenate(
            [q_ref[(g * per + h) * dim : (g * per + h + 1) * dim, :] for h in range(per)], axis=1
        )

        def body(c, state):
            top, total, acc = state
            at = pl.ds(pl.multiple_of(c * chunk, chunk), chunk)
            s = jnp.dot(keys[g, at, :], q, preferred_element_type=jnp.float32)
            t = s * factor + jnp.concatenate([bias_ref[at, :]] * per, axis=1)
            new = jnp.maximum(top, jnp.max(t, axis=0, keepdims=True))
            p = jnp.exp2(t - new)
            scale = jnp.exp2(top - new)
            total = total * scale + jnp.sum(p, axis=0, keepdims=True)
            v = chunks[c, (kv_heads + g) * dim : (kv_heads + g + 1) * dim, :]
            acc = acc * scale + jnp.dot(
                v, p.astype(jnp.bfloat16), preferred_element_type=jnp.float32
            )
            return new, total, acc

        start = (
            jnp.full((1, wide), NEGATIVE, jnp.float32),
            jnp.zeros((1, wide), jnp.float32),
            jnp.zeros((dim, wide), jnp.float32),
        )
        state = lax.fori_loop(0, jnp.where(is_prompt, n_prompt, base), body, start)
        top, total, acc = lax.fori_loop(base, base + jnp.where(is_prompt, 0, n_own), body, state)
        acc = acc / total
        top = top + jnp.log2(total)
        outs += [acc[:, h * tile : (h + 1) * tile] for h in range(per)]
        sums += [top[:, h * tile : (h + 1) * tile] for h in range(per)]
        if g < kv_heads - 1:
            for r in range(blocks // 2):
                line.step((i - 1) * blocks + r)
    attended = jnp.concatenate(outs, axis=0).T.astype(jnp.bfloat16)
    out_ref[...] = attended
    lse_ref[...] = jnp.concatenate(sums, axis=0)
    term = contract_last(attended, wo_ref[...]).astype(jnp.bfloat16)
    for r in range(blocks):
        part[i * blocks + r] = term[r * cut : (r + 1) * cut]

    line.start(i * blocks, blocks)
    for r in range(blocks // 2, blocks):
        line.step((i - 1) * blocks + r)

    @pl.when(i == pl.num_programs(0) - 1)
    def _():
        @pl.loop(0, blocks)
        def _(r):
            line.step(i * blocks + r)

        line.drain()


def attend(q_t, prompt_all, kvt_cont, bias, packed_full, q_heads, kv_heads, cid):
    dim = HEAD_SIZE
    count, kv2, prompt_rows, cont_rows, chunk = attend_shape(prompt_all, kvt_cont)
    q_cols, rows = q_t.shape
    width = packed_full.shape[0]
    keys_all = bias.shape[0]
    tile, cut = 128, 32
    whole = pl.BlockSpec(memory_space=pltpu.VMEM)
    by_col = lambda i: (0, i)
    return pl.pallas_call(
        functools.partial(
            attend_kernel,
            (count, prompt_rows, chunk),
            dim,
            kv_heads,
            q_heads // kv_heads,
            tile,
            cut,
        ),
        grid=(rows // tile,),
        in_specs=[
            pl.BlockSpec((q_cols, tile), by_col),
            whole,
            whole,
            pl.BlockSpec((keys_all, tile), by_col),
            pl.BlockSpec((width, q_cols), lambda i: (0, 0), pipeline_mode=pl.Buffered(1)),
        ],
        out_specs=[
            pl.BlockSpec((tile, q_cols), lambda i: (i, 0)),
            pl.BlockSpec((q_heads, tile), by_col),
            pl.BlockSpec(memory_space=pl.ANY),
        ],
        out_shape=[
            jax.ShapeDtypeStruct((rows, q_cols), jnp.bfloat16),
            jax.ShapeDtypeStruct((q_heads, rows), jnp.float32),
            jax.ShapeDtypeStruct((rows, width), jnp.bfloat16),
        ],
        scratch_shapes=[
            pltpu.VMEM((kv_heads, keys_all, dim), jnp.bfloat16),
            pltpu.VMEM((keys_all // chunk, kv2, chunk), jnp.bfloat16),
            *line_scratch((rows // cut, cut, width)),
        ],
        compiler_params=pltpu.CompilerParams(
            collective_id=cid, has_side_effects=True, vmem_limit_bytes=40 << 20
        ),
        cost_estimate=pl.CostEstimate(
            flops=120_000_000_000, bytes_accessed=40 << 20, transcendentals=0
        ),
    )(q_t, prompt_all, kvt_cont, bias, packed_full)


def feed_back_kernel(
    cut,
    gate_ref,
    up_ref,
    hidden_ref,
    wd_ref,
    wg_ref,
    wu_ref,
    cot_ref,
    normed_ref,
    grads_ref,
    up_grads_ref,
    mlp_ref,
    sum_ref,
    part,
    recv,
    out,
    sems,
    sink_sems,
):
    n = pl.program_id(0)
    rows, wide = gate_ref.shape
    per = rows // cut
    line = Line(part, recv, out, sum_ref, sems, sink_sems)

    back = contract_last(gate_ref[...], wg_ref[...]) + contract_last(up_ref[...], wu_ref[...])
    back = back.astype(jnp.bfloat16)
    for r in range(per):
        part[n * per + r] = back[r * cut : (r + 1) * cut]

    @pl.when(n == 0)
    def _():
        line.greet()

    line.start(n * per, per)

    def steps(low, high):
        for r in range(low, high):
            line.step(n * per + r)

    grads_ref[:, :wide] = contract_first(cot_ref[...], hidden_ref[...]).astype(jnp.bfloat16)
    steps(0, per // 4)
    grads_ref[:, wide:] = contract_first(normed_ref[...], gate_ref[...]).astype(
        jnp.bfloat16
    )
    steps(per // 4, per // 2)
    up_grads_ref[...] = contract_first(normed_ref[...], up_ref[...]).astype(jnp.bfloat16)
    steps(per // 2, per - per // 4)
    mlp_ref[0] = contract_last(hidden_ref[...], wd_ref[...]).astype(jnp.bfloat16)
    steps(per - per // 4, per)

    @pl.when(n == pl.num_programs(0) - 1)
    def _():
        line.drain()


def feed_back(grad_gate, grad_up, hidden, mlp_full, cot, normed, cid):
    rows, wide = hidden.shape
    width = cot.shape[1]
    size = SIZE
    cut = math.gcd(rows, size)
    tiles = width // size
    blocks = (tiles * rows // cut, cut, size)
    whole = pl.BlockSpec(memory_space=pltpu.VMEM)
    return pl.pallas_call(
        functools.partial(feed_back_kernel, cut),
        grid=(tiles,),
        in_specs=[whole] * 3
        + [pl.BlockSpec((size, wide), lambda n, k=k: (n, k)) for k in range(3)]
        + [pl.BlockSpec((rows, size), lambda n: (0, n))] * 2,
        out_specs=[
            pl.BlockSpec((size, 2 * wide), lambda n: (n, 0)),
            pl.BlockSpec((size, wide), lambda n: (n, 0)),
            pl.BlockSpec((1, rows, size), lambda n: (n, 0, 0)),
            pl.BlockSpec(memory_space=pl.ANY),
        ],
        out_shape=[
            jax.ShapeDtypeStruct((width, 2 * wide), jnp.bfloat16),
            jax.ShapeDtypeStruct((width, wide), jnp.bfloat16),
            jax.ShapeDtypeStruct((tiles, rows, size), jnp.bfloat16),
            jax.ShapeDtypeStruct((rows, width), jnp.bfloat16),
        ],
        scratch_shapes=line_scratch(blocks),
        compiler_params=pltpu.CompilerParams(
            collective_id=cid, has_side_effects=True, vmem_limit_bytes=58 << 20
        ),
        cost_estimate=pl.CostEstimate(
            flops=12 * rows * wide * width, bytes_accessed=200 << 20, transcendentals=0
        ),
    )(grad_gate, grad_up, hidden, mlp_full, mlp_full, mlp_full, cot, normed)


def window_kernel(
    shape,
    dim,
    kv_heads,
    per,
    tile,
    q_ref,
    all_ref,
    cont_ref,
    bias_ref,
    out_ref,
    lse_ref,
    back_ref,
    cot_ref,
    x_ref,
    attn_ref,
    gain_ref,
    wo_ref,
    cos_ref,
    sin_ref,
    cos_own_ref,
    sin_own_ref,
    normed_ref,
    up_grads_ref,
    mlp_ref,
    gq_out_ref,
    gkv_ref,
    gm_ref,
    grads_ref,
    sum_ref,
    keys,
    values,
    chunks,
    gk,
    gv,
    go,
    gq_ref,
    send_ref,
    got,
    own_ref,
    kv_sems,
    part,
    recv,
    out,
    sems,
    sink_sems,
):
    count, prompt_rows, chunk = shape
    i = pl.program_id(0)
    line = Line(part, recv, out, sum_ref, sems, sink_sems)
    context = lax.axis_index("context")
    prompt_tiles = prompt_rows // tile
    tiles = gq_ref.shape[0]
    slots = SLOTS
    spots = 2 + kv_heads

    def step(k):
        for s in range(k * slots // spots, (k + 1) * slots // spots):
            line.step(i * slots + s)

    def send(k):
        peer = lax.rem(context + k, count)
        return pltpu.make_async_remote_copy(
            send_ref.at[peer],
            got.at[k],
            kv_sems.at[0, k],
            kv_sems.at[1, k],
            device_id={"context": peer},
            device_id_type=MESH,
        )

    root = dim ** (-0.5)
    half = dim // 2

    @pl.when(i == 0)
    def _():
        load = pltpu.make_async_copy(mlp_ref, part, sink_sems.at[0])
        load.start()
        fill_keys(chunk, dim, kv_heads, all_ref, cont_ref, [keys, values], chunks)
        gk[...] = jnp.zeros_like(gk)
        gv[...] = jnp.zeros_like(gv)
        go[...] = jnp.zeros_like(go)
        line.greet("context", count)
        load.wait()
        line.start(0, line.blocks)

    @pl.when(i < tiles)
    def _():
        middle = x_ref[...].astype(jnp.float32) + attn_ref[...].astype(jnp.float32)
        inverse = lax.rsqrt(jnp.mean(middle * middle, axis=-1, keepdims=True) + EPS)
        unit = middle * inverse
        grad_unit = back_ref[...].astype(jnp.float32) * gain_ref[...]
        grad_middle = cot_ref[...].astype(jnp.float32) + norm_back(grad_unit, unit, inverse)
        gm_ref[...] = grad_middle
        grad_b = grad_middle.astype(jnp.bfloat16)
        step(0)
        grad_t = (
            jnp.dot(grad_b, wo_ref[...], preferred_element_type=jnp.float32).astype(jnp.bfloat16)
        ).astype(jnp.float32).T
        go[...] += contract_first(grad_b, out_ref[...])
        step(1)

        is_prompt, n_prompt, base, n_own = trip_count(tile, chunk, i, prompt_rows, count)
        factor = root * LOG2E
        prod = grad_t * out_ref[...].astype(jnp.float32).T
        grad_t = grad_t.astype(jnp.bfloat16)
        cosine, sine = cos_ref[...], sin_ref[...]
        pieces = []
        for g in range(kv_heads):
            heads = [g * per + h for h in range(per)]
            q = jnp.concatenate([q_ref[h * dim : (h + 1) * dim, :] for h in heads], axis=1)
            grad = jnp.concatenate([grad_t[h * dim : (h + 1) * dim] for h in heads], axis=1)
            inner = jnp.concatenate(
                [jnp.sum(prod[h * dim : (h + 1) * dim], axis=0, keepdims=True) for h in heads], axis=1
            )
            lse = jnp.concatenate([lse_ref[h : h + 1, :] for h in heads], axis=1)

            def body(c, acc):
                at = pl.ds(pl.multiple_of(c * chunk, chunk), chunk)
                s = jnp.dot(keys[g, at, :], q, preferred_element_type=jnp.float32)
                b = bias_ref[at, :]
                p = jnp.exp2(s * factor + (jnp.concatenate([b] * per, axis=1) - lse))
                dp = jnp.dot(values[g, at, :], grad, preferred_element_type=jnp.float32)
                ds = (p * (dp - inner)).astype(jnp.bfloat16)
                gv[g, at, :] += contract_last(p.astype(jnp.bfloat16), grad)
                gk[g, at, :] += contract_last(ds, q)
                k_t = chunks[c, g * dim : (g + 1) * dim, :]
                return acc + jnp.dot(k_t, ds, preferred_element_type=jnp.float32)

            acc = jnp.zeros((dim, per * tile), jnp.float32)
            acc = lax.fori_loop(0, jnp.where(is_prompt, n_prompt, base), body, acc)
            acc = lax.fori_loop(base, base + jnp.where(is_prompt, 0, n_own), body, acc)
            acc = acc * root
            for h in range(per):
                first = acc[:half, h * tile : (h + 1) * tile]
                second = acc[half:, h * tile : (h + 1) * tile]
                pieces += [first * cosine + second * sine, second * cosine - first * sine]
            step(2 + g)
        rows_q = jnp.concatenate(pieces, axis=0).T.astype(jnp.bfloat16)
        gq_ref[i] = rows_q
        gq_out_ref[...] = rows_q

    @pl.when(i == tiles - 1)
    def _():
        for g in range(kv_heads):
            for n, (acc, scale) in enumerate(((gk, root), (gv, 1.0))):
                at = (n * kv_heads + g) * dim
                for c in range(count):
                    rows = acc[g, c * prompt_rows : (c + 1) * prompt_rows, :]
                    send_ref[c, at : at + dim, :] = (rows * scale).T.astype(jnp.bfloat16)
                own_ref[at : at + dim, :] = (acc[g, count * prompt_rows :, :] * scale).T
        for k in range(1, count):
            send(k).start()

    @pl.when(i == tiles)
    def _():
        line.step(tiles * slots)
        kv_dim = kv_heads * dim

        def finish(flat, cosine, sine):
            pieces = []
            for at in range(0, kv_dim, dim):
                first, second = flat[at : at + half], flat[at + half : at + dim]
                pieces += [first * cosine + second * sine, second * cosine - first * sine]
            pieces.append(flat[kv_dim:])
            return jnp.concatenate(pieces, axis=0).T.astype(jnp.bfloat16)

        cosine, sine = cos_own_ref[...], sin_own_ref[...]
        gkv_ref[prompt_rows:, :] = finish(
            own_ref[...], cosine[:, prompt_rows:], sine[:, prompt_rows:]
        )
        total = send_ref[context].astype(jnp.float32)
        for k in range(1, count):
            send(k).wait()
            total += got[k].astype(jnp.float32)
        gkv_ref[:prompt_rows, :] = finish(
            total, cosine[:, :prompt_rows], sine[:, :prompt_rows]
        )

    @pl.when(i >= tiles)
    def _():
        n = i - tiles
        later = pl.num_programs(0) - tiles
        rest = line.blocks - tiles * slots - 1
        q_cols = go.shape[1]
        wide = up_grads_ref.shape[1]
        grads_ref[:, :wide] = up_grads_ref[...]
        grads_ref[:, wide : wide + q_cols] = go[pl.ds(pl.multiple_of(n * SIZE, SIZE), SIZE), :].astype(
            jnp.bfloat16
        )
        total = jnp.zeros((SIZE, q_cols), jnp.float32)
        for k in range(tiles):
            total += contract_first(normed_ref[k * tile : (k + 1) * tile, :], gq_ref[k])
        grads_ref[:, wide + q_cols : wide + 2 * q_cols] = total.astype(jnp.bfloat16)
        grads_ref[:, wide + 2 * q_cols :] = contract_first(normed_ref[...], gkv_ref[...]).astype(
            jnp.bfloat16
        )
        low = tiles * slots + 1 + lax.div(n * rest, later)
        high = tiles * slots + 1 + lax.div((n + 1) * rest, later)

        @pl.loop(low, high)
        def _(t):
            line.step(t)

        @pl.when(n == later - 1)
        def _():
            line.drain()


def window(
    q_t,
    prompt_all,
    kvt_cont,
    bias,
    attended,
    lse,
    back,
    cot,
    x,
    attn_sum,
    gain,
    packed_full,
    cos_t,
    sin_t,
    normed,
    up_grads,
    mlp_part,
    q_heads,
    kv_heads,
    cid,
):
    dim = HEAD_SIZE
    count, kv2, prompt_rows, cont_rows, chunk = attend_shape(prompt_all, kvt_cont)
    rows, width = cot.shape
    q_cols = q_heads * dim
    keys_all = bias.shape[0]
    tile = 128
    whole = pl.BlockSpec(memory_space=pltpu.VMEM)
    anywhere = pl.BlockSpec(memory_space=pl.ANY)
    tiles, later = rows // tile, width // SIZE
    grad_cols = up_grads.shape[1] + 2 * q_cols + kv2
    early = lambda i: jnp.minimum(i, tiles - 1)
    late = lambda i: jnp.maximum(i - tiles, 0)
    by_col = lambda i: (0, early(i))
    by_row = lambda i: (early(i), 0)
    fixed = lambda i: (0, 0)
    return pl.pallas_call(
        functools.partial(
            window_kernel, (count, prompt_rows, chunk), dim, kv_heads, q_heads // kv_heads, tile
        ),
        grid=(tiles + later,),
        in_specs=[
            pl.BlockSpec((q_cols, tile), by_col),
            whole,
            whole,
            pl.BlockSpec((keys_all, tile), by_col),
            pl.BlockSpec((tile, q_cols), by_row),
            pl.BlockSpec((q_heads, tile), by_col),
            pl.BlockSpec((tile, width), by_row),
            pl.BlockSpec((tile, width), by_row),
            pl.BlockSpec((tile, width), by_row),
            pl.BlockSpec((tile, width), by_row),
            pl.BlockSpec((1, width), fixed),
            pl.BlockSpec((width, q_cols), fixed, pipeline_mode=pl.Buffered(1)),
            pl.BlockSpec((dim // 2, tile), by_col),
            pl.BlockSpec((dim // 2, tile), by_col),
            whole,
            whole,
            pl.BlockSpec((rows, SIZE), lambda i: (0, late(i))),
            pl.BlockSpec((SIZE, up_grads.shape[1]), lambda i: (late(i), 0)),
            anywhere,
        ],
        out_specs=[
            pl.BlockSpec((tile, q_cols), by_row),
            pl.BlockSpec((rows, kv2), fixed),
            pl.BlockSpec((tile, width), by_row),
            pl.BlockSpec((SIZE, grad_cols), lambda i: (late(i), 0)),
            anywhere,
        ],
        out_shape=[
            jax.ShapeDtypeStruct((rows, q_cols), jnp.bfloat16),
            jax.ShapeDtypeStruct((rows, kv2), jnp.bfloat16),
            jax.ShapeDtypeStruct((rows, width), jnp.float32),
            jax.ShapeDtypeStruct((width, grad_cols), jnp.bfloat16),
            jax.ShapeDtypeStruct((rows, width), jnp.bfloat16),
        ],
        scratch_shapes=[
            pltpu.VMEM((kv_heads, keys_all, dim), jnp.bfloat16),
            pltpu.VMEM((kv_heads, keys_all, dim), jnp.bfloat16),
            pltpu.VMEM((keys_all // chunk, kv2, chunk), jnp.bfloat16),
            pltpu.VMEM((kv_heads, keys_all, dim), jnp.float32),
            pltpu.VMEM((kv_heads, keys_all, dim), jnp.float32),
            pltpu.VMEM((width, q_cols), jnp.float32),
            pltpu.VMEM((tiles, tile, q_cols), jnp.bfloat16),
            pltpu.VMEM((count, kv2, prompt_rows), jnp.bfloat16),
            pltpu.VMEM((count, kv2, prompt_rows), jnp.bfloat16),
            pltpu.VMEM((kv2, cont_rows), jnp.float32),
            pltpu.SemaphoreType.DMA((2, count)),
            *line_scratch(mlp_part.shape),
        ],
        compiler_params=pltpu.CompilerParams(
            collective_id=cid, has_side_effects=True, vmem_limit_bytes=60 << 20
        ),
        cost_estimate=pl.CostEstimate(
            flops=120_000_000_000, bytes_accessed=200 << 20, transcendentals=0
        ),
    )(
        q_t,
        prompt_all,
        kvt_cont,
        bias,
        attended,
        lse,
        back,
        cot,
        x,
        attn_sum,
        gain,
        packed_full,
        cos_t,
        sin_t,
        cos_t,
        sin_t,
        normed,
        up_grads,
        mlp_part,
    )


def product_kernel(cut, spans, lhs_refs, w_ref, sum_ref, part, recv, out, sems, sink_sems):
    n = pl.program_id(0)
    per = sum_ref.shape[0] // cut
    line = Line(part, recv, out, sum_ref, sems, sink_sems)
    term = sum(
        contract_last(ref[...], w_ref[:, low:high]) for ref, (low, high) in zip(lhs_refs, spans)
    ).astype(jnp.bfloat16)
    for r in range(per):
        part[n * per + r] = term[r * cut : (r + 1) * cut]

    @pl.when(n == 0)
    def _():
        line.greet()

    line.start(n * per, per)
    for r in range(per):
        line.step(n * per + r)

    @pl.when(n == pl.num_programs(0) - 1)
    def _():
        line.drain()


def product_sum(lhs, spans, weights, cid):
    rows = lhs[0].shape[0]
    width, cols = weights.shape
    cut = math.gcd(rows, SIZE)
    tiles = width // SIZE
    blocks = (tiles * rows // cut, cut, SIZE)

    def body(*refs):
        product_kernel(cut, spans, refs[: len(lhs)], *refs[len(lhs) :])

    return pl.pallas_call(
        body,
        grid=(tiles,),
        in_specs=[pl.BlockSpec(memory_space=pltpu.VMEM)] * len(lhs)
        + [pl.BlockSpec((SIZE, cols), lambda n: (n, 0))],
        out_specs=pl.BlockSpec(memory_space=pl.ANY),
        out_shape=jax.ShapeDtypeStruct((rows, width), jnp.bfloat16),
        scratch_shapes=line_scratch(blocks),
        compiler_params=pltpu.CompilerParams(
            collective_id=cid, has_side_effects=True, vmem_limit_bytes=40 << 20
        ),
        cost_estimate=pl.CostEstimate(
            flops=120_000_000_000, bytes_accessed=40 << 20, transcendentals=0
        ),
    )(*lhs, weights)


def feed_kernel(
    x_ref,
    attn_ref,
    gain_ref,
    cot_ref,
    wd_ref,
    wg_ref,
    wu_ref,
    normed_ref,
    hidden_ref,
    gate_grad_ref,
    up_grad_ref,
):
    @pl.when(pl.program_id(0) == 0)
    def _():
        @pl.loop(0, x_ref.shape[0] // 64)
        def _(r):
            at = pl.ds(pl.multiple_of(r * 64, 64), 64)
            middle = x_ref[at, :].astype(jnp.float32) + attn_ref[at, :].astype(jnp.float32)
            unit, _ = normalize(middle)
            normed_ref[at, :] = (unit * gain_ref[...]).astype(jnp.bfloat16)

    gate = jnp.dot(normed_ref[...], wg_ref[...], preferred_element_type=jnp.float32)
    up = jnp.dot(normed_ref[...], wu_ref[...], preferred_element_type=jnp.float32)
    grad_hidden = jnp.dot(cot_ref[...], wd_ref[...], preferred_element_type=jnp.float32)
    sigmoid = 1.0 / (1.0 + jnp.exp(-gate))
    silu = gate * sigmoid
    hidden_ref[...] = (silu * up).astype(jnp.bfloat16)
    gate_grad_ref[...] = (grad_hidden * up * sigmoid * (1.0 + gate * (1.0 - sigmoid))).astype(
        jnp.bfloat16
    )
    up_grad_ref[...] = (grad_hidden * silu).astype(jnp.bfloat16)


def feed(x, attn_sum, gain, cot, mlp_full):
    rows, width = x.shape
    wide = mlp_full.shape[1] // 3
    tiles = wide // SIZE
    whole = pl.BlockSpec(memory_space=pltpu.VMEM)
    tile = pl.BlockSpec((rows, SIZE), lambda n: (0, n))
    return pl.pallas_call(
        feed_kernel,
        grid=(tiles,),
        in_specs=[whole] * 4
        + [pl.BlockSpec((width, SIZE), lambda n, k=k: (0, k * tiles + n)) for k in range(3)],
        out_specs=[
            pl.BlockSpec((rows, width), lambda n: (0, 0), pipeline_mode=pl.Buffered(1)),
            tile,
            tile,
            tile,
        ],
        out_shape=[jax.ShapeDtypeStruct((rows, width), jnp.bfloat16)]
        + [jax.ShapeDtypeStruct((rows, wide), jnp.bfloat16)] * 3,
        compiler_params=pltpu.CompilerParams(vmem_limit_bytes=58 << 20),
        cost_estimate=pl.CostEstimate(
            flops=6 * rows * width * wide, bytes_accessed=60 << 20, transcendentals=rows * wide
        ),
    )(x, attn_sum, gain, cot, mlp_full, mlp_full, mlp_full)


def finish_kernel(
    prompt_tiles, x_ref, attn_ref, mlp_ref, gm_ref, back_ref, gain_ref, po_ref, co_ref, pg_ref, cg_ref
):
    i = pl.program_id(0)
    x = x_ref[...].astype(jnp.float32)
    result = (x + attn_ref[...].astype(jnp.float32)) + mlp_ref[...].astype(jnp.float32)
    result = result.astype(jnp.bfloat16)
    unit, inverse = normalize(x)
    grad = gm_ref[...] + norm_back(back_ref[...].astype(jnp.float32) * gain_ref[...], unit, inverse)

    @pl.when(i < prompt_tiles)
    def _():
        po_ref[...] = result
        pg_ref[...] = grad

    @pl.when(i >= prompt_tiles)
    def _():
        co_ref[...] = result
        cg_ref[...] = grad


def finish(x, attn_sum, mlp_sum, grad_middle, back, gain, prompt_rows):
    rows, width = x.shape
    tile = 128
    prompt_tiles = prompt_rows // tile
    every = pl.BlockSpec((tile, width), lambda i: (i, 0))
    first = pl.BlockSpec((tile, width), lambda i: (jnp.minimum(i, prompt_tiles - 1), 0))
    second = pl.BlockSpec((tile, width), lambda i: (jnp.maximum(i - prompt_tiles, 0), 0))
    shapes = [(prompt_rows, width), (rows - prompt_rows, width)]
    return pl.pallas_call(
        functools.partial(finish_kernel, prompt_tiles),
        grid=(rows // tile,),
        in_specs=[every] * 5 + [pl.BlockSpec((1, width), lambda i: (0, 0))],
        out_specs=[first, second, first, second],
        out_shape=[jax.ShapeDtypeStruct(shape, jnp.bfloat16) for shape in shapes]
        + [jax.ShapeDtypeStruct(shape, jnp.float32) for shape in shapes],
        compiler_params=pltpu.CompilerParams(vmem_limit_bytes=40 << 20),
        cost_estimate=pl.CostEstimate(
            flops=20 * x.size, bytes_accessed=20 * x.size, transcendentals=0
        ),
    )(x, attn_sum, mlp_sum, grad_middle, back, gain)


def per_device(
    prompt_x,
    cont_x,
    prompt_len,
    cont_seg,
    attn_gain,
    q_weight,
    key_matrix,
    value_matrix,
    o_weight,
    mlp_gain,
    gate_weight,
    up_weight,
    down_weight,
    prompt_cot,
    cont_cot,
):
    head_dim = HEAD_SIZE
    data = ("dp", "context")
    prompt_rows = prompt_x.shape[0]
    cont_rows = cont_x.shape[0]
    prompt_total = prompt_rows * lax.axis_size("context")
    q_cols = q_weight.shape[1]
    kv_cols = key_matrix.shape[1]
    q_heads = q_cols // head_dim
    kv_heads = kv_cols // head_dim
    qkv_cols = q_cols + 2 * kv_cols
    qkv_wide = qkv_cols + 2 + -(qkv_cols + 2) % 128
    hidden_cols = gate_weight.shape[1]
    wide = hidden_cols + -hidden_cols % 256
    packed = jnp.concatenate(
        [
            o_weight,
            q_weight,
            key_matrix,
            value_matrix,
            attn_gain[:, None],
            mlp_gain[:, None],
            jnp.zeros((q_weight.shape[0], qkv_wide - qkv_cols - 2), jnp.bfloat16),
        ],
        axis=1,
    )
    packed_full = lax.all_gather(packed, data, axis=0, tiled=True)
    context_pos = lax.axis_index("context")
    prompt_pos = context_pos * prompt_rows + jnp.arange(prompt_rows, dtype=jnp.int32)
    segment = cont_seg[0]
    earlier = jnp.sum((segment[None, :] < segment[:, None]).astype(jnp.int32), axis=1)
    local_index = jnp.arange(cont_rows, dtype=jnp.int32)
    length = prompt_len[0]
    cont_pos = length + local_index - earlier
    position = jnp.concatenate([prompt_pos, cont_pos]).astype(jnp.float32)
    inv_freq = THETA ** (-jnp.arange(head_dim // 2, dtype=jnp.float32) * 2.0 / head_dim)
    angle_table = inv_freq[:, None] * position[None, :]
    cosine = jnp.cos(angle_table)
    sine_table = jnp.sin(angle_table)
    key_index = jnp.arange(prompt_total, dtype=jnp.int32)
    prompt_mask = jnp.concatenate(
        [key_index[:, None] <= prompt_pos[None, :], jnp.zeros((cont_rows, prompt_rows), jnp.bool_)],
        axis=0,
    )
    own_mask = (segment[:, None] == segment[None, :]) & (
        local_index[:, None] <= local_index[None, :]
    )
    reach_mask = jnp.broadcast_to(key_index[:, None] < length, (prompt_total, cont_rows))
    allowed = jnp.concatenate(
        [prompt_mask, jnp.concatenate([reach_mask, own_mask], axis=0)], axis=1
    )
    bias = jnp.where(allowed, 0.0, NEGATIVE)
    x_all = jnp.concatenate([prompt_x, cont_x], axis=0)
    grad_out = jnp.concatenate([prompt_cot, cont_cot], axis=0)
    fill = ((0, 0), (0, wide - hidden_cols))
    mlp_shard = jnp.concatenate(
        [jnp.pad(w, fill) for w in (down_weight, gate_weight, up_weight)], axis=1
    )
    packed_full, bias, x_all, grad_out, mlp_shard, cosine, sine_table = lax.optimization_barrier(
        (packed_full, bias, x_all, grad_out, mlp_shard, cosine, sine_table)
    )
    gain_one = packed_full[:, q_cols + qkv_cols].astype(jnp.float32)[None, :]
    gain_two = packed_full[:, q_cols + qkv_cols + 1].astype(jnp.float32)[None, :]
    first_normed, q_t, kv_t = project_rope(
        x_all, packed_full, gain_one, cosine, sine_table, q_heads, kv_heads
    )
    prompt_all = context_gather(kv_t[:, :prompt_rows], 4)
    prompt_all, mlp_shard = lax.optimization_barrier((prompt_all, mlp_shard))
    mlp_full = lax.all_gather(mlp_shard, data, axis=0, tiled=True)
    cont_kv = kv_t[:, prompt_rows:]
    attn_out, lse, attn_sum = attend(
        q_t, prompt_all, cont_kv, bias, packed_full, q_heads, kv_heads, 0
    )
    normed_two, hidden, grad_gate, grad_up = feed(x_all, attn_sum, gain_two, grad_out, mlp_full)
    mlp_grads, up_grads, mlp_part, back_two = feed_back(
        grad_gate, grad_up, hidden, mlp_full, grad_out, normed_two, 1
    )

    def scatter(values):
        return lax.psum_scatter(values, data, scatter_dimension=0, tiled=True).astype(jnp.float32)

    cut = math.gcd(prompt_rows + cont_rows, SIZE)
    grad_q, grad_kv, grad_middle, grad_rest, mlp_sum = window(
        q_t,
        prompt_all,
        cont_kv,
        bias,
        attn_out,
        lse,
        back_two,
        grad_out,
        x_all,
        attn_sum,
        gain_two,
        packed_full,
        cosine,
        sine_table,
        first_normed,
        up_grads,
        mlp_part.reshape(-1, cut, SIZE),
        q_heads,
        kv_heads,
        3,
    )
    mlp_own = scatter(mlp_grads)
    grad_q, grad_rest, mlp_own = lax.optimization_barrier((grad_q, grad_rest, mlp_own))
    back_one = product_sum(
        [grad_q, grad_kv], [(q_cols, 2 * q_cols), (2 * q_cols, q_cols + qkv_cols)], packed_full, 2
    )
    back_one, mlp_own = lax.optimization_barrier((back_one, mlp_own))
    outs = finish(x_all, attn_sum, mlp_sum, grad_middle, back_one, gain_one, prompt_rows)
    down_own = mlp_own[:, :hidden_cols]
    gate_own = mlp_own[:, wide : wide + hidden_cols]
    rest_own = scatter(grad_rest)
    up_own = rest_own[:, :hidden_cols]
    o_own = rest_own[:, wide : wide + q_cols]
    q_own = rest_own[:, wide + q_cols : wide + 2 * q_cols]
    k_own = rest_own[:, wide + 2 * q_cols : wide + 2 * q_cols + kv_cols]
    v_own = rest_own[:, wide + 2 * q_cols + kv_cols :]

    def row_dot(weight, grad):
        return jnp.sum(weight.astype(jnp.float32) * grad, axis=1)

    gain_rows = jnp.stack(
        [
            (row_dot(q_weight, q_own) + row_dot(key_matrix, k_own) + row_dot(value_matrix, v_own))
            / attn_gain.astype(jnp.float32),
            (row_dot(gate_weight, gate_own) + row_dot(up_weight, up_own))
            / mlp_gain.astype(jnp.float32),
        ]
    )
    gain_rows = tensor_total(gain_rows, 5)
    owned = (gain_rows[0], q_own, k_own, v_own, o_own, gain_rows[1], gate_own, up_own, down_own)
    return (*outs, *owned)


def solution(mesh):
    in_specs = (
        P(("dp", "context"), None),
        P(("dp", "context"), None),
        P("dp"),
        P(("dp", "context"), None),
        P(("dp", "context")),
        P(("dp", "context"), "tensor"),
        P(("dp", "context"), "tensor"),
        P(("dp", "context"), "tensor"),
        P(("dp", "context"), "tensor"),
        P(("dp", "context")),
        P(("dp", "context"), "tensor"),
        P(("dp", "context"), "tensor"),
        P(("dp", "context"), "tensor"),
        P(("dp", "context"), None),
        P(("dp", "context"), None),
    )
    out_specs = (
        P(("dp", "context"), None),
        P(("dp", "context"), None),
        P(("dp", "context"), None),
        P(("dp", "context"), None),
        P(("dp", "context")),
        P(("dp", "context"), "tensor"),
        P(("dp", "context"), "tensor"),
        P(("dp", "context"), "tensor"),
        P(("dp", "context"), "tensor"),
        P(("dp", "context")),
        P(("dp", "context"), "tensor"),
        P(("dp", "context"), "tensor"),
        P(("dp", "context"), "tensor"),
    )
    return jax.shard_map(
        per_device, mesh=mesh, in_specs=in_specs, out_specs=out_specs, check_vma=False
    )
```

```python
import functools
import math

import jax
import jax.numpy as jnp
from jax import lax
from jax.experimental import pallas as pl
from jax.experimental.pallas import tpu as pltpu
from jax.sharding import PartitionSpec as P

HEAD_SIZE = 80


EPS = 1e-05
THETA = 10000.0
NEGATIVE = -1e30
LOG2E = math.log2(math.e)
MESH = pl.DeviceIdType.MESH
AXIS = "tensor"
LAG = 3
SIZE = 256
SLOTS = 3


def normalize(values):
    inverse = lax.rsqrt(jnp.mean(values * values, axis=-1, keepdims=True) + EPS)
    return (values * inverse, inverse)


def norm_back(grad_unit, unit_rows, inverse):
    inner_sum = jnp.mean(grad_unit * unit_rows, axis=-1, keepdims=True)
    return inverse * (grad_unit - unit_rows * inner_sum)


def contract_last(left_side, right_side):
    return lax.dot_general(
        left_side, right_side, (((1,), (1,)), ((), ())), preferred_element_type=jnp.float32
    )


def contract_first(left_side, right_side):
    return lax.dot_general(
        left_side, right_side, (((0,), (0,)), ((), ())), preferred_element_type=jnp.float32
    )


def greet(axis, count):
    me = lax.axis_index(axis)
    barrier = pltpu.get_barrier_semaphore()
    for k in range(1, count):
        peer = lax.rem(me + k, count)
        pl.semaphore_signal(barrier, inc=1, device_id={axis: peer}, device_id_type=MESH)
    pl.semaphore_wait(barrier, count - 1)


def rope_kernel(
    q_heads,
    kv_heads,
    dim,
    prompt_steps,
    x_ref,
    w_ref,
    cos_ref,
    sin_ref,
    normed_ref,
    qt_ref,
    kvt_ref,
    gains_ref,
    all_ref,
    own,
    send,
    recv,
    local,
):
    i = pl.program_id(0)
    count = all_ref.shape[0]
    me = lax.axis_index("context")
    last = (q_heads + 2 * kv_heads + q_heads) * dim

    @pl.when(i == 0)
    def _():
        greet("context", count)
        low = last - last % 128
        turned = w_ref[:, low:].astype(jnp.float32).T
        gains_ref[...] = turned[last - low : last - low + 8]

    rows = x_ref[...].astype(jnp.float32)
    inverse = lax.rsqrt(jnp.mean(rows * rows, axis=-1, keepdims=True) + EPS)
    normed = (rows * inverse * gains_ref[0:1, :]).astype(jnp.bfloat16)
    normed_ref[...] = normed
    flat = jnp.dot(
        normed, w_ref[:, q_heads * dim :], preferred_element_type=jnp.float32
    ).T
    cosine, sine = cos_ref[...], sin_ref[...]
    half = dim // 2
    pieces = []
    for head in range(q_heads + kv_heads):
        first = flat[head * dim : head * dim + half]
        second = flat[head * dim + half : (head + 1) * dim]
        turned = jnp.concatenate(
            [first * cosine - second * sine, second * cosine + first * sine], axis=0
        ).astype(jnp.bfloat16)
        if head < q_heads:
            qt_ref[head * dim : (head + 1) * dim, :] = turned
        else:
            pieces.append(turned)
    at = (q_heads + kv_heads) * dim
    pieces.append(flat[at : at + kv_heads * dim].astype(jnp.bfloat16))
    low = 0
    for piece in pieces:
        kvt_ref[low : low + piece.shape[0], :] = piece
        low += piece.shape[0]
    step = x_ref.shape[0]
    for k in range(prompt_steps):

        @pl.when(i == k)
        def _():
            own[:, k * step : (k + 1) * step] = kvt_ref[...]

    def exchange(k):
        peer = lax.rem(me + k, count)
        return pltpu.make_async_remote_copy(
            own,
            all_ref.at[me],
            send.at[k],
            recv.at[k],
            device_id={"context": peer},
            device_id_type=MESH,
        )

    keep = pltpu.make_async_copy(own, all_ref.at[me], local)

    @pl.when(i == prompt_steps - 1)
    def _():
        for k in range(1, count):
            exchange(k).start()
        keep.start()

    @pl.when(i == pl.num_programs(0) - 1)
    def _():
        for k in range(1, count):
            exchange(k).wait()
        keep.wait()


def project_rope(x, packed_full, cos_t, sin_t, q_heads, kv_heads, prompt_rows, cid):
    rows, width = x.shape
    dim = HEAD_SIZE
    count = lax.axis_size("context")
    step = math.gcd(math.gcd(rows, prompt_rows), 256)
    cols_wide = packed_full.shape[1]
    kv2 = 2 * kv_heads * dim
    by_row = lambda i: (i, 0)
    by_col = lambda i: (0, i)
    fixed = lambda i: (0, 0)
    return pl.pallas_call(
        functools.partial(rope_kernel, q_heads, kv_heads, dim, prompt_rows // step),
        grid=(rows // step,),
        in_specs=[
            pl.BlockSpec((step, width), by_row),
            pl.BlockSpec(packed_full.shape, fixed, pipeline_mode=pl.Buffered(1)),
            pl.BlockSpec((dim // 2, step), by_col),
            pl.BlockSpec((dim // 2, step), by_col),
        ],
        out_specs=[
            pl.BlockSpec((step, width), by_row),
            pl.BlockSpec((q_heads * dim, step), by_col),
            pl.BlockSpec((kv2, step), by_col),
            pl.BlockSpec((8, width), fixed),
            pl.BlockSpec(memory_space=pltpu.HBM),
        ],
        out_shape=[
            jax.ShapeDtypeStruct((rows, width), jnp.bfloat16),
            jax.ShapeDtypeStruct((q_heads * dim, rows), jnp.bfloat16),
            jax.ShapeDtypeStruct((kv2, rows), jnp.bfloat16),
            jax.ShapeDtypeStruct((8, width), jnp.float32),
            jax.ShapeDtypeStruct((count, kv2, prompt_rows), jnp.bfloat16),
        ],
        scratch_shapes=[
            pltpu.VMEM((kv2, prompt_rows), jnp.bfloat16),
            pltpu.SemaphoreType.DMA((count,)),
            pltpu.SemaphoreType.DMA((count,)),
            pltpu.SemaphoreType.DMA,
        ],
        compiler_params=pltpu.CompilerParams(
            collective_id=cid, has_side_effects=True, vmem_limit_bytes=48 << 20
        ),
        cost_estimate=pl.CostEstimate(
            flops=2 * rows * width * cols_wide,
            bytes_accessed=4 * x.size + 2 * width * cols_wide,
            transcendentals=0,
        ),
    )(x, packed_full, cos_t, sin_t)


def attend_shape(prompt_all, kvt_cont):
    count, kv2, prompt_rows = prompt_all.shape
    cont_rows = kvt_cont.shape[1] - prompt_rows
    chunk = math.gcd(math.gcd(prompt_rows, cont_rows), 256)
    return count, kv2, prompt_rows, cont_rows, chunk


def total_kernel(count, part_ref, out_ref, got, send, recv):
    greet(AXIS, count)
    me = lax.axis_index(AXIS)
    copies = []
    for k in range(1, count):
        peer = lax.rem(me + k, count)
        copy = pltpu.make_async_remote_copy(
            part_ref,
            got.at[me],
            send.at[k],
            recv.at[k],
            device_id={AXIS: peer},
            device_id_type=MESH,
        )
        copy.start()
        copies.append(copy)
    got[me] = part_ref[...]
    for copy in copies:
        copy.wait()
    total = got[0]
    for k in range(1, count):
        total += got[k]
    out_ref[...] = total


def tensor_total(part, cid):
    count = lax.axis_size(AXIS)
    return pl.pallas_call(
        functools.partial(total_kernel, count),
        out_shape=jax.ShapeDtypeStruct(part.shape, part.dtype),
        in_specs=[pl.BlockSpec(memory_space=pltpu.VMEM)],
        out_specs=pl.BlockSpec(memory_space=pltpu.VMEM),
        scratch_shapes=[
            pltpu.VMEM((count, *part.shape), part.dtype),
            pltpu.SemaphoreType.DMA((count,)),
            pltpu.SemaphoreType.DMA((count,)),
        ],
        compiler_params=pltpu.CompilerParams(collective_id=cid, has_side_effects=True),
        cost_estimate=pl.CostEstimate(flops=0, bytes_accessed=4 << 20, transcendentals=0),
    )(part)


def plane_kernel(
    prompt_total,
    o_ref,
    q_ref,
    kt_ref,
    vt_ref,
    again_ref,
    mgain_ref,
    info_ref,
    w0_ref,
    w1_ref,
    w2_ref,
    px_ref,
    cx_ref,
    pc_ref,
    cc_ref,
    all_ref,
    shard_ref,
    x_ref,
    cot_ref,
    bias_ref,
    own_ref,
    stage,
    send,
    recv,
    local,
):
    dp, context = lax.axis_index("dp"), lax.axis_index("context")
    side = {"context": 1 - context}
    along = {"dp": lax.rem(dp + 2, 4)}
    twin_dp = dp + 1 - 2 * lax.rem(dp, 2)
    twin = {"dp": twin_dp}
    barrier = pltpu.get_barrier_semaphore()
    for peer in (side, along, twin):
        pl.semaphore_signal(barrier, inc=1, device_id=peer, device_id_type=MESH)
    pl.semaphore_wait(barrier, 3)
    rows = own_ref.shape[0]
    q_cols = q_ref.shape[1]
    own_ref[:, :q_cols] = o_ref[...]
    own_ref[:, q_cols : 2 * q_cols] = q_ref[...]
    small = [kt_ref[...], vt_ref[...], again_ref[...], mgain_ref[...]]
    rest = own_ref.shape[1] - 2 * q_cols
    used = sum(part.shape[0] for part in small)
    small.append(jnp.zeros((rest - used, rows), jnp.bfloat16))
    own_ref[:, 2 * q_cols :] = (
        jnp.concatenate([part.astype(jnp.float32) for part in small], axis=0).T
    ).astype(jnp.bfloat16)
    half = rows // 2
    mine = 2 * dp + context
    from_side = 2 * dp + 1 - context
    from_along = 2 * lax.rem(dp + 2, 4) + context
    from_far = 2 * lax.rem(dp + 2, 4) + 1 - context

    def spot(block, h):
        return pl.ds(pl.multiple_of(block * rows + h * half, half), half)

    def copy(k, block, h, peer, first=False):
        source = own_ref.at[pl.ds(h * half, half)] if first else all_ref.at[spot(block, h)]
        return pltpu.make_async_remote_copy(
            source,
            all_ref.at[spot(block, h)],
            send.at[k],
            recv.at[k],
            device_id=peer,
            device_id_type=MESH,
        )

    def land(k, block, h):
        return pltpu.make_async_remote_copy(
            own_ref.at[pl.ds(h * half, half)],
            all_ref.at[spot(block, h)],
            send.at[k],
            recv.at[k],
            device_id=side,
            device_id_type=MESH,
        )

    started = []

    def go(*args, **kwargs):
        one = copy(*args, **kwargs)
        one.start()
        started.append(one)

    go(0, mine, 0, side, first=True)
    go(2, mine, 1, along, first=True)
    go(1, mine, 1, side, first=True)
    go(3, mine, 0, along, first=True)
    go(6, mine, 0, twin, first=True)
    go(7, mine, 1, twin, first=True)
    prompt_rows = px_ref.shape[0]
    moves = [
        pltpu.make_async_copy(own_ref, all_ref.at[pl.ds(pl.multiple_of(mine * rows, rows), rows)], local.at[0]),
    ]
    moves[0].start()
    joins = []
    for k, (source, target, low) in enumerate(
        (
            (px_ref, x_ref, 0),
            (cx_ref, x_ref, prompt_rows),
            (pc_ref, cot_ref, 0),
            (cc_ref, cot_ref, prompt_rows),
        )
    ):
        rows_at = pl.ds((k % 2) * prompt_rows, source.shape[0])
        load = pltpu.make_async_copy(source, stage.at[k // 2, rows_at], local.at[1 + k])
        load.start()
        joins.append(
            (
                load,
                pltpu.make_async_copy(
                    stage.at[k // 2, rows_at],
                    target.at[pl.ds(low, source.shape[0])],
                    local.at[5 + k],
                ),
            )
        )
    cols = w0_ref.shape[1]
    wide = shard_ref.shape[1] // 3
    for k, ref in enumerate((w0_ref, w1_ref, w2_ref)):
        shard_ref[:, k * wide : k * wide + cols] = ref[...]
        shard_ref[:, k * wide + cols : (k + 1) * wide] = jnp.zeros(
            (rows, wide - cols), jnp.bfloat16
        )
    cont_rows = cx_ref.shape[0]
    block = 128

    def fill_bias(low, count, at, columns, rule):
        @pl.loop(0, count // block)
        def _(c):
            key = lax.broadcasted_iota(jnp.int32, (block, columns), 0) + c * block
            query = lax.broadcasted_iota(jnp.int32, (block, columns), 1)
            rows_at = pl.ds(pl.multiple_of(low + c * block, block), block)
            bias_ref[rows_at, at : at + columns] = jnp.where(
                rule(key, query), 0.0, NEGATIVE
            ).astype(jnp.bfloat16)

    first = context * prompt_rows
    earlier, length = info_ref[0:1, :], info_ref[1:2, :]
    fill_bias(0, prompt_total, 0, prompt_rows, lambda k, q: k <= q + first)
    fill_bias(prompt_total, cont_rows, 0, prompt_rows, lambda k, q: k < 0)
    fill_bias(0, prompt_total, prompt_rows, cont_rows, lambda k, q: k < length)
    fill_bias(
        prompt_total, cont_rows, prompt_rows, cont_rows, lambda k, q: (k >= earlier) & (k <= q)
    )
    for load, save in joins:
        load.wait()
        save.start()
        moves.append(save)
    land(0, from_side, 0).wait_recv()
    go(4, from_side, 0, along)
    go(8, from_side, 0, twin)
    land(2, from_along, 1).wait_recv()
    go(5, from_along, 1, side)
    go(9, from_along, 1, twin)
    land(1, from_side, 1).wait_recv()
    go(10, from_side, 1, twin)
    land(3, from_along, 0).wait_recv()
    go(11, from_along, 0, twin)
    land(4, from_far, 0).wait_recv()
    go(12, from_far, 0, twin)
    land(5, from_far, 1).wait_recv()
    go(13, from_far, 1, twin)
    base = 2 * twin_dp
    other = 2 * lax.rem(twin_dp + 2, 4)
    for k, block, h in (
        (6, base + context, 0),
        (7, base + context, 1),
        (8, base + 1 - context, 0),
        (9, other + context, 1),
        (10, base + 1 - context, 1),
        (11, other + context, 0),
        (12, other + 1 - context, 0),
        (13, other + 1 - context, 1),
    ):
        land(k, block, h).wait_recv()
    for one in started:
        one.wait_send()
    for move in moves:
        move.wait()


def plane_gather(
    attn, gains, info, weights, wide, attn_wide, prompt_x, cont_x, prompt_cot, cont_cot, cid
):
    o_weight, q_weight, key_matrix, value_matrix = attn
    rows = q_weight.shape[0]
    count = lax.axis_size("dp") * lax.axis_size("context")
    prompt_rows, width = prompt_x.shape
    total = prompt_rows + cont_x.shape[0]
    prompt_total = prompt_rows * lax.axis_size("context")
    hbm = pl.BlockSpec(memory_space=pltpu.HBM)
    vmem = pl.BlockSpec(memory_space=pltpu.VMEM)
    both = jax.ShapeDtypeStruct((total, width), jnp.bfloat16)
    return pl.pallas_call(
        functools.partial(plane_kernel, prompt_total),
        out_shape=[
            jax.ShapeDtypeStruct((count * rows, attn_wide), jnp.bfloat16),
            jax.ShapeDtypeStruct((rows, 3 * wide), jnp.bfloat16),
            both,
            both,
            jax.ShapeDtypeStruct((prompt_total + cont_x.shape[0], total), jnp.bfloat16),
        ],
        in_specs=[vmem] * 10 + [hbm] * 4,
        out_specs=[hbm, vmem, hbm, hbm, vmem],
        scratch_shapes=[
            pltpu.VMEM((rows, attn_wide), jnp.bfloat16),
            pltpu.VMEM((2, total, width), jnp.bfloat16),
            pltpu.SemaphoreType.DMA((14,)),
            pltpu.SemaphoreType.DMA((14,)),
            pltpu.SemaphoreType.DMA((9,)),
        ],
        compiler_params=pltpu.CompilerParams(
            collective_id=cid, has_side_effects=True, vmem_limit_bytes=60 << 20
        ),
        cost_estimate=pl.CostEstimate(
            flops=30_000_000_000, bytes_accessed=40 << 20, transcendentals=0
        ),
    )(
        o_weight,
        q_weight,
        key_matrix.T,
        value_matrix.T,
        gains[0][None, :],
        gains[1][None, :],
        info,
        *weights,
        prompt_x,
        cont_x,
        prompt_cot,
        cont_cot,
    )


def fill_keys(chunk, dim, kv_heads, all_ref, cont_ref, rows_of, chunks_ref):
    count, _, prompt_rows = all_ref.shape
    per = prompt_rows // chunk
    total = count * per + (cont_ref.shape[1] - prompt_rows) // chunk
    for c in range(total):
        if c < count * per:
            block = all_ref[c // per, :, (c % per) * chunk : (c % per + 1) * chunk]
        else:
            at = prompt_rows + (c - count * per) * chunk
            block = cont_ref[:, at : at + chunk]
        chunks_ref[c] = block
        for n, target in enumerate(rows_of):
            for g in range(kv_heads):
                at = (n * kv_heads + g) * dim
                target[g, c * chunk : (c + 1) * chunk, :] = (
                    block[at : at + dim].astype(jnp.float32).T.astype(jnp.bfloat16)
                )


def trip_count(tile, chunk, i, prompt_rows, count):
    me = lax.axis_index("context")
    prompt_tiles = prompt_rows // tile
    n_prompt = lax.div(me * prompt_rows + (i + 1) * tile + chunk - 1, chunk)
    n_own = lax.div((i - prompt_tiles + 1) * tile + chunk - 1, chunk)
    return i < prompt_tiles, n_prompt, count * prompt_rows // chunk, n_own


class Line:
    def __init__(self, part, recv, out, sink, sems, sink_sems):
        self.part, self.recv, self.out, self.sink = part, recv, out, sink
        self.per = sink.shape[0] // out.shape[1]
        self.sems, self.sink_sems = sems, sink_sems
        self.blocks = out.shape[0]
        me, n = lax.axis_index(AXIS), lax.axis_size(AXIS)
        self.outer = (me == 0) | (me == n - 1)
        self.inner = jnp.logical_not(self.outer)
        self.mate = jnp.where(me < n // 2, 1 - me, 2 * n - 3 - me)
        self.across = n - 1 - me

    def copy(self, k, source, target, peer, b):
        return pltpu.make_async_remote_copy(
            source.at[b],
            target.at[b],
            self.sems.at[2 * k, b],
            self.sems.at[2 * k + 1, b],
            device_id={AXIS: peer},
            device_id_type=MESH,
        )

    def up(self, b):
        return self.copy(0, self.part, self.recv, self.mate, b)

    def mid(self, b):
        return self.copy(1, self.part, self.out, self.across, b)

    def down(self, b):
        return self.copy(2, self.out, self.out, self.mate, b)

    def keep(self, b):
        _, rows, cols = self.out.shape
        at = (
            pl.ds(pl.multiple_of(lax.rem(b, self.per) * rows, rows), rows),
            pl.ds(pl.multiple_of(lax.div(b, self.per) * cols, cols), cols),
        )
        return pltpu.make_async_copy(self.out.at[b], self.sink.at[at], self.sink_sems.at[b])

    def greet(self, axis=None, count=1):
        barrier = pltpu.get_barrier_semaphore()
        pl.semaphore_signal(barrier, inc=1, device_id={AXIS: self.mate}, device_id_type=MESH)
        for k in range(1, count):
            peer = lax.rem(lax.axis_index(axis) + k, count)
            pl.semaphore_signal(barrier, inc=1, device_id={axis: peer}, device_id_type=MESH)

        @pl.when(self.inner)
        def _():
            pl.semaphore_signal(barrier, inc=1, device_id={AXIS: self.across}, device_id_type=MESH)
            pl.semaphore_wait(barrier, 1 + count)

        @pl.when(self.outer)
        def _():
            pl.semaphore_wait(barrier, count)

    def start(self, first, count):
        @pl.when(self.outer)
        def _():
            @pl.loop(0, count)
            def _(k):
                self.up(first + k).start()

    def step(self, t):
        @pl.when(self.inner & (t >= 0) & (t < self.blocks))
        def _():
            self.up(t).wait_recv()
            self.part[t] = (
                self.part[t].astype(jnp.float32) + self.recv[t].astype(jnp.float32)
            ).astype(jnp.bfloat16)
            self.mid(t).start()

        @pl.when(self.inner & (t >= LAG) & (t < self.blocks + LAG))
        def _():
            b = t - LAG
            self.mid(b).wait()
            self.out[b] = (
                self.part[b].astype(jnp.float32) + self.out[b].astype(jnp.float32)
            ).astype(jnp.bfloat16)
            self.down(b).start()
            self.keep(b).start()

    def drain(self):
        for k in range(LAG):
            self.step(self.blocks + k)

        @pl.when(self.outer)
        def _():
            @pl.loop(0, self.blocks)
            def _(b):
                self.down(b).wait_recv()
                self.keep(b).start()
                self.up(b).wait_send()

        @pl.when(self.inner)
        def _():
            @pl.loop(0, self.blocks)
            def _(b):
                self.down(b).wait_send()

        @pl.loop(0, self.blocks)
        def _(b):
            self.keep(b).wait()


def line_scratch(shape):
    return [pltpu.VMEM(shape, jnp.bfloat16)] * 3 + [
        pltpu.SemaphoreType.DMA((6, shape[0])),
        pltpu.SemaphoreType.DMA((shape[0],)),
    ]


def attend_kernel(
    shape,
    dim,
    kv_heads,
    per,
    tile,
    cut,
    q_ref,
    all_ref,
    cont_ref,
    bias_ref,
    wo_ref,
    out_ref,
    lse_ref,
    sum_ref,
    keys,
    chunks,
    part,
    recv,
    out,
    sems,
    sink_sems,
):
    count, prompt_rows, chunk = shape
    i = pl.program_id(0)
    line = Line(part, recv, out, sum_ref, sems, sink_sems)
    blocks = tile // cut

    @pl.when(i == 0)
    def _():
        fill_keys(chunk, dim, kv_heads, all_ref, cont_ref, [keys], chunks)
        line.greet()

    is_prompt, n_prompt, base, n_own = trip_count(tile, chunk, i, prompt_rows, count)
    wide = per * tile
    factor = dim ** (-0.5) * LOG2E
    outs, sums = [], []
    for g in range(kv_heads):
        q = jnp.concatenate(
            [q_ref[(g * per + h) * dim : (g * per + h + 1) * dim, :] for h in range(per)], axis=1
        )

        def body(c, state):
            top, total, acc = state
            at = pl.ds(pl.multiple_of(c * chunk, chunk), chunk)
            s = jnp.dot(keys[g, at, :], q, preferred_element_type=jnp.float32)
            t = s * factor + jnp.concatenate([bias_ref[at, :].astype(jnp.float32)] * per, axis=1)
            new = jnp.maximum(top, jnp.max(t, axis=0, keepdims=True))
            p = jnp.exp2(t - new)
            scale = jnp.exp2(top - new)
            total = total * scale + jnp.sum(p, axis=0, keepdims=True)
            v = chunks[c, (kv_heads + g) * dim : (kv_heads + g + 1) * dim, :]
            acc = acc * scale + jnp.dot(
                v, p.astype(jnp.bfloat16), preferred_element_type=jnp.float32
            )
            return new, total, acc

        start = (
            jnp.full((1, wide), NEGATIVE, jnp.float32),
            jnp.zeros((1, wide), jnp.float32),
            jnp.zeros((dim, wide), jnp.float32),
        )
        state = lax.fori_loop(0, jnp.where(is_prompt, n_prompt, base), body, start)
        top, total, acc = lax.fori_loop(base, base + jnp.where(is_prompt, 0, n_own), body, state)
        acc = acc / total
        top = top + jnp.log2(total)
        outs += [acc[:, h * tile : (h + 1) * tile] for h in range(per)]
        sums += [top[:, h * tile : (h + 1) * tile] for h in range(per)]
        if g < kv_heads - 1:
            for r in range(blocks // 2):
                line.step((i - 1) * blocks + r)
    attended = jnp.concatenate(outs, axis=0).T.astype(jnp.bfloat16)
    out_ref[...] = attended
    lse_ref[...] = jnp.concatenate(sums, axis=0)
    term = contract_last(attended, wo_ref[...]).astype(jnp.bfloat16)
    for r in range(blocks):
        part[i * blocks + r] = term[r * cut : (r + 1) * cut]

    line.start(i * blocks, blocks)
    for r in range(blocks // 2, blocks):
        line.step((i - 1) * blocks + r)

    @pl.when(i == pl.num_programs(0) - 1)
    def _():
        @pl.loop(0, blocks)
        def _(r):
            line.step(i * blocks + r)

        line.drain()


def attend(q_t, prompt_all, kvt_cont, bias, packed_full, q_heads, kv_heads, cid):
    dim = HEAD_SIZE
    count, kv2, prompt_rows, cont_rows, chunk = attend_shape(prompt_all, kvt_cont)
    q_cols, rows = q_t.shape
    width = packed_full.shape[0]
    keys_all = bias.shape[0]
    tile, cut = 128, 32
    whole = pl.BlockSpec(memory_space=pltpu.VMEM)
    by_col = lambda i: (0, i)
    return pl.pallas_call(
        functools.partial(
            attend_kernel,
            (count, prompt_rows, chunk),
            dim,
            kv_heads,
            q_heads // kv_heads,
            tile,
            cut,
        ),
        grid=(rows // tile,),
        in_specs=[
            pl.BlockSpec((q_cols, tile), by_col),
            whole,
            whole,
            pl.BlockSpec((keys_all, tile), by_col),
            pl.BlockSpec((width, q_cols), lambda i: (0, 0), pipeline_mode=pl.Buffered(1)),
        ],
        out_specs=[
            pl.BlockSpec((tile, q_cols), lambda i: (i, 0)),
            pl.BlockSpec((q_heads, tile), by_col),
            pl.BlockSpec(memory_space=pl.ANY),
        ],
        out_shape=[
            jax.ShapeDtypeStruct((rows, q_cols), jnp.bfloat16),
            jax.ShapeDtypeStruct((q_heads, rows), jnp.float32),
            jax.ShapeDtypeStruct((rows, width), jnp.bfloat16),
        ],
        scratch_shapes=[
            pltpu.VMEM((kv_heads, keys_all, dim), jnp.bfloat16),
            pltpu.VMEM((keys_all // chunk, kv2, chunk), jnp.bfloat16),
            *line_scratch((rows // cut, cut, width)),
        ],
        compiler_params=pltpu.CompilerParams(
            collective_id=cid, has_side_effects=True, vmem_limit_bytes=40 << 20
        ),
        cost_estimate=pl.CostEstimate(
            flops=120_000_000_000, bytes_accessed=40 << 20, transcendentals=0
        ),
    )(q_t, prompt_all, kvt_cont, bias, packed_full)


def feed_back_kernel(
    cut,
    gate_ref,
    up_ref,
    hidden_ref,
    wd_ref,
    wg_ref,
    wu_ref,
    cot_ref,
    normed_ref,
    grads_ref,
    up_grads_ref,
    mlp_ref,
    sum_ref,
    part,
    recv,
    out,
    sems,
    sink_sems,
):
    n = pl.program_id(0)
    rows, wide = gate_ref.shape
    per = rows // cut
    line = Line(part, recv, out, sum_ref, sems, sink_sems)

    back = contract_last(gate_ref[...], wg_ref[...]) + contract_last(up_ref[...], wu_ref[...])
    back = back.astype(jnp.bfloat16)
    for r in range(per):
        part[n * per + r] = back[r * cut : (r + 1) * cut]

    @pl.when(n == 0)
    def _():
        line.greet()

    line.start(n * per, per)

    def steps(low, high):
        for r in range(low, high):
            line.step(n * per + r)

    grads_ref[:, :wide] = contract_first(cot_ref[...], hidden_ref[...]).astype(jnp.bfloat16)
    steps(0, per // 4)
    grads_ref[:, wide:] = contract_first(normed_ref[...], gate_ref[...]).astype(
        jnp.bfloat16
    )
    steps(per // 4, per // 2)
    up_grads_ref[...] = contract_first(normed_ref[...], up_ref[...]).astype(jnp.bfloat16)
    steps(per // 2, per - per // 4)
    mlp_ref[0] = contract_last(hidden_ref[...], wd_ref[...]).astype(jnp.bfloat16)
    steps(per - per // 4, per)

    @pl.when(n == pl.num_programs(0) - 1)
    def _():
        line.drain()


def feed_back(grad_gate, grad_up, hidden, mlp_full, cot, normed, cid):
    rows, wide = hidden.shape
    width = cot.shape[1]
    size = SIZE
    cut = math.gcd(rows, size)
    tiles = width // size
    blocks = (tiles * rows // cut, cut, size)
    whole = pl.BlockSpec(memory_space=pltpu.VMEM)
    return pl.pallas_call(
        functools.partial(feed_back_kernel, cut),
        grid=(tiles,),
        in_specs=[whole] * 3
        + [pl.BlockSpec((size, wide), lambda n, k=k: (n, k)) for k in range(3)]
        + [pl.BlockSpec((rows, size), lambda n: (0, n))] * 2,
        out_specs=[
            pl.BlockSpec((size, 2 * wide), lambda n: (n, 0)),
            pl.BlockSpec((size, wide), lambda n: (n, 0)),
            pl.BlockSpec((1, rows, size), lambda n: (n, 0, 0)),
            pl.BlockSpec(memory_space=pl.ANY),
        ],
        out_shape=[
            jax.ShapeDtypeStruct((width, 2 * wide), jnp.bfloat16),
            jax.ShapeDtypeStruct((width, wide), jnp.bfloat16),
            jax.ShapeDtypeStruct((tiles, rows, size), jnp.bfloat16),
            jax.ShapeDtypeStruct((rows, width), jnp.bfloat16),
        ],
        scratch_shapes=line_scratch(blocks),
        compiler_params=pltpu.CompilerParams(
            collective_id=cid, has_side_effects=True, vmem_limit_bytes=58 << 20
        ),
        cost_estimate=pl.CostEstimate(
            flops=12 * rows * wide * width, bytes_accessed=200 << 20, transcendentals=0
        ),
    )(grad_gate, grad_up, hidden, mlp_full, mlp_full, mlp_full, cot, normed)


def window_kernel(
    shape,
    dim,
    kv_heads,
    per,
    tile,
    q_ref,
    all_ref,
    cont_ref,
    bias_ref,
    out_ref,
    lse_ref,
    back_ref,
    cot_ref,
    x_ref,
    attn_ref,
    gain_ref,
    wo_ref,
    cos_ref,
    sin_ref,
    cos_own_ref,
    sin_own_ref,
    normed_ref,
    up_grads_ref,
    mlp_ref,
    gq_out_ref,
    gkv_ref,
    gm_ref,
    grads_ref,
    sum_ref,
    keys,
    values,
    chunks,
    gk,
    gv,
    go,
    gq_ref,
    send_ref,
    got,
    own_ref,
    kv_sems,
    part,
    recv,
    out,
    sems,
    sink_sems,
):
    count, prompt_rows, chunk = shape
    i = pl.program_id(0)
    line = Line(part, recv, out, sum_ref, sems, sink_sems)
    context = lax.axis_index("context")
    prompt_tiles = prompt_rows // tile
    tiles = gq_ref.shape[0]
    slots = SLOTS
    spots = 2 + kv_heads

    def step(k):
        for s in range(k * slots // spots, (k + 1) * slots // spots):
            line.step(i * slots + s)

    def send(k):
        peer = lax.rem(context + k, count)
        return pltpu.make_async_remote_copy(
            send_ref.at[peer],
            got.at[k],
            kv_sems.at[0, k],
            kv_sems.at[1, k],
            device_id={"context": peer},
            device_id_type=MESH,
        )

    root = dim ** (-0.5)
    half = dim // 2

    @pl.when(i == 0)
    def _():
        load = pltpu.make_async_copy(mlp_ref, part, sink_sems.at[0])
        load.start()
        fill_keys(chunk, dim, kv_heads, all_ref, cont_ref, [keys, values], chunks)
        gk[...] = jnp.zeros_like(gk)
        gv[...] = jnp.zeros_like(gv)
        go[...] = jnp.zeros_like(go)
        line.greet("context", count)
        load.wait()
        line.start(0, line.blocks)

    @pl.when(i < tiles)
    def _():
        middle = x_ref[...].astype(jnp.float32) + attn_ref[...].astype(jnp.float32)
        inverse = lax.rsqrt(jnp.mean(middle * middle, axis=-1, keepdims=True) + EPS)
        unit = middle * inverse
        grad_unit = back_ref[...].astype(jnp.float32) * gain_ref[...]
        grad_middle = cot_ref[...].astype(jnp.float32) + norm_back(grad_unit, unit, inverse)
        gm_ref[...] = grad_middle
        grad_b = grad_middle.astype(jnp.bfloat16)
        step(0)
        grad_t = (
            jnp.dot(grad_b, wo_ref[...], preferred_element_type=jnp.float32).astype(jnp.bfloat16)
        ).astype(jnp.float32).T
        go[...] += contract_first(grad_b, out_ref[...])
        step(1)

        is_prompt, n_prompt, base, n_own = trip_count(tile, chunk, i, prompt_rows, count)
        factor = root * LOG2E
        prod = grad_t * out_ref[...].astype(jnp.float32).T
        grad_t = grad_t.astype(jnp.bfloat16)
        cosine, sine = cos_ref[...], sin_ref[...]
        pieces = []
        for g in range(kv_heads):
            heads = [g * per + h for h in range(per)]
            q = jnp.concatenate([q_ref[h * dim : (h + 1) * dim, :] for h in heads], axis=1)
            grad = jnp.concatenate([grad_t[h * dim : (h + 1) * dim] for h in heads], axis=1)
            inner = jnp.concatenate(
                [jnp.sum(prod[h * dim : (h + 1) * dim], axis=0, keepdims=True) for h in heads], axis=1
            )
            lse = jnp.concatenate([lse_ref[h : h + 1, :] for h in heads], axis=1)

            def body(c, acc):
                at = pl.ds(pl.multiple_of(c * chunk, chunk), chunk)
                s = jnp.dot(keys[g, at, :], q, preferred_element_type=jnp.float32)
                b = bias_ref[at, :].astype(jnp.float32)
                p = jnp.exp2(s * factor + (jnp.concatenate([b] * per, axis=1) - lse))
                dp = jnp.dot(values[g, at, :], grad, preferred_element_type=jnp.float32)
                ds = (p * (dp - inner)).astype(jnp.bfloat16)
                gv[g, at, :] += contract_last(p.astype(jnp.bfloat16), grad)
                gk[g, at, :] += contract_last(ds, q)
                k_t = chunks[c, g * dim : (g + 1) * dim, :]
                return acc + jnp.dot(k_t, ds, preferred_element_type=jnp.float32)

            acc = jnp.zeros((dim, per * tile), jnp.float32)
            acc = lax.fori_loop(0, jnp.where(is_prompt, n_prompt, base), body, acc)
            acc = lax.fori_loop(base, base + jnp.where(is_prompt, 0, n_own), body, acc)
            acc = acc * root
            for h in range(per):
                first = acc[:half, h * tile : (h + 1) * tile]
                second = acc[half:, h * tile : (h + 1) * tile]
                pieces += [first * cosine + second * sine, second * cosine - first * sine]
            step(2 + g)
        rows_q = jnp.concatenate(pieces, axis=0).T.astype(jnp.bfloat16)
        gq_ref[i] = rows_q
        gq_out_ref[...] = rows_q

    @pl.when(i == tiles - 1)
    def _():
        for g in range(kv_heads):
            for n, (acc, scale) in enumerate(((gk, root), (gv, 1.0))):
                at = (n * kv_heads + g) * dim
                for c in range(count):
                    rows = acc[g, c * prompt_rows : (c + 1) * prompt_rows, :]
                    send_ref[c, at : at + dim, :] = (rows * scale).T.astype(jnp.bfloat16)
                own_ref[at : at + dim, :] = (acc[g, count * prompt_rows :, :] * scale).T
        for k in range(1, count):
            send(k).start()

    @pl.when(i == tiles)
    def _():
        line.step(tiles * slots)
        kv_dim = kv_heads * dim

        def finish(flat, cosine, sine):
            pieces = []
            for at in range(0, kv_dim, dim):
                first, second = flat[at : at + half], flat[at + half : at + dim]
                pieces += [first * cosine + second * sine, second * cosine - first * sine]
            pieces.append(flat[kv_dim:])
            return jnp.concatenate(pieces, axis=0).T.astype(jnp.bfloat16)

        cosine, sine = cos_own_ref[...], sin_own_ref[...]
        gkv_ref[prompt_rows:, :] = finish(
            own_ref[...], cosine[:, prompt_rows:], sine[:, prompt_rows:]
        )
        total = send_ref[context].astype(jnp.float32)
        for k in range(1, count):
            send(k).wait()
            total += got[k].astype(jnp.float32)
        gkv_ref[:prompt_rows, :] = finish(
            total, cosine[:, :prompt_rows], sine[:, :prompt_rows]
        )

    @pl.when(i >= tiles)
    def _():
        n = i - tiles
        later = pl.num_programs(0) - tiles
        rest = line.blocks - tiles * slots - 1
        q_cols = go.shape[1]
        wide = up_grads_ref.shape[1]
        grads_ref[:, :wide] = up_grads_ref[...]
        grads_ref[:, wide : wide + q_cols] = go[pl.ds(pl.multiple_of(n * SIZE, SIZE), SIZE), :].astype(
            jnp.bfloat16
        )
        total = jnp.zeros((SIZE, q_cols), jnp.float32)
        for k in range(tiles):
            total += contract_first(normed_ref[k * tile : (k + 1) * tile, :], gq_ref[k])
        grads_ref[:, wide + q_cols : wide + 2 * q_cols] = total.astype(jnp.bfloat16)
        grads_ref[:, wide + 2 * q_cols :] = contract_first(normed_ref[...], gkv_ref[...]).astype(
            jnp.bfloat16
        )
        low = tiles * slots + 1 + lax.div(n * rest, later)
        high = tiles * slots + 1 + lax.div((n + 1) * rest, later)

        @pl.loop(low, high)
        def _(t):
            line.step(t)

        @pl.when(n == later - 1)
        def _():
            line.drain()


def window(
    q_t,
    prompt_all,
    kvt_cont,
    bias,
    attended,
    lse,
    back,
    cot,
    x,
    attn_sum,
    gain,
    packed_full,
    cos_t,
    sin_t,
    normed,
    up_grads,
    mlp_part,
    q_heads,
    kv_heads,
    cid,
):
    dim = HEAD_SIZE
    count, kv2, prompt_rows, cont_rows, chunk = attend_shape(prompt_all, kvt_cont)
    rows, width = cot.shape
    q_cols = q_heads * dim
    keys_all = bias.shape[0]
    tile = 128
    whole = pl.BlockSpec(memory_space=pltpu.VMEM)
    anywhere = pl.BlockSpec(memory_space=pl.ANY)
    tiles, later = rows // tile, width // SIZE
    grad_cols = up_grads.shape[1] + 2 * q_cols + kv2
    early = lambda i: jnp.minimum(i, tiles - 1)
    late = lambda i: jnp.maximum(i - tiles, 0)
    by_col = lambda i: (0, early(i))
    by_row = lambda i: (early(i), 0)
    fixed = lambda i: (0, 0)
    return pl.pallas_call(
        functools.partial(
            window_kernel, (count, prompt_rows, chunk), dim, kv_heads, q_heads // kv_heads, tile
        ),
        grid=(tiles + later,),
        in_specs=[
            pl.BlockSpec((q_cols, tile), by_col),
            whole,
            whole,
            pl.BlockSpec((keys_all, tile), by_col),
            pl.BlockSpec((tile, q_cols), by_row),
            pl.BlockSpec((q_heads, tile), by_col),
            pl.BlockSpec((tile, width), by_row),
            pl.BlockSpec((tile, width), by_row),
            pl.BlockSpec((tile, width), by_row),
            pl.BlockSpec((tile, width), by_row),
            pl.BlockSpec((1, width), fixed),
            pl.BlockSpec((width, q_cols), fixed, pipeline_mode=pl.Buffered(1)),
            pl.BlockSpec((dim // 2, tile), by_col),
            pl.BlockSpec((dim // 2, tile), by_col),
            whole,
            whole,
            pl.BlockSpec((rows, SIZE), lambda i: (0, late(i))),
            pl.BlockSpec((SIZE, up_grads.shape[1]), lambda i: (late(i), 0)),
            anywhere,
        ],
        out_specs=[
            pl.BlockSpec((tile, q_cols), by_row),
            pl.BlockSpec((rows, kv2), fixed),
            pl.BlockSpec((tile, width), by_row),
            pl.BlockSpec((SIZE, grad_cols), lambda i: (late(i), 0)),
            anywhere,
        ],
        out_shape=[
            jax.ShapeDtypeStruct((rows, q_cols), jnp.bfloat16),
            jax.ShapeDtypeStruct((rows, kv2), jnp.bfloat16),
            jax.ShapeDtypeStruct((rows, width), jnp.float32),
            jax.ShapeDtypeStruct((width, grad_cols), jnp.bfloat16),
            jax.ShapeDtypeStruct((rows, width), jnp.bfloat16),
        ],
        scratch_shapes=[
            pltpu.VMEM((kv_heads, keys_all, dim), jnp.bfloat16),
            pltpu.VMEM((kv_heads, keys_all, dim), jnp.bfloat16),
            pltpu.VMEM((keys_all // chunk, kv2, chunk), jnp.bfloat16),
            pltpu.VMEM((kv_heads, keys_all, dim), jnp.float32),
            pltpu.VMEM((kv_heads, keys_all, dim), jnp.float32),
            pltpu.VMEM((width, q_cols), jnp.float32),
            pltpu.VMEM((tiles, tile, q_cols), jnp.bfloat16),
            pltpu.VMEM((count, kv2, prompt_rows), jnp.bfloat16),
            pltpu.VMEM((count, kv2, prompt_rows), jnp.bfloat16),
            pltpu.VMEM((kv2, cont_rows), jnp.float32),
            pltpu.SemaphoreType.DMA((2, count)),
            *line_scratch(mlp_part.shape),
        ],
        compiler_params=pltpu.CompilerParams(
            collective_id=cid, has_side_effects=True, vmem_limit_bytes=60 << 20
        ),
        cost_estimate=pl.CostEstimate(
            flops=120_000_000_000, bytes_accessed=200 << 20, transcendentals=0
        ),
    )(
        q_t,
        prompt_all,
        kvt_cont,
        bias,
        attended,
        lse,
        back,
        cot,
        x,
        attn_sum,
        gain,
        packed_full,
        cos_t,
        sin_t,
        cos_t,
        sin_t,
        normed,
        up_grads,
        mlp_part,
    )


def product_kernel(cut, spans, lhs_refs, w_ref, sum_ref, part, recv, out, sems, sink_sems):
    n = pl.program_id(0)
    per = sum_ref.shape[0] // cut
    line = Line(part, recv, out, sum_ref, sems, sink_sems)
    term = sum(
        contract_last(ref[...], w_ref[:, low:high]) for ref, (low, high) in zip(lhs_refs, spans)
    ).astype(jnp.bfloat16)
    for r in range(per):
        part[n * per + r] = term[r * cut : (r + 1) * cut]

    @pl.when(n == 0)
    def _():
        line.greet()

    line.start(n * per, per)
    for r in range(per):
        line.step(n * per + r)

    @pl.when(n == pl.num_programs(0) - 1)
    def _():
        line.drain()


def product_sum(lhs, spans, weights, cid):
    rows = lhs[0].shape[0]
    width, cols = weights.shape
    cut = math.gcd(rows, SIZE)
    tiles = width // SIZE
    blocks = (tiles * rows // cut, cut, SIZE)

    def body(*refs):
        product_kernel(cut, spans, refs[: len(lhs)], *refs[len(lhs) :])

    return pl.pallas_call(
        body,
        grid=(tiles,),
        in_specs=[pl.BlockSpec(memory_space=pltpu.VMEM)] * len(lhs)
        + [pl.BlockSpec((SIZE, cols), lambda n: (n, 0))],
        out_specs=pl.BlockSpec(memory_space=pl.ANY),
        out_shape=jax.ShapeDtypeStruct((rows, width), jnp.bfloat16),
        scratch_shapes=line_scratch(blocks),
        compiler_params=pltpu.CompilerParams(
            collective_id=cid, has_side_effects=True, vmem_limit_bytes=40 << 20
        ),
        cost_estimate=pl.CostEstimate(
            flops=120_000_000_000, bytes_accessed=40 << 20, transcendentals=0
        ),
    )(*lhs, weights)


def feed_kernel(
    x_ref,
    attn_ref,
    gain_ref,
    cot_ref,
    wd_ref,
    wg_ref,
    wu_ref,
    normed_ref,
    hidden_ref,
    gate_grad_ref,
    up_grad_ref,
):
    @pl.when(pl.program_id(0) == 0)
    def _():
        @pl.loop(0, x_ref.shape[0] // 64)
        def _(r):
            at = pl.ds(pl.multiple_of(r * 64, 64), 64)
            middle = x_ref[at, :].astype(jnp.float32) + attn_ref[at, :].astype(jnp.float32)
            unit, _ = normalize(middle)
            normed_ref[at, :] = (unit * gain_ref[...]).astype(jnp.bfloat16)

    gate = jnp.dot(normed_ref[...], wg_ref[...], preferred_element_type=jnp.float32)
    up = jnp.dot(normed_ref[...], wu_ref[...], preferred_element_type=jnp.float32)
    grad_hidden = jnp.dot(cot_ref[...], wd_ref[...], preferred_element_type=jnp.float32)
    sigmoid = 1.0 / (1.0 + jnp.exp(-gate))
    silu = gate * sigmoid
    hidden_ref[...] = (silu * up).astype(jnp.bfloat16)
    gate_grad_ref[...] = (grad_hidden * up * sigmoid * (1.0 + gate * (1.0 - sigmoid))).astype(
        jnp.bfloat16
    )
    up_grad_ref[...] = (grad_hidden * silu).astype(jnp.bfloat16)


def feed(x, attn_sum, gain, cot, mlp_full):
    rows, width = x.shape
    wide = mlp_full.shape[1] // 3
    tiles = wide // SIZE
    whole = pl.BlockSpec(memory_space=pltpu.VMEM)
    tile = pl.BlockSpec((rows, SIZE), lambda n: (0, n))
    return pl.pallas_call(
        feed_kernel,
        grid=(tiles,),
        in_specs=[whole] * 4
        + [pl.BlockSpec((width, SIZE), lambda n, k=k: (0, k * tiles + n)) for k in range(3)],
        out_specs=[
            pl.BlockSpec((rows, width), lambda n: (0, 0), pipeline_mode=pl.Buffered(1)),
            tile,
            tile,
            tile,
        ],
        out_shape=[jax.ShapeDtypeStruct((rows, width), jnp.bfloat16)]
        + [jax.ShapeDtypeStruct((rows, wide), jnp.bfloat16)] * 3,
        compiler_params=pltpu.CompilerParams(vmem_limit_bytes=58 << 20),
        cost_estimate=pl.CostEstimate(
            flops=6 * rows * width * wide, bytes_accessed=60 << 20, transcendentals=rows * wide
        ),
    )(x, attn_sum, gain, cot, mlp_full, mlp_full, mlp_full)


def finish_kernel(
    prompt_tiles, x_ref, attn_ref, mlp_ref, gm_ref, back_ref, gain_ref, po_ref, co_ref, pg_ref, cg_ref
):
    i = pl.program_id(0)
    x = x_ref[...].astype(jnp.float32)
    result = (x + attn_ref[...].astype(jnp.float32)) + mlp_ref[...].astype(jnp.float32)
    result = result.astype(jnp.bfloat16)
    unit, inverse = normalize(x)
    grad = gm_ref[...] + norm_back(back_ref[...].astype(jnp.float32) * gain_ref[...], unit, inverse)

    @pl.when(i < prompt_tiles)
    def _():
        po_ref[...] = result
        pg_ref[...] = grad

    @pl.when(i >= prompt_tiles)
    def _():
        co_ref[...] = result
        cg_ref[...] = grad


def finish(x, attn_sum, mlp_sum, grad_middle, back, gain, prompt_rows):
    rows, width = x.shape
    tile = 128
    prompt_tiles = prompt_rows // tile
    every = pl.BlockSpec((tile, width), lambda i: (i, 0))
    first = pl.BlockSpec((tile, width), lambda i: (jnp.minimum(i, prompt_tiles - 1), 0))
    second = pl.BlockSpec((tile, width), lambda i: (jnp.maximum(i - prompt_tiles, 0), 0))
    shapes = [(prompt_rows, width), (rows - prompt_rows, width)]
    return pl.pallas_call(
        functools.partial(finish_kernel, prompt_tiles),
        grid=(rows // tile,),
        in_specs=[every] * 5 + [pl.BlockSpec((1, width), lambda i: (0, 0))],
        out_specs=[first, second, first, second],
        out_shape=[jax.ShapeDtypeStruct(shape, jnp.bfloat16) for shape in shapes]
        + [jax.ShapeDtypeStruct(shape, jnp.float32) for shape in shapes],
        compiler_params=pltpu.CompilerParams(vmem_limit_bytes=40 << 20),
        cost_estimate=pl.CostEstimate(
            flops=20 * x.size, bytes_accessed=20 * x.size, transcendentals=0
        ),
    )(x, attn_sum, mlp_sum, grad_middle, back, gain)


def per_device(
    prompt_x,
    cont_x,
    prompt_len,
    cont_seg,
    attn_gain,
    q_weight,
    key_matrix,
    value_matrix,
    o_weight,
    mlp_gain,
    gate_weight,
    up_weight,
    down_weight,
    prompt_cot,
    cont_cot,
):
    head_dim = HEAD_SIZE
    data = ("dp", "context")
    prompt_rows = prompt_x.shape[0]
    cont_rows = cont_x.shape[0]
    prompt_total = prompt_rows * lax.axis_size("context")
    q_cols = q_weight.shape[1]
    kv_cols = key_matrix.shape[1]
    q_heads = q_cols // head_dim
    kv_heads = kv_cols // head_dim
    qkv_cols = q_cols + 2 * kv_cols
    qkv_wide = qkv_cols + 2 + -(qkv_cols + 2) % 128
    hidden_cols = gate_weight.shape[1]
    wide = hidden_cols + -hidden_cols % 256
    context_pos = lax.axis_index("context")
    prompt_pos = context_pos * prompt_rows + jnp.arange(prompt_rows, dtype=jnp.int32)
    segment = cont_seg[0]
    earlier = jnp.sum((segment[None, :] < segment[:, None]).astype(jnp.int32), axis=1)
    local_index = jnp.arange(cont_rows, dtype=jnp.int32)
    length = prompt_len[0]
    cont_pos = length + local_index - earlier
    position = jnp.concatenate([prompt_pos, cont_pos]).astype(jnp.float32)
    inv_freq = THETA ** (-jnp.arange(head_dim // 2, dtype=jnp.float32) * 2.0 / head_dim)
    angle_table = inv_freq[:, None] * position[None, :]
    cosine = jnp.cos(angle_table)
    sine_table = jnp.sin(angle_table)
    shards = (down_weight, gate_weight, up_weight)
    attn_shards = (o_weight, q_weight, key_matrix, value_matrix)
    if lax.axis_size("dp") == 4 and lax.axis_size("context") == 2:
        info = jnp.stack([earlier, jnp.broadcast_to(length, earlier.shape)])
        packed_full, mlp_shard, x_all, grad_out, bias = plane_gather(
            attn_shards,
            (attn_gain, mlp_gain),
            info,
            shards,
            wide,
            q_cols + qkv_wide,
            prompt_x,
            cont_x,
            prompt_cot,
            cont_cot,
            6,
        )
    else:
        packed = jnp.concatenate([*attn_shards, attn_gain[:, None], mlp_gain[:, None]], axis=1)
        packed = jnp.pad(packed, ((0, 0), (0, q_cols + qkv_wide - packed.shape[1])))
        packed_full = lax.all_gather(packed, data, axis=0, tiled=True)
        fill = ((0, 0), (0, wide - hidden_cols))
        mlp_shard = jnp.concatenate([jnp.pad(w, fill) for w in shards], axis=1)
        x_all = jnp.concatenate([prompt_x, cont_x], axis=0)
        grad_out = jnp.concatenate([prompt_cot, cont_cot], axis=0)
        key_index = jnp.arange(prompt_total, dtype=jnp.int32)
        prompt_mask = jnp.concatenate(
            [
                key_index[:, None] <= prompt_pos[None, :],
                jnp.zeros((cont_rows, prompt_rows), jnp.bool_),
            ],
            axis=0,
        )
        own_mask = (segment[:, None] == segment[None, :]) & (
            local_index[:, None] <= local_index[None, :]
        )
        reach_mask = jnp.broadcast_to(key_index[:, None] < length, (prompt_total, cont_rows))
        allowed = jnp.concatenate(
            [prompt_mask, jnp.concatenate([reach_mask, own_mask], axis=0)], axis=1
        )
        bias = jnp.where(allowed, 0.0, NEGATIVE).astype(jnp.bfloat16)
    first_normed, q_t, cont_kv, gains, prompt_all = project_rope(
        x_all, packed_full, cosine, sine_table, q_heads, kv_heads, prompt_rows, 4
    )
    gain_one, gain_two = gains[0:1], gains[1:2]
    prompt_all, mlp_shard = lax.optimization_barrier((prompt_all, mlp_shard))
    mlp_full = lax.all_gather(mlp_shard, data, axis=0, tiled=True)
    attn_out, lse, attn_sum = attend(
        q_t, prompt_all, cont_kv, bias, packed_full, q_heads, kv_heads, 0
    )
    normed_two, hidden, grad_gate, grad_up = feed(x_all, attn_sum, gain_two, grad_out, mlp_full)
    mlp_grads, up_grads, mlp_part, back_two = feed_back(
        grad_gate, grad_up, hidden, mlp_full, grad_out, normed_two, 1
    )

    def scatter(values):
        return lax.psum_scatter(values, data, scatter_dimension=0, tiled=True).astype(jnp.float32)

    cut = math.gcd(prompt_rows + cont_rows, SIZE)
    grad_q, grad_kv, grad_middle, grad_rest, mlp_sum = window(
        q_t,
        prompt_all,
        cont_kv,
        bias,
        attn_out,
        lse,
        back_two,
        grad_out,
        x_all,
        attn_sum,
        gain_two,
        packed_full,
        cosine,
        sine_table,
        first_normed,
        up_grads,
        mlp_part.reshape(-1, cut, SIZE),
        q_heads,
        kv_heads,
        3,
    )
    mlp_own = scatter(mlp_grads)
    grad_q, grad_rest, mlp_own = lax.optimization_barrier((grad_q, grad_rest, mlp_own))
    back_one = product_sum(
        [grad_q, grad_kv], [(q_cols, 2 * q_cols), (2 * q_cols, q_cols + qkv_cols)], packed_full, 2
    )
    back_one, mlp_own = lax.optimization_barrier((back_one, mlp_own))
    outs = finish(x_all, attn_sum, mlp_sum, grad_middle, back_one, gain_one, prompt_rows)
    down_own = mlp_own[:, :hidden_cols]
    gate_own = mlp_own[:, wide : wide + hidden_cols]
    rest_own = scatter(grad_rest)
    up_own = rest_own[:, :hidden_cols]
    o_own = rest_own[:, wide : wide + q_cols]
    q_own = rest_own[:, wide + q_cols : wide + 2 * q_cols]
    k_own = rest_own[:, wide + 2 * q_cols : wide + 2 * q_cols + kv_cols]
    v_own = rest_own[:, wide + 2 * q_cols + kv_cols :]

    def row_dot(weight, grad):
        return jnp.sum(weight.astype(jnp.float32) * grad, axis=1)

    gain_rows = jnp.stack(
        [
            (row_dot(q_weight, q_own) + row_dot(key_matrix, k_own) + row_dot(value_matrix, v_own))
            / attn_gain.astype(jnp.float32),
            (row_dot(gate_weight, gate_own) + row_dot(up_weight, up_own))
            / mlp_gain.astype(jnp.float32),
        ]
    )
    gain_rows = tensor_total(gain_rows, 5)
    owned = (gain_rows[0], q_own, k_own, v_own, o_own, gain_rows[1], gate_own, up_own, down_own)
    return (*outs, *owned)


def solution(mesh):
    in_specs = (
        P(("dp", "context"), None),
        P(("dp", "context"), None),
        P("dp"),
        P(("dp", "context"), None),
        P(("dp", "context")),
        P(("dp", "context"), "tensor"),
        P(("dp", "context"), "tensor"),
        P(("dp", "context"), "tensor"),
        P(("dp", "context"), "tensor"),
        P(("dp", "context")),
        P(("dp", "context"), "tensor"),
        P(("dp", "context"), "tensor"),
        P(("dp", "context"), "tensor"),
        P(("dp", "context"), None),
        P(("dp", "context"), None),
    )
    out_specs = (
        P(("dp", "context"), None),
        P(("dp", "context"), None),
        P(("dp", "context"), None),
        P(("dp", "context"), None),
        P(("dp", "context")),
        P(("dp", "context"), "tensor"),
        P(("dp", "context"), "tensor"),
        P(("dp", "context"), "tensor"),
        P(("dp", "context"), "tensor"),
        P(("dp", "context")),
        P(("dp", "context"), "tensor"),
        P(("dp", "context"), "tensor"),
        P(("dp", "context"), "tensor"),
    )
    return jax.shard_map(
        per_device, mesh=mesh, in_specs=in_specs, out_specs=out_specs, check_vma=False
    )
```

```python
import functools
import math

import jax
import jax.numpy as jnp
from jax import lax
from jax.experimental import pallas as pl
from jax.experimental.pallas import tpu as pltpu
from jax.sharding import PartitionSpec as P

HEAD_SIZE = 80


EPS = 1e-05
THETA = 10000.0
NEGATIVE = -1e30
LOG2E = math.log2(math.e)
MESH = pl.DeviceIdType.MESH
AXIS = "tensor"
LAG = 3
SIZE = 256
SLOTS = 4


def normalize(values):
    inverse = lax.rsqrt(jnp.mean(values * values, axis=-1, keepdims=True) + EPS)
    return (values * inverse, inverse)


def norm_back(grad_unit, unit_rows, inverse):
    inner_sum = jnp.mean(grad_unit * unit_rows, axis=-1, keepdims=True)
    return inverse * (grad_unit - unit_rows * inner_sum)


def contract_last(left_side, right_side):
    return lax.dot_general(
        left_side, right_side, (((1,), (1,)), ((), ())), preferred_element_type=jnp.float32
    )


def contract_first(left_side, right_side):
    return lax.dot_general(
        left_side, right_side, (((0,), (0,)), ((), ())), preferred_element_type=jnp.float32
    )


def greet(axis, count):
    me = lax.axis_index(axis)
    barrier = pltpu.get_barrier_semaphore()
    for k in range(1, count):
        peer = lax.rem(me + k, count)
        pl.semaphore_signal(barrier, inc=1, device_id={axis: peer}, device_id_type=MESH)
    pl.semaphore_wait(barrier, count - 1)


def rope_kernel(
    q_heads,
    kv_heads,
    dim,
    prompt_steps,
    x_ref,
    w_ref,
    cos_ref,
    sin_ref,
    normed_ref,
    qt_ref,
    kvt_ref,
    gains_ref,
    all_ref,
    own,
    send,
    recv,
    local,
):
    i = pl.program_id(0)
    count = all_ref.shape[0]
    me = lax.axis_index("context")
    last = (q_heads + 2 * kv_heads + q_heads) * dim

    @pl.when(i == 0)
    def _():
        greet("context", count)
        low = last - last % 128
        turned = w_ref[:, low:].astype(jnp.float32).T
        gains_ref[...] = turned[last - low : last - low + 8]

    rows = x_ref[...].astype(jnp.float32)
    inverse = lax.rsqrt(jnp.mean(rows * rows, axis=-1, keepdims=True) + EPS)
    normed = (rows * inverse * gains_ref[0:1, :]).astype(jnp.bfloat16)
    normed_ref[...] = normed
    flat = jnp.dot(
        normed, w_ref[:, q_heads * dim :], preferred_element_type=jnp.float32
    ).T
    cosine, sine = cos_ref[...], sin_ref[...]
    half = dim // 2
    pieces = []
    for head in range(q_heads + kv_heads):
        first = flat[head * dim : head * dim + half]
        second = flat[head * dim + half : (head + 1) * dim]
        turned = jnp.concatenate(
            [first * cosine - second * sine, second * cosine + first * sine], axis=0
        ).astype(jnp.bfloat16)
        if head < q_heads:
            qt_ref[head * dim : (head + 1) * dim, :] = turned
        else:
            pieces.append(turned)
    at = (q_heads + kv_heads) * dim
    pieces.append(flat[at : at + kv_heads * dim].astype(jnp.bfloat16))
    low = 0
    for piece in pieces:
        kvt_ref[low : low + piece.shape[0], :] = piece
        low += piece.shape[0]
    step = x_ref.shape[0]
    for k in range(prompt_steps):

        @pl.when(i == k)
        def _():
            own[:, k * step : (k + 1) * step] = kvt_ref[...]

    def exchange(k):
        peer = lax.rem(me + k, count)
        return pltpu.make_async_remote_copy(
            own,
            all_ref.at[me],
            send.at[k],
            recv.at[k],
            device_id={"context": peer},
            device_id_type=MESH,
        )

    keep = pltpu.make_async_copy(own, all_ref.at[me], local)

    @pl.when(i == prompt_steps - 1)
    def _():
        for k in range(1, count):
            exchange(k).start()
        keep.start()

    @pl.when(i == pl.num_programs(0) - 1)
    def _():
        for k in range(1, count):
            exchange(k).wait()
        keep.wait()


def project_rope(x, packed_full, cos_t, sin_t, q_heads, kv_heads, prompt_rows, cid):
    rows, width = x.shape
    dim = HEAD_SIZE
    count = lax.axis_size("context")
    step = math.gcd(math.gcd(rows, prompt_rows), 256)
    cols_wide = packed_full.shape[1]
    kv2 = 2 * kv_heads * dim
    by_row = lambda i: (i, 0)
    by_col = lambda i: (0, i)
    fixed = lambda i: (0, 0)
    return pl.pallas_call(
        functools.partial(rope_kernel, q_heads, kv_heads, dim, prompt_rows // step),
        grid=(rows // step,),
        in_specs=[
            pl.BlockSpec((step, width), by_row),
            pl.BlockSpec(packed_full.shape, fixed, pipeline_mode=pl.Buffered(1)),
            pl.BlockSpec((dim // 2, step), by_col),
            pl.BlockSpec((dim // 2, step), by_col),
        ],
        out_specs=[
            pl.BlockSpec((step, width), by_row),
            pl.BlockSpec((q_heads * dim, step), by_col),
            pl.BlockSpec((kv2, step), by_col),
            pl.BlockSpec((8, width), fixed),
            pl.BlockSpec(memory_space=pltpu.HBM),
        ],
        out_shape=[
            jax.ShapeDtypeStruct((rows, width), jnp.bfloat16),
            jax.ShapeDtypeStruct((q_heads * dim, rows), jnp.bfloat16),
            jax.ShapeDtypeStruct((kv2, rows), jnp.bfloat16),
            jax.ShapeDtypeStruct((8, width), jnp.float32),
            jax.ShapeDtypeStruct((count, kv2, prompt_rows), jnp.bfloat16),
        ],
        scratch_shapes=[
            pltpu.VMEM((kv2, prompt_rows), jnp.bfloat16),
            pltpu.SemaphoreType.DMA((count,)),
            pltpu.SemaphoreType.DMA((count,)),
            pltpu.SemaphoreType.DMA,
        ],
        compiler_params=pltpu.CompilerParams(
            collective_id=cid, has_side_effects=True, vmem_limit_bytes=48 << 20
        ),
        cost_estimate=pl.CostEstimate(
            flops=2 * rows * width * cols_wide,
            bytes_accessed=4 * x.size + 2 * width * cols_wide,
            transcendentals=0,
        ),
    )(x, packed_full, cos_t, sin_t)


def attend_shape(prompt_all, kvt_cont):
    count, kv2, prompt_rows = prompt_all.shape
    cont_rows = kvt_cont.shape[1] - prompt_rows
    chunk = math.gcd(math.gcd(prompt_rows, cont_rows), 256)
    return count, kv2, prompt_rows, cont_rows, chunk


def total_kernel(count, part_ref, out_ref, got, send, recv):
    greet(AXIS, count)
    me = lax.axis_index(AXIS)
    copies = []
    for k in range(1, count):
        peer = lax.rem(me + k, count)
        copy = pltpu.make_async_remote_copy(
            part_ref,
            got.at[me],
            send.at[k],
            recv.at[k],
            device_id={AXIS: peer},
            device_id_type=MESH,
        )
        copy.start()
        copies.append(copy)
    got[me] = part_ref[...]
    for copy in copies:
        copy.wait()
    total = got[0]
    for k in range(1, count):
        total += got[k]
    out_ref[...] = total


def tensor_total(part, cid):
    count = lax.axis_size(AXIS)
    return pl.pallas_call(
        functools.partial(total_kernel, count),
        out_shape=jax.ShapeDtypeStruct(part.shape, part.dtype),
        in_specs=[pl.BlockSpec(memory_space=pltpu.VMEM)],
        out_specs=pl.BlockSpec(memory_space=pltpu.VMEM),
        scratch_shapes=[
            pltpu.VMEM((count, *part.shape), part.dtype),
            pltpu.SemaphoreType.DMA((count,)),
            pltpu.SemaphoreType.DMA((count,)),
        ],
        compiler_params=pltpu.CompilerParams(collective_id=cid, has_side_effects=True),
        cost_estimate=pl.CostEstimate(flops=0, bytes_accessed=4 << 20, transcendentals=0),
    )(part)


def plane_kernel(
    prompt_total,
    o_ref,
    q_ref,
    kt_ref,
    vt_ref,
    again_ref,
    mgain_ref,
    info_ref,
    w0_ref,
    w1_ref,
    w2_ref,
    px_ref,
    cx_ref,
    pc_ref,
    cc_ref,
    all_ref,
    shard_ref,
    x_ref,
    cot_ref,
    bias_ref,
    own_ref,
    stage,
    send,
    recv,
    local,
):
    dp, context = lax.axis_index("dp"), lax.axis_index("context")
    side = {"context": 1 - context}
    along = {"dp": lax.rem(dp + 2, 4)}
    twin_dp = dp + 1 - 2 * lax.rem(dp, 2)
    twin = {"dp": twin_dp}
    barrier = pltpu.get_barrier_semaphore()
    for peer in (side, along, twin):
        pl.semaphore_signal(barrier, inc=1, device_id=peer, device_id_type=MESH)
    pl.semaphore_wait(barrier, 3)
    rows = own_ref.shape[0]
    q_cols = q_ref.shape[1]
    own_ref[:, :q_cols] = o_ref[...]
    own_ref[:, q_cols : 2 * q_cols] = q_ref[...]
    small = [kt_ref[...], vt_ref[...], again_ref[...], mgain_ref[...]]
    rest = own_ref.shape[1] - 2 * q_cols
    used = sum(part.shape[0] for part in small)
    small.append(jnp.zeros((rest - used, rows), jnp.bfloat16))
    own_ref[:, 2 * q_cols :] = (
        jnp.concatenate([part.astype(jnp.float32) for part in small], axis=0).T
    ).astype(jnp.bfloat16)
    half = rows // 2
    mine = 2 * dp + context
    from_side = 2 * dp + 1 - context
    from_along = 2 * lax.rem(dp + 2, 4) + context
    from_far = 2 * lax.rem(dp + 2, 4) + 1 - context

    def spot(block, h):
        return pl.ds(pl.multiple_of(block * rows + h * half, half), half)

    def copy(k, block, h, peer, first=False):
        source = own_ref.at[pl.ds(h * half, half)] if first else all_ref.at[spot(block, h)]
        return pltpu.make_async_remote_copy(
            source,
            all_ref.at[spot(block, h)],
            send.at[k],
            recv.at[k],
            device_id=peer,
            device_id_type=MESH,
        )

    def land(k, block, h):
        return pltpu.make_async_remote_copy(
            own_ref.at[pl.ds(h * half, half)],
            all_ref.at[spot(block, h)],
            send.at[k],
            recv.at[k],
            device_id=side,
            device_id_type=MESH,
        )

    started = []

    def go(*args, **kwargs):
        one = copy(*args, **kwargs)
        one.start()
        started.append(one)

    go(0, mine, 0, side, first=True)
    go(2, mine, 1, along, first=True)
    go(1, mine, 1, side, first=True)
    go(3, mine, 0, along, first=True)
    go(6, mine, 0, twin, first=True)
    go(7, mine, 1, twin, first=True)
    prompt_rows = px_ref.shape[0]
    moves = [
        pltpu.make_async_copy(own_ref, all_ref.at[pl.ds(pl.multiple_of(mine * rows, rows), rows)], local.at[0]),
    ]
    moves[0].start()
    joins = []
    for k, (source, target, low) in enumerate(
        (
            (px_ref, x_ref, 0),
            (cx_ref, x_ref, prompt_rows),
            (pc_ref, cot_ref, 0),
            (cc_ref, cot_ref, prompt_rows),
        )
    ):
        rows_at = pl.ds((k % 2) * prompt_rows, source.shape[0])
        load = pltpu.make_async_copy(source, stage.at[k // 2, rows_at], local.at[1 + k])
        load.start()
        joins.append(
            (
                load,
                pltpu.make_async_copy(
                    stage.at[k // 2, rows_at],
                    target.at[pl.ds(low, source.shape[0])],
                    local.at[5 + k],
                ),
            )
        )
    cols = w0_ref.shape[1]
    wide = shard_ref.shape[1] // 3
    for k, ref in enumerate((w0_ref, w1_ref, w2_ref)):
        shard_ref[:, k * wide : k * wide + cols] = ref[...]
        shard_ref[:, k * wide + cols : (k + 1) * wide] = jnp.zeros(
            (rows, wide - cols), jnp.bfloat16
        )
    cont_rows = cx_ref.shape[0]
    block = 128

    def fill_bias(low, count, at, columns, rule):
        @pl.loop(0, count // block)
        def _(c):
            key = lax.broadcasted_iota(jnp.int32, (block, columns), 0) + c * block
            query = lax.broadcasted_iota(jnp.int32, (block, columns), 1)
            rows_at = pl.ds(pl.multiple_of(low + c * block, block), block)
            bias_ref[rows_at, at : at + columns] = jnp.where(
                rule(key, query), 0.0, NEGATIVE
            ).astype(jnp.bfloat16)

    first = context * prompt_rows
    earlier, length = info_ref[0:1, :], info_ref[1:2, :]
    fill_bias(0, prompt_total, 0, prompt_rows, lambda k, q: k <= q + first)
    fill_bias(prompt_total, cont_rows, 0, prompt_rows, lambda k, q: k < 0)
    fill_bias(0, prompt_total, prompt_rows, cont_rows, lambda k, q: k < length)
    fill_bias(
        prompt_total, cont_rows, prompt_rows, cont_rows, lambda k, q: (k >= earlier) & (k <= q)
    )
    for load, save in joins:
        load.wait()
        save.start()
        moves.append(save)
    land(0, from_side, 0).wait_recv()
    go(4, from_side, 0, along)
    go(8, from_side, 0, twin)
    land(2, from_along, 1).wait_recv()
    go(5, from_along, 1, side)
    go(9, from_along, 1, twin)
    land(1, from_side, 1).wait_recv()
    go(10, from_side, 1, twin)
    land(3, from_along, 0).wait_recv()
    go(11, from_along, 0, twin)
    land(4, from_far, 0).wait_recv()
    go(12, from_far, 0, twin)
    land(5, from_far, 1).wait_recv()
    go(13, from_far, 1, twin)
    base = 2 * twin_dp
    other = 2 * lax.rem(twin_dp + 2, 4)
    for k, block, h in (
        (6, base + context, 0),
        (7, base + context, 1),
        (8, base + 1 - context, 0),
        (9, other + context, 1),
        (10, base + 1 - context, 1),
        (11, other + context, 0),
        (12, other + 1 - context, 0),
        (13, other + 1 - context, 1),
    ):
        land(k, block, h).wait_recv()
    for one in started:
        one.wait_send()
    for move in moves:
        move.wait()


def plane_gather(
    attn, gains, info, weights, wide, attn_wide, prompt_x, cont_x, prompt_cot, cont_cot, cid
):
    o_weight, q_weight, key_matrix, value_matrix = attn
    rows = q_weight.shape[0]
    count = lax.axis_size("dp") * lax.axis_size("context")
    prompt_rows, width = prompt_x.shape
    total = prompt_rows + cont_x.shape[0]
    prompt_total = prompt_rows * lax.axis_size("context")
    hbm = pl.BlockSpec(memory_space=pltpu.HBM)
    vmem = pl.BlockSpec(memory_space=pltpu.VMEM)
    both = jax.ShapeDtypeStruct((total, width), jnp.bfloat16)
    return pl.pallas_call(
        functools.partial(plane_kernel, prompt_total),
        out_shape=[
            jax.ShapeDtypeStruct((count * rows, attn_wide), jnp.bfloat16),
            jax.ShapeDtypeStruct((rows, 3 * wide), jnp.bfloat16),
            both,
            both,
            jax.ShapeDtypeStruct((prompt_total + cont_x.shape[0], total), jnp.bfloat16),
        ],
        in_specs=[vmem] * 10 + [hbm] * 4,
        out_specs=[hbm, vmem, hbm, hbm, vmem],
        scratch_shapes=[
            pltpu.VMEM((rows, attn_wide), jnp.bfloat16),
            pltpu.VMEM((2, total, width), jnp.bfloat16),
            pltpu.SemaphoreType.DMA((14,)),
            pltpu.SemaphoreType.DMA((14,)),
            pltpu.SemaphoreType.DMA((9,)),
        ],
        compiler_params=pltpu.CompilerParams(
            collective_id=cid, has_side_effects=True, vmem_limit_bytes=60 << 20
        ),
        cost_estimate=pl.CostEstimate(
            flops=30_000_000_000, bytes_accessed=40 << 20, transcendentals=0
        ),
    )(
        o_weight,
        q_weight,
        key_matrix.T,
        value_matrix.T,
        gains[0][None, :],
        gains[1][None, :],
        info,
        *weights,
        prompt_x,
        cont_x,
        prompt_cot,
        cont_cot,
    )


def fill_keys(chunk, dim, kv_heads, all_ref, cont_ref, rows_of, chunks_ref):
    count, _, prompt_rows = all_ref.shape
    per = prompt_rows // chunk
    total = count * per + (cont_ref.shape[1] - prompt_rows) // chunk
    for c in range(total):
        if c < count * per:
            block = all_ref[c // per, :, (c % per) * chunk : (c % per + 1) * chunk]
        else:
            at = prompt_rows + (c - count * per) * chunk
            block = cont_ref[:, at : at + chunk]
        chunks_ref[c] = block
        for n, target in enumerate(rows_of):
            for g in range(kv_heads):
                at = (n * kv_heads + g) * dim
                target[g, c * chunk : (c + 1) * chunk, :] = (
                    block[at : at + dim].astype(jnp.float32).T.astype(jnp.bfloat16)
                )


def trip_count(tile, chunk, i, prompt_rows, count):
    me = lax.axis_index("context")
    prompt_tiles = prompt_rows // tile
    n_prompt = lax.div(me * prompt_rows + (i + 1) * tile + chunk - 1, chunk)
    n_own = lax.div((i - prompt_tiles + 1) * tile + chunk - 1, chunk)
    return i < prompt_tiles, n_prompt, count * prompt_rows // chunk, n_own


class Line:
    def __init__(self, part, recv, out, sink, sems, sink_sems, ready=None):
        self.ready = ready
        self.part, self.recv, self.out, self.sink = part, recv, out, sink
        self.per = sink.shape[0] // out.shape[1]
        self.sems, self.sink_sems = sems, sink_sems
        self.blocks = out.shape[0]
        me, n = lax.axis_index(AXIS), lax.axis_size(AXIS)
        self.outer = (me == 0) | (me == n - 1)
        self.inner = jnp.logical_not(self.outer)
        self.mate = jnp.where(me < n // 2, 1 - me, 2 * n - 3 - me)
        self.across = n - 1 - me

    def copy(self, k, source, target, peer, b):
        return pltpu.make_async_remote_copy(
            source.at[b],
            target.at[b],
            self.sems.at[2 * k, b],
            self.sems.at[2 * k + 1, b],
            device_id={AXIS: peer},
            device_id_type=MESH,
        )

    def up(self, b):
        return self.copy(0, self.part, self.recv, self.mate, b)

    def mid(self, b):
        return self.copy(1, self.part, self.out, self.across, b)

    def down(self, b):
        return self.copy(2, self.out, self.out, self.mate, b)

    def keep(self, b):
        _, rows, cols = self.out.shape
        at = (
            pl.ds(pl.multiple_of(lax.rem(b, self.per) * rows, rows), rows),
            pl.ds(pl.multiple_of(lax.div(b, self.per) * cols, cols), cols),
        )
        return pltpu.make_async_copy(self.out.at[b], self.sink.at[at], self.sink_sems.at[b])

    def greet(self, axis=None, count=1):
        barrier = pltpu.get_barrier_semaphore()
        pl.semaphore_signal(barrier, inc=1, device_id={AXIS: self.mate}, device_id_type=MESH)
        for k in range(1, count):
            peer = lax.rem(lax.axis_index(axis) + k, count)
            pl.semaphore_signal(barrier, inc=1, device_id={axis: peer}, device_id_type=MESH)

        @pl.when(self.inner)
        def _():
            pl.semaphore_signal(barrier, inc=1, device_id={AXIS: self.across}, device_id_type=MESH)
            pl.semaphore_wait(barrier, 1 + count)

        @pl.when(self.outer)
        def _():
            pl.semaphore_wait(barrier, count)

    def start(self, first, count):
        @pl.when(self.outer)
        def _():
            @pl.loop(0, count)
            def _(k):
                self.up(first + k).start()

    def step(self, t):
        @pl.when(self.inner & (t >= 0) & (t < self.blocks))
        def _():
            self.up(t).wait_recv()
            self.part[t] = (
                self.part[t].astype(jnp.float32) + self.recv[t].astype(jnp.float32)
            ).astype(jnp.bfloat16)
            self.mid(t).start()

        @pl.when(self.inner & (t >= LAG) & (t < self.blocks + LAG))
        def _():
            b = t - LAG
            self.mid(b).wait_recv()
            self.out[b] = (
                self.part[b].astype(jnp.float32) + self.out[b].astype(jnp.float32)
            ).astype(jnp.bfloat16)
            self.down(b).start()
            self.keep(b).start()
            if self.ready is not None:
                self.ready(b)

    def drain(self):
        for k in range(LAG):
            self.step(self.blocks + k)

        @pl.when(self.outer)
        def _():
            @pl.loop(0, self.blocks)
            def _(b):
                self.down(b).wait_recv()
                self.keep(b).start()
                if self.ready is not None:
                    self.ready(b)
                self.up(b).wait_send()

        @pl.when(self.inner)
        def _():
            @pl.loop(0, self.blocks)
            def _(b):
                self.mid(b).wait_send()
                self.down(b).wait_send()

        @pl.loop(0, self.blocks)
        def _(b):
            self.keep(b).wait()


def line_scratch(shape):
    return [pltpu.VMEM(shape, jnp.bfloat16)] * 3 + [
        pltpu.SemaphoreType.DMA((6, shape[0])),
        pltpu.SemaphoreType.DMA((shape[0],)),
    ]


def attend_kernel(
    shape,
    dim,
    kv_heads,
    per,
    tile,
    cut,
    q_ref,
    all_ref,
    cont_ref,
    bias_ref,
    wo_ref,
    x_ref,
    gains_ref,
    out_ref,
    lse_ref,
    sum_ref,
    normed_ref,
    keys,
    chunks,
    norm_buf,
    norm_sems,
    part,
    recv,
    out,
    sems,
    sink_sems,
):
    count, prompt_rows, chunk = shape
    i = pl.program_id(0)

    def norm_out(b):
        at = pl.ds(pl.multiple_of(b * cut, cut), cut)
        return pltpu.make_async_copy(norm_buf.at[b], normed_ref.at[at], norm_sems.at[b])

    def ready(b):
        at = pl.ds(pl.multiple_of(b * cut, cut), cut)
        unit, _ = normalize(x_ref[at, :].astype(jnp.float32) + out[b].astype(jnp.float32))
        norm_buf[b] = (unit * gains_ref[1:2, :]).astype(jnp.bfloat16)
        norm_out(b).start()

    line = Line(part, recv, out, sum_ref, sems, sink_sems, ready)
    blocks = tile // cut

    @pl.when(i == 0)
    def _():
        fill_keys(chunk, dim, kv_heads, all_ref, cont_ref, [keys], chunks)
        line.greet()

    is_prompt, n_prompt, base, n_own = trip_count(tile, chunk, i, prompt_rows, count)
    wide = per * tile
    factor = dim ** (-0.5) * LOG2E
    outs, sums = [], []
    for g in range(kv_heads):
        q = jnp.concatenate(
            [q_ref[(g * per + h) * dim : (g * per + h + 1) * dim, :] for h in range(per)], axis=1
        )

        def body(c, state):
            top, total, acc = state
            at = pl.ds(pl.multiple_of(c * chunk, chunk), chunk)
            s = jnp.dot(keys[g, at, :], q, preferred_element_type=jnp.float32)
            t = s * factor + jnp.concatenate([bias_ref[at, :].astype(jnp.float32)] * per, axis=1)
            new = jnp.maximum(top, jnp.max(t, axis=0, keepdims=True))
            p = jnp.exp2(t - new)
            scale = jnp.exp2(top - new)
            total = total * scale + jnp.sum(p, axis=0, keepdims=True)
            v = chunks[c, (kv_heads + g) * dim : (kv_heads + g + 1) * dim, :]
            acc = acc * scale + jnp.dot(
                v, p.astype(jnp.bfloat16), preferred_element_type=jnp.float32
            )
            return new, total, acc

        start = (
            jnp.full((1, wide), NEGATIVE, jnp.float32),
            jnp.zeros((1, wide), jnp.float32),
            jnp.zeros((dim, wide), jnp.float32),
        )
        state = lax.fori_loop(0, jnp.where(is_prompt, n_prompt, base), body, start)
        top, total, acc = lax.fori_loop(base, base + jnp.where(is_prompt, 0, n_own), body, state)
        acc = acc / total
        top = top + jnp.log2(total)
        outs += [acc[:, h * tile : (h + 1) * tile] for h in range(per)]
        sums += [top[:, h * tile : (h + 1) * tile] for h in range(per)]
        if g < kv_heads - 1:
            for r in range(blocks // 2):
                line.step((i - 1) * blocks + r)
    attended = jnp.concatenate(outs, axis=0).T.astype(jnp.bfloat16)
    out_ref[...] = attended
    lse_ref[...] = jnp.concatenate(sums, axis=0)
    term = contract_last(attended, wo_ref[...]).astype(jnp.bfloat16)
    for r in range(blocks):
        part[i * blocks + r] = term[r * cut : (r + 1) * cut]

    line.start(i * blocks, blocks)
    for r in range(blocks // 2, blocks):
        line.step((i - 1) * blocks + r)

    @pl.when(i == pl.num_programs(0) - 1)
    def _():
        @pl.loop(0, blocks)
        def _(r):
            line.step(i * blocks + r)

        line.drain()

        @pl.loop(0, line.blocks)
        def _(b):
            norm_out(b).wait()


def attend(q_t, prompt_all, kvt_cont, bias, packed_full, x, gains, q_heads, kv_heads, cid):
    dim = HEAD_SIZE
    count, kv2, prompt_rows, cont_rows, chunk = attend_shape(prompt_all, kvt_cont)
    q_cols, rows = q_t.shape
    width = packed_full.shape[0]
    keys_all = bias.shape[0]
    tile, cut = 128, 16
    whole = pl.BlockSpec(memory_space=pltpu.VMEM)
    by_col = lambda i: (0, i)
    return pl.pallas_call(
        functools.partial(
            attend_kernel,
            (count, prompt_rows, chunk),
            dim,
            kv_heads,
            q_heads // kv_heads,
            tile,
            cut,
        ),
        grid=(rows // tile,),
        in_specs=[
            pl.BlockSpec((q_cols, tile), by_col),
            whole,
            whole,
            pl.BlockSpec((keys_all, tile), by_col),
            pl.BlockSpec((width, q_cols), lambda i: (0, 0), pipeline_mode=pl.Buffered(1)),
            whole,
            whole,
        ],
        out_specs=[
            pl.BlockSpec((tile, q_cols), lambda i: (i, 0)),
            pl.BlockSpec((q_heads, tile), by_col),
            pl.BlockSpec(memory_space=pl.ANY),
            pl.BlockSpec(memory_space=pl.ANY),
        ],
        out_shape=[
            jax.ShapeDtypeStruct((rows, q_cols), jnp.bfloat16),
            jax.ShapeDtypeStruct((q_heads, rows), jnp.float32),
            jax.ShapeDtypeStruct((rows, width), jnp.bfloat16),
            jax.ShapeDtypeStruct((rows, width), jnp.bfloat16),
        ],
        scratch_shapes=[
            pltpu.VMEM((kv_heads, keys_all, dim), jnp.bfloat16),
            pltpu.VMEM((keys_all // chunk, kv2, chunk), jnp.bfloat16),
            pltpu.VMEM((rows // cut, cut, width), jnp.bfloat16),
            pltpu.SemaphoreType.DMA((rows // cut,)),
            *line_scratch((rows // cut, cut, width)),
        ],
        compiler_params=pltpu.CompilerParams(
            collective_id=cid, has_side_effects=True, vmem_limit_bytes=56 << 20
        ),
        cost_estimate=pl.CostEstimate(
            flops=120_000_000_000, bytes_accessed=40 << 20, transcendentals=0
        ),
    )(q_t, prompt_all, kvt_cont, bias, packed_full, x, gains)


def feed_back_kernel(
    cut,
    gate_ref,
    up_ref,
    hidden_ref,
    wd_ref,
    wg_ref,
    wu_ref,
    cot_ref,
    normed_ref,
    grads_ref,
    up_grads_ref,
    mlp_ref,
    sum_ref,
    part,
    recv,
    out,
    sems,
    sink_sems,
):
    n = pl.program_id(0)
    rows, wide = gate_ref.shape
    per = rows // cut
    line = Line(part, recv, out, sum_ref, sems, sink_sems)

    back = contract_last(gate_ref[...], wg_ref[...]) + contract_last(up_ref[...], wu_ref[...])
    back = back.astype(jnp.bfloat16)
    for r in range(per):
        part[n * per + r] = back[r * cut : (r + 1) * cut]

    @pl.when(n == 0)
    def _():
        line.greet()

    line.start(n * per, per)

    def steps(low, high):
        for r in range(low, high):
            line.step(n * per + r)

    grads_ref[:, :wide] = contract_first(cot_ref[...], hidden_ref[...]).astype(jnp.bfloat16)
    steps(0, per // 4)
    grads_ref[:, wide:] = contract_first(normed_ref[...], gate_ref[...]).astype(
        jnp.bfloat16
    )
    steps(per // 4, per // 2)
    up_grads_ref[...] = contract_first(normed_ref[...], up_ref[...]).astype(jnp.bfloat16)
    steps(per // 2, per - per // 4)
    mlp_ref[0] = contract_last(hidden_ref[...], wd_ref[...]).astype(jnp.bfloat16)
    steps(per - per // 4, per)

    @pl.when(n == pl.num_programs(0) - 1)
    def _():
        line.drain()


def feed_back(grad_gate, grad_up, hidden, mlp_full, cot, normed, cid):
    rows, wide = hidden.shape
    width = cot.shape[1]
    size = SIZE
    cut = math.gcd(rows, size)
    tiles = width // size
    blocks = (tiles * rows // cut, cut, size)
    whole = pl.BlockSpec(memory_space=pltpu.VMEM)
    return pl.pallas_call(
        functools.partial(feed_back_kernel, cut),
        grid=(tiles,),
        in_specs=[whole] * 3
        + [pl.BlockSpec((size, wide), lambda n, k=k: (n, k)) for k in range(3)]
        + [pl.BlockSpec((rows, size), lambda n: (0, n))] * 2,
        out_specs=[
            pl.BlockSpec((size, 2 * wide), lambda n: (n, 0)),
            pl.BlockSpec((size, wide), lambda n: (n, 0)),
            pl.BlockSpec((1, rows, size), lambda n: (n, 0, 0)),
            pl.BlockSpec(memory_space=pl.ANY),
        ],
        out_shape=[
            jax.ShapeDtypeStruct((width, 2 * wide), jnp.bfloat16),
            jax.ShapeDtypeStruct((width, wide), jnp.bfloat16),
            jax.ShapeDtypeStruct((tiles, rows, size), jnp.bfloat16),
            jax.ShapeDtypeStruct((rows, width), jnp.bfloat16),
        ],
        scratch_shapes=line_scratch(blocks),
        compiler_params=pltpu.CompilerParams(
            collective_id=cid, has_side_effects=True, vmem_limit_bytes=58 << 20
        ),
        cost_estimate=pl.CostEstimate(
            flops=12 * rows * wide * width, bytes_accessed=200 << 20, transcendentals=0
        ),
    )(grad_gate, grad_up, hidden, mlp_full, mlp_full, mlp_full, cot, normed)


def window_kernel(
    shape,
    dim,
    kv_heads,
    per,
    tile,
    q_ref,
    all_ref,
    cont_ref,
    bias_ref,
    out_ref,
    lse_ref,
    back_ref,
    cot_ref,
    x_ref,
    attn_ref,
    gain_ref,
    wo_ref,
    cos_ref,
    sin_ref,
    cos_own_ref,
    sin_own_ref,
    normed_ref,
    att_ref,
    up_grads_ref,
    mlp_ref,
    gq_out_ref,
    gkv_ref,
    gm_ref,
    grads_ref,
    sum_ref,
    keys,
    values,
    chunks,
    gk,
    gv,
    gm,
    gq_ref,
    send_ref,
    got,
    own_ref,
    kv_sems,
    part,
    recv,
    out,
    sems,
    sink_sems,
):
    count, prompt_rows, chunk = shape
    i = pl.program_id(0)
    line = Line(part, recv, out, sum_ref, sems, sink_sems)
    context = lax.axis_index("context")
    prompt_tiles = prompt_rows // tile
    tiles = gq_ref.shape[0] // tile
    slots = SLOTS
    spots = 2 + kv_heads

    def step(k):
        for s in range(k * slots // spots, (k + 1) * slots // spots):
            line.step(i * slots + s)

    def send(k):
        peer = lax.rem(context + k, count)
        return pltpu.make_async_remote_copy(
            send_ref.at[peer],
            got.at[k],
            kv_sems.at[0, k],
            kv_sems.at[1, k],
            device_id={"context": peer},
            device_id_type=MESH,
        )

    root = dim ** (-0.5)
    half = dim // 2

    @pl.when(i == 0)
    def _():
        load = pltpu.make_async_copy(mlp_ref, part, sink_sems.at[0])
        load.start()
        fill_keys(chunk, dim, kv_heads, all_ref, cont_ref, [keys, values], chunks)
        gk[...] = jnp.zeros_like(gk)
        gv[...] = jnp.zeros_like(gv)
        line.greet("context", count)
        load.wait()
        line.start(0, line.blocks)

    @pl.when(i < tiles)
    def _():
        middle = x_ref[...].astype(jnp.float32) + attn_ref[...].astype(jnp.float32)
        inverse = lax.rsqrt(jnp.mean(middle * middle, axis=-1, keepdims=True) + EPS)
        unit = middle * inverse
        grad_unit = back_ref[...].astype(jnp.float32) * gain_ref[...]
        grad_middle = cot_ref[...].astype(jnp.float32) + norm_back(grad_unit, unit, inverse)
        gm_ref[...] = grad_middle.astype(jnp.bfloat16)
        grad_b = grad_middle.astype(jnp.bfloat16)
        step(0)
        grad_t = (
            jnp.dot(grad_b, wo_ref[...], preferred_element_type=jnp.float32).astype(jnp.bfloat16)
        ).astype(jnp.float32).T
        gm[pl.ds(pl.multiple_of(i * tile, tile), tile), :] = grad_b
        step(1)

        is_prompt, n_prompt, base, n_own = trip_count(tile, chunk, i, prompt_rows, count)
        factor = root * LOG2E
        prod = grad_t * out_ref[...].astype(jnp.float32).T
        grad_t = grad_t.astype(jnp.bfloat16)
        cosine, sine = cos_ref[...], sin_ref[...]
        pieces = []
        for g in range(kv_heads):
            heads = [g * per + h for h in range(per)]
            q = jnp.concatenate([q_ref[h * dim : (h + 1) * dim, :] for h in heads], axis=1)
            grad = jnp.concatenate([grad_t[h * dim : (h + 1) * dim] for h in heads], axis=1)
            inner = jnp.concatenate(
                [jnp.sum(prod[h * dim : (h + 1) * dim], axis=0, keepdims=True) for h in heads], axis=1
            )
            lse = jnp.concatenate([lse_ref[h : h + 1, :] for h in heads], axis=1)

            def body(c, acc):
                at = pl.ds(pl.multiple_of(c * chunk, chunk), chunk)
                s = jnp.dot(keys[g, at, :], q, preferred_element_type=jnp.float32)
                b = bias_ref[at, :].astype(jnp.float32)
                p = jnp.exp2(s * factor + (jnp.concatenate([b] * per, axis=1) - lse))
                dp = jnp.dot(values[g, at, :], grad, preferred_element_type=jnp.float32)
                ds = (p * (dp - inner)).astype(jnp.bfloat16)
                gv[g, at, :] += contract_last(p.astype(jnp.bfloat16), grad)
                gk[g, at, :] += contract_last(ds, q)
                k_t = chunks[c, g * dim : (g + 1) * dim, :]
                return acc + jnp.dot(k_t, ds, preferred_element_type=jnp.float32)

            acc = jnp.zeros((dim, per * tile), jnp.float32)
            acc = lax.fori_loop(0, jnp.where(is_prompt, n_prompt, base), body, acc)
            acc = lax.fori_loop(base, base + jnp.where(is_prompt, 0, n_own), body, acc)
            acc = acc * root
            for h in range(per):
                first = acc[:half, h * tile : (h + 1) * tile]
                second = acc[half:, h * tile : (h + 1) * tile]
                pieces += [first * cosine + second * sine, second * cosine - first * sine]
            step(2 + g)
        rows_q = jnp.concatenate(pieces, axis=0).T.astype(jnp.bfloat16)
        gq_ref[pl.ds(pl.multiple_of(i * tile, tile), tile), :] = rows_q
        gq_out_ref[...] = rows_q

    @pl.when(i == tiles - 1)
    def _():
        for g in range(kv_heads):
            for n, (acc, scale) in enumerate(((gk, root), (gv, 1.0))):
                at = (n * kv_heads + g) * dim
                for c in range(count):
                    rows = acc[g, c * prompt_rows : (c + 1) * prompt_rows, :]
                    send_ref[c, at : at + dim, :] = (rows * scale).T.astype(jnp.bfloat16)
                own_ref[at : at + dim, :] = (acc[g, count * prompt_rows :, :] * scale).T
        for k in range(1, count):
            send(k).start()

    @pl.when(i == tiles)
    def _():
        line.step(tiles * slots)
        kv_dim = kv_heads * dim

        def finish(flat, cosine, sine):
            pieces = []
            for at in range(0, kv_dim, dim):
                first, second = flat[at : at + half], flat[at + half : at + dim]
                pieces += [first * cosine + second * sine, second * cosine - first * sine]
            pieces.append(flat[kv_dim:])
            return jnp.concatenate(pieces, axis=0).T.astype(jnp.bfloat16)

        cosine, sine = cos_own_ref[...], sin_own_ref[...]
        gkv_ref[prompt_rows:, :] = finish(
            own_ref[...], cosine[:, prompt_rows:], sine[:, prompt_rows:]
        )
        total = send_ref[context].astype(jnp.float32)
        for k in range(1, count):
            send(k).wait()
            total += got[k].astype(jnp.float32)
        gkv_ref[:prompt_rows, :] = finish(
            total, cosine[:, :prompt_rows], sine[:, :prompt_rows]
        )

    @pl.when(i >= tiles)
    def _():
        n = i - tiles
        later = pl.num_programs(0) - tiles
        rest = line.blocks - tiles * slots - 1
        q_cols = gq_ref.shape[1]
        wide = up_grads_ref.shape[1]
        here = pl.ds(pl.multiple_of(n * SIZE, SIZE), SIZE)
        grads_ref[:, :wide] = up_grads_ref[...]
        grads_ref[:, wide : wide + q_cols] = contract_first(gm[:, here], att_ref[...]).astype(
            jnp.bfloat16
        )
        grads_ref[:, wide + q_cols : wide + 2 * q_cols] = contract_first(
            normed_ref[...], gq_ref[...]
        ).astype(jnp.bfloat16)
        grads_ref[:, wide + 2 * q_cols :] = contract_first(normed_ref[...], gkv_ref[...]).astype(
            jnp.bfloat16
        )
        low = tiles * slots + 1 + lax.div(n * rest, later)
        high = tiles * slots + 1 + lax.div((n + 1) * rest, later)

        @pl.loop(low, high)
        def _(t):
            line.step(t)

        @pl.when(n == later - 1)
        def _():
            line.drain()


def window(
    q_t,
    prompt_all,
    kvt_cont,
    bias,
    attended,
    lse,
    back,
    cot,
    x,
    attn_sum,
    gain,
    packed_full,
    cos_t,
    sin_t,
    normed,
    up_grads,
    mlp_part,
    q_heads,
    kv_heads,
    cid,
):
    dim = HEAD_SIZE
    count, kv2, prompt_rows, cont_rows, chunk = attend_shape(prompt_all, kvt_cont)
    rows, width = cot.shape
    q_cols = q_heads * dim
    keys_all = bias.shape[0]
    tile = 128
    whole = pl.BlockSpec(memory_space=pltpu.VMEM)
    anywhere = pl.BlockSpec(memory_space=pl.ANY)
    tiles, later = rows // tile, width // SIZE
    grad_cols = up_grads.shape[1] + 2 * q_cols + kv2
    early = lambda i: jnp.minimum(i, tiles - 1)
    late = lambda i: jnp.maximum(i - tiles, 0)
    by_col = lambda i: (0, early(i))
    by_row = lambda i: (early(i), 0)
    fixed = lambda i: (0, 0)
    return pl.pallas_call(
        functools.partial(
            window_kernel, (count, prompt_rows, chunk), dim, kv_heads, q_heads // kv_heads, tile
        ),
        grid=(tiles + later,),
        in_specs=[
            pl.BlockSpec((q_cols, tile), by_col),
            whole,
            whole,
            pl.BlockSpec((keys_all, tile), by_col),
            pl.BlockSpec((tile, q_cols), by_row),
            pl.BlockSpec((q_heads, tile), by_col),
            pl.BlockSpec((tile, width), by_row),
            pl.BlockSpec((tile, width), by_row),
            pl.BlockSpec((tile, width), by_row),
            pl.BlockSpec((tile, width), by_row),
            pl.BlockSpec((1, width), fixed),
            pl.BlockSpec((width, q_cols), fixed, pipeline_mode=pl.Buffered(1)),
            pl.BlockSpec((dim // 2, tile), by_col),
            pl.BlockSpec((dim // 2, tile), by_col),
            whole,
            whole,
            pl.BlockSpec((rows, SIZE), lambda i: (0, late(i))),
            whole,
            pl.BlockSpec((SIZE, up_grads.shape[1]), lambda i: (late(i), 0)),
            anywhere,
        ],
        out_specs=[
            pl.BlockSpec((tile, q_cols), by_row),
            pl.BlockSpec((rows, kv2), fixed),
            pl.BlockSpec((tile, width), by_row),
            pl.BlockSpec((SIZE, grad_cols), lambda i: (late(i), 0)),
            anywhere,
        ],
        out_shape=[
            jax.ShapeDtypeStruct((rows, q_cols), jnp.bfloat16),
            jax.ShapeDtypeStruct((rows, kv2), jnp.bfloat16),
            jax.ShapeDtypeStruct((rows, width), jnp.bfloat16),
            jax.ShapeDtypeStruct((width, grad_cols), jnp.bfloat16),
            jax.ShapeDtypeStruct((rows, width), jnp.bfloat16),
        ],
        scratch_shapes=[
            pltpu.VMEM((kv_heads, keys_all, dim), jnp.bfloat16),
            pltpu.VMEM((kv_heads, keys_all, dim), jnp.bfloat16),
            pltpu.VMEM((keys_all // chunk, kv2, chunk), jnp.bfloat16),
            pltpu.VMEM((kv_heads, keys_all, dim), jnp.float32),
            pltpu.VMEM((kv_heads, keys_all, dim), jnp.float32),
            pltpu.VMEM((rows, width), jnp.bfloat16),
            pltpu.VMEM((rows, q_cols), jnp.bfloat16),
            pltpu.VMEM((count, kv2, prompt_rows), jnp.bfloat16),
            pltpu.VMEM((count, kv2, prompt_rows), jnp.bfloat16),
            pltpu.VMEM((kv2, cont_rows), jnp.float32),
            pltpu.SemaphoreType.DMA((2, count)),
            *line_scratch(mlp_part.shape),
        ],
        compiler_params=pltpu.CompilerParams(
            collective_id=cid, has_side_effects=True, vmem_limit_bytes=60 << 20
        ),
        cost_estimate=pl.CostEstimate(
            flops=120_000_000_000, bytes_accessed=200 << 20, transcendentals=0
        ),
    )(
        q_t,
        prompt_all,
        kvt_cont,
        bias,
        attended,
        lse,
        back,
        cot,
        x,
        attn_sum,
        gain,
        packed_full,
        cos_t,
        sin_t,
        cos_t,
        sin_t,
        normed,
        attended,
        up_grads,
        mlp_part,
    )


def product_kernel(cut, spans, lhs_refs, w_ref, sum_ref, part, recv, out, sems, sink_sems):
    n = pl.program_id(0)
    per = sum_ref.shape[0] // cut
    line = Line(part, recv, out, sum_ref, sems, sink_sems)
    term = sum(
        contract_last(ref[...], w_ref[:, low:high]) for ref, (low, high) in zip(lhs_refs, spans)
    ).astype(jnp.bfloat16)
    for r in range(per):
        part[n * per + r] = term[r * cut : (r + 1) * cut]

    @pl.when(n == 0)
    def _():
        line.greet()

    line.start(n * per, per)
    for r in range(per):
        line.step(n * per + r)

    @pl.when(n == pl.num_programs(0) - 1)
    def _():
        line.drain()


def product_sum(lhs, spans, weights, cid):
    rows = lhs[0].shape[0]
    width, cols = weights.shape
    cut = math.gcd(rows, 128)
    tiles = width // SIZE
    blocks = (tiles * rows // cut, cut, SIZE)

    def body(*refs):
        product_kernel(cut, spans, refs[: len(lhs)], *refs[len(lhs) :])

    return pl.pallas_call(
        body,
        grid=(tiles,),
        in_specs=[pl.BlockSpec(memory_space=pltpu.VMEM)] * len(lhs)
        + [pl.BlockSpec((SIZE, cols), lambda n: (n, 0))],
        out_specs=pl.BlockSpec(memory_space=pl.ANY),
        out_shape=jax.ShapeDtypeStruct((rows, width), jnp.bfloat16),
        scratch_shapes=line_scratch(blocks),
        compiler_params=pltpu.CompilerParams(
            collective_id=cid, has_side_effects=True, vmem_limit_bytes=40 << 20
        ),
        cost_estimate=pl.CostEstimate(
            flops=120_000_000_000, bytes_accessed=40 << 20, transcendentals=0
        ),
    )(*lhs, weights)


def feed_kernel(
    normed_ref,
    cot_ref,
    wd_ref,
    wg_ref,
    wu_ref,
    hidden_ref,
    gate_grad_ref,
    up_grad_ref,
):
    gate = jnp.dot(normed_ref[...], wg_ref[...], preferred_element_type=jnp.float32)
    up = jnp.dot(normed_ref[...], wu_ref[...], preferred_element_type=jnp.float32)
    grad_hidden = jnp.dot(cot_ref[...], wd_ref[...], preferred_element_type=jnp.float32)
    sigmoid = 1.0 / (1.0 + jnp.exp(-gate))
    silu = gate * sigmoid
    hidden_ref[...] = (silu * up).astype(jnp.bfloat16)
    gate_grad_ref[...] = (grad_hidden * up * sigmoid * (1.0 + gate * (1.0 - sigmoid))).astype(
        jnp.bfloat16
    )
    up_grad_ref[...] = (grad_hidden * silu).astype(jnp.bfloat16)


def feed(normed, cot, mlp_full):
    rows, width = cot.shape
    wide = mlp_full.shape[1] // 3
    tiles = wide // SIZE
    whole = pl.BlockSpec(memory_space=pltpu.VMEM)
    tile = pl.BlockSpec((rows, SIZE), lambda n: (0, n))
    return pl.pallas_call(
        feed_kernel,
        grid=(tiles,),
        in_specs=[whole] * 2
        + [pl.BlockSpec((width, SIZE), lambda n, k=k: (0, k * tiles + n)) for k in range(3)],
        out_specs=[
            tile,
            tile,
            tile,
        ],
        out_shape=[jax.ShapeDtypeStruct((rows, wide), jnp.bfloat16)] * 3,
        compiler_params=pltpu.CompilerParams(vmem_limit_bytes=58 << 20),
        cost_estimate=pl.CostEstimate(
            flops=6 * rows * width * wide, bytes_accessed=60 << 20, transcendentals=rows * wide
        ),
    )(normed, cot, mlp_full, mlp_full, mlp_full)


def finish_kernel(
    prompt_tiles, x_ref, attn_ref, mlp_ref, gm_ref, back_ref, gain_ref, po_ref, co_ref, pg_ref, cg_ref
):
    i = pl.program_id(0)
    x = x_ref[...].astype(jnp.float32)
    result = (x + attn_ref[...].astype(jnp.float32)) + mlp_ref[...].astype(jnp.float32)
    result = result.astype(jnp.bfloat16)
    unit, inverse = normalize(x)
    grad = gm_ref[...].astype(jnp.float32) + norm_back(back_ref[...].astype(jnp.float32) * gain_ref[...], unit, inverse)

    @pl.when(i < prompt_tiles)
    def _():
        po_ref[...] = result
        pg_ref[...] = grad

    @pl.when(i >= prompt_tiles)
    def _():
        co_ref[...] = result
        cg_ref[...] = grad


def finish(x, attn_sum, mlp_sum, grad_middle, back, gain, prompt_rows):
    rows, width = x.shape
    tile = 128
    prompt_tiles = prompt_rows // tile
    every = pl.BlockSpec((tile, width), lambda i: (i, 0))
    first = pl.BlockSpec((tile, width), lambda i: (jnp.minimum(i, prompt_tiles - 1), 0))
    second = pl.BlockSpec((tile, width), lambda i: (jnp.maximum(i - prompt_tiles, 0), 0))
    shapes = [(prompt_rows, width), (rows - prompt_rows, width)]
    return pl.pallas_call(
        functools.partial(finish_kernel, prompt_tiles),
        grid=(rows // tile,),
        in_specs=[every] * 5 + [pl.BlockSpec((1, width), lambda i: (0, 0))],
        out_specs=[first, second, first, second],
        out_shape=[jax.ShapeDtypeStruct(shape, jnp.bfloat16) for shape in shapes]
        + [jax.ShapeDtypeStruct(shape, jnp.float32) for shape in shapes],
        compiler_params=pltpu.CompilerParams(vmem_limit_bytes=40 << 20),
        cost_estimate=pl.CostEstimate(
            flops=20 * x.size, bytes_accessed=20 * x.size, transcendentals=0
        ),
    )(x, attn_sum, mlp_sum, grad_middle, back, gain)


def per_device(
    prompt_x,
    cont_x,
    prompt_len,
    cont_seg,
    attn_gain,
    q_weight,
    key_matrix,
    value_matrix,
    o_weight,
    mlp_gain,
    gate_weight,
    up_weight,
    down_weight,
    prompt_cot,
    cont_cot,
):
    head_dim = HEAD_SIZE
    data = ("dp", "context")
    prompt_rows = prompt_x.shape[0]
    cont_rows = cont_x.shape[0]
    prompt_total = prompt_rows * lax.axis_size("context")
    q_cols = q_weight.shape[1]
    kv_cols = key_matrix.shape[1]
    q_heads = q_cols // head_dim
    kv_heads = kv_cols // head_dim
    qkv_cols = q_cols + 2 * kv_cols
    qkv_wide = qkv_cols + 2 + -(qkv_cols + 2) % 128
    hidden_cols = gate_weight.shape[1]
    wide = hidden_cols + -hidden_cols % 256
    context_pos = lax.axis_index("context")
    prompt_pos = context_pos * prompt_rows + jnp.arange(prompt_rows, dtype=jnp.int32)
    segment = cont_seg[0]
    earlier = jnp.sum((segment[None, :] < segment[:, None]).astype(jnp.int32), axis=1)
    local_index = jnp.arange(cont_rows, dtype=jnp.int32)
    length = prompt_len[0]
    cont_pos = length + local_index - earlier
    position = jnp.concatenate([prompt_pos, cont_pos]).astype(jnp.float32)
    inv_freq = THETA ** (-jnp.arange(head_dim // 2, dtype=jnp.float32) * 2.0 / head_dim)
    angle_table = inv_freq[:, None] * position[None, :]
    cosine = jnp.cos(angle_table)
    sine_table = jnp.sin(angle_table)
    shards = (down_weight, gate_weight, up_weight)
    attn_shards = (o_weight, q_weight, key_matrix, value_matrix)
    if lax.axis_size("dp") == 4 and lax.axis_size("context") == 2:
        info = jnp.stack([earlier, jnp.broadcast_to(length, earlier.shape)])
        packed_full, mlp_shard, x_all, grad_out, bias = plane_gather(
            attn_shards,
            (attn_gain, mlp_gain),
            info,
            shards,
            wide,
            q_cols + qkv_wide,
            prompt_x,
            cont_x,
            prompt_cot,
            cont_cot,
            6,
        )
    else:
        packed = jnp.concatenate([*attn_shards, attn_gain[:, None], mlp_gain[:, None]], axis=1)
        packed = jnp.pad(packed, ((0, 0), (0, q_cols + qkv_wide - packed.shape[1])))
        packed_full = lax.all_gather(packed, data, axis=0, tiled=True)
        fill = ((0, 0), (0, wide - hidden_cols))
        mlp_shard = jnp.concatenate([jnp.pad(w, fill) for w in shards], axis=1)
        x_all = jnp.concatenate([prompt_x, cont_x], axis=0)
        grad_out = jnp.concatenate([prompt_cot, cont_cot], axis=0)
        key_index = jnp.arange(prompt_total, dtype=jnp.int32)
        prompt_mask = jnp.concatenate(
            [
                key_index[:, None] <= prompt_pos[None, :],
                jnp.zeros((cont_rows, prompt_rows), jnp.bool_),
            ],
            axis=0,
        )
        own_mask = (segment[:, None] == segment[None, :]) & (
            local_index[:, None] <= local_index[None, :]
        )
        reach_mask = jnp.broadcast_to(key_index[:, None] < length, (prompt_total, cont_rows))
        allowed = jnp.concatenate(
            [prompt_mask, jnp.concatenate([reach_mask, own_mask], axis=0)], axis=1
        )
        bias = jnp.where(allowed, 0.0, NEGATIVE).astype(jnp.bfloat16)
    first_normed, q_t, cont_kv, gains, prompt_all = project_rope(
        x_all, packed_full, cosine, sine_table, q_heads, kv_heads, prompt_rows, 4
    )
    gain_one, gain_two = gains[0:1], gains[1:2]
    prompt_all, mlp_shard = lax.optimization_barrier((prompt_all, mlp_shard))
    mlp_full = lax.all_gather(mlp_shard, data, axis=0, tiled=True)
    attn_out, lse, attn_sum, normed_two = attend(
        q_t, prompt_all, cont_kv, bias, packed_full, x_all, gains, q_heads, kv_heads, 0
    )
    hidden, grad_gate, grad_up = feed(normed_two, grad_out, mlp_full)
    mlp_grads, up_grads, mlp_part, back_two = feed_back(
        grad_gate, grad_up, hidden, mlp_full, grad_out, normed_two, 1
    )

    def scatter(values):
        return lax.psum_scatter(values, data, scatter_dimension=0, tiled=True).astype(jnp.float32)

    cut = math.gcd(prompt_rows + cont_rows, SIZE)
    grad_q, grad_kv, grad_middle, grad_rest, mlp_sum = window(
        q_t,
        prompt_all,
        cont_kv,
        bias,
        attn_out,
        lse,
        back_two,
        grad_out,
        x_all,
        attn_sum,
        gain_two,
        packed_full,
        cosine,
        sine_table,
        first_normed,
        up_grads,
        mlp_part.reshape(-1, cut, SIZE),
        q_heads,
        kv_heads,
        3,
    )
    mlp_own = scatter(mlp_grads)
    grad_q, grad_rest, mlp_own = lax.optimization_barrier((grad_q, grad_rest, mlp_own))
    back_one = product_sum(
        [grad_q, grad_kv], [(q_cols, 2 * q_cols), (2 * q_cols, q_cols + qkv_cols)], packed_full, 2
    )
    back_one, mlp_own = lax.optimization_barrier((back_one, mlp_own))
    outs = finish(x_all, attn_sum, mlp_sum, grad_middle, back_one, gain_one, prompt_rows)
    down_own = mlp_own[:, :hidden_cols]
    gate_own = mlp_own[:, wide : wide + hidden_cols]
    rest_own = scatter(grad_rest)
    up_own = rest_own[:, :hidden_cols]
    o_own = rest_own[:, wide : wide + q_cols]
    q_own = rest_own[:, wide + q_cols : wide + 2 * q_cols]
    k_own = rest_own[:, wide + 2 * q_cols : wide + 2 * q_cols + kv_cols]
    v_own = rest_own[:, wide + 2 * q_cols + kv_cols :]

    def row_dot(weight, grad):
        return jnp.sum(weight.astype(jnp.float32) * grad, axis=1)

    gain_rows = jnp.stack(
        [
            (row_dot(q_weight, q_own) + row_dot(key_matrix, k_own) + row_dot(value_matrix, v_own))
            / attn_gain.astype(jnp.float32),
            (row_dot(gate_weight, gate_own) + row_dot(up_weight, up_own))
            / mlp_gain.astype(jnp.float32),
        ]
    )
    gain_rows = tensor_total(gain_rows, 5)
    owned = (gain_rows[0], q_own, k_own, v_own, o_own, gain_rows[1], gate_own, up_own, down_own)
    return (*outs, *owned)


def solution(mesh):
    in_specs = (
        P(("dp", "context"), None),
        P(("dp", "context"), None),
        P("dp"),
        P(("dp", "context"), None),
        P(("dp", "context")),
        P(("dp", "context"), "tensor"),
        P(("dp", "context"), "tensor"),
        P(("dp", "context"), "tensor"),
        P(("dp", "context"), "tensor"),
        P(("dp", "context")),
        P(("dp", "context"), "tensor"),
        P(("dp", "context"), "tensor"),
        P(("dp", "context"), "tensor"),
        P(("dp", "context"), None),
        P(("dp", "context"), None),
    )
    out_specs = (
        P(("dp", "context"), None),
        P(("dp", "context"), None),
        P(("dp", "context"), None),
        P(("dp", "context"), None),
        P(("dp", "context")),
        P(("dp", "context"), "tensor"),
        P(("dp", "context"), "tensor"),
        P(("dp", "context"), "tensor"),
        P(("dp", "context"), "tensor"),
        P(("dp", "context")),
        P(("dp", "context"), "tensor"),
        P(("dp", "context"), "tensor"),
        P(("dp", "context"), "tensor"),
    )
    return jax.shard_map(
        per_device, mesh=mesh, in_specs=in_specs, out_specs=out_specs, check_vma=False
    )
```

```python
import functools
import math

import jax
import jax.numpy as jnp
from jax import lax
from jax.experimental import pallas as pl
from jax.experimental.pallas import tpu as pltpu
from jax.sharding import PartitionSpec as P

HEAD_SIZE = 80


EPS = 1e-05
THETA = 10000.0
NEGATIVE = -1e30
LOG2E = math.log2(math.e)
MESH = pl.DeviceIdType.MESH
AXIS = "tensor"
LAG = 3
SIZE = 256
FEED_STEPS = 10
SLOTS = 4


def normalize(values):
    inverse = lax.rsqrt(jnp.mean(values * values, axis=-1, keepdims=True) + EPS)
    return (values * inverse, inverse)


def norm_back(grad_unit, unit_rows, inverse):
    inner_sum = jnp.mean(grad_unit * unit_rows, axis=-1, keepdims=True)
    return inverse * (grad_unit - unit_rows * inner_sum)


def contract_last(left_side, right_side):
    return lax.dot_general(
        left_side, right_side, (((1,), (1,)), ((), ())), preferred_element_type=jnp.float32
    )


def contract_first(left_side, right_side):
    return lax.dot_general(
        left_side, right_side, (((0,), (0,)), ((), ())), preferred_element_type=jnp.float32
    )


def greet(axis, count):
    me = lax.axis_index(axis)
    barrier = pltpu.get_barrier_semaphore()
    for k in range(1, count):
        peer = lax.rem(me + k, count)
        pl.semaphore_signal(barrier, inc=1, device_id={axis: peer}, device_id_type=MESH)
    pl.semaphore_wait(barrier, count - 1)


def rope_kernel(
    q_heads,
    kv_heads,
    dim,
    prompt_steps,
    x_ref,
    w_ref,
    cos_ref,
    sin_ref,
    normed_ref,
    qt_ref,
    kvt_ref,
    gains_ref,
    all_ref,
    own,
    send,
    recv,
    local,
):
    i = pl.program_id(0)
    count = all_ref.shape[0]
    me = lax.axis_index("context")
    last = (q_heads + 2 * kv_heads + q_heads) * dim

    @pl.when(i == 0)
    def _():
        greet("context", count)
        low = last - last % 128
        turned = w_ref[:, low:].astype(jnp.float32).T
        gains_ref[...] = turned[last - low : last - low + 8]

    rows = x_ref[...].astype(jnp.float32)
    inverse = lax.rsqrt(jnp.mean(rows * rows, axis=-1, keepdims=True) + EPS)
    normed = (rows * inverse * gains_ref[0:1, :]).astype(jnp.bfloat16)
    normed_ref[...] = normed
    flat = jnp.dot(
        normed, w_ref[:, q_heads * dim :], preferred_element_type=jnp.float32
    ).T
    cosine, sine = cos_ref[...], sin_ref[...]
    half = dim // 2
    pieces = []
    for head in range(q_heads + kv_heads):
        first = flat[head * dim : head * dim + half]
        second = flat[head * dim + half : (head + 1) * dim]
        turned = jnp.concatenate(
            [first * cosine - second * sine, second * cosine + first * sine], axis=0
        ).astype(jnp.bfloat16)
        if head < q_heads:
            qt_ref[head * dim : (head + 1) * dim, :] = turned
        else:
            pieces.append(turned)
    at = (q_heads + kv_heads) * dim
    pieces.append(flat[at : at + kv_heads * dim].astype(jnp.bfloat16))
    low = 0
    for piece in pieces:
        kvt_ref[low : low + piece.shape[0], :] = piece
        low += piece.shape[0]
    step = x_ref.shape[0]
    for k in range(prompt_steps):

        @pl.when(i == k)
        def _():
            own[:, k * step : (k + 1) * step] = kvt_ref[...]

    def exchange(k):
        peer = lax.rem(me + k, count)
        return pltpu.make_async_remote_copy(
            own,
            all_ref.at[me],
            send.at[k],
            recv.at[k],
            device_id={"context": peer},
            device_id_type=MESH,
        )

    keep = pltpu.make_async_copy(own, all_ref.at[me], local)

    @pl.when(i == prompt_steps - 1)
    def _():
        for k in range(1, count):
            exchange(k).start()
        keep.start()

    @pl.when(i == pl.num_programs(0) - 1)
    def _():
        for k in range(1, count):
            exchange(k).wait()
        keep.wait()


def project_rope(x, packed_full, cos_t, sin_t, q_heads, kv_heads, prompt_rows, cid):
    rows, width = x.shape
    dim = HEAD_SIZE
    count = lax.axis_size("context")
    step = math.gcd(math.gcd(rows, prompt_rows), 256)
    cols_wide = packed_full.shape[1]
    kv2 = 2 * kv_heads * dim
    by_row = lambda i: (i, 0)
    by_col = lambda i: (0, i)
    fixed = lambda i: (0, 0)
    return pl.pallas_call(
        functools.partial(rope_kernel, q_heads, kv_heads, dim, prompt_rows // step),
        grid=(rows // step,),
        in_specs=[
            pl.BlockSpec((step, width), by_row),
            pl.BlockSpec(packed_full.shape, fixed, pipeline_mode=pl.Buffered(1)),
            pl.BlockSpec((dim // 2, step), by_col),
            pl.BlockSpec((dim // 2, step), by_col),
        ],
        out_specs=[
            pl.BlockSpec((step, width), by_row),
            pl.BlockSpec((q_heads * dim, step), by_col),
            pl.BlockSpec((kv2, step), by_col),
            pl.BlockSpec((8, width), fixed),
            pl.BlockSpec(memory_space=pltpu.HBM),
        ],
        out_shape=[
            jax.ShapeDtypeStruct((rows, width), jnp.bfloat16),
            jax.ShapeDtypeStruct((q_heads * dim, rows), jnp.bfloat16),
            jax.ShapeDtypeStruct((kv2, rows), jnp.bfloat16),
            jax.ShapeDtypeStruct((8, width), jnp.float32),
            jax.ShapeDtypeStruct((count, kv2, prompt_rows), jnp.bfloat16),
        ],
        scratch_shapes=[
            pltpu.VMEM((kv2, prompt_rows), jnp.bfloat16),
            pltpu.SemaphoreType.DMA((count,)),
            pltpu.SemaphoreType.DMA((count,)),
            pltpu.SemaphoreType.DMA,
        ],
        compiler_params=pltpu.CompilerParams(
            collective_id=cid, has_side_effects=True, vmem_limit_bytes=48 << 20
        ),
        cost_estimate=pl.CostEstimate(
            flops=2 * rows * width * cols_wide,
            bytes_accessed=4 * x.size + 2 * width * cols_wide,
            transcendentals=0,
        ),
    )(x, packed_full, cos_t, sin_t)


def attend_shape(prompt_all, kvt_cont):
    count, kv2, prompt_rows = prompt_all.shape
    cont_rows = kvt_cont.shape[1] - prompt_rows
    chunk = math.gcd(math.gcd(prompt_rows, cont_rows), 256)
    return count, kv2, prompt_rows, cont_rows, chunk


def total_kernel(count, part_ref, out_ref, got, send, recv):
    greet(AXIS, count)
    me = lax.axis_index(AXIS)
    copies = []
    for k in range(1, count):
        peer = lax.rem(me + k, count)
        copy = pltpu.make_async_remote_copy(
            part_ref,
            got.at[me],
            send.at[k],
            recv.at[k],
            device_id={AXIS: peer},
            device_id_type=MESH,
        )
        copy.start()
        copies.append(copy)
    got[me] = part_ref[...]
    for copy in copies:
        copy.wait()
    total = got[0]
    for k in range(1, count):
        total += got[k]
    out_ref[...] = total


def tensor_total(part, cid):
    count = lax.axis_size(AXIS)
    return pl.pallas_call(
        functools.partial(total_kernel, count),
        out_shape=jax.ShapeDtypeStruct(part.shape, part.dtype),
        in_specs=[pl.BlockSpec(memory_space=pltpu.VMEM)],
        out_specs=pl.BlockSpec(memory_space=pltpu.VMEM),
        scratch_shapes=[
            pltpu.VMEM((count, *part.shape), part.dtype),
            pltpu.SemaphoreType.DMA((count,)),
            pltpu.SemaphoreType.DMA((count,)),
        ],
        compiler_params=pltpu.CompilerParams(collective_id=cid, has_side_effects=True),
        cost_estimate=pl.CostEstimate(flops=0, bytes_accessed=4 << 20, transcendentals=0),
    )(part)


def plane_kernel(
    prompt_total,
    o_ref,
    q_ref,
    kt_ref,
    vt_ref,
    again_ref,
    mgain_ref,
    info_ref,
    w0_ref,
    w1_ref,
    w2_ref,
    px_ref,
    cx_ref,
    pc_ref,
    cc_ref,
    all_ref,
    shard_ref,
    x_ref,
    cot_ref,
    bias_ref,
    own_ref,
    stage,
    send,
    recv,
    local,
):
    dp, context = lax.axis_index("dp"), lax.axis_index("context")
    side = {"context": 1 - context}
    along = {"dp": lax.rem(dp + 2, 4)}
    twin_dp = dp + 1 - 2 * lax.rem(dp, 2)
    twin = {"dp": twin_dp}
    barrier = pltpu.get_barrier_semaphore()
    for peer in (side, along, twin):
        pl.semaphore_signal(barrier, inc=1, device_id=peer, device_id_type=MESH)
    pl.semaphore_wait(barrier, 3)
    rows = own_ref.shape[0]
    q_cols = q_ref.shape[1]
    own_ref[:, :q_cols] = o_ref[...]
    own_ref[:, q_cols : 2 * q_cols] = q_ref[...]
    small = [kt_ref[...], vt_ref[...], again_ref[...], mgain_ref[...]]
    rest = own_ref.shape[1] - 2 * q_cols
    used = sum(part.shape[0] for part in small)
    small.append(jnp.zeros((rest - used, rows), jnp.bfloat16))
    own_ref[:, 2 * q_cols :] = (
        jnp.concatenate([part.astype(jnp.float32) for part in small], axis=0).T
    ).astype(jnp.bfloat16)
    half = rows // 2
    mine = 2 * dp + context
    from_side = 2 * dp + 1 - context
    from_along = 2 * lax.rem(dp + 2, 4) + context
    from_far = 2 * lax.rem(dp + 2, 4) + 1 - context

    def spot(block, h):
        return pl.ds(pl.multiple_of(block * rows + h * half, half), half)

    def copy(k, block, h, peer, first=False):
        source = own_ref.at[pl.ds(h * half, half)] if first else all_ref.at[spot(block, h)]
        return pltpu.make_async_remote_copy(
            source,
            all_ref.at[spot(block, h)],
            send.at[k],
            recv.at[k],
            device_id=peer,
            device_id_type=MESH,
        )

    def land(k, block, h):
        return pltpu.make_async_remote_copy(
            own_ref.at[pl.ds(h * half, half)],
            all_ref.at[spot(block, h)],
            send.at[k],
            recv.at[k],
            device_id=side,
            device_id_type=MESH,
        )

    started = []

    def go(*args, **kwargs):
        one = copy(*args, **kwargs)
        one.start()
        started.append(one)

    go(0, mine, 0, side, first=True)
    go(2, mine, 1, along, first=True)
    go(1, mine, 1, side, first=True)
    go(3, mine, 0, along, first=True)
    go(6, mine, 0, twin, first=True)
    go(7, mine, 1, twin, first=True)
    prompt_rows = px_ref.shape[0]
    moves = [
        pltpu.make_async_copy(own_ref, all_ref.at[pl.ds(pl.multiple_of(mine * rows, rows), rows)], local.at[0]),
    ]
    moves[0].start()
    joins = []
    for k, (source, target, low) in enumerate(
        (
            (px_ref, x_ref, 0),
            (cx_ref, x_ref, prompt_rows),
            (pc_ref, cot_ref, 0),
            (cc_ref, cot_ref, prompt_rows),
        )
    ):
        rows_at = pl.ds((k % 2) * prompt_rows, source.shape[0])
        load = pltpu.make_async_copy(source, stage.at[k // 2, rows_at], local.at[1 + k])
        load.start()
        joins.append(
            (
                load,
                pltpu.make_async_copy(
                    stage.at[k // 2, rows_at],
                    target.at[pl.ds(low, source.shape[0])],
                    local.at[5 + k],
                ),
            )
        )
    cols = w0_ref.shape[1]
    wide = shard_ref.shape[1] // 3
    for k, ref in enumerate((w0_ref, w1_ref, w2_ref)):
        shard_ref[:, k * wide : k * wide + cols] = ref[...]
        shard_ref[:, k * wide + cols : (k + 1) * wide] = jnp.zeros(
            (rows, wide - cols), jnp.bfloat16
        )
    cont_rows = cx_ref.shape[0]
    block = 128

    def fill_bias(low, count, at, columns, rule):
        @pl.loop(0, count // block)
        def _(c):
            key = lax.broadcasted_iota(jnp.int32, (block, columns), 0) + c * block
            query = lax.broadcasted_iota(jnp.int32, (block, columns), 1)
            rows_at = pl.ds(pl.multiple_of(low + c * block, block), block)
            bias_ref[rows_at, at : at + columns] = jnp.where(
                rule(key, query), 0.0, NEGATIVE
            ).astype(jnp.bfloat16)

    first = context * prompt_rows
    earlier, length = info_ref[0:1, :], info_ref[1:2, :]
    fill_bias(0, prompt_total, 0, prompt_rows, lambda k, q: k <= q + first)
    fill_bias(prompt_total, cont_rows, 0, prompt_rows, lambda k, q: k < 0)
    fill_bias(0, prompt_total, prompt_rows, cont_rows, lambda k, q: k < length)
    fill_bias(
        prompt_total, cont_rows, prompt_rows, cont_rows, lambda k, q: (k >= earlier) & (k <= q)
    )
    for load, save in joins:
        load.wait()
        save.start()
        moves.append(save)
    land(0, from_side, 0).wait_recv()
    go(4, from_side, 0, along)
    go(8, from_side, 0, twin)
    land(2, from_along, 1).wait_recv()
    go(5, from_along, 1, side)
    go(9, from_along, 1, twin)
    land(1, from_side, 1).wait_recv()
    go(10, from_side, 1, twin)
    land(3, from_along, 0).wait_recv()
    go(11, from_along, 0, twin)
    land(4, from_far, 0).wait_recv()
    go(12, from_far, 0, twin)
    land(5, from_far, 1).wait_recv()
    go(13, from_far, 1, twin)
    base = 2 * twin_dp
    other = 2 * lax.rem(twin_dp + 2, 4)
    for k, block, h in (
        (6, base + context, 0),
        (7, base + context, 1),
        (8, base + 1 - context, 0),
        (9, other + context, 1),
        (10, base + 1 - context, 1),
        (11, other + context, 0),
        (12, other + 1 - context, 0),
        (13, other + 1 - context, 1),
    ):
        land(k, block, h).wait_recv()
    for one in started:
        one.wait_send()
    for move in moves:
        move.wait()


def plane_gather(
    attn, gains, info, weights, wide, attn_wide, prompt_x, cont_x, prompt_cot, cont_cot, cid
):
    o_weight, q_weight, key_matrix, value_matrix = attn
    rows = q_weight.shape[0]
    count = lax.axis_size("dp") * lax.axis_size("context")
    prompt_rows, width = prompt_x.shape
    total = prompt_rows + cont_x.shape[0]
    prompt_total = prompt_rows * lax.axis_size("context")
    hbm = pl.BlockSpec(memory_space=pltpu.HBM)
    vmem = pl.BlockSpec(memory_space=pltpu.VMEM)
    both = jax.ShapeDtypeStruct((total, width), jnp.bfloat16)
    return pl.pallas_call(
        functools.partial(plane_kernel, prompt_total),
        out_shape=[
            jax.ShapeDtypeStruct((count * rows, attn_wide), jnp.bfloat16),
            jax.ShapeDtypeStruct((rows, 3 * wide), jnp.bfloat16),
            both,
            both,
            jax.ShapeDtypeStruct((prompt_total + cont_x.shape[0], total), jnp.bfloat16),
        ],
        in_specs=[vmem] * 10 + [hbm] * 4,
        out_specs=[hbm, vmem, hbm, hbm, vmem],
        scratch_shapes=[
            pltpu.VMEM((rows, attn_wide), jnp.bfloat16),
            pltpu.VMEM((2, total, width), jnp.bfloat16),
            pltpu.SemaphoreType.DMA((14,)),
            pltpu.SemaphoreType.DMA((14,)),
            pltpu.SemaphoreType.DMA((9,)),
        ],
        compiler_params=pltpu.CompilerParams(
            collective_id=cid, has_side_effects=True, vmem_limit_bytes=60 << 20
        ),
        cost_estimate=pl.CostEstimate(
            flops=30_000_000_000, bytes_accessed=40 << 20, transcendentals=0
        ),
    )(
        o_weight,
        q_weight,
        key_matrix.T,
        value_matrix.T,
        gains[0][None, :],
        gains[1][None, :],
        info,
        *weights,
        prompt_x,
        cont_x,
        prompt_cot,
        cont_cot,
    )


def fill_keys(chunk, dim, kv_heads, all_ref, cont_ref, rows_of, chunks_ref):
    count, _, prompt_rows = all_ref.shape
    per = prompt_rows // chunk
    total = count * per + (cont_ref.shape[1] - prompt_rows) // chunk
    for c in range(total):
        if c < count * per:
            block = all_ref[c // per, :, (c % per) * chunk : (c % per + 1) * chunk]
        else:
            at = prompt_rows + (c - count * per) * chunk
            block = cont_ref[:, at : at + chunk]
        chunks_ref[c] = block
        for n, target in enumerate(rows_of):
            for g in range(kv_heads):
                at = (n * kv_heads + g) * dim
                target[g, c * chunk : (c + 1) * chunk, :] = (
                    block[at : at + dim].astype(jnp.float32).T.astype(jnp.bfloat16)
                )


def trip_count(tile, chunk, i, prompt_rows, count):
    me = lax.axis_index("context")
    prompt_tiles = prompt_rows // tile
    n_prompt = lax.div(me * prompt_rows + (i + 1) * tile + chunk - 1, chunk)
    n_own = lax.div((i - prompt_tiles + 1) * tile + chunk - 1, chunk)
    return i < prompt_tiles, n_prompt, count * prompt_rows // chunk, n_own


class Line:
    def __init__(self, part, recv, out, sink, sems, sink_sems, ready=None, place=None):
        self.ready, self.place = ready, place
        self.part, self.recv, self.out, self.sink = part, recv, out, sink
        self.per = sink.shape[0] // out.shape[1]
        self.sems, self.sink_sems = sems, sink_sems
        self.blocks = out.shape[0]
        me, n = lax.axis_index(AXIS), lax.axis_size(AXIS)
        self.outer = (me == 0) | (me == n - 1)
        self.inner = jnp.logical_not(self.outer)
        self.mate = jnp.where(me < n // 2, 1 - me, 2 * n - 3 - me)
        self.across = n - 1 - me

    def copy(self, k, source, target, peer, b):
        return pltpu.make_async_remote_copy(
            source.at[b],
            target.at[b],
            self.sems.at[2 * k, b],
            self.sems.at[2 * k + 1, b],
            device_id={AXIS: peer},
            device_id_type=MESH,
        )

    def up(self, b):
        return self.copy(0, self.part, self.recv, self.mate, b)

    def mid(self, b):
        return self.copy(1, self.part, self.out, self.across, b)

    def down(self, b):
        return self.copy(2, self.out, self.out, self.mate, b)

    def keep(self, b):
        _, rows, cols = self.out.shape
        row, col = lax.rem(b, self.per), lax.div(b, self.per)
        if self.place is not None:
            row, col = self.place(b)
        at = (
            pl.ds(pl.multiple_of(row * rows, rows), rows),
            pl.ds(pl.multiple_of(col * cols, cols), cols),
        )
        return pltpu.make_async_copy(self.out.at[b], self.sink.at[at], self.sink_sems.at[b])

    def greet(self, axis=None, count=1):
        barrier = pltpu.get_barrier_semaphore()
        pl.semaphore_signal(barrier, inc=1, device_id={AXIS: self.mate}, device_id_type=MESH)
        for k in range(1, count):
            peer = lax.rem(lax.axis_index(axis) + k, count)
            pl.semaphore_signal(barrier, inc=1, device_id={axis: peer}, device_id_type=MESH)

        @pl.when(self.inner)
        def _():
            pl.semaphore_signal(barrier, inc=1, device_id={AXIS: self.across}, device_id_type=MESH)
            pl.semaphore_wait(barrier, 1 + count)

        @pl.when(self.outer)
        def _():
            pl.semaphore_wait(barrier, count)

    def start(self, first, count):
        @pl.when(self.outer)
        def _():
            @pl.loop(0, count)
            def _(k):
                self.up(first + k).start()

    def step(self, t):
        @pl.when(self.inner & (t >= 0) & (t < self.blocks))
        def _():
            self.up(t).wait_recv()
            self.part[t] = (
                self.part[t].astype(jnp.float32) + self.recv[t].astype(jnp.float32)
            ).astype(jnp.bfloat16)
            self.mid(t).start()

        @pl.when(self.inner & (t >= LAG) & (t < self.blocks + LAG))
        def _():
            b = t - LAG
            self.mid(b).wait_recv()
            self.out[b] = (
                self.part[b].astype(jnp.float32) + self.out[b].astype(jnp.float32)
            ).astype(jnp.bfloat16)
            self.down(b).start()
            self.keep(b).start()
            if self.ready is not None:
                self.ready(b)

    def drain(self):
        for k in range(LAG):
            self.step(self.blocks + k)

        @pl.when(self.outer)
        def _():
            @pl.loop(0, self.blocks)
            def _(b):
                self.down(b).wait_recv()
                self.keep(b).start()
                if self.ready is not None:
                    self.ready(b)
                self.up(b).wait_send()

        @pl.when(self.inner)
        def _():
            @pl.loop(0, self.blocks)
            def _(b):
                self.mid(b).wait_send()
                self.down(b).wait_send()

        @pl.loop(0, self.blocks)
        def _(b):
            self.keep(b).wait()


def line_scratch(shape):
    return [pltpu.VMEM(shape, jnp.bfloat16)] * 3 + [
        pltpu.SemaphoreType.DMA((6, shape[0])),
        pltpu.SemaphoreType.DMA((shape[0],)),
    ]


def attend_kernel(
    shape,
    dim,
    kv_heads,
    per,
    tile,
    cut,
    q_ref,
    all_ref,
    cont_ref,
    bias_ref,
    wo_ref,
    x_ref,
    gains_ref,
    out_ref,
    lse_ref,
    sum_ref,
    normed_ref,
    keys,
    chunks,
    norm_buf,
    norm_sems,
    part,
    recv,
    out,
    sems,
    sink_sems,
):
    count, prompt_rows, chunk = shape
    i = pl.program_id(0)

    def norm_out(b):
        at = pl.ds(pl.multiple_of(b * cut, cut), cut)
        return pltpu.make_async_copy(norm_buf.at[b], normed_ref.at[at], norm_sems.at[b])

    def ready(b):
        at = pl.ds(pl.multiple_of(b * cut, cut), cut)
        unit, _ = normalize(x_ref[at, :].astype(jnp.float32) + out[b].astype(jnp.float32))
        norm_buf[b] = (unit * gains_ref[1:2, :]).astype(jnp.bfloat16)
        norm_out(b).start()

    line = Line(part, recv, out, sum_ref, sems, sink_sems, ready)
    blocks = tile // cut

    @pl.when(i == 0)
    def _():
        fill_keys(chunk, dim, kv_heads, all_ref, cont_ref, [keys], chunks)
        line.greet()

    is_prompt, n_prompt, base, n_own = trip_count(tile, chunk, i, prompt_rows, count)
    wide = per * tile
    factor = dim ** (-0.5) * LOG2E
    outs, sums = [], []
    for g in range(kv_heads):
        q = jnp.concatenate(
            [q_ref[(g * per + h) * dim : (g * per + h + 1) * dim, :] for h in range(per)], axis=1
        )

        def body(c, state):
            top, total, acc = state
            at = pl.ds(pl.multiple_of(c * chunk, chunk), chunk)
            s = jnp.dot(keys[g, at, :], q, preferred_element_type=jnp.float32)
            t = s * factor + jnp.concatenate([bias_ref[at, :].astype(jnp.float32)] * per, axis=1)
            new = jnp.maximum(top, jnp.max(t, axis=0, keepdims=True))
            p = jnp.exp2(t - new)
            scale = jnp.exp2(top - new)
            total = total * scale + jnp.sum(p, axis=0, keepdims=True)
            v = chunks[c, (kv_heads + g) * dim : (kv_heads + g + 1) * dim, :]
            acc = acc * scale + jnp.dot(
                v, p.astype(jnp.bfloat16), preferred_element_type=jnp.float32
            )
            return new, total, acc

        start = (
            jnp.full((1, wide), NEGATIVE, jnp.float32),
            jnp.zeros((1, wide), jnp.float32),
            jnp.zeros((dim, wide), jnp.float32),
        )
        state = lax.fori_loop(0, jnp.where(is_prompt, n_prompt, base), body, start)
        top, total, acc = lax.fori_loop(base, base + jnp.where(is_prompt, 0, n_own), body, state)
        acc = acc / total
        top = top + jnp.log2(total)
        outs += [acc[:, h * tile : (h + 1) * tile] for h in range(per)]
        sums += [top[:, h * tile : (h + 1) * tile] for h in range(per)]
        if g < kv_heads - 1:
            for r in range(blocks // 2):
                line.step((i - 1) * blocks + r)
    attended = jnp.concatenate(outs, axis=0).T.astype(jnp.bfloat16)
    out_ref[...] = attended
    lse_ref[...] = jnp.concatenate(sums, axis=0)
    term = contract_last(attended, wo_ref[...]).astype(jnp.bfloat16)
    for r in range(blocks):
        part[i * blocks + r] = term[r * cut : (r + 1) * cut]

    line.start(i * blocks, blocks)
    for r in range(blocks // 2, blocks):
        line.step((i - 1) * blocks + r)

    @pl.when(i == pl.num_programs(0) - 1)
    def _():
        @pl.loop(0, blocks)
        def _(r):
            line.step(i * blocks + r)

        line.drain()

        @pl.loop(0, line.blocks)
        def _(b):
            norm_out(b).wait()


def attend(q_t, prompt_all, kvt_cont, bias, packed_full, x, gains, q_heads, kv_heads, cid):
    dim = HEAD_SIZE
    count, kv2, prompt_rows, cont_rows, chunk = attend_shape(prompt_all, kvt_cont)
    q_cols, rows = q_t.shape
    width = packed_full.shape[0]
    keys_all = bias.shape[0]
    tile, cut = 128, 16
    whole = pl.BlockSpec(memory_space=pltpu.VMEM)
    by_col = lambda i: (0, i)
    return pl.pallas_call(
        functools.partial(
            attend_kernel,
            (count, prompt_rows, chunk),
            dim,
            kv_heads,
            q_heads // kv_heads,
            tile,
            cut,
        ),
        grid=(rows // tile,),
        in_specs=[
            pl.BlockSpec((q_cols, tile), by_col),
            whole,
            whole,
            pl.BlockSpec((keys_all, tile), by_col),
            pl.BlockSpec((width, q_cols), lambda i: (0, 0), pipeline_mode=pl.Buffered(1)),
            whole,
            whole,
        ],
        out_specs=[
            pl.BlockSpec((tile, q_cols), lambda i: (i, 0)),
            pl.BlockSpec((q_heads, tile), by_col),
            pl.BlockSpec(memory_space=pl.ANY),
            pl.BlockSpec(memory_space=pl.ANY),
        ],
        out_shape=[
            jax.ShapeDtypeStruct((rows, q_cols), jnp.bfloat16),
            jax.ShapeDtypeStruct((q_heads, rows), jnp.float32),
            jax.ShapeDtypeStruct((rows, width), jnp.bfloat16),
            jax.ShapeDtypeStruct((rows, width), jnp.bfloat16),
        ],
        scratch_shapes=[
            pltpu.VMEM((kv_heads, keys_all, dim), jnp.bfloat16),
            pltpu.VMEM((keys_all // chunk, kv2, chunk), jnp.bfloat16),
            pltpu.VMEM((rows // cut, cut, width), jnp.bfloat16),
            pltpu.SemaphoreType.DMA((rows // cut,)),
            *line_scratch((rows // cut, cut, width)),
        ],
        compiler_params=pltpu.CompilerParams(
            collective_id=cid, has_side_effects=True, vmem_limit_bytes=56 << 20
        ),
        cost_estimate=pl.CostEstimate(
            flops=120_000_000_000, bytes_accessed=40 << 20, transcendentals=0
        ),
    )(q_t, prompt_all, kvt_cont, bias, packed_full, x, gains)


def feed_back_kernel(
    cut,
    hidden_in,
    gate_in,
    up_in,
    normed_late,
    cot_late,
    fd_ref,
    fg_ref,
    fu_ref,
    wd_ref,
    wg_ref,
    wu_ref,
    cot_ref,
    normed_ref,
    grads_ref,
    up_grads_ref,
    mlp_ref,
    sum_ref,
    hidden,
    gate,
    up,
    late_sems,
    part,
    recv,
    out,
    sems,
    sink_sems,
):
    i = pl.program_id(0)
    rows, wide = gate.shape
    first = hidden_in.shape[0]
    tiles = sum_ref.shape[1] // SIZE
    feeds = wide // SIZE
    low, high = first // cut, (rows - first) // cut
    split = tiles * low

    def place(b):
        early = b < split
        c = b - split
        row = jnp.where(early, lax.rem(b, low), low + lax.rem(c, high))
        return row, jnp.where(early, lax.div(b, low), lax.div(c, high))

    line = Line(part, recv, out, sum_ref, sems, sink_sems, place=place)

    def loads():
        return [
            pltpu.make_async_copy(source, target.at[pl.ds(0, first)], late_sems.at[k])
            for k, (source, target) in enumerate(((gate_in, gate), (up_in, up), (hidden_in, hidden)))
        ]

    def produce(at, block, count):
        back = contract_last(gate[at, :], wg_ref[...]) + contract_last(up[at, :], wu_ref[...])
        back = back.astype(jnp.bfloat16)
        for r in range(count):
            part[block + r] = back[r * cut : (r + 1) * cut]
        line.start(block, count)

    def steps(start, stop):
        @pl.loop(start, stop)
        def _(t):
            line.step(t)

    @pl.when(i == 0)
    def _():
        for load in loads():
            load.start()
        line.greet()
        for load in loads():
            load.wait()

    @pl.when(i < tiles)
    def _():
        produce(slice(0, first), i * low, low)

    beside = min(split, FEED_STEPS)

    @pl.when((i >= tiles) & (i < tiles + feeds))
    def _():
        m = i - tiles
        here = pl.ds(pl.multiple_of(m * SIZE, SIZE), SIZE)
        hidden[first:, here], gate[first:, here], up[first:, here] = feed_tile(
            normed_late[...], cot_late[...], fd_ref[...], fg_ref[...], fu_ref[...]
        )
        steps(lax.div(m * beside, feeds), lax.div((m + 1) * beside, feeds))

    @pl.when(i >= tiles + feeds)
    def _():
        n = i - tiles - feeds
        produce(slice(first, rows), split + n * high, high)
        rest = line.blocks - beside
        spots = 4

        def step(k):
            start = beside + lax.div((n * spots + k) * rest, tiles * spots)
            steps(start, beside + lax.div((n * spots + k + 1) * rest, tiles * spots))

        step(0)
        grads_ref[:, :wide] = contract_first(cot_ref[...], hidden[...]).astype(jnp.bfloat16)
        step(1)
        grads_ref[:, wide:] = contract_first(normed_ref[...], gate[...]).astype(jnp.bfloat16)
        step(2)
        up_grads_ref[...] = contract_first(normed_ref[...], up[...]).astype(jnp.bfloat16)
        step(3)
        mlp_ref[0] = contract_last(hidden[...], wd_ref[...]).astype(jnp.bfloat16)

        @pl.when(n == tiles - 1)
        def _():
            line.drain()


def feed_back(hidden, grad_gate, grad_up, mlp_full, cot, normed, cid):
    first, wide = hidden.shape
    rows, width = cot.shape
    cut = math.gcd(math.gcd(rows, first), SIZE)
    tiles, feeds = width // SIZE, wide // SIZE
    blocks = (tiles * rows // cut, cut, SIZE)
    anywhere = pl.BlockSpec(memory_space=pltpu.HBM)
    second = lambda i: (first // (rows - first), 0)
    late = lambda i: jnp.maximum(i - tiles - feeds, 0)
    back = lambda i: jnp.where(i < tiles, i, late(i))
    ahead = lambda i: jnp.clip(i - tiles, 0, feeds - 1)
    return pl.pallas_call(
        functools.partial(feed_back_kernel, cut),
        grid=(2 * tiles + feeds,),
        in_specs=[anywhere] * 3
        + [pl.BlockSpec((rows - first, width), second, pipeline_mode=pl.Buffered(1))] * 2
        + [pl.BlockSpec((width, SIZE), lambda i, k=k: (0, k * feeds + ahead(i))) for k in range(3)]
        + [pl.BlockSpec((SIZE, wide), lambda i: (late(i), 0))]
        + [pl.BlockSpec((SIZE, wide), lambda i, k=k: (back(i), k)) for k in (1, 2)]
        + [pl.BlockSpec((rows, SIZE), lambda i: (0, late(i)))] * 2,
        out_specs=[
            pl.BlockSpec((SIZE, 2 * wide), lambda i: (late(i), 0)),
            pl.BlockSpec((SIZE, wide), lambda i: (late(i), 0)),
            pl.BlockSpec((1, rows, SIZE), lambda i: (late(i), 0, 0)),
            pl.BlockSpec(memory_space=pl.ANY),
        ],
        out_shape=[
            jax.ShapeDtypeStruct((width, 2 * wide), jnp.bfloat16),
            jax.ShapeDtypeStruct((width, wide), jnp.bfloat16),
            jax.ShapeDtypeStruct((tiles, rows, SIZE), jnp.bfloat16),
            jax.ShapeDtypeStruct((rows, width), jnp.bfloat16),
        ],
        scratch_shapes=[
            pltpu.VMEM((rows, wide), jnp.bfloat16),
            pltpu.VMEM((rows, wide), jnp.bfloat16),
            pltpu.VMEM((rows, wide), jnp.bfloat16),
            pltpu.SemaphoreType.DMA((3,)),
            *line_scratch(blocks),
        ],
        compiler_params=pltpu.CompilerParams(
            collective_id=cid, has_side_effects=True, vmem_limit_bytes=61 << 20
        ),
        cost_estimate=pl.CostEstimate(
            flops=12 * rows * wide * width, bytes_accessed=200 << 20, transcendentals=0
        ),
    )(
        hidden,
        grad_gate,
        grad_up,
        normed,
        cot,
        mlp_full,
        mlp_full,
        mlp_full,
        mlp_full,
        mlp_full,
        mlp_full,
        cot,
        normed,
    )


def window_kernel(
    shape,
    dim,
    kv_heads,
    per,
    tile,
    q_ref,
    all_ref,
    cont_ref,
    bias_ref,
    out_ref,
    lse_ref,
    back_ref,
    cot_ref,
    x_ref,
    attn_ref,
    gain_ref,
    wo_ref,
    cos_ref,
    sin_ref,
    cos_own_ref,
    sin_own_ref,
    normed_ref,
    att_ref,
    up_grads_ref,
    mlp_ref,
    gq_out_ref,
    gkv_ref,
    gm_ref,
    grads_ref,
    sum_ref,
    keys,
    values,
    chunks,
    gk,
    gv,
    gm,
    gq_ref,
    send_ref,
    got,
    own_ref,
    kv_sems,
    part,
    recv,
    out,
    sems,
    sink_sems,
):
    count, prompt_rows, chunk = shape
    i = pl.program_id(0)
    line = Line(part, recv, out, sum_ref, sems, sink_sems)
    context = lax.axis_index("context")
    prompt_tiles = prompt_rows // tile
    tiles = gq_ref.shape[0] // tile
    slots = SLOTS
    spots = 2 + kv_heads

    def step(k):
        for s in range(k * slots // spots, (k + 1) * slots // spots):
            line.step(i * slots + s)

    def send(k):
        peer = lax.rem(context + k, count)
        return pltpu.make_async_remote_copy(
            send_ref.at[peer],
            got.at[k],
            kv_sems.at[0, k],
            kv_sems.at[1, k],
            device_id={"context": peer},
            device_id_type=MESH,
        )

    root = dim ** (-0.5)
    half = dim // 2

    @pl.when(i == 0)
    def _():
        load = pltpu.make_async_copy(mlp_ref, part, sink_sems.at[0])
        load.start()
        fill_keys(chunk, dim, kv_heads, all_ref, cont_ref, [keys, values], chunks)
        gk[...] = jnp.zeros_like(gk)
        gv[...] = jnp.zeros_like(gv)
        line.greet("context", count)
        load.wait()
        line.start(0, line.blocks)

    @pl.when(i < tiles)
    def _():
        middle = x_ref[...].astype(jnp.float32) + attn_ref[...].astype(jnp.float32)
        inverse = lax.rsqrt(jnp.mean(middle * middle, axis=-1, keepdims=True) + EPS)
        unit = middle * inverse
        grad_unit = back_ref[...].astype(jnp.float32) * gain_ref[...]
        grad_middle = cot_ref[...].astype(jnp.float32) + norm_back(grad_unit, unit, inverse)
        gm_ref[...] = grad_middle.astype(jnp.bfloat16)
        grad_b = grad_middle.astype(jnp.bfloat16)
        step(0)
        grad_t = (
            jnp.dot(grad_b, wo_ref[...], preferred_element_type=jnp.float32).astype(jnp.bfloat16)
        ).astype(jnp.float32).T
        gm[pl.ds(pl.multiple_of(i * tile, tile), tile), :] = grad_b
        step(1)

        is_prompt, n_prompt, base, n_own = trip_count(tile, chunk, i, prompt_rows, count)
        factor = root * LOG2E
        prod = grad_t * out_ref[...].astype(jnp.float32).T
        grad_t = grad_t.astype(jnp.bfloat16)
        cosine, sine = cos_ref[...], sin_ref[...]
        pieces = []
        for g in range(kv_heads):
            heads = [g * per + h for h in range(per)]
            q = jnp.concatenate([q_ref[h * dim : (h + 1) * dim, :] for h in heads], axis=1)
            grad = jnp.concatenate([grad_t[h * dim : (h + 1) * dim] for h in heads], axis=1)
            inner = jnp.concatenate(
                [jnp.sum(prod[h * dim : (h + 1) * dim], axis=0, keepdims=True) for h in heads], axis=1
            )
            lse = jnp.concatenate([lse_ref[h : h + 1, :] for h in heads], axis=1)

            def body(c, acc):
                at = pl.ds(pl.multiple_of(c * chunk, chunk), chunk)
                s = jnp.dot(keys[g, at, :], q, preferred_element_type=jnp.float32)
                b = bias_ref[at, :].astype(jnp.float32)
                p = jnp.exp2(s * factor + (jnp.concatenate([b] * per, axis=1) - lse))
                dp = jnp.dot(values[g, at, :], grad, preferred_element_type=jnp.float32)
                ds = (p * (dp - inner)).astype(jnp.bfloat16)
                gv[g, at, :] += contract_last(p.astype(jnp.bfloat16), grad)
                gk[g, at, :] += contract_last(ds, q)
                k_t = chunks[c, g * dim : (g + 1) * dim, :]
                return acc + jnp.dot(k_t, ds, preferred_element_type=jnp.float32)

            acc = jnp.zeros((dim, per * tile), jnp.float32)
            acc = lax.fori_loop(0, jnp.where(is_prompt, n_prompt, base), body, acc)
            acc = lax.fori_loop(base, base + jnp.where(is_prompt, 0, n_own), body, acc)
            acc = acc * root
            for h in range(per):
                first = acc[:half, h * tile : (h + 1) * tile]
                second = acc[half:, h * tile : (h + 1) * tile]
                pieces += [first * cosine + second * sine, second * cosine - first * sine]
            step(2 + g)
        rows_q = jnp.concatenate(pieces, axis=0).T.astype(jnp.bfloat16)
        gq_ref[pl.ds(pl.multiple_of(i * tile, tile), tile), :] = rows_q
        gq_out_ref[...] = rows_q

    @pl.when(i == tiles - 1)
    def _():
        for g in range(kv_heads):
            for n, (acc, scale) in enumerate(((gk, root), (gv, 1.0))):
                at = (n * kv_heads + g) * dim
                for c in range(count):
                    rows = acc[g, c * prompt_rows : (c + 1) * prompt_rows, :]
                    send_ref[c, at : at + dim, :] = (rows * scale).T.astype(jnp.bfloat16)
                own_ref[at : at + dim, :] = (acc[g, count * prompt_rows :, :] * scale).T
        for k in range(1, count):
            send(k).start()

    @pl.when(i == tiles)
    def _():
        line.step(tiles * slots)
        kv_dim = kv_heads * dim

        def finish(flat, cosine, sine):
            pieces = []
            for at in range(0, kv_dim, dim):
                first, second = flat[at : at + half], flat[at + half : at + dim]
                pieces += [first * cosine + second * sine, second * cosine - first * sine]
            pieces.append(flat[kv_dim:])
            return jnp.concatenate(pieces, axis=0).T.astype(jnp.bfloat16)

        cosine, sine = cos_own_ref[...], sin_own_ref[...]
        gkv_ref[prompt_rows:, :] = finish(
            own_ref[...], cosine[:, prompt_rows:], sine[:, prompt_rows:]
        )
        total = send_ref[context].astype(jnp.float32)
        for k in range(1, count):
            send(k).wait()
            total += got[k].astype(jnp.float32)
        gkv_ref[:prompt_rows, :] = finish(
            total, cosine[:, :prompt_rows], sine[:, :prompt_rows]
        )

    @pl.when(i >= tiles)
    def _():
        n = i - tiles
        later = pl.num_programs(0) - tiles
        rest = line.blocks - tiles * slots - 1
        q_cols = gq_ref.shape[1]
        wide = up_grads_ref.shape[1]
        here = pl.ds(pl.multiple_of(n * SIZE, SIZE), SIZE)
        grads_ref[:, :wide] = up_grads_ref[...]
        grads_ref[:, wide : wide + q_cols] = contract_first(gm[:, here], att_ref[...]).astype(
            jnp.bfloat16
        )
        grads_ref[:, wide + q_cols : wide + 2 * q_cols] = contract_first(
            normed_ref[...], gq_ref[...]
        ).astype(jnp.bfloat16)
        grads_ref[:, wide + 2 * q_cols :] = contract_first(normed_ref[...], gkv_ref[...]).astype(
            jnp.bfloat16
        )
        low = tiles * slots + 1 + lax.div(n * rest, later)
        high = tiles * slots + 1 + lax.div((n + 1) * rest, later)

        @pl.loop(low, high)
        def _(t):
            line.step(t)

        @pl.when(n == later - 1)
        def _():
            line.drain()


def window(
    q_t,
    prompt_all,
    kvt_cont,
    bias,
    attended,
    lse,
    back,
    cot,
    x,
    attn_sum,
    gain,
    packed_full,
    cos_t,
    sin_t,
    normed,
    up_grads,
    mlp_part,
    q_heads,
    kv_heads,
    cid,
):
    dim = HEAD_SIZE
    count, kv2, prompt_rows, cont_rows, chunk = attend_shape(prompt_all, kvt_cont)
    rows, width = cot.shape
    q_cols = q_heads * dim
    keys_all = bias.shape[0]
    tile = 128
    whole = pl.BlockSpec(memory_space=pltpu.VMEM)
    anywhere = pl.BlockSpec(memory_space=pl.ANY)
    tiles, later = rows // tile, width // SIZE
    grad_cols = up_grads.shape[1] + 2 * q_cols + kv2
    early = lambda i: jnp.minimum(i, tiles - 1)
    late = lambda i: jnp.maximum(i - tiles, 0)
    by_col = lambda i: (0, early(i))
    by_row = lambda i: (early(i), 0)
    fixed = lambda i: (0, 0)
    return pl.pallas_call(
        functools.partial(
            window_kernel, (count, prompt_rows, chunk), dim, kv_heads, q_heads // kv_heads, tile
        ),
        grid=(tiles + later,),
        in_specs=[
            pl.BlockSpec((q_cols, tile), by_col),
            whole,
            whole,
            pl.BlockSpec((keys_all, tile), by_col),
            pl.BlockSpec((tile, q_cols), by_row),
            pl.BlockSpec((q_heads, tile), by_col),
            pl.BlockSpec((tile, width), by_row),
            pl.BlockSpec((tile, width), by_row),
            pl.BlockSpec((tile, width), by_row),
            pl.BlockSpec((tile, width), by_row),
            pl.BlockSpec((1, width), fixed),
            pl.BlockSpec((width, q_cols), fixed, pipeline_mode=pl.Buffered(1)),
            pl.BlockSpec((dim // 2, tile), by_col),
            pl.BlockSpec((dim // 2, tile), by_col),
            whole,
            whole,
            pl.BlockSpec((rows, SIZE), lambda i: (0, late(i))),
            whole,
            pl.BlockSpec((SIZE, up_grads.shape[1]), lambda i: (late(i), 0)),
            anywhere,
        ],
        out_specs=[
            pl.BlockSpec((tile, q_cols), by_row),
            pl.BlockSpec((rows, kv2), fixed),
            pl.BlockSpec((tile, width), by_row),
            pl.BlockSpec((SIZE, grad_cols), lambda i: (late(i), 0)),
            anywhere,
        ],
        out_shape=[
            jax.ShapeDtypeStruct((rows, q_cols), jnp.bfloat16),
            jax.ShapeDtypeStruct((rows, kv2), jnp.bfloat16),
            jax.ShapeDtypeStruct((rows, width), jnp.bfloat16),
            jax.ShapeDtypeStruct((width, grad_cols), jnp.bfloat16),
            jax.ShapeDtypeStruct((rows, width), jnp.bfloat16),
        ],
        scratch_shapes=[
            pltpu.VMEM((kv_heads, keys_all, dim), jnp.bfloat16),
            pltpu.VMEM((kv_heads, keys_all, dim), jnp.bfloat16),
            pltpu.VMEM((keys_all // chunk, kv2, chunk), jnp.bfloat16),
            pltpu.VMEM((kv_heads, keys_all, dim), jnp.float32),
            pltpu.VMEM((kv_heads, keys_all, dim), jnp.float32),
            pltpu.VMEM((rows, width), jnp.bfloat16),
            pltpu.VMEM((rows, q_cols), jnp.bfloat16),
            pltpu.VMEM((count, kv2, prompt_rows), jnp.bfloat16),
            pltpu.VMEM((count, kv2, prompt_rows), jnp.bfloat16),
            pltpu.VMEM((kv2, cont_rows), jnp.float32),
            pltpu.SemaphoreType.DMA((2, count)),
            *line_scratch(mlp_part.shape),
        ],
        compiler_params=pltpu.CompilerParams(
            collective_id=cid, has_side_effects=True, vmem_limit_bytes=60 << 20
        ),
        cost_estimate=pl.CostEstimate(
            flops=120_000_000_000, bytes_accessed=200 << 20, transcendentals=0
        ),
    )(
        q_t,
        prompt_all,
        kvt_cont,
        bias,
        attended,
        lse,
        back,
        cot,
        x,
        attn_sum,
        gain,
        packed_full,
        cos_t,
        sin_t,
        cos_t,
        sin_t,
        normed,
        attended,
        up_grads,
        mlp_part,
    )


def product_kernel(cut, spans, lhs_refs, w_ref, sum_ref, part, recv, out, sems, sink_sems):
    n = pl.program_id(0)
    per = sum_ref.shape[0] // cut
    line = Line(part, recv, out, sum_ref, sems, sink_sems)
    term = sum(
        contract_last(ref[...], w_ref[:, low:high]) for ref, (low, high) in zip(lhs_refs, spans)
    ).astype(jnp.bfloat16)
    for r in range(per):
        part[n * per + r] = term[r * cut : (r + 1) * cut]

    @pl.when(n == 0)
    def _():
        line.greet()

    line.start(n * per, per)
    for r in range(per):
        line.step(n * per + r)

    @pl.when(n == pl.num_programs(0) - 1)
    def _():
        line.drain()


def product_sum(lhs, spans, weights, cid):
    rows = lhs[0].shape[0]
    width, cols = weights.shape
    cut = math.gcd(rows, 128)
    tiles = width // SIZE
    blocks = (tiles * rows // cut, cut, SIZE)

    def body(*refs):
        product_kernel(cut, spans, refs[: len(lhs)], *refs[len(lhs) :])

    return pl.pallas_call(
        body,
        grid=(tiles,),
        in_specs=[pl.BlockSpec(memory_space=pltpu.VMEM)] * len(lhs)
        + [pl.BlockSpec((SIZE, cols), lambda n: (n, 0))],
        out_specs=pl.BlockSpec(memory_space=pl.ANY),
        out_shape=jax.ShapeDtypeStruct((rows, width), jnp.bfloat16),
        scratch_shapes=line_scratch(blocks),
        compiler_params=pltpu.CompilerParams(
            collective_id=cid, has_side_effects=True, vmem_limit_bytes=40 << 20
        ),
        cost_estimate=pl.CostEstimate(
            flops=120_000_000_000, bytes_accessed=40 << 20, transcendentals=0
        ),
    )(*lhs, weights)


def feed_tile(normed, cot, wd, wg, wu):
    gate = jnp.dot(normed, wg, preferred_element_type=jnp.float32)
    up = jnp.dot(normed, wu, preferred_element_type=jnp.float32)
    grad_hidden = jnp.dot(cot, wd, preferred_element_type=jnp.float32)
    sigmoid = 1.0 / (1.0 + jnp.exp(-gate))
    silu = gate * sigmoid
    return (
        (silu * up).astype(jnp.bfloat16),
        (grad_hidden * up * sigmoid * (1.0 + gate * (1.0 - sigmoid))).astype(jnp.bfloat16),
        (grad_hidden * silu).astype(jnp.bfloat16),
    )


def feed_kernel(normed_ref, cot_ref, wd_ref, wg_ref, wu_ref, hidden_ref, gate_ref, up_ref):
    hidden_ref[...], gate_ref[...], up_ref[...] = feed_tile(
        normed_ref[...], cot_ref[...], wd_ref[...], wg_ref[...], wu_ref[...]
    )


def feed(normed, cot, mlp_full, rows):
    width = cot.shape[1]
    wide = mlp_full.shape[1] // 3
    tiles = wide // SIZE
    tile = pl.BlockSpec((rows, SIZE), lambda n: (0, n))
    return pl.pallas_call(
        feed_kernel,
        grid=(tiles,),
        in_specs=[pl.BlockSpec((rows, width), lambda n: (0, 0), pipeline_mode=pl.Buffered(1))] * 2
        + [pl.BlockSpec((width, SIZE), lambda n, k=k: (0, k * tiles + n)) for k in range(3)],
        out_specs=[
            tile,
            tile,
            tile,
        ],
        out_shape=[jax.ShapeDtypeStruct((rows, wide), jnp.bfloat16)] * 3,
        compiler_params=pltpu.CompilerParams(vmem_limit_bytes=58 << 20),
        cost_estimate=pl.CostEstimate(
            flops=6 * rows * width * wide, bytes_accessed=60 << 20, transcendentals=rows * wide
        ),
    )(normed, cot, mlp_full, mlp_full, mlp_full)


def finish_kernel(
    prompt_tiles, x_ref, attn_ref, mlp_ref, gm_ref, back_ref, gain_ref, po_ref, co_ref, pg_ref, cg_ref
):
    i = pl.program_id(0)
    x = x_ref[...].astype(jnp.float32)
    result = (x + attn_ref[...].astype(jnp.float32)) + mlp_ref[...].astype(jnp.float32)
    result = result.astype(jnp.bfloat16)
    unit, inverse = normalize(x)
    grad = gm_ref[...].astype(jnp.float32) + norm_back(back_ref[...].astype(jnp.float32) * gain_ref[...], unit, inverse)

    @pl.when(i < prompt_tiles)
    def _():
        po_ref[...] = result
        pg_ref[...] = grad

    @pl.when(i >= prompt_tiles)
    def _():
        co_ref[...] = result
        cg_ref[...] = grad


def finish(x, attn_sum, mlp_sum, grad_middle, back, gain, prompt_rows):
    rows, width = x.shape
    tile = 128
    prompt_tiles = prompt_rows // tile
    every = pl.BlockSpec((tile, width), lambda i: (i, 0))
    first = pl.BlockSpec((tile, width), lambda i: (jnp.minimum(i, prompt_tiles - 1), 0))
    second = pl.BlockSpec((tile, width), lambda i: (jnp.maximum(i - prompt_tiles, 0), 0))
    shapes = [(prompt_rows, width), (rows - prompt_rows, width)]
    return pl.pallas_call(
        functools.partial(finish_kernel, prompt_tiles),
        grid=(rows // tile,),
        in_specs=[every] * 5 + [pl.BlockSpec((1, width), lambda i: (0, 0))],
        out_specs=[first, second, first, second],
        out_shape=[jax.ShapeDtypeStruct(shape, jnp.bfloat16) for shape in shapes]
        + [jax.ShapeDtypeStruct(shape, jnp.float32) for shape in shapes],
        compiler_params=pltpu.CompilerParams(vmem_limit_bytes=40 << 20),
        cost_estimate=pl.CostEstimate(
            flops=20 * x.size, bytes_accessed=20 * x.size, transcendentals=0
        ),
    )(x, attn_sum, mlp_sum, grad_middle, back, gain)


def per_device(
    prompt_x,
    cont_x,
    prompt_len,
    cont_seg,
    attn_gain,
    q_weight,
    key_matrix,
    value_matrix,
    o_weight,
    mlp_gain,
    gate_weight,
    up_weight,
    down_weight,
    prompt_cot,
    cont_cot,
):
    head_dim = HEAD_SIZE
    data = ("dp", "context")
    prompt_rows = prompt_x.shape[0]
    cont_rows = cont_x.shape[0]
    prompt_total = prompt_rows * lax.axis_size("context")
    q_cols = q_weight.shape[1]
    kv_cols = key_matrix.shape[1]
    q_heads = q_cols // head_dim
    kv_heads = kv_cols // head_dim
    qkv_cols = q_cols + 2 * kv_cols
    qkv_wide = qkv_cols + 2 + -(qkv_cols + 2) % 128
    hidden_cols = gate_weight.shape[1]
    wide = hidden_cols + -hidden_cols % 256
    context_pos = lax.axis_index("context")
    prompt_pos = context_pos * prompt_rows + jnp.arange(prompt_rows, dtype=jnp.int32)
    segment = cont_seg[0]
    earlier = jnp.sum((segment[None, :] < segment[:, None]).astype(jnp.int32), axis=1)
    local_index = jnp.arange(cont_rows, dtype=jnp.int32)
    length = prompt_len[0]
    cont_pos = length + local_index - earlier
    position = jnp.concatenate([prompt_pos, cont_pos]).astype(jnp.float32)
    inv_freq = THETA ** (-jnp.arange(head_dim // 2, dtype=jnp.float32) * 2.0 / head_dim)
    angle_table = inv_freq[:, None] * position[None, :]
    cosine = jnp.cos(angle_table)
    sine_table = jnp.sin(angle_table)
    shards = (down_weight, gate_weight, up_weight)
    attn_shards = (o_weight, q_weight, key_matrix, value_matrix)
    if lax.axis_size("dp") == 4 and lax.axis_size("context") == 2:
        info = jnp.stack([earlier, jnp.broadcast_to(length, earlier.shape)])
        packed_full, mlp_shard, x_all, grad_out, bias = plane_gather(
            attn_shards,
            (attn_gain, mlp_gain),
            info,
            shards,
            wide,
            q_cols + qkv_wide,
            prompt_x,
            cont_x,
            prompt_cot,
            cont_cot,
            6,
        )
    else:
        packed = jnp.concatenate([*attn_shards, attn_gain[:, None], mlp_gain[:, None]], axis=1)
        packed = jnp.pad(packed, ((0, 0), (0, q_cols + qkv_wide - packed.shape[1])))
        packed_full = lax.all_gather(packed, data, axis=0, tiled=True)
        fill = ((0, 0), (0, wide - hidden_cols))
        mlp_shard = jnp.concatenate([jnp.pad(w, fill) for w in shards], axis=1)
        x_all = jnp.concatenate([prompt_x, cont_x], axis=0)
        grad_out = jnp.concatenate([prompt_cot, cont_cot], axis=0)
        key_index = jnp.arange(prompt_total, dtype=jnp.int32)
        prompt_mask = jnp.concatenate(
            [
                key_index[:, None] <= prompt_pos[None, :],
                jnp.zeros((cont_rows, prompt_rows), jnp.bool_),
            ],
            axis=0,
        )
        own_mask = (segment[:, None] == segment[None, :]) & (
            local_index[:, None] <= local_index[None, :]
        )
        reach_mask = jnp.broadcast_to(key_index[:, None] < length, (prompt_total, cont_rows))
        allowed = jnp.concatenate(
            [prompt_mask, jnp.concatenate([reach_mask, own_mask], axis=0)], axis=1
        )
        bias = jnp.where(allowed, 0.0, NEGATIVE).astype(jnp.bfloat16)
    first_normed, q_t, cont_kv, gains, prompt_all = project_rope(
        x_all, packed_full, cosine, sine_table, q_heads, kv_heads, prompt_rows, 4
    )
    gain_one, gain_two = gains[0:1], gains[1:2]
    prompt_all, mlp_shard = lax.optimization_barrier((prompt_all, mlp_shard))
    mlp_full = lax.all_gather(mlp_shard, data, axis=0, tiled=True)
    attn_out, lse, attn_sum, normed_two = attend(
        q_t, prompt_all, cont_kv, bias, packed_full, x_all, gains, q_heads, kv_heads, 0
    )
    rows = prompt_rows + cont_rows
    early_rows = rows // 2 if rows % 1024 == 0 else rows - rows // 5
    hidden, grad_gate, grad_up = feed(normed_two, grad_out, mlp_full, early_rows)
    mlp_grads, up_grads, mlp_part, back_two = feed_back(
        hidden, grad_gate, grad_up, mlp_full, grad_out, normed_two, 1
    )

    def scatter(values):
        return lax.psum_scatter(values, data, scatter_dimension=0, tiled=True).astype(jnp.float32)

    cut = math.gcd(prompt_rows + cont_rows, SIZE)
    grad_q, grad_kv, grad_middle, grad_rest, mlp_sum = window(
        q_t,
        prompt_all,
        cont_kv,
        bias,
        attn_out,
        lse,
        back_two,
        grad_out,
        x_all,
        attn_sum,
        gain_two,
        packed_full,
        cosine,
        sine_table,
        first_normed,
        up_grads,
        mlp_part.reshape(-1, cut, SIZE),
        q_heads,
        kv_heads,
        3,
    )
    mlp_own = scatter(mlp_grads)
    grad_q, grad_rest, mlp_own = lax.optimization_barrier((grad_q, grad_rest, mlp_own))
    back_one = product_sum(
        [grad_q, grad_kv], [(q_cols, 2 * q_cols), (2 * q_cols, q_cols + qkv_cols)], packed_full, 2
    )
    back_one, mlp_own = lax.optimization_barrier((back_one, mlp_own))
    outs = finish(x_all, attn_sum, mlp_sum, grad_middle, back_one, gain_one, prompt_rows)
    down_own = mlp_own[:, :hidden_cols]
    gate_own = mlp_own[:, wide : wide + hidden_cols]
    rest_own = scatter(grad_rest)
    up_own = rest_own[:, :hidden_cols]
    o_own = rest_own[:, wide : wide + q_cols]
    q_own = rest_own[:, wide + q_cols : wide + 2 * q_cols]
    k_own = rest_own[:, wide + 2 * q_cols : wide + 2 * q_cols + kv_cols]
    v_own = rest_own[:, wide + 2 * q_cols + kv_cols :]

    def row_dot(weight, grad):
        return jnp.sum(weight.astype(jnp.float32) * grad, axis=1)

    gain_rows = jnp.stack(
        [
            (row_dot(q_weight, q_own) + row_dot(key_matrix, k_own) + row_dot(value_matrix, v_own))
            / attn_gain.astype(jnp.float32),
            (row_dot(gate_weight, gate_own) + row_dot(up_weight, up_own))
            / mlp_gain.astype(jnp.float32),
        ]
    )
    gain_rows = tensor_total(gain_rows, 5)
    owned = (gain_rows[0], q_own, k_own, v_own, o_own, gain_rows[1], gate_own, up_own, down_own)
    return (*outs, *owned)


def solution(mesh):
    in_specs = (
        P(("dp", "context"), None),
        P(("dp", "context"), None),
        P("dp"),
        P(("dp", "context"), None),
        P(("dp", "context")),
        P(("dp", "context"), "tensor"),
        P(("dp", "context"), "tensor"),
        P(("dp", "context"), "tensor"),
        P(("dp", "context"), "tensor"),
        P(("dp", "context")),
        P(("dp", "context"), "tensor"),
        P(("dp", "context"), "tensor"),
        P(("dp", "context"), "tensor"),
        P(("dp", "context"), None),
        P(("dp", "context"), None),
    )
    out_specs = (
        P(("dp", "context"), None),
        P(("dp", "context"), None),
        P(("dp", "context"), None),
        P(("dp", "context"), None),
        P(("dp", "context")),
        P(("dp", "context"), "tensor"),
        P(("dp", "context"), "tensor"),
        P(("dp", "context"), "tensor"),
        P(("dp", "context"), "tensor"),
        P(("dp", "context")),
        P(("dp", "context"), "tensor"),
        P(("dp", "context"), "tensor"),
        P(("dp", "context"), "tensor"),
    )
    return jax.shard_map(
        per_device, mesh=mesh, in_specs=in_specs, out_specs=out_specs, check_vma=False
    )
```

```python
import functools
import math

import jax
import jax.numpy as jnp
from jax import lax
from jax.experimental import pallas as pl
from jax.experimental.pallas import tpu as pltpu
from jax.sharding import PartitionSpec as P

HEAD_SIZE = 80


EPS = 1e-05
THETA = 10000.0
NEGATIVE = -1e30
LOG2E = math.log2(math.e)
MESH = pl.DeviceIdType.MESH
AXIS = "tensor"
LAG = 3
SIZE = 256
FEED_STEPS = 10
SLOTS = 7


def normalize(values):
    inverse = lax.rsqrt(jnp.mean(values * values, axis=-1, keepdims=True) + EPS)
    return (values * inverse, inverse)


def norm_back(grad_unit, unit_rows, inverse):
    inner_sum = jnp.mean(grad_unit * unit_rows, axis=-1, keepdims=True)
    return inverse * (grad_unit - unit_rows * inner_sum)


def contract_last(left_side, right_side):
    return lax.dot_general(
        left_side, right_side, (((1,), (1,)), ((), ())), preferred_element_type=jnp.float32
    )


def contract_first(left_side, right_side):
    return lax.dot_general(
        left_side, right_side, (((0,), (0,)), ((), ())), preferred_element_type=jnp.float32
    )


def greet(axis, count):
    me = lax.axis_index(axis)
    barrier = pltpu.get_barrier_semaphore()
    for k in range(1, count):
        peer = lax.rem(me + k, count)
        pl.semaphore_signal(barrier, inc=1, device_id={axis: peer}, device_id_type=MESH)
    pl.semaphore_wait(barrier, count - 1)


def rope_kernel(
    q_heads,
    kv_heads,
    dim,
    prompt_steps,
    x_ref,
    w_ref,
    cos_ref,
    sin_ref,
    normed_ref,
    qt_ref,
    kvt_ref,
    gains_ref,
    all_ref,
    own,
    send,
    recv,
    local,
):
    i = pl.program_id(0)
    count = all_ref.shape[0]
    me = lax.axis_index("context")
    last = (q_heads + 2 * kv_heads + q_heads) * dim

    @pl.when(i == 0)
    def _():
        greet("context", count)
        low = last - last % 128
        turned = w_ref[:, low:].astype(jnp.float32).T
        gains_ref[...] = turned[last - low : last - low + 8]

    rows = x_ref[...].astype(jnp.float32)
    inverse = lax.rsqrt(jnp.mean(rows * rows, axis=-1, keepdims=True) + EPS)
    normed = (rows * inverse * gains_ref[0:1, :]).astype(jnp.bfloat16)
    normed_ref[...] = normed
    flat = jnp.dot(
        normed, w_ref[:, q_heads * dim :], preferred_element_type=jnp.float32
    ).T
    cosine, sine = cos_ref[...], sin_ref[...]
    half = dim // 2
    pieces = []
    for head in range(q_heads + kv_heads):
        first = flat[head * dim : head * dim + half]
        second = flat[head * dim + half : (head + 1) * dim]
        turned = jnp.concatenate(
            [first * cosine - second * sine, second * cosine + first * sine], axis=0
        ).astype(jnp.bfloat16)
        if head < q_heads:
            qt_ref[head * dim : (head + 1) * dim, :] = turned
        else:
            pieces.append(turned)
    at = (q_heads + kv_heads) * dim
    pieces.append(flat[at : at + kv_heads * dim].astype(jnp.bfloat16))
    low = 0
    for piece in pieces:
        kvt_ref[low : low + piece.shape[0], :] = piece
        low += piece.shape[0]
    step = x_ref.shape[0]
    for k in range(prompt_steps):

        @pl.when(i == k)
        def _():
            own[:, k * step : (k + 1) * step] = kvt_ref[...]

    def exchange(k):
        peer = lax.rem(me + k, count)
        return pltpu.make_async_remote_copy(
            own,
            all_ref.at[me],
            send.at[k],
            recv.at[k],
            device_id={"context": peer},
            device_id_type=MESH,
        )

    keep = pltpu.make_async_copy(own, all_ref.at[me], local)

    @pl.when(i == prompt_steps - 1)
    def _():
        for k in range(1, count):
            exchange(k).start()
        keep.start()

    @pl.when(i == pl.num_programs(0) - 1)
    def _():
        for k in range(1, count):
            exchange(k).wait()
        keep.wait()


def project_rope(x, packed_full, cos_t, sin_t, q_heads, kv_heads, prompt_rows, cid):
    rows, width = x.shape
    dim = HEAD_SIZE
    count = lax.axis_size("context")
    step = math.gcd(math.gcd(rows, prompt_rows), 256)
    cols_wide = packed_full.shape[1]
    kv2 = 2 * kv_heads * dim
    by_row = lambda i: (i, 0)
    by_col = lambda i: (0, i)
    fixed = lambda i: (0, 0)
    return pl.pallas_call(
        functools.partial(rope_kernel, q_heads, kv_heads, dim, prompt_rows // step),
        grid=(rows // step,),
        in_specs=[
            pl.BlockSpec((step, width), by_row),
            pl.BlockSpec(packed_full.shape, fixed, pipeline_mode=pl.Buffered(1)),
            pl.BlockSpec((dim // 2, step), by_col),
            pl.BlockSpec((dim // 2, step), by_col),
        ],
        out_specs=[
            pl.BlockSpec((step, width), by_row),
            pl.BlockSpec((q_heads * dim, step), by_col),
            pl.BlockSpec((kv2, step), by_col),
            pl.BlockSpec((8, width), fixed),
            pl.BlockSpec(memory_space=pltpu.HBM),
        ],
        out_shape=[
            jax.ShapeDtypeStruct((rows, width), jnp.bfloat16),
            jax.ShapeDtypeStruct((q_heads * dim, rows), jnp.bfloat16),
            jax.ShapeDtypeStruct((kv2, rows), jnp.bfloat16),
            jax.ShapeDtypeStruct((8, width), jnp.float32),
            jax.ShapeDtypeStruct((count, kv2, prompt_rows), jnp.bfloat16),
        ],
        scratch_shapes=[
            pltpu.VMEM((kv2, prompt_rows), jnp.bfloat16),
            pltpu.SemaphoreType.DMA((count,)),
            pltpu.SemaphoreType.DMA((count,)),
            pltpu.SemaphoreType.DMA,
        ],
        compiler_params=pltpu.CompilerParams(
            collective_id=cid, has_side_effects=True, vmem_limit_bytes=48 << 20
        ),
        cost_estimate=pl.CostEstimate(
            flops=2 * rows * width * cols_wide,
            bytes_accessed=4 * x.size + 2 * width * cols_wide,
            transcendentals=0,
        ),
    )(x, packed_full, cos_t, sin_t)


def attend_shape(prompt_all, kvt_cont):
    count, kv2, prompt_rows = prompt_all.shape
    cont_rows = kvt_cont.shape[1] - prompt_rows
    chunk = math.gcd(math.gcd(prompt_rows, cont_rows), 256)
    return count, kv2, prompt_rows, cont_rows, chunk


def total_kernel(count, part_ref, out_ref, got, send, recv):
    greet(AXIS, count)
    me = lax.axis_index(AXIS)
    copies = []
    for k in range(1, count):
        peer = lax.rem(me + k, count)
        copy = pltpu.make_async_remote_copy(
            part_ref,
            got.at[me],
            send.at[k],
            recv.at[k],
            device_id={AXIS: peer},
            device_id_type=MESH,
        )
        copy.start()
        copies.append(copy)
    got[me] = part_ref[...]
    for copy in copies:
        copy.wait()
    total = got[0]
    for k in range(1, count):
        total += got[k]
    out_ref[...] = total


def tensor_total(part, cid):
    count = lax.axis_size(AXIS)
    return pl.pallas_call(
        functools.partial(total_kernel, count),
        out_shape=jax.ShapeDtypeStruct(part.shape, part.dtype),
        in_specs=[pl.BlockSpec(memory_space=pltpu.VMEM)],
        out_specs=pl.BlockSpec(memory_space=pltpu.VMEM),
        scratch_shapes=[
            pltpu.VMEM((count, *part.shape), part.dtype),
            pltpu.SemaphoreType.DMA((count,)),
            pltpu.SemaphoreType.DMA((count,)),
        ],
        compiler_params=pltpu.CompilerParams(collective_id=cid, has_side_effects=True),
        cost_estimate=pl.CostEstimate(flops=0, bytes_accessed=4 << 20, transcendentals=0),
    )(part)


def plane_kernel(
    prompt_total,
    o_ref,
    q_ref,
    kt_ref,
    vt_ref,
    again_ref,
    mgain_ref,
    info_ref,
    w0_ref,
    w1_ref,
    w2_ref,
    px_ref,
    cx_ref,
    pc_ref,
    cc_ref,
    all_ref,
    shard_ref,
    x_ref,
    cot_ref,
    bias_ref,
    own_ref,
    stage,
    send,
    recv,
    local,
):
    dp, context = lax.axis_index("dp"), lax.axis_index("context")
    side = {"context": 1 - context}
    along = {"dp": lax.rem(dp + 2, 4)}
    twin_dp = dp + 1 - 2 * lax.rem(dp, 2)
    twin = {"dp": twin_dp}
    barrier = pltpu.get_barrier_semaphore()
    for peer in (side, along, twin):
        pl.semaphore_signal(barrier, inc=1, device_id=peer, device_id_type=MESH)
    pl.semaphore_wait(barrier, 3)
    rows = own_ref.shape[0]
    q_cols = q_ref.shape[1]
    own_ref[:, :q_cols] = o_ref[...]
    own_ref[:, q_cols : 2 * q_cols] = q_ref[...]
    small = [kt_ref[...], vt_ref[...], again_ref[...], mgain_ref[...]]
    rest = own_ref.shape[1] - 2 * q_cols
    used = sum(part.shape[0] for part in small)
    small.append(jnp.zeros((rest - used, rows), jnp.bfloat16))
    own_ref[:, 2 * q_cols :] = (
        jnp.concatenate([part.astype(jnp.float32) for part in small], axis=0).T
    ).astype(jnp.bfloat16)
    half = rows // 2
    mine = 2 * dp + context
    from_side = 2 * dp + 1 - context
    from_along = 2 * lax.rem(dp + 2, 4) + context
    from_far = 2 * lax.rem(dp + 2, 4) + 1 - context

    def spot(block, h):
        return pl.ds(pl.multiple_of(block * rows + h * half, half), half)

    def copy(k, block, h, peer, first=False):
        source = own_ref.at[pl.ds(h * half, half)] if first else all_ref.at[spot(block, h)]
        return pltpu.make_async_remote_copy(
            source,
            all_ref.at[spot(block, h)],
            send.at[k],
            recv.at[k],
            device_id=peer,
            device_id_type=MESH,
        )

    def land(k, block, h):
        return pltpu.make_async_remote_copy(
            own_ref.at[pl.ds(h * half, half)],
            all_ref.at[spot(block, h)],
            send.at[k],
            recv.at[k],
            device_id=side,
            device_id_type=MESH,
        )

    started = []

    def go(*args, **kwargs):
        one = copy(*args, **kwargs)
        one.start()
        started.append(one)

    go(0, mine, 0, side, first=True)
    go(2, mine, 1, along, first=True)
    go(1, mine, 1, side, first=True)
    go(3, mine, 0, along, first=True)
    go(6, mine, 0, twin, first=True)
    go(7, mine, 1, twin, first=True)
    prompt_rows = px_ref.shape[0]
    moves = [
        pltpu.make_async_copy(own_ref, all_ref.at[pl.ds(pl.multiple_of(mine * rows, rows), rows)], local.at[0]),
    ]
    moves[0].start()
    joins = []
    for k, (source, target, low) in enumerate(
        (
            (px_ref, x_ref, 0),
            (cx_ref, x_ref, prompt_rows),
            (pc_ref, cot_ref, 0),
            (cc_ref, cot_ref, prompt_rows),
        )
    ):
        rows_at = pl.ds((k % 2) * prompt_rows, source.shape[0])
        load = pltpu.make_async_copy(source, stage.at[k // 2, rows_at], local.at[1 + k])
        load.start()
        joins.append(
            (
                load,
                pltpu.make_async_copy(
                    stage.at[k // 2, rows_at],
                    target.at[pl.ds(low, source.shape[0])],
                    local.at[5 + k],
                ),
            )
        )
    cols = w0_ref.shape[1]
    wide = shard_ref.shape[1] // 3
    for k, ref in enumerate((w0_ref, w1_ref, w2_ref)):
        shard_ref[:, k * wide : k * wide + cols] = ref[...]
        shard_ref[:, k * wide + cols : (k + 1) * wide] = jnp.zeros(
            (rows, wide - cols), jnp.bfloat16
        )
    cont_rows = cx_ref.shape[0]
    block = 128

    def fill_bias(low, count, at, columns, rule):
        @pl.loop(0, count // block)
        def _(c):
            key = lax.broadcasted_iota(jnp.int32, (block, columns), 0) + c * block
            query = lax.broadcasted_iota(jnp.int32, (block, columns), 1)
            rows_at = pl.ds(pl.multiple_of(low + c * block, block), block)
            bias_ref[rows_at, at : at + columns] = jnp.where(
                rule(key, query), 0.0, NEGATIVE
            ).astype(jnp.bfloat16)

    first = context * prompt_rows
    earlier, length = info_ref[0:1, :], info_ref[1:2, :]
    fill_bias(0, prompt_total, 0, prompt_rows, lambda k, q: k <= q + first)
    fill_bias(prompt_total, cont_rows, 0, prompt_rows, lambda k, q: k < 0)
    fill_bias(0, prompt_total, prompt_rows, cont_rows, lambda k, q: k < length)
    fill_bias(
        prompt_total, cont_rows, prompt_rows, cont_rows, lambda k, q: (k >= earlier) & (k <= q)
    )
    for load, save in joins:
        load.wait()
        save.start()
        moves.append(save)
    land(0, from_side, 0).wait_recv()
    go(4, from_side, 0, along)
    go(8, from_side, 0, twin)
    land(2, from_along, 1).wait_recv()
    go(5, from_along, 1, side)
    go(9, from_along, 1, twin)
    land(1, from_side, 1).wait_recv()
    go(10, from_side, 1, twin)
    land(3, from_along, 0).wait_recv()
    go(11, from_along, 0, twin)
    land(4, from_far, 0).wait_recv()
    go(12, from_far, 0, twin)
    land(5, from_far, 1).wait_recv()
    go(13, from_far, 1, twin)
    base = 2 * twin_dp
    other = 2 * lax.rem(twin_dp + 2, 4)
    for k, block, h in (
        (6, base + context, 0),
        (7, base + context, 1),
        (8, base + 1 - context, 0),
        (9, other + context, 1),
        (10, base + 1 - context, 1),
        (11, other + context, 0),
        (12, other + 1 - context, 0),
        (13, other + 1 - context, 1),
    ):
        land(k, block, h).wait_recv()
    for one in started:
        one.wait_send()
    for move in moves:
        move.wait()


def plane_gather(
    attn, gains, info, weights, wide, attn_wide, prompt_x, cont_x, prompt_cot, cont_cot, cid
):
    o_weight, q_weight, key_matrix, value_matrix = attn
    rows = q_weight.shape[0]
    count = lax.axis_size("dp") * lax.axis_size("context")
    prompt_rows, width = prompt_x.shape
    total = prompt_rows + cont_x.shape[0]
    prompt_total = prompt_rows * lax.axis_size("context")
    hbm = pl.BlockSpec(memory_space=pltpu.HBM)
    vmem = pl.BlockSpec(memory_space=pltpu.VMEM)
    both = jax.ShapeDtypeStruct((total, width), jnp.bfloat16)
    return pl.pallas_call(
        functools.partial(plane_kernel, prompt_total),
        out_shape=[
            jax.ShapeDtypeStruct((count * rows, attn_wide), jnp.bfloat16),
            jax.ShapeDtypeStruct((rows, 3 * wide), jnp.bfloat16),
            both,
            both,
            jax.ShapeDtypeStruct((prompt_total + cont_x.shape[0], total), jnp.bfloat16),
        ],
        in_specs=[vmem] * 10 + [hbm] * 4,
        out_specs=[hbm, vmem, hbm, hbm, vmem],
        scratch_shapes=[
            pltpu.VMEM((rows, attn_wide), jnp.bfloat16),
            pltpu.VMEM((2, total, width), jnp.bfloat16),
            pltpu.SemaphoreType.DMA((14,)),
            pltpu.SemaphoreType.DMA((14,)),
            pltpu.SemaphoreType.DMA((9,)),
        ],
        compiler_params=pltpu.CompilerParams(
            collective_id=cid, has_side_effects=True, vmem_limit_bytes=60 << 20
        ),
        cost_estimate=pl.CostEstimate(
            flops=30_000_000_000, bytes_accessed=40 << 20, transcendentals=0
        ),
    )(
        o_weight,
        q_weight,
        key_matrix.T,
        value_matrix.T,
        gains[0][None, :],
        gains[1][None, :],
        info,
        *weights,
        prompt_x,
        cont_x,
        prompt_cot,
        cont_cot,
    )


def fill_keys(chunk, dim, kv_heads, all_ref, cont_ref, rows_of, chunks_ref):
    count, _, prompt_rows = all_ref.shape
    per = prompt_rows // chunk
    total = count * per + (cont_ref.shape[1] - prompt_rows) // chunk
    for c in range(total):
        if c < count * per:
            block = all_ref[c // per, :, (c % per) * chunk : (c % per + 1) * chunk]
        else:
            at = prompt_rows + (c - count * per) * chunk
            block = cont_ref[:, at : at + chunk]
        chunks_ref[c] = block
        for n, target in enumerate(rows_of):
            for g in range(kv_heads):
                at = (n * kv_heads + g) * dim
                target[g, c * chunk : (c + 1) * chunk, :] = (
                    block[at : at + dim].astype(jnp.float32).T.astype(jnp.bfloat16)
                )


def trip_count(tile, chunk, i, prompt_rows, count):
    me = lax.axis_index("context")
    prompt_tiles = prompt_rows // tile
    n_prompt = lax.div(me * prompt_rows + (i + 1) * tile + chunk - 1, chunk)
    n_own = lax.div((i - prompt_tiles + 1) * tile + chunk - 1, chunk)
    return i < prompt_tiles, n_prompt, count * prompt_rows // chunk, n_own


class Line:
    def __init__(self, part, recv, out, sink, sems, sink_sems, ready=None, place=None):
        self.ready, self.place = ready, place
        self.part, self.recv, self.out, self.sink = part, recv, out, sink
        self.per = sink.shape[0] // out.shape[1]
        self.sems, self.sink_sems = sems, sink_sems
        self.blocks = out.shape[0]
        me, n = lax.axis_index(AXIS), lax.axis_size(AXIS)
        self.outer = (me == 0) | (me == n - 1)
        self.inner = jnp.logical_not(self.outer)
        self.mate = jnp.where(me < n // 2, 1 - me, 2 * n - 3 - me)
        self.across = n - 1 - me

    def copy(self, k, source, target, peer, b):
        return pltpu.make_async_remote_copy(
            source.at[b],
            target.at[b],
            self.sems.at[2 * k, b],
            self.sems.at[2 * k + 1, b],
            device_id={AXIS: peer},
            device_id_type=MESH,
        )

    def up(self, b):
        return self.copy(0, self.part, self.recv, self.mate, b)

    def mid(self, b):
        return self.copy(1, self.part, self.out, self.across, b)

    def down(self, b):
        return self.copy(2, self.out, self.out, self.mate, b)

    def keep(self, b):
        _, rows, cols = self.out.shape
        row, col = lax.rem(b, self.per), lax.div(b, self.per)
        if self.place is not None:
            row, col = self.place(b)
        at = (
            pl.ds(pl.multiple_of(row * rows, rows), rows),
            pl.ds(pl.multiple_of(col * cols, cols), cols),
        )
        return pltpu.make_async_copy(self.out.at[b], self.sink.at[at], self.sink_sems.at[b])

    def greet(self, axis=None, count=1):
        barrier = pltpu.get_barrier_semaphore()
        pl.semaphore_signal(barrier, inc=1, device_id={AXIS: self.mate}, device_id_type=MESH)
        for k in range(1, count):
            peer = lax.rem(lax.axis_index(axis) + k, count)
            pl.semaphore_signal(barrier, inc=1, device_id={axis: peer}, device_id_type=MESH)

        @pl.when(self.inner)
        def _():
            pl.semaphore_signal(barrier, inc=1, device_id={AXIS: self.across}, device_id_type=MESH)
            pl.semaphore_wait(barrier, 1 + count)

        @pl.when(self.outer)
        def _():
            pl.semaphore_wait(barrier, count)

    def start(self, first, count):
        @pl.when(self.outer)
        def _():
            @pl.loop(0, count)
            def _(k):
                self.up(first + k).start()

    def step(self, t):
        @pl.when(self.inner & (t >= 0) & (t < self.blocks))
        def _():
            self.up(t).wait_recv()
            self.part[t] = (
                self.part[t].astype(jnp.float32) + self.recv[t].astype(jnp.float32)
            ).astype(jnp.bfloat16)
            self.mid(t).start()

        @pl.when(self.inner & (t >= LAG) & (t < self.blocks + LAG))
        def _():
            b = t - LAG
            self.mid(b).wait_recv()
            self.out[b] = (
                self.part[b].astype(jnp.float32) + self.out[b].astype(jnp.float32)
            ).astype(jnp.bfloat16)
            self.down(b).start()
            self.keep(b).start()
            if self.ready is not None:
                self.ready(b)

    def drain(self):
        for k in range(LAG):
            self.step(self.blocks + k)

        @pl.when(self.outer)
        def _():
            @pl.loop(0, self.blocks)
            def _(b):
                self.down(b).wait_recv()
                self.keep(b).start()
                if self.ready is not None:
                    self.ready(b)
                self.up(b).wait_send()

        @pl.when(self.inner)
        def _():
            @pl.loop(0, self.blocks)
            def _(b):
                self.mid(b).wait_send()
                self.down(b).wait_send()

        @pl.loop(0, self.blocks)
        def _(b):
            self.keep(b).wait()


def line_scratch(shape):
    return [pltpu.VMEM(shape, jnp.bfloat16)] * 3 + [
        pltpu.SemaphoreType.DMA((6, shape[0])),
        pltpu.SemaphoreType.DMA((shape[0],)),
    ]


def attend_kernel(
    shape,
    dim,
    kv_heads,
    per,
    tile,
    cut,
    q_ref,
    all_ref,
    cont_ref,
    bias_ref,
    wo_ref,
    x_ref,
    gains_ref,
    out_ref,
    lse_ref,
    sum_ref,
    normed_ref,
    keys,
    chunks,
    norm_buf,
    norm_sems,
    part,
    recv,
    out,
    sems,
    sink_sems,
):
    count, prompt_rows, chunk = shape
    i = pl.program_id(0)

    def norm_out(b):
        at = pl.ds(pl.multiple_of(b * cut, cut), cut)
        return pltpu.make_async_copy(norm_buf.at[b], normed_ref.at[at], norm_sems.at[b])

    def ready(b):
        at = pl.ds(pl.multiple_of(b * cut, cut), cut)
        unit, _ = normalize(x_ref[at, :].astype(jnp.float32) + out[b].astype(jnp.float32))
        norm_buf[b] = (unit * gains_ref[1:2, :]).astype(jnp.bfloat16)
        norm_out(b).start()

    line = Line(part, recv, out, sum_ref, sems, sink_sems, ready)
    blocks = tile // cut

    @pl.when(i == 0)
    def _():
        fill_keys(chunk, dim, kv_heads, all_ref, cont_ref, [keys], chunks)
        line.greet()

    is_prompt, n_prompt, base, n_own = trip_count(tile, chunk, i, prompt_rows, count)
    wide = per * tile
    factor = dim ** (-0.5) * LOG2E
    outs, sums = [], []
    for g in range(kv_heads):
        q = jnp.concatenate(
            [q_ref[(g * per + h) * dim : (g * per + h + 1) * dim, :] for h in range(per)], axis=1
        )

        def body(c, state):
            top, total, acc = state
            at = pl.ds(pl.multiple_of(c * chunk, chunk), chunk)
            s = jnp.dot(keys[g, at, :], q, preferred_element_type=jnp.float32)
            t = s * factor + jnp.concatenate([bias_ref[at, :].astype(jnp.float32)] * per, axis=1)
            new = jnp.maximum(top, jnp.max(t, axis=0, keepdims=True))
            p = jnp.exp2(t - new)
            scale = jnp.exp2(top - new)
            total = total * scale + jnp.sum(p, axis=0, keepdims=True)
            v = chunks[c, (kv_heads + g) * dim : (kv_heads + g + 1) * dim, :]
            acc = acc * scale + jnp.dot(
                v, p.astype(jnp.bfloat16), preferred_element_type=jnp.float32
            )
            return new, total, acc

        start = (
            jnp.full((1, wide), NEGATIVE, jnp.float32),
            jnp.zeros((1, wide), jnp.float32),
            jnp.zeros((dim, wide), jnp.float32),
        )
        state = lax.fori_loop(0, jnp.where(is_prompt, n_prompt, base), body, start)
        top, total, acc = lax.fori_loop(base, base + jnp.where(is_prompt, 0, n_own), body, state)
        acc = acc / total
        top = top + jnp.log2(total)
        outs += [acc[:, h * tile : (h + 1) * tile] for h in range(per)]
        sums += [top[:, h * tile : (h + 1) * tile] for h in range(per)]
        if g < kv_heads - 1:
            for r in range(blocks // 2):
                line.step((i - 1) * blocks + r)
    attended = jnp.concatenate(outs, axis=0).T.astype(jnp.bfloat16)
    out_ref[...] = attended
    lse_ref[...] = jnp.concatenate(sums, axis=0)
    term = contract_last(attended, wo_ref[...]).astype(jnp.bfloat16)
    for r in range(blocks):
        part[i * blocks + r] = term[r * cut : (r + 1) * cut]

    line.start(i * blocks, blocks)
    for r in range(blocks // 2, blocks):
        line.step((i - 1) * blocks + r)

    @pl.when(i == pl.num_programs(0) - 1)
    def _():
        @pl.loop(0, blocks)
        def _(r):
            line.step(i * blocks + r)

        line.drain()

        @pl.loop(0, line.blocks)
        def _(b):
            norm_out(b).wait()


def attend(q_t, prompt_all, kvt_cont, bias, packed_full, x, gains, q_heads, kv_heads, cid):
    dim = HEAD_SIZE
    count, kv2, prompt_rows, cont_rows, chunk = attend_shape(prompt_all, kvt_cont)
    q_cols, rows = q_t.shape
    width = packed_full.shape[0]
    keys_all = bias.shape[0]
    tile, cut = 128, 16
    whole = pl.BlockSpec(memory_space=pltpu.VMEM)
    by_col = lambda i: (0, i)
    return pl.pallas_call(
        functools.partial(
            attend_kernel,
            (count, prompt_rows, chunk),
            dim,
            kv_heads,
            q_heads // kv_heads,
            tile,
            cut,
        ),
        grid=(rows // tile,),
        in_specs=[
            pl.BlockSpec((q_cols, tile), by_col),
            whole,
            whole,
            pl.BlockSpec((keys_all, tile), by_col),
            pl.BlockSpec((width, q_cols), lambda i: (0, 0), pipeline_mode=pl.Buffered(1)),
            whole,
            whole,
        ],
        out_specs=[
            pl.BlockSpec((tile, q_cols), lambda i: (i, 0)),
            pl.BlockSpec((q_heads, tile), by_col),
            pl.BlockSpec(memory_space=pl.ANY),
            pl.BlockSpec(memory_space=pl.ANY),
        ],
        out_shape=[
            jax.ShapeDtypeStruct((rows, q_cols), jnp.bfloat16),
            jax.ShapeDtypeStruct((q_heads, rows), jnp.float32),
            jax.ShapeDtypeStruct((rows, width), jnp.bfloat16),
            jax.ShapeDtypeStruct((rows, width), jnp.bfloat16),
        ],
        scratch_shapes=[
            pltpu.VMEM((kv_heads, keys_all, dim), jnp.bfloat16),
            pltpu.VMEM((keys_all // chunk, kv2, chunk), jnp.bfloat16),
            pltpu.VMEM((rows // cut, cut, width), jnp.bfloat16),
            pltpu.SemaphoreType.DMA((rows // cut,)),
            *line_scratch((rows // cut, cut, width)),
        ],
        compiler_params=pltpu.CompilerParams(
            collective_id=cid, has_side_effects=True, vmem_limit_bytes=56 << 20
        ),
        cost_estimate=pl.CostEstimate(
            flops=120_000_000_000, bytes_accessed=40 << 20, transcendentals=0
        ),
    )(q_t, prompt_all, kvt_cont, bias, packed_full, x, gains)


def feed_back_kernel(
    cut,
    hidden_in,
    gate_in,
    up_in,
    normed_late,
    cot_late,
    fd_ref,
    fg_ref,
    fu_ref,
    wd_ref,
    wg_ref,
    wu_ref,
    cot_ref,
    normed_ref,
    grads_ref,
    up_grads_ref,
    mlp_ref,
    sum_ref,
    hidden,
    gate,
    up,
    late_sems,
    part,
    recv,
    out,
    sems,
    sink_sems,
):
    i = pl.program_id(0)
    rows, wide = gate.shape
    first = hidden_in.shape[0]
    tiles = sum_ref.shape[1] // SIZE
    feeds = wide // SIZE
    low, high = first // cut, (rows - first) // cut
    split = tiles * low

    def place(b):
        early = b < split
        c = b - split
        row = jnp.where(early, lax.rem(b, low), low + lax.rem(c, high))
        return row, jnp.where(early, lax.div(b, low), lax.div(c, high))

    line = Line(part, recv, out, sum_ref, sems, sink_sems, place=place)

    def loads():
        return [
            pltpu.make_async_copy(source, target.at[pl.ds(0, first)], late_sems.at[k])
            for k, (source, target) in enumerate(((gate_in, gate), (up_in, up), (hidden_in, hidden)))
        ]

    def produce(at, block, count):
        back = contract_last(gate[at, :], wg_ref[...]) + contract_last(up[at, :], wu_ref[...])
        back = back.astype(jnp.bfloat16)
        for r in range(count):
            part[block + r] = back[r * cut : (r + 1) * cut]
        line.start(block, count)

    def steps(start, stop):
        @pl.loop(start, stop)
        def _(t):
            line.step(t)

    @pl.when(i == 0)
    def _():
        for load in loads():
            load.start()
        line.greet()
        for load in loads():
            load.wait()

    @pl.when(i < tiles)
    def _():
        produce(slice(0, first), i * low, low)

    beside = min(split, FEED_STEPS)

    @pl.when((i >= tiles) & (i < tiles + feeds))
    def _():
        m = i - tiles
        here = pl.ds(pl.multiple_of(m * SIZE, SIZE), SIZE)
        hidden[first:, here], gate[first:, here], up[first:, here] = feed_tile(
            normed_late[...], cot_late[...], fd_ref[...], fg_ref[...], fu_ref[...]
        )
        steps(lax.div(m * beside, feeds), lax.div((m + 1) * beside, feeds))

    @pl.when(i >= tiles + feeds)
    def _():
        n = i - tiles - feeds
        produce(slice(first, rows), split + n * high, high)
        rest = line.blocks - beside
        spots = 4

        def step(k):
            start = beside + lax.div((n * spots + k) * rest, tiles * spots)
            steps(start, beside + lax.div((n * spots + k + 1) * rest, tiles * spots))

        step(0)
        grads_ref[:, :wide] = contract_first(cot_ref[...], hidden[...]).astype(jnp.bfloat16)
        step(1)
        grads_ref[:, wide:] = contract_first(normed_ref[...], gate[...]).astype(jnp.bfloat16)
        step(2)
        up_grads_ref[...] = contract_first(normed_ref[...], up[...]).astype(jnp.bfloat16)
        step(3)
        mlp_ref[0] = contract_last(hidden[...], wd_ref[...]).astype(jnp.bfloat16)

        @pl.when(n == tiles - 1)
        def _():
            line.drain()


def feed_back(hidden, grad_gate, grad_up, mlp_full, cot, normed, cid):
    first, wide = hidden.shape
    rows, width = cot.shape
    cut = math.gcd(math.gcd(rows, first), SIZE)
    tiles, feeds = width // SIZE, wide // SIZE
    blocks = (tiles * rows // cut, cut, SIZE)
    anywhere = pl.BlockSpec(memory_space=pltpu.HBM)
    second = lambda i: (first // (rows - first), 0)
    late = lambda i: jnp.maximum(i - tiles - feeds, 0)
    back = lambda i: jnp.where(i < tiles, i, late(i))
    ahead = lambda i: jnp.clip(i - tiles, 0, feeds - 1)
    return pl.pallas_call(
        functools.partial(feed_back_kernel, cut),
        grid=(2 * tiles + feeds,),
        in_specs=[anywhere] * 3
        + [pl.BlockSpec((rows - first, width), second, pipeline_mode=pl.Buffered(1))] * 2
        + [pl.BlockSpec((width, SIZE), lambda i, k=k: (0, k * feeds + ahead(i))) for k in range(3)]
        + [pl.BlockSpec((SIZE, wide), lambda i: (late(i), 0))]
        + [pl.BlockSpec((SIZE, wide), lambda i, k=k: (back(i), k)) for k in (1, 2)]
        + [pl.BlockSpec((rows, SIZE), lambda i: (0, late(i)))] * 2,
        out_specs=[
            pl.BlockSpec((SIZE, 2 * wide), lambda i: (late(i), 0)),
            pl.BlockSpec((SIZE, wide), lambda i: (late(i), 0)),
            pl.BlockSpec((1, rows, SIZE), lambda i: (late(i), 0, 0)),
            pl.BlockSpec(memory_space=pl.ANY),
        ],
        out_shape=[
            jax.ShapeDtypeStruct((width, 2 * wide), jnp.bfloat16),
            jax.ShapeDtypeStruct((width, wide), jnp.bfloat16),
            jax.ShapeDtypeStruct((tiles, rows, SIZE), jnp.bfloat16),
            jax.ShapeDtypeStruct((rows, width), jnp.bfloat16),
        ],
        scratch_shapes=[
            pltpu.VMEM((rows, wide), jnp.bfloat16),
            pltpu.VMEM((rows, wide), jnp.bfloat16),
            pltpu.VMEM((rows, wide), jnp.bfloat16),
            pltpu.SemaphoreType.DMA((3,)),
            *line_scratch(blocks),
        ],
        compiler_params=pltpu.CompilerParams(
            collective_id=cid, has_side_effects=True, vmem_limit_bytes=61 << 20
        ),
        cost_estimate=pl.CostEstimate(
            flops=12 * rows * wide * width, bytes_accessed=200 << 20, transcendentals=0
        ),
    )(
        hidden,
        grad_gate,
        grad_up,
        normed,
        cot,
        mlp_full,
        mlp_full,
        mlp_full,
        mlp_full,
        mlp_full,
        mlp_full,
        cot,
        normed,
    )


def window_kernel(
    shape,
    dim,
    kv_heads,
    per,
    tile,
    q_ref,
    all_ref,
    cont_ref,
    bias_ref,
    out_ref,
    lse_ref,
    back_ref,
    cot_ref,
    x_ref,
    attn_ref,
    gain_ref,
    wo_ref,
    cos_ref,
    sin_ref,
    cos_own_ref,
    sin_own_ref,
    normed_ref,
    att_ref,
    up_grads_ref,
    mlp_ref,
    gq_out_ref,
    gkv_ref,
    gm_ref,
    grads_ref,
    sum_ref,
    keys,
    values,
    chunks,
    gk,
    gv,
    gm,
    gq_ref,
    send_ref,
    got,
    own_ref,
    kv_sems,
    part,
    recv,
    out,
    sems,
    sink_sems,
):
    count, prompt_rows, chunk = shape
    i = pl.program_id(0)
    line = Line(part, recv, out, sum_ref, sems, sink_sems)
    context = lax.axis_index("context")
    prompt_tiles = prompt_rows // tile
    tiles = gq_ref.shape[0] // tile
    slots = SLOTS
    spots = 2 + kv_heads

    def step(k):
        for s in range(k * slots // spots, (k + 1) * slots // spots):
            line.step(i * slots + s)

    def send(k):
        peer = lax.rem(context + k, count)
        return pltpu.make_async_remote_copy(
            send_ref.at[peer],
            got.at[k],
            kv_sems.at[0, k],
            kv_sems.at[1, k],
            device_id={"context": peer},
            device_id_type=MESH,
        )

    root = dim ** (-0.5)
    half = dim // 2

    @pl.when(i == 0)
    def _():
        load = pltpu.make_async_copy(mlp_ref, part, sink_sems.at[0])
        load.start()
        fill_keys(chunk, dim, kv_heads, all_ref, cont_ref, [keys, values], chunks)
        gk[...] = jnp.zeros_like(gk)
        gv[...] = jnp.zeros_like(gv)
        line.greet("context", count)
        load.wait()
        line.start(0, line.blocks)

    @pl.when(i < tiles)
    def _():
        middle = x_ref[...].astype(jnp.float32) + attn_ref[...].astype(jnp.float32)
        inverse = lax.rsqrt(jnp.mean(middle * middle, axis=-1, keepdims=True) + EPS)
        unit = middle * inverse
        grad_unit = back_ref[...].astype(jnp.float32) * gain_ref[...]
        grad_middle = cot_ref[...].astype(jnp.float32) + norm_back(grad_unit, unit, inverse)
        gm_ref[...] = grad_middle.astype(jnp.bfloat16)
        grad_b = grad_middle.astype(jnp.bfloat16)
        step(0)
        grad_t = (
            jnp.dot(grad_b, wo_ref[...], preferred_element_type=jnp.float32).astype(jnp.bfloat16)
        ).astype(jnp.float32).T
        gm[pl.ds(pl.multiple_of(i * tile, tile), tile), :] = grad_b
        step(1)

        is_prompt, n_prompt, base, n_own = trip_count(tile, chunk, i, prompt_rows, count)
        factor = root * LOG2E
        prod = grad_t * out_ref[...].astype(jnp.float32).T
        grad_t = grad_t.astype(jnp.bfloat16)
        cosine, sine = cos_ref[...], sin_ref[...]
        pieces = []
        for g in range(kv_heads):
            heads = [g * per + h for h in range(per)]
            q = jnp.concatenate([q_ref[h * dim : (h + 1) * dim, :] for h in heads], axis=1)
            grad = jnp.concatenate([grad_t[h * dim : (h + 1) * dim] for h in heads], axis=1)
            inner = jnp.concatenate(
                [jnp.sum(prod[h * dim : (h + 1) * dim], axis=0, keepdims=True) for h in heads], axis=1
            )
            lse = jnp.concatenate([lse_ref[h : h + 1, :] for h in heads], axis=1)

            def body(c, acc):
                at = pl.ds(pl.multiple_of(c * chunk, chunk), chunk)
                s = jnp.dot(keys[g, at, :], q, preferred_element_type=jnp.float32)
                b = bias_ref[at, :].astype(jnp.float32)
                p = jnp.exp2(s * factor + (jnp.concatenate([b] * per, axis=1) - lse))
                dp = jnp.dot(values[g, at, :], grad, preferred_element_type=jnp.float32)
                ds = (p * (dp - inner)).astype(jnp.bfloat16)
                gv[g, at, :] += contract_last(p.astype(jnp.bfloat16), grad)
                gk[g, at, :] += contract_last(ds, q)
                k_t = chunks[c, g * dim : (g + 1) * dim, :]
                return acc + jnp.dot(k_t, ds, preferred_element_type=jnp.float32)

            acc = jnp.zeros((dim, per * tile), jnp.float32)
            acc = lax.fori_loop(0, jnp.where(is_prompt, n_prompt, base), body, acc)
            acc = lax.fori_loop(base, base + jnp.where(is_prompt, 0, n_own), body, acc)
            acc = acc * root
            for h in range(per):
                first = acc[:half, h * tile : (h + 1) * tile]
                second = acc[half:, h * tile : (h + 1) * tile]
                pieces += [first * cosine + second * sine, second * cosine - first * sine]
            step(2 + g)
        rows_q = jnp.concatenate(pieces, axis=0).T.astype(jnp.bfloat16)
        gq_ref[pl.ds(pl.multiple_of(i * tile, tile), tile), :] = rows_q
        gq_out_ref[...] = rows_q

    @pl.when(i == tiles - 1)
    def _():
        for g in range(kv_heads):
            for n, (acc, scale) in enumerate(((gk, root), (gv, 1.0))):
                at = (n * kv_heads + g) * dim
                for c in range(count):
                    rows = acc[g, c * prompt_rows : (c + 1) * prompt_rows, :]
                    send_ref[c, at : at + dim, :] = (rows * scale).T.astype(jnp.bfloat16)
                own_ref[at : at + dim, :] = (acc[g, count * prompt_rows :, :] * scale).T
        for k in range(1, count):
            send(k).start()

    @pl.when(i == tiles)
    def _():
        line.step(tiles * slots)
        kv_dim = kv_heads * dim

        def finish(flat, cosine, sine):
            pieces = []
            for at in range(0, kv_dim, dim):
                first, second = flat[at : at + half], flat[at + half : at + dim]
                pieces += [first * cosine + second * sine, second * cosine - first * sine]
            pieces.append(flat[kv_dim:])
            return jnp.concatenate(pieces, axis=0).T.astype(jnp.bfloat16)

        cosine, sine = cos_own_ref[...], sin_own_ref[...]
        gkv_ref[prompt_rows:, :] = finish(
            own_ref[...], cosine[:, prompt_rows:], sine[:, prompt_rows:]
        )
        total = send_ref[context].astype(jnp.float32)
        for k in range(1, count):
            send(k).wait()
            total += got[k].astype(jnp.float32)
        gkv_ref[:prompt_rows, :] = finish(
            total, cosine[:, :prompt_rows], sine[:, :prompt_rows]
        )

    @pl.when(i >= tiles)
    def _():
        n = i - tiles
        later = pl.num_programs(0) - tiles
        rest = line.blocks - tiles * slots - 1
        q_cols = gq_ref.shape[1]
        wide = up_grads_ref.shape[1]
        here = pl.ds(pl.multiple_of(n * SIZE, SIZE), SIZE)
        grads_ref[:, :wide] = up_grads_ref[...]
        grads_ref[:, wide : wide + q_cols] = contract_first(gm[:, here], att_ref[...]).astype(
            jnp.bfloat16
        )
        grads_ref[:, wide + q_cols : wide + 2 * q_cols] = contract_first(
            normed_ref[...], gq_ref[...]
        ).astype(jnp.bfloat16)
        grads_ref[:, wide + 2 * q_cols :] = contract_first(normed_ref[...], gkv_ref[...]).astype(
            jnp.bfloat16
        )
        low = tiles * slots + 1 + lax.div(n * rest, later)
        high = tiles * slots + 1 + lax.div((n + 1) * rest, later)

        @pl.loop(low, high)
        def _(t):
            line.step(t)

        @pl.when(n == later - 1)
        def _():
            line.drain()


def window(
    q_t,
    prompt_all,
    kvt_cont,
    bias,
    attended,
    lse,
    back,
    cot,
    x,
    attn_sum,
    gain,
    packed_full,
    cos_t,
    sin_t,
    normed,
    up_grads,
    mlp_part,
    q_heads,
    kv_heads,
    cid,
):
    dim = HEAD_SIZE
    count, kv2, prompt_rows, cont_rows, chunk = attend_shape(prompt_all, kvt_cont)
    rows, width = cot.shape
    q_cols = q_heads * dim
    keys_all = bias.shape[0]
    tile = 128
    whole = pl.BlockSpec(memory_space=pltpu.VMEM)
    anywhere = pl.BlockSpec(memory_space=pl.ANY)
    tiles, later = rows // tile, width // SIZE
    grad_cols = up_grads.shape[1] + 2 * q_cols + kv2
    early = lambda i: jnp.minimum(i, tiles - 1)
    late = lambda i: jnp.maximum(i - tiles, 0)
    by_col = lambda i: (0, early(i))
    by_row = lambda i: (early(i), 0)
    fixed = lambda i: (0, 0)
    return pl.pallas_call(
        functools.partial(
            window_kernel, (count, prompt_rows, chunk), dim, kv_heads, q_heads // kv_heads, tile
        ),
        grid=(tiles + later,),
        in_specs=[
            pl.BlockSpec((q_cols, tile), by_col),
            whole,
            whole,
            pl.BlockSpec((keys_all, tile), by_col),
            pl.BlockSpec((tile, q_cols), by_row),
            pl.BlockSpec((q_heads, tile), by_col),
            pl.BlockSpec((tile, width), by_row),
            pl.BlockSpec((tile, width), by_row),
            pl.BlockSpec((tile, width), by_row),
            pl.BlockSpec((tile, width), by_row),
            pl.BlockSpec((1, width), fixed),
            pl.BlockSpec((width, q_cols), fixed, pipeline_mode=pl.Buffered(1)),
            pl.BlockSpec((dim // 2, tile), by_col),
            pl.BlockSpec((dim // 2, tile), by_col),
            whole,
            whole,
            pl.BlockSpec((rows, SIZE), lambda i: (0, late(i))),
            whole,
            pl.BlockSpec((SIZE, up_grads.shape[1]), lambda i: (late(i), 0)),
            anywhere,
        ],
        out_specs=[
            pl.BlockSpec((tile, q_cols), by_row),
            pl.BlockSpec((rows, kv2), fixed),
            pl.BlockSpec((tile, width), by_row),
            pl.BlockSpec((SIZE, grad_cols), lambda i: (late(i), 0)),
            anywhere,
        ],
        out_shape=[
            jax.ShapeDtypeStruct((rows, q_cols), jnp.bfloat16),
            jax.ShapeDtypeStruct((rows, kv2), jnp.bfloat16),
            jax.ShapeDtypeStruct((rows, width), jnp.bfloat16),
            jax.ShapeDtypeStruct((width, grad_cols), jnp.bfloat16),
            jax.ShapeDtypeStruct((rows, width), jnp.bfloat16),
        ],
        scratch_shapes=[
            pltpu.VMEM((kv_heads, keys_all, dim), jnp.bfloat16),
            pltpu.VMEM((kv_heads, keys_all, dim), jnp.bfloat16),
            pltpu.VMEM((keys_all // chunk, kv2, chunk), jnp.bfloat16),
            pltpu.VMEM((kv_heads, keys_all, dim), jnp.float32),
            pltpu.VMEM((kv_heads, keys_all, dim), jnp.float32),
            pltpu.VMEM((rows, width), jnp.bfloat16),
            pltpu.VMEM((rows, q_cols), jnp.bfloat16),
            pltpu.VMEM((count, kv2, prompt_rows), jnp.bfloat16),
            pltpu.VMEM((count, kv2, prompt_rows), jnp.bfloat16),
            pltpu.VMEM((kv2, cont_rows), jnp.float32),
            pltpu.SemaphoreType.DMA((2, count)),
            *line_scratch(mlp_part.shape),
        ],
        compiler_params=pltpu.CompilerParams(
            collective_id=cid, has_side_effects=True, vmem_limit_bytes=60 << 20
        ),
        cost_estimate=pl.CostEstimate(
            flops=120_000_000_000, bytes_accessed=200 << 20, transcendentals=0
        ),
    )(
        q_t,
        prompt_all,
        kvt_cont,
        bias,
        attended,
        lse,
        back,
        cot,
        x,
        attn_sum,
        gain,
        packed_full,
        cos_t,
        sin_t,
        cos_t,
        sin_t,
        normed,
        attended,
        up_grads,
        mlp_part,
    )


def product_kernel(cut, spans, lhs_refs, w_ref, sum_ref, part, recv, out, sems, sink_sems):
    n = pl.program_id(0)
    per = sum_ref.shape[0] // cut
    line = Line(part, recv, out, sum_ref, sems, sink_sems)
    term = sum(
        contract_last(ref[...], w_ref[:, low:high]) for ref, (low, high) in zip(lhs_refs, spans)
    ).astype(jnp.bfloat16)
    for r in range(per):
        part[n * per + r] = term[r * cut : (r + 1) * cut]

    @pl.when(n == 0)
    def _():
        line.greet()

    line.start(n * per, per)
    for r in range(per):
        line.step(n * per + r)

    @pl.when(n == pl.num_programs(0) - 1)
    def _():
        line.drain()


def product_sum(lhs, spans, weights, cid):
    rows = lhs[0].shape[0]
    width, cols = weights.shape
    cut = math.gcd(rows, 128)
    tiles = width // SIZE
    blocks = (tiles * rows // cut, cut, SIZE)

    def body(*refs):
        product_kernel(cut, spans, refs[: len(lhs)], *refs[len(lhs) :])

    return pl.pallas_call(
        body,
        grid=(tiles,),
        in_specs=[pl.BlockSpec(memory_space=pltpu.VMEM)] * len(lhs)
        + [pl.BlockSpec((SIZE, cols), lambda n: (n, 0))],
        out_specs=pl.BlockSpec(memory_space=pl.ANY),
        out_shape=jax.ShapeDtypeStruct((rows, width), jnp.bfloat16),
        scratch_shapes=line_scratch(blocks),
        compiler_params=pltpu.CompilerParams(
            collective_id=cid, has_side_effects=True, vmem_limit_bytes=40 << 20
        ),
        cost_estimate=pl.CostEstimate(
            flops=120_000_000_000, bytes_accessed=40 << 20, transcendentals=0
        ),
    )(*lhs, weights)


def feed_tile(normed, cot, wd, wg, wu):
    gate = jnp.dot(normed, wg, preferred_element_type=jnp.float32)
    up = jnp.dot(normed, wu, preferred_element_type=jnp.float32)
    grad_hidden = jnp.dot(cot, wd, preferred_element_type=jnp.float32)
    sigmoid = 1.0 / (1.0 + jnp.exp(-gate))
    silu = gate * sigmoid
    return (
        (silu * up).astype(jnp.bfloat16),
        (grad_hidden * up * sigmoid * (1.0 + gate * (1.0 - sigmoid))).astype(jnp.bfloat16),
        (grad_hidden * silu).astype(jnp.bfloat16),
    )


def feed_kernel(normed_ref, cot_ref, wd_ref, wg_ref, wu_ref, hidden_ref, gate_ref, up_ref):
    hidden_ref[...], gate_ref[...], up_ref[...] = feed_tile(
        normed_ref[...], cot_ref[...], wd_ref[...], wg_ref[...], wu_ref[...]
    )


def feed(normed, cot, mlp_full, rows):
    width = cot.shape[1]
    wide = mlp_full.shape[1] // 3
    tiles = wide // SIZE
    tile = pl.BlockSpec((rows, SIZE), lambda n: (0, n))
    return pl.pallas_call(
        feed_kernel,
        grid=(tiles,),
        in_specs=[pl.BlockSpec((rows, width), lambda n: (0, 0), pipeline_mode=pl.Buffered(1))] * 2
        + [pl.BlockSpec((width, SIZE), lambda n, k=k: (0, k * tiles + n)) for k in range(3)],
        out_specs=[
            tile,
            tile,
            tile,
        ],
        out_shape=[jax.ShapeDtypeStruct((rows, wide), jnp.bfloat16)] * 3,
        compiler_params=pltpu.CompilerParams(vmem_limit_bytes=58 << 20),
        cost_estimate=pl.CostEstimate(
            flops=6 * rows * width * wide, bytes_accessed=60 << 20, transcendentals=rows * wide
        ),
    )(normed, cot, mlp_full, mlp_full, mlp_full)


def finish_kernel(
    prompt_tiles, x_ref, attn_ref, mlp_ref, gm_ref, back_ref, gain_ref, po_ref, co_ref, pg_ref, cg_ref
):
    i = pl.program_id(0)
    x = x_ref[...].astype(jnp.float32)
    result = (x + attn_ref[...].astype(jnp.float32)) + mlp_ref[...].astype(jnp.float32)
    result = result.astype(jnp.bfloat16)
    unit, inverse = normalize(x)
    grad = gm_ref[...].astype(jnp.float32) + norm_back(back_ref[...].astype(jnp.float32) * gain_ref[...], unit, inverse)

    @pl.when(i < prompt_tiles)
    def _():
        po_ref[...] = result
        pg_ref[...] = grad

    @pl.when(i >= prompt_tiles)
    def _():
        co_ref[...] = result
        cg_ref[...] = grad


def finish(x, attn_sum, mlp_sum, grad_middle, back, gain, prompt_rows):
    rows, width = x.shape
    tile = 128
    prompt_tiles = prompt_rows // tile
    every = pl.BlockSpec((tile, width), lambda i: (i, 0))
    first = pl.BlockSpec((tile, width), lambda i: (jnp.minimum(i, prompt_tiles - 1), 0))
    second = pl.BlockSpec((tile, width), lambda i: (jnp.maximum(i - prompt_tiles, 0), 0))
    shapes = [(prompt_rows, width), (rows - prompt_rows, width)]
    return pl.pallas_call(
        functools.partial(finish_kernel, prompt_tiles),
        grid=(rows // tile,),
        in_specs=[every] * 5 + [pl.BlockSpec((1, width), lambda i: (0, 0))],
        out_specs=[first, second, first, second],
        out_shape=[jax.ShapeDtypeStruct(shape, jnp.bfloat16) for shape in shapes]
        + [jax.ShapeDtypeStruct(shape, jnp.float32) for shape in shapes],
        compiler_params=pltpu.CompilerParams(vmem_limit_bytes=40 << 20),
        cost_estimate=pl.CostEstimate(
            flops=20 * x.size, bytes_accessed=20 * x.size, transcendentals=0
        ),
    )(x, attn_sum, mlp_sum, grad_middle, back, gain)


def per_device(
    prompt_x,
    cont_x,
    prompt_len,
    cont_seg,
    attn_gain,
    q_weight,
    key_matrix,
    value_matrix,
    o_weight,
    mlp_gain,
    gate_weight,
    up_weight,
    down_weight,
    prompt_cot,
    cont_cot,
):
    head_dim = HEAD_SIZE
    data = ("dp", "context")
    prompt_rows = prompt_x.shape[0]
    cont_rows = cont_x.shape[0]
    prompt_total = prompt_rows * lax.axis_size("context")
    q_cols = q_weight.shape[1]
    kv_cols = key_matrix.shape[1]
    q_heads = q_cols // head_dim
    kv_heads = kv_cols // head_dim
    qkv_cols = q_cols + 2 * kv_cols
    qkv_wide = qkv_cols + 2 + -(qkv_cols + 2) % 128
    hidden_cols = gate_weight.shape[1]
    wide = hidden_cols + -hidden_cols % 256
    context_pos = lax.axis_index("context")
    prompt_pos = context_pos * prompt_rows + jnp.arange(prompt_rows, dtype=jnp.int32)
    segment = cont_seg[0]
    earlier = jnp.sum((segment[None, :] < segment[:, None]).astype(jnp.int32), axis=1)
    local_index = jnp.arange(cont_rows, dtype=jnp.int32)
    length = prompt_len[0]
    cont_pos = length + local_index - earlier
    position = jnp.concatenate([prompt_pos, cont_pos]).astype(jnp.float32)
    inv_freq = THETA ** (-jnp.arange(head_dim // 2, dtype=jnp.float32) * 2.0 / head_dim)
    angle_table = inv_freq[:, None] * position[None, :]
    cosine = jnp.cos(angle_table)
    sine_table = jnp.sin(angle_table)
    shards = (down_weight, gate_weight, up_weight)
    attn_shards = (o_weight, q_weight, key_matrix, value_matrix)
    if lax.axis_size("dp") == 4 and lax.axis_size("context") == 2:
        info = jnp.stack([earlier, jnp.broadcast_to(length, earlier.shape)])
        packed_full, mlp_shard, x_all, grad_out, bias = plane_gather(
            attn_shards,
            (attn_gain, mlp_gain),
            info,
            shards,
            wide,
            q_cols + qkv_wide,
            prompt_x,
            cont_x,
            prompt_cot,
            cont_cot,
            6,
        )
    else:
        packed = jnp.concatenate([*attn_shards, attn_gain[:, None], mlp_gain[:, None]], axis=1)
        packed = jnp.pad(packed, ((0, 0), (0, q_cols + qkv_wide - packed.shape[1])))
        packed_full = lax.all_gather(packed, data, axis=0, tiled=True)
        fill = ((0, 0), (0, wide - hidden_cols))
        mlp_shard = jnp.concatenate([jnp.pad(w, fill) for w in shards], axis=1)
        x_all = jnp.concatenate([prompt_x, cont_x], axis=0)
        grad_out = jnp.concatenate([prompt_cot, cont_cot], axis=0)
        key_index = jnp.arange(prompt_total, dtype=jnp.int32)
        prompt_mask = jnp.concatenate(
            [
                key_index[:, None] <= prompt_pos[None, :],
                jnp.zeros((cont_rows, prompt_rows), jnp.bool_),
            ],
            axis=0,
        )
        own_mask = (segment[:, None] == segment[None, :]) & (
            local_index[:, None] <= local_index[None, :]
        )
        reach_mask = jnp.broadcast_to(key_index[:, None] < length, (prompt_total, cont_rows))
        allowed = jnp.concatenate(
            [prompt_mask, jnp.concatenate([reach_mask, own_mask], axis=0)], axis=1
        )
        bias = jnp.where(allowed, 0.0, NEGATIVE).astype(jnp.bfloat16)
    first_normed, q_t, cont_kv, gains, prompt_all = project_rope(
        x_all, packed_full, cosine, sine_table, q_heads, kv_heads, prompt_rows, 4
    )
    gain_one, gain_two = gains[0:1], gains[1:2]
    prompt_all, mlp_shard = lax.optimization_barrier((prompt_all, mlp_shard))
    mlp_full = lax.all_gather(mlp_shard, data, axis=0, tiled=True)
    attn_out, lse, attn_sum, normed_two = attend(
        q_t, prompt_all, cont_kv, bias, packed_full, x_all, gains, q_heads, kv_heads, 0
    )
    rows = prompt_rows + cont_rows
    early_rows = rows // 2 if rows % 1024 == 0 else rows - rows // 5
    hidden, grad_gate, grad_up = feed(normed_two, grad_out, mlp_full, early_rows)
    mlp_grads, up_grads, mlp_part, back_two = feed_back(
        hidden, grad_gate, grad_up, mlp_full, grad_out, normed_two, 1
    )

    def scatter(values):
        return lax.psum_scatter(values, data, scatter_dimension=0, tiled=True)

    cut = math.gcd(prompt_rows + cont_rows, SIZE // 2)
    grad_q, grad_kv, grad_middle, grad_rest, mlp_sum = window(
        q_t,
        prompt_all,
        cont_kv,
        bias,
        attn_out,
        lse,
        back_two,
        grad_out,
        x_all,
        attn_sum,
        gain_two,
        packed_full,
        cosine,
        sine_table,
        first_normed,
        up_grads,
        mlp_part.reshape(-1, cut, SIZE),
        q_heads,
        kv_heads,
        3,
    )
    mlp_own = scatter(mlp_grads)
    grad_q, grad_rest, mlp_own = lax.optimization_barrier((grad_q, grad_rest, mlp_own))
    back_one = product_sum(
        [grad_q, grad_kv], [(q_cols, 2 * q_cols), (2 * q_cols, q_cols + qkv_cols)], packed_full, 2
    )
    back_one, mlp_own = lax.optimization_barrier((back_one, mlp_own))
    outs = finish(x_all, attn_sum, mlp_sum, grad_middle, back_one, gain_one, prompt_rows)
    down_own = mlp_own[:, :hidden_cols].astype(jnp.float32)
    gate_own = mlp_own[:, wide : wide + hidden_cols].astype(jnp.float32)
    rest_own = scatter(grad_rest)
    up_own = rest_own[:, :hidden_cols].astype(jnp.float32)
    o_own = rest_own[:, wide : wide + q_cols].astype(jnp.float32)
    q_own = rest_own[:, wide + q_cols : wide + 2 * q_cols].astype(jnp.float32)
    k_own = rest_own[:, wide + 2 * q_cols : wide + 2 * q_cols + kv_cols].astype(jnp.float32)
    v_own = rest_own[:, wide + 2 * q_cols + kv_cols :].astype(jnp.float32)

    def row_dot(weight, grad):
        return jnp.sum(weight.astype(jnp.float32) * grad, axis=1)

    gain_rows = jnp.stack(
        [
            (row_dot(q_weight, q_own) + row_dot(key_matrix, k_own) + row_dot(value_matrix, v_own))
            / attn_gain.astype(jnp.float32),
            (row_dot(gate_weight, gate_own) + row_dot(up_weight, up_own))
            / mlp_gain.astype(jnp.float32),
        ]
    )
    gain_rows = tensor_total(gain_rows, 5)
    owned = (gain_rows[0], q_own, k_own, v_own, o_own, gain_rows[1], gate_own, up_own, down_own)
    return (*outs, *owned)


def solution(mesh):
    in_specs = (
        P(("dp", "context"), None),
        P(("dp", "context"), None),
        P("dp"),
        P(("dp", "context"), None),
        P(("dp", "context")),
        P(("dp", "context"), "tensor"),
        P(("dp", "context"), "tensor"),
        P(("dp", "context"), "tensor"),
        P(("dp", "context"), "tensor"),
        P(("dp", "context")),
        P(("dp", "context"), "tensor"),
        P(("dp", "context"), "tensor"),
        P(("dp", "context"), "tensor"),
        P(("dp", "context"), None),
        P(("dp", "context"), None),
    )
    out_specs = (
        P(("dp", "context"), None),
        P(("dp", "context"), None),
        P(("dp", "context"), None),
        P(("dp", "context"), None),
        P(("dp", "context")),
        P(("dp", "context"), "tensor"),
        P(("dp", "context"), "tensor"),
        P(("dp", "context"), "tensor"),
        P(("dp", "context"), "tensor"),
        P(("dp", "context")),
        P(("dp", "context"), "tensor"),
        P(("dp", "context"), "tensor"),
        P(("dp", "context"), "tensor"),
    )
    return jax.shard_map(
        per_device, mesh=mesh, in_specs=in_specs, out_specs=out_specs, check_vma=False
    )
```

```python
import functools
import math

import jax
import jax.numpy as jnp
from jax import lax
from jax.experimental import pallas as pl
from jax.experimental.pallas import tpu as pltpu
from jax.sharding import PartitionSpec as P

HEAD_SIZE = 80


EPS = 1e-05
THETA = 10000.0
NEGATIVE = -1e30
LOG2E = math.log2(math.e)
MESH = pl.DeviceIdType.MESH
AXIS = "tensor"
LAG = 3
SIZE = 256
FEED_STEPS = 10
SLOTS = 7


def normalize(values):
    inverse = lax.rsqrt(jnp.mean(values * values, axis=-1, keepdims=True) + EPS)
    return (values * inverse, inverse)


def norm_back(grad_unit, unit_rows, inverse):
    inner_sum = jnp.mean(grad_unit * unit_rows, axis=-1, keepdims=True)
    return inverse * (grad_unit - unit_rows * inner_sum)


def contract_last(left_side, right_side):
    return lax.dot_general(
        left_side, right_side, (((1,), (1,)), ((), ())), preferred_element_type=jnp.float32
    )


def contract_first(left_side, right_side):
    return lax.dot_general(
        left_side, right_side, (((0,), (0,)), ((), ())), preferred_element_type=jnp.float32
    )


def greet(axis, count):
    me = lax.axis_index(axis)
    barrier = pltpu.get_barrier_semaphore()
    for k in range(1, count):
        peer = lax.rem(me + k, count)
        pl.semaphore_signal(barrier, inc=1, device_id={axis: peer}, device_id_type=MESH)
    pl.semaphore_wait(barrier, count - 1)


def rope_kernel(
    q_heads,
    kv_heads,
    dim,
    prompt_steps,
    x_ref,
    w_ref,
    cos_ref,
    sin_ref,
    normed_ref,
    qt_ref,
    kvt_ref,
    gains_ref,
    all_ref,
    own,
    send,
    recv,
    local,
):
    i = pl.program_id(0)
    count = all_ref.shape[0]
    me = lax.axis_index("context")
    last = (q_heads + 2 * kv_heads + q_heads) * dim

    @pl.when(i == 0)
    def _():
        greet("context", count)
        low = last - last % 128
        turned = w_ref[:, low:].astype(jnp.float32).T
        gains_ref[...] = turned[last - low : last - low + 8]

    rows = x_ref[...].astype(jnp.float32)
    inverse = lax.rsqrt(jnp.mean(rows * rows, axis=-1, keepdims=True) + EPS)
    normed = (rows * inverse * gains_ref[0:1, :]).astype(jnp.bfloat16)
    normed_ref[...] = normed
    flat = jnp.dot(
        normed, w_ref[:, q_heads * dim :], preferred_element_type=jnp.float32
    ).T
    cosine, sine = cos_ref[...], sin_ref[...]
    half = dim // 2
    pieces = []
    for head in range(q_heads + kv_heads):
        first = flat[head * dim : head * dim + half]
        second = flat[head * dim + half : (head + 1) * dim]
        turned = jnp.concatenate(
            [first * cosine - second * sine, second * cosine + first * sine], axis=0
        ).astype(jnp.bfloat16)
        if head < q_heads:
            qt_ref[head * dim : (head + 1) * dim, :] = turned
        else:
            pieces.append(turned)
    at = (q_heads + kv_heads) * dim
    pieces.append(flat[at : at + kv_heads * dim].astype(jnp.bfloat16))
    low = 0
    for piece in pieces:
        kvt_ref[low : low + piece.shape[0], :] = piece
        low += piece.shape[0]
    step = x_ref.shape[0]
    for k in range(prompt_steps):

        @pl.when(i == k)
        def _():
            own[:, k * step : (k + 1) * step] = kvt_ref[...]

    def exchange(k):
        peer = lax.rem(me + k, count)
        return pltpu.make_async_remote_copy(
            own,
            all_ref.at[me],
            send.at[k],
            recv.at[k],
            device_id={"context": peer},
            device_id_type=MESH,
        )

    keep = pltpu.make_async_copy(own, all_ref.at[me], local)

    @pl.when(i == prompt_steps - 1)
    def _():
        for k in range(1, count):
            exchange(k).start()
        keep.start()

    @pl.when(i == pl.num_programs(0) - 1)
    def _():
        for k in range(1, count):
            exchange(k).wait()
        keep.wait()


def project_rope(x, packed_full, cos_t, sin_t, q_heads, kv_heads, prompt_rows, cid):
    rows, width = x.shape
    dim = HEAD_SIZE
    count = lax.axis_size("context")
    step = math.gcd(math.gcd(rows, prompt_rows), 256)
    cols_wide = packed_full.shape[1]
    kv2 = 2 * kv_heads * dim
    by_row = lambda i: (i, 0)
    by_col = lambda i: (0, i)
    fixed = lambda i: (0, 0)
    return pl.pallas_call(
        functools.partial(rope_kernel, q_heads, kv_heads, dim, prompt_rows // step),
        grid=(rows // step,),
        in_specs=[
            pl.BlockSpec((step, width), by_row),
            pl.BlockSpec(packed_full.shape, fixed, pipeline_mode=pl.Buffered(1)),
            pl.BlockSpec((dim // 2, step), by_col),
            pl.BlockSpec((dim // 2, step), by_col),
        ],
        out_specs=[
            pl.BlockSpec((step, width), by_row),
            pl.BlockSpec((q_heads * dim, step), by_col),
            pl.BlockSpec((kv2, step), by_col),
            pl.BlockSpec((8, width), fixed),
            pl.BlockSpec(memory_space=pltpu.HBM),
        ],
        out_shape=[
            jax.ShapeDtypeStruct((rows, width), jnp.bfloat16),
            jax.ShapeDtypeStruct((q_heads * dim, rows), jnp.bfloat16),
            jax.ShapeDtypeStruct((kv2, rows), jnp.bfloat16),
            jax.ShapeDtypeStruct((8, width), jnp.float32),
            jax.ShapeDtypeStruct((count, kv2, prompt_rows), jnp.bfloat16),
        ],
        scratch_shapes=[
            pltpu.VMEM((kv2, prompt_rows), jnp.bfloat16),
            pltpu.SemaphoreType.DMA((count,)),
            pltpu.SemaphoreType.DMA((count,)),
            pltpu.SemaphoreType.DMA,
        ],
        compiler_params=pltpu.CompilerParams(
            collective_id=cid, has_side_effects=True, vmem_limit_bytes=48 << 20
        ),
        cost_estimate=pl.CostEstimate(
            flops=2 * rows * width * cols_wide,
            bytes_accessed=4 * x.size + 2 * width * cols_wide,
            transcendentals=0,
        ),
    )(x, packed_full, cos_t, sin_t)


def attend_shape(prompt_all, kvt_cont):
    count, kv2, prompt_rows = prompt_all.shape
    cont_rows = kvt_cont.shape[1] - prompt_rows
    chunk = math.gcd(math.gcd(prompt_rows, cont_rows), 256)
    return count, kv2, prompt_rows, cont_rows, chunk


def total_kernel(count, part_ref, out_ref, got, send, recv):
    greet(AXIS, count)
    me = lax.axis_index(AXIS)
    copies = []
    for k in range(1, count):
        peer = lax.rem(me + k, count)
        copy = pltpu.make_async_remote_copy(
            part_ref,
            got.at[me],
            send.at[k],
            recv.at[k],
            device_id={AXIS: peer},
            device_id_type=MESH,
        )
        copy.start()
        copies.append(copy)
    got[me] = part_ref[...]
    for copy in copies:
        copy.wait()
    total = got[0]
    for k in range(1, count):
        total += got[k]
    out_ref[...] = total


def tensor_total(part, cid):
    count = lax.axis_size(AXIS)
    return pl.pallas_call(
        functools.partial(total_kernel, count),
        out_shape=jax.ShapeDtypeStruct(part.shape, part.dtype),
        in_specs=[pl.BlockSpec(memory_space=pltpu.VMEM)],
        out_specs=pl.BlockSpec(memory_space=pltpu.VMEM),
        scratch_shapes=[
            pltpu.VMEM((count, *part.shape), part.dtype),
            pltpu.SemaphoreType.DMA((count,)),
            pltpu.SemaphoreType.DMA((count,)),
        ],
        compiler_params=pltpu.CompilerParams(collective_id=cid, has_side_effects=True),
        cost_estimate=pl.CostEstimate(flops=0, bytes_accessed=4 << 20, transcendentals=0),
    )(part)


def plane_kernel(
    prompt_total,
    o_ref,
    q_ref,
    kt_ref,
    vt_ref,
    again_ref,
    mgain_ref,
    info_ref,
    w0_ref,
    w1_ref,
    w2_ref,
    px_ref,
    cx_ref,
    pc_ref,
    cc_ref,
    all_ref,
    shard_ref,
    x_ref,
    cot_ref,
    bias_ref,
    own_ref,
    stage,
    send,
    recv,
    local,
):
    dp, context = lax.axis_index("dp"), lax.axis_index("context")
    side = {"context": 1 - context}
    along = {"dp": lax.rem(dp + 2, 4)}
    twin_dp = dp + 1 - 2 * lax.rem(dp, 2)
    twin = {"dp": twin_dp}
    barrier = pltpu.get_barrier_semaphore()
    for peer in (side, along, twin):
        pl.semaphore_signal(barrier, inc=1, device_id=peer, device_id_type=MESH)
    pl.semaphore_wait(barrier, 3)
    rows = own_ref.shape[0]
    q_cols = q_ref.shape[1]
    own_ref[:, :q_cols] = o_ref[...]
    own_ref[:, q_cols : 2 * q_cols] = q_ref[...]
    small = [kt_ref[...], vt_ref[...], again_ref[...], mgain_ref[...]]
    rest = own_ref.shape[1] - 2 * q_cols
    used = sum(part.shape[0] for part in small)
    small.append(jnp.zeros((rest - used, rows), jnp.bfloat16))
    own_ref[:, 2 * q_cols :] = (
        jnp.concatenate([part.astype(jnp.float32) for part in small], axis=0).T
    ).astype(jnp.bfloat16)
    half = rows // 2
    mine = 2 * dp + context
    from_side = 2 * dp + 1 - context
    from_along = 2 * lax.rem(dp + 2, 4) + context
    from_far = 2 * lax.rem(dp + 2, 4) + 1 - context

    def spot(block, h):
        return pl.ds(pl.multiple_of(block * rows + h * half, half), half)

    def copy(k, block, h, peer, first=False):
        source = own_ref.at[pl.ds(h * half, half)] if first else all_ref.at[spot(block, h)]
        return pltpu.make_async_remote_copy(
            source,
            all_ref.at[spot(block, h)],
            send.at[k],
            recv.at[k],
            device_id=peer,
            device_id_type=MESH,
        )

    def land(k, block, h):
        return pltpu.make_async_remote_copy(
            own_ref.at[pl.ds(h * half, half)],
            all_ref.at[spot(block, h)],
            send.at[k],
            recv.at[k],
            device_id=side,
            device_id_type=MESH,
        )

    started = []

    def go(*args, **kwargs):
        one = copy(*args, **kwargs)
        one.start()
        started.append(one)

    go(0, mine, 0, side, first=True)
    go(2, mine, 1, along, first=True)
    go(1, mine, 1, side, first=True)
    go(3, mine, 0, along, first=True)
    go(6, mine, 0, twin, first=True)
    go(7, mine, 1, twin, first=True)
    prompt_rows = px_ref.shape[0]
    moves = [
        pltpu.make_async_copy(own_ref, all_ref.at[pl.ds(pl.multiple_of(mine * rows, rows), rows)], local.at[0]),
    ]
    moves[0].start()
    joins = []
    for k, (source, target, low) in enumerate(
        (
            (px_ref, x_ref, 0),
            (cx_ref, x_ref, prompt_rows),
            (pc_ref, cot_ref, 0),
            (cc_ref, cot_ref, prompt_rows),
        )
    ):
        rows_at = pl.ds((k % 2) * prompt_rows, source.shape[0])
        load = pltpu.make_async_copy(source, stage.at[k // 2, rows_at], local.at[1 + k])
        load.start()
        joins.append(
            (
                load,
                pltpu.make_async_copy(
                    stage.at[k // 2, rows_at],
                    target.at[pl.ds(low, source.shape[0])],
                    local.at[5 + k],
                ),
            )
        )
    cols = w0_ref.shape[1]
    wide = shard_ref.shape[1] // 3
    for k, ref in enumerate((w0_ref, w1_ref, w2_ref)):
        shard_ref[:, k * wide : k * wide + cols] = ref[...]
        shard_ref[:, k * wide + cols : (k + 1) * wide] = jnp.zeros(
            (rows, wide - cols), jnp.bfloat16
        )
    cont_rows = cx_ref.shape[0]
    block = 128

    def fill_bias(low, count, at, columns, rule):
        @pl.loop(0, count // block)
        def _(c):
            key = lax.broadcasted_iota(jnp.int32, (block, columns), 0) + c * block
            query = lax.broadcasted_iota(jnp.int32, (block, columns), 1)
            rows_at = pl.ds(pl.multiple_of(low + c * block, block), block)
            bias_ref[rows_at, at : at + columns] = jnp.where(
                rule(key, query), 0.0, NEGATIVE
            ).astype(jnp.bfloat16)

    first = context * prompt_rows
    earlier, length = info_ref[0:1, :], info_ref[1:2, :]
    fill_bias(0, prompt_total, 0, prompt_rows, lambda k, q: k <= q + first)
    fill_bias(prompt_total, cont_rows, 0, prompt_rows, lambda k, q: k < 0)
    fill_bias(0, prompt_total, prompt_rows, cont_rows, lambda k, q: k < length)
    fill_bias(
        prompt_total, cont_rows, prompt_rows, cont_rows, lambda k, q: (k >= earlier) & (k <= q)
    )
    for load, save in joins:
        load.wait()
        save.start()
        moves.append(save)
    land(0, from_side, 0).wait_recv()
    go(4, from_side, 0, along)
    go(8, from_side, 0, twin)
    land(2, from_along, 1).wait_recv()
    go(5, from_along, 1, side)
    go(9, from_along, 1, twin)
    land(1, from_side, 1).wait_recv()
    go(10, from_side, 1, twin)
    land(3, from_along, 0).wait_recv()
    go(11, from_along, 0, twin)
    land(4, from_far, 0).wait_recv()
    go(12, from_far, 0, twin)
    land(5, from_far, 1).wait_recv()
    go(13, from_far, 1, twin)
    base = 2 * twin_dp
    other = 2 * lax.rem(twin_dp + 2, 4)
    for k, block, h in (
        (6, base + context, 0),
        (7, base + context, 1),
        (8, base + 1 - context, 0),
        (9, other + context, 1),
        (10, base + 1 - context, 1),
        (11, other + context, 0),
        (12, other + 1 - context, 0),
        (13, other + 1 - context, 1),
    ):
        land(k, block, h).wait_recv()
    for one in started:
        one.wait_send()
    for move in moves:
        move.wait()


def plane_gather(
    attn, gains, info, weights, wide, attn_wide, prompt_x, cont_x, prompt_cot, cont_cot, cid
):
    o_weight, q_weight, key_matrix, value_matrix = attn
    rows = q_weight.shape[0]
    count = lax.axis_size("dp") * lax.axis_size("context")
    prompt_rows, width = prompt_x.shape
    total = prompt_rows + cont_x.shape[0]
    prompt_total = prompt_rows * lax.axis_size("context")
    hbm = pl.BlockSpec(memory_space=pltpu.HBM)
    vmem = pl.BlockSpec(memory_space=pltpu.VMEM)
    both = jax.ShapeDtypeStruct((total, width), jnp.bfloat16)
    return pl.pallas_call(
        functools.partial(plane_kernel, prompt_total),
        out_shape=[
            jax.ShapeDtypeStruct((count * rows, attn_wide), jnp.bfloat16),
            jax.ShapeDtypeStruct((rows, 3 * wide), jnp.bfloat16),
            both,
            both,
            jax.ShapeDtypeStruct((prompt_total + cont_x.shape[0], total), jnp.bfloat16),
        ],
        in_specs=[vmem] * 10 + [hbm] * 4,
        out_specs=[hbm, vmem, hbm, hbm, vmem],
        scratch_shapes=[
            pltpu.VMEM((rows, attn_wide), jnp.bfloat16),
            pltpu.VMEM((2, total, width), jnp.bfloat16),
            pltpu.SemaphoreType.DMA((14,)),
            pltpu.SemaphoreType.DMA((14,)),
            pltpu.SemaphoreType.DMA((9,)),
        ],
        compiler_params=pltpu.CompilerParams(
            collective_id=cid, has_side_effects=True, vmem_limit_bytes=60 << 20
        ),
        cost_estimate=pl.CostEstimate(
            flops=30_000_000_000, bytes_accessed=40 << 20, transcendentals=0
        ),
    )(
        o_weight,
        q_weight,
        key_matrix.T,
        value_matrix.T,
        gains[0][None, :],
        gains[1][None, :],
        info,
        *weights,
        prompt_x,
        cont_x,
        prompt_cot,
        cont_cot,
    )


def fill_keys(chunk, dim, kv_heads, all_ref, cont_ref, rows_of, chunks_ref):
    count, _, prompt_rows = all_ref.shape
    per = prompt_rows // chunk
    total = count * per + (cont_ref.shape[1] - prompt_rows) // chunk
    for c in range(total):
        if c < count * per:
            block = all_ref[c // per, :, (c % per) * chunk : (c % per + 1) * chunk]
        else:
            at = prompt_rows + (c - count * per) * chunk
            block = cont_ref[:, at : at + chunk]
        chunks_ref[c] = block
        for n, target in enumerate(rows_of):
            for g in range(kv_heads):
                at = (n * kv_heads + g) * dim
                target[g, c * chunk : (c + 1) * chunk, :] = (
                    block[at : at + dim].astype(jnp.float32).T.astype(jnp.bfloat16)
                )


def trip_count(tile, chunk, i, prompt_rows, count):
    me = lax.axis_index("context")
    prompt_tiles = prompt_rows // tile
    n_prompt = lax.div(me * prompt_rows + (i + 1) * tile + chunk - 1, chunk)
    n_own = lax.div((i - prompt_tiles + 1) * tile + chunk - 1, chunk)
    return i < prompt_tiles, n_prompt, count * prompt_rows // chunk, n_own


class Line:
    def __init__(self, part, recv, out, sink, sems, sink_sems, ready=None, place=None):
        self.ready, self.place = ready, place
        self.part, self.recv, self.out, self.sink = part, recv, out, sink
        self.per = sink.shape[0] // out.shape[1]
        self.sems, self.sink_sems = sems, sink_sems
        self.blocks = out.shape[0]
        me, n = lax.axis_index(AXIS), lax.axis_size(AXIS)
        self.outer = (me == 0) | (me == n - 1)
        self.inner = jnp.logical_not(self.outer)
        self.mate = jnp.where(me < n // 2, 1 - me, 2 * n - 3 - me)
        self.across = n - 1 - me

    def copy(self, k, source, target, peer, b):
        return pltpu.make_async_remote_copy(
            source.at[b],
            target.at[b],
            self.sems.at[2 * k, b],
            self.sems.at[2 * k + 1, b],
            device_id={AXIS: peer},
            device_id_type=MESH,
        )

    def up(self, b):
        return self.copy(0, self.part, self.recv, self.mate, b)

    def mid(self, b):
        return self.copy(1, self.part, self.out, self.across, b)

    def down(self, b):
        return self.copy(2, self.out, self.out, self.mate, b)

    def keep(self, b):
        _, rows, cols = self.out.shape
        row, col = lax.rem(b, self.per), lax.div(b, self.per)
        if self.place is not None:
            row, col = self.place(b)
        at = (
            pl.ds(pl.multiple_of(row * rows, rows), rows),
            pl.ds(pl.multiple_of(col * cols, cols), cols),
        )
        return pltpu.make_async_copy(self.out.at[b], self.sink.at[at], self.sink_sems.at[b])

    def greet(self, axis=None, count=1):
        barrier = pltpu.get_barrier_semaphore()
        pl.semaphore_signal(barrier, inc=1, device_id={AXIS: self.mate}, device_id_type=MESH)
        for k in range(1, count):
            peer = lax.rem(lax.axis_index(axis) + k, count)
            pl.semaphore_signal(barrier, inc=1, device_id={axis: peer}, device_id_type=MESH)

        @pl.when(self.inner)
        def _():
            pl.semaphore_signal(barrier, inc=1, device_id={AXIS: self.across}, device_id_type=MESH)
            pl.semaphore_wait(barrier, 1 + count)

        @pl.when(self.outer)
        def _():
            pl.semaphore_wait(barrier, count)

    def start(self, first, count):
        @pl.when(self.outer)
        def _():
            @pl.loop(0, count)
            def _(k):
                self.up(first + k).start()

    def step(self, t):
        @pl.when(self.inner & (t >= 0) & (t < self.blocks))
        def _():
            self.up(t).wait_recv()
            self.part[t] = (
                self.part[t].astype(jnp.float32) + self.recv[t].astype(jnp.float32)
            ).astype(jnp.bfloat16)
            self.mid(t).start()

        @pl.when(self.inner & (t >= LAG) & (t < self.blocks + LAG))
        def _():
            b = t - LAG
            self.mid(b).wait_recv()
            self.out[b] = (
                self.part[b].astype(jnp.float32) + self.out[b].astype(jnp.float32)
            ).astype(jnp.bfloat16)
            self.down(b).start()
            self.keep(b).start()
            if self.ready is not None:
                self.ready(b)

    def drain(self):
        for k in range(LAG):
            self.step(self.blocks + k)

        @pl.when(self.outer)
        def _():
            @pl.loop(0, self.blocks)
            def _(b):
                self.down(b).wait_recv()
                self.keep(b).start()
                if self.ready is not None:
                    self.ready(b)
                self.up(b).wait_send()

        @pl.when(self.inner)
        def _():
            @pl.loop(0, self.blocks)
            def _(b):
                self.mid(b).wait_send()
                self.down(b).wait_send()

        @pl.loop(0, self.blocks)
        def _(b):
            self.keep(b).wait()


def line_scratch(shape):
    return [pltpu.VMEM(shape, jnp.bfloat16)] * 3 + [
        pltpu.SemaphoreType.DMA((6, shape[0])),
        pltpu.SemaphoreType.DMA((shape[0],)),
    ]


def attend_kernel(
    shape,
    dim,
    kv_heads,
    per,
    tile,
    cut,
    q_ref,
    all_ref,
    cont_ref,
    bias_ref,
    wo_ref,
    x_ref,
    gains_ref,
    out_ref,
    lse_ref,
    sum_ref,
    normed_ref,
    keys,
    chunks,
    norm_buf,
    norm_sems,
    part,
    recv,
    out,
    sems,
    sink_sems,
):
    count, prompt_rows, chunk = shape
    i = pl.program_id(0)

    def norm_out(b):
        at = pl.ds(pl.multiple_of(b * cut, cut), cut)
        return pltpu.make_async_copy(norm_buf.at[b], normed_ref.at[at], norm_sems.at[b])

    def ready(b):
        at = pl.ds(pl.multiple_of(b * cut, cut), cut)
        unit, _ = normalize(x_ref[at, :].astype(jnp.float32) + out[b].astype(jnp.float32))
        norm_buf[b] = (unit * gains_ref[1:2, :]).astype(jnp.bfloat16)
        norm_out(b).start()

    line = Line(part, recv, out, sum_ref, sems, sink_sems, ready)
    blocks = tile // cut

    @pl.when(i == 0)
    def _():
        fill_keys(chunk, dim, kv_heads, all_ref, cont_ref, [keys], chunks)
        line.greet()

    is_prompt, n_prompt, base, n_own = trip_count(tile, chunk, i, prompt_rows, count)
    wide = per * tile
    factor = dim ** (-0.5) * LOG2E
    outs, sums = [], []
    for g in range(kv_heads):
        q = jnp.concatenate(
            [q_ref[(g * per + h) * dim : (g * per + h + 1) * dim, :] for h in range(per)], axis=1
        )

        def body(c, state):
            top, total, acc = state
            at = pl.ds(pl.multiple_of(c * chunk, chunk), chunk)
            s = jnp.dot(keys[g, at, :], q, preferred_element_type=jnp.float32)
            t = s * factor + jnp.concatenate([bias_ref[at, :].astype(jnp.float32)] * per, axis=1)
            new = jnp.maximum(top, jnp.max(t, axis=0, keepdims=True))
            p = jnp.exp2(t - new)
            scale = jnp.exp2(top - new)
            total = total * scale + jnp.sum(p, axis=0, keepdims=True)
            v = chunks[c, (kv_heads + g) * dim : (kv_heads + g + 1) * dim, :]
            acc = acc * scale + jnp.dot(
                v, p.astype(jnp.bfloat16), preferred_element_type=jnp.float32
            )
            return new, total, acc

        start = (
            jnp.full((1, wide), NEGATIVE, jnp.float32),
            jnp.zeros((1, wide), jnp.float32),
            jnp.zeros((dim, wide), jnp.float32),
        )
        state = lax.fori_loop(0, jnp.where(is_prompt, n_prompt, base), body, start)
        top, total, acc = lax.fori_loop(base, base + jnp.where(is_prompt, 0, n_own), body, state)
        acc = acc / total
        top = top + jnp.log2(total)
        outs += [acc[:, h * tile : (h + 1) * tile] for h in range(per)]
        sums += [top[:, h * tile : (h + 1) * tile] for h in range(per)]
        if g < kv_heads - 1:
            for r in range(blocks // 2):
                line.step((i - 1) * blocks + r)
    attended = jnp.concatenate(outs, axis=0).T.astype(jnp.bfloat16)
    out_ref[...] = attended
    lse_ref[...] = jnp.concatenate(sums, axis=0)
    term = contract_last(attended, wo_ref[...]).astype(jnp.bfloat16)
    for r in range(blocks):
        part[i * blocks + r] = term[r * cut : (r + 1) * cut]

    line.start(i * blocks, blocks)
    for r in range(blocks // 2, blocks):
        line.step((i - 1) * blocks + r)

    @pl.when(i == pl.num_programs(0) - 1)
    def _():
        @pl.loop(0, blocks)
        def _(r):
            line.step(i * blocks + r)

        line.drain()

        @pl.loop(0, line.blocks)
        def _(b):
            norm_out(b).wait()


def attend(q_t, prompt_all, kvt_cont, bias, packed_full, x, gains, q_heads, kv_heads, cid):
    dim = HEAD_SIZE
    count, kv2, prompt_rows, cont_rows, chunk = attend_shape(prompt_all, kvt_cont)
    q_cols, rows = q_t.shape
    width = packed_full.shape[0]
    keys_all = bias.shape[0]
    tile, cut = 128, 16
    whole = pl.BlockSpec(memory_space=pltpu.VMEM)
    by_col = lambda i: (0, i)
    return pl.pallas_call(
        functools.partial(
            attend_kernel,
            (count, prompt_rows, chunk),
            dim,
            kv_heads,
            q_heads // kv_heads,
            tile,
            cut,
        ),
        grid=(rows // tile,),
        in_specs=[
            pl.BlockSpec((q_cols, tile), by_col),
            whole,
            whole,
            pl.BlockSpec((keys_all, tile), by_col),
            pl.BlockSpec((width, q_cols), lambda i: (0, 0), pipeline_mode=pl.Buffered(1)),
            whole,
            whole,
        ],
        out_specs=[
            pl.BlockSpec((tile, q_cols), lambda i: (i, 0)),
            pl.BlockSpec((q_heads, tile), by_col),
            pl.BlockSpec(memory_space=pl.ANY),
            pl.BlockSpec(memory_space=pl.ANY),
        ],
        out_shape=[
            jax.ShapeDtypeStruct((rows, q_cols), jnp.bfloat16),
            jax.ShapeDtypeStruct((q_heads, rows), jnp.float32),
            jax.ShapeDtypeStruct((rows, width), jnp.bfloat16),
            jax.ShapeDtypeStruct((rows, width), jnp.bfloat16),
        ],
        scratch_shapes=[
            pltpu.VMEM((kv_heads, keys_all, dim), jnp.bfloat16),
            pltpu.VMEM((keys_all // chunk, kv2, chunk), jnp.bfloat16),
            pltpu.VMEM((rows // cut, cut, width), jnp.bfloat16),
            pltpu.SemaphoreType.DMA((rows // cut,)),
            *line_scratch((rows // cut, cut, width)),
        ],
        compiler_params=pltpu.CompilerParams(
            collective_id=cid, has_side_effects=True, vmem_limit_bytes=56 << 20
        ),
        cost_estimate=pl.CostEstimate(
            flops=120_000_000_000, bytes_accessed=40 << 20, transcendentals=0
        ),
    )(q_t, prompt_all, kvt_cont, bias, packed_full, x, gains)


def feed_back_kernel(
    cut,
    hidden_in,
    gate_in,
    up_in,
    normed_late,
    cot_late,
    fd_ref,
    fg_ref,
    fu_ref,
    wd_ref,
    wg_ref,
    wu_ref,
    cot_ref,
    normed_ref,
    grads_ref,
    up_grads_ref,
    mlp_ref,
    sum_ref,
    hidden,
    gate,
    up,
    late_sems,
    part,
    recv,
    out,
    sems,
    sink_sems,
):
    i = pl.program_id(0)
    rows, wide = gate.shape
    first = hidden_in.shape[0]
    tiles = sum_ref.shape[1] // SIZE
    feeds = wide // SIZE
    low, high = first // cut, (rows - first) // cut
    split = tiles * low

    def place(b):
        early = b < split
        c = b - split
        row = jnp.where(early, lax.rem(b, low), low + lax.rem(c, high))
        return row, jnp.where(early, lax.div(b, low), lax.div(c, high))

    line = Line(part, recv, out, sum_ref, sems, sink_sems, place=place)

    def loads():
        return [
            pltpu.make_async_copy(source, target.at[pl.ds(0, first)], late_sems.at[k])
            for k, (source, target) in enumerate(((gate_in, gate), (up_in, up), (hidden_in, hidden)))
        ]

    def produce(at, block, count):
        back = contract_last(gate[at, :], wg_ref[...]) + contract_last(up[at, :], wu_ref[...])
        back = back.astype(jnp.bfloat16)
        for r in range(count):
            part[block + r] = back[r * cut : (r + 1) * cut]
        line.start(block, count)

    def steps(start, stop):
        @pl.loop(start, stop)
        def _(t):
            line.step(t)

    @pl.when(i == 0)
    def _():
        for load in loads():
            load.start()
        line.greet()
        for load in loads():
            load.wait()

    @pl.when(i < tiles)
    def _():
        produce(slice(0, first), i * low, low)

    beside = min(split, FEED_STEPS)

    @pl.when((i >= tiles) & (i < tiles + feeds))
    def _():
        m = i - tiles
        here = pl.ds(pl.multiple_of(m * SIZE, SIZE), SIZE)
        hidden[first:, here], gate[first:, here], up[first:, here] = feed_tile(
            normed_late[...], cot_late[...], fd_ref[...], fg_ref[...], fu_ref[...]
        )
        steps(lax.div(m * beside, feeds), lax.div((m + 1) * beside, feeds))

    @pl.when(i >= tiles + feeds)
    def _():
        n = i - tiles - feeds
        produce(slice(first, rows), split + n * high, high)
        rest = line.blocks - beside
        spots = 4

        def step(k):
            start = beside + lax.div((n * spots + k) * rest, tiles * spots)
            steps(start, beside + lax.div((n * spots + k + 1) * rest, tiles * spots))

        step(0)
        grads_ref[:, :wide] = contract_first(cot_ref[...], hidden[...]).astype(jnp.bfloat16)
        step(1)
        grads_ref[:, wide:] = contract_first(normed_ref[...], gate[...]).astype(jnp.bfloat16)
        step(2)
        up_grads_ref[...] = contract_first(normed_ref[...], up[...]).astype(jnp.bfloat16)
        step(3)
        mlp_ref[0] = contract_last(hidden[...], wd_ref[...]).astype(jnp.bfloat16)

        @pl.when(n == tiles - 1)
        def _():
            line.drain()


def feed_back(hidden, grad_gate, grad_up, mlp_full, cot, normed, cid):
    first, wide = hidden.shape
    rows, width = cot.shape
    cut = math.gcd(math.gcd(rows, first), SIZE)
    tiles, feeds = width // SIZE, wide // SIZE
    blocks = (tiles * rows // cut, cut, SIZE)
    anywhere = pl.BlockSpec(memory_space=pltpu.HBM)
    second = lambda i: (first // (rows - first), 0)
    late = lambda i: jnp.maximum(i - tiles - feeds, 0)
    back = lambda i: jnp.where(i < tiles, i, late(i))
    ahead = lambda i: jnp.clip(i - tiles, 0, feeds - 1)
    return pl.pallas_call(
        functools.partial(feed_back_kernel, cut),
        grid=(2 * tiles + feeds,),
        in_specs=[anywhere] * 3
        + [pl.BlockSpec((rows - first, width), second, pipeline_mode=pl.Buffered(1))] * 2
        + [pl.BlockSpec((width, SIZE), lambda i, k=k: (0, k * feeds + ahead(i))) for k in range(3)]
        + [pl.BlockSpec((SIZE, wide), lambda i: (late(i), 0))]
        + [pl.BlockSpec((SIZE, wide), lambda i, k=k: (back(i), k)) for k in (1, 2)]
        + [pl.BlockSpec((rows, SIZE), lambda i: (0, late(i)))] * 2,
        out_specs=[
            pl.BlockSpec((SIZE, 2 * wide), lambda i: (late(i), 0)),
            pl.BlockSpec((SIZE, wide), lambda i: (late(i), 0)),
            pl.BlockSpec((1, rows, SIZE), lambda i: (late(i), 0, 0)),
            pl.BlockSpec(memory_space=pl.ANY),
        ],
        out_shape=[
            jax.ShapeDtypeStruct((width, 2 * wide), jnp.bfloat16),
            jax.ShapeDtypeStruct((width, wide), jnp.bfloat16),
            jax.ShapeDtypeStruct((tiles, rows, SIZE), jnp.bfloat16),
            jax.ShapeDtypeStruct((rows, width), jnp.bfloat16),
        ],
        scratch_shapes=[
            pltpu.VMEM((rows, wide), jnp.bfloat16),
            pltpu.VMEM((rows, wide), jnp.bfloat16),
            pltpu.VMEM((rows, wide), jnp.bfloat16),
            pltpu.SemaphoreType.DMA((3,)),
            *line_scratch(blocks),
        ],
        compiler_params=pltpu.CompilerParams(
            collective_id=cid, has_side_effects=True, vmem_limit_bytes=61 << 20
        ),
        cost_estimate=pl.CostEstimate(
            flops=12 * rows * wide * width, bytes_accessed=200 << 20, transcendentals=0
        ),
    )(
        hidden,
        grad_gate,
        grad_up,
        normed,
        cot,
        mlp_full,
        mlp_full,
        mlp_full,
        mlp_full,
        mlp_full,
        mlp_full,
        cot,
        normed,
    )


def window_kernel(
    shape,
    dim,
    kv_heads,
    per,
    tile,
    q_ref,
    all_ref,
    cont_ref,
    bias_ref,
    out_ref,
    lse_ref,
    back_ref,
    cot_ref,
    x_ref,
    attn_ref,
    gain_ref,
    wo_ref,
    cos_ref,
    sin_ref,
    cos_own_ref,
    sin_own_ref,
    normed_ref,
    att_ref,
    up_grads_ref,
    mlp_ref,
    gq_out_ref,
    gkv_ref,
    gm_ref,
    grads_ref,
    sum_ref,
    keys,
    values,
    chunks,
    gk,
    gv,
    gm,
    gq_ref,
    send_ref,
    got,
    own_ref,
    kv_sems,
    part,
    recv,
    out,
    sems,
    sink_sems,
):
    count, prompt_rows, chunk = shape
    i = pl.program_id(0)
    line = Line(part, recv, out, sum_ref, sems, sink_sems)
    context = lax.axis_index("context")
    prompt_tiles = prompt_rows // tile
    tiles = gq_ref.shape[0] // tile
    slots = SLOTS
    spots = 2 + kv_heads

    def step(k):
        for s in range(k * slots // spots, (k + 1) * slots // spots):
            line.step(i * slots + s)

    def send(k):
        peer = lax.rem(context + k, count)
        return pltpu.make_async_remote_copy(
            send_ref.at[peer],
            got.at[k],
            kv_sems.at[0, k],
            kv_sems.at[1, k],
            device_id={"context": peer},
            device_id_type=MESH,
        )

    root = dim ** (-0.5)
    half = dim // 2

    @pl.when(i == 0)
    def _():
        load = pltpu.make_async_copy(mlp_ref, part, sink_sems.at[0])
        load.start()
        fill_keys(chunk, dim, kv_heads, all_ref, cont_ref, [keys, values], chunks)
        gk[...] = jnp.zeros_like(gk)
        gv[...] = jnp.zeros_like(gv)
        line.greet("context", count)
        load.wait()
        line.start(0, line.blocks)

    @pl.when(i < tiles)
    def _():
        middle = x_ref[...].astype(jnp.float32) + attn_ref[...].astype(jnp.float32)
        inverse = lax.rsqrt(jnp.mean(middle * middle, axis=-1, keepdims=True) + EPS)
        unit = middle * inverse
        grad_unit = back_ref[...].astype(jnp.float32) * gain_ref[...]
        grad_middle = cot_ref[...].astype(jnp.float32) + norm_back(grad_unit, unit, inverse)
        gm_ref[...] = grad_middle.astype(jnp.bfloat16)
        grad_b = grad_middle.astype(jnp.bfloat16)
        step(0)
        grad_t = (
            jnp.dot(grad_b, wo_ref[...], preferred_element_type=jnp.float32).astype(jnp.bfloat16)
        ).astype(jnp.float32).T
        gm[pl.ds(pl.multiple_of(i * tile, tile), tile), :] = grad_b
        step(1)

        is_prompt, n_prompt, base, n_own = trip_count(tile, chunk, i, prompt_rows, count)
        factor = root * LOG2E
        prod = grad_t * out_ref[...].astype(jnp.float32).T
        grad_t = grad_t.astype(jnp.bfloat16)
        cosine, sine = cos_ref[...], sin_ref[...]
        pieces = []
        for g in range(kv_heads):
            heads = [g * per + h for h in range(per)]
            q = jnp.concatenate([q_ref[h * dim : (h + 1) * dim, :] for h in heads], axis=1)
            grad = jnp.concatenate([grad_t[h * dim : (h + 1) * dim] for h in heads], axis=1)
            inner = jnp.concatenate(
                [jnp.sum(prod[h * dim : (h + 1) * dim], axis=0, keepdims=True) for h in heads], axis=1
            )
            lse = jnp.concatenate([lse_ref[h : h + 1, :] for h in heads], axis=1)

            def body(c, acc):
                at = pl.ds(pl.multiple_of(c * chunk, chunk), chunk)
                s = jnp.dot(keys[g, at, :], q, preferred_element_type=jnp.float32)
                b = bias_ref[at, :].astype(jnp.float32)
                p = jnp.exp2(s * factor + (jnp.concatenate([b] * per, axis=1) - lse))
                dp = jnp.dot(values[g, at, :], grad, preferred_element_type=jnp.float32)
                ds = (p * (dp - inner)).astype(jnp.bfloat16)
                gv[g, at, :] += contract_last(p.astype(jnp.bfloat16), grad)
                gk[g, at, :] += contract_last(ds, q)
                k_t = chunks[c, g * dim : (g + 1) * dim, :]
                return acc + jnp.dot(k_t, ds, preferred_element_type=jnp.float32)

            acc = jnp.zeros((dim, per * tile), jnp.float32)
            acc = lax.fori_loop(0, jnp.where(is_prompt, n_prompt, base), body, acc)
            acc = lax.fori_loop(base, base + jnp.where(is_prompt, 0, n_own), body, acc)
            acc = acc * root
            for h in range(per):
                first = acc[:half, h * tile : (h + 1) * tile]
                second = acc[half:, h * tile : (h + 1) * tile]
                pieces += [first * cosine + second * sine, second * cosine - first * sine]
            step(2 + g)
        rows_q = jnp.concatenate(pieces, axis=0).T.astype(jnp.bfloat16)
        gq_ref[pl.ds(pl.multiple_of(i * tile, tile), tile), :] = rows_q
        gq_out_ref[...] = rows_q

    @pl.when(i == tiles - 1)
    def _():
        for g in range(kv_heads):
            for n, (acc, scale) in enumerate(((gk, root), (gv, 1.0))):
                at = (n * kv_heads + g) * dim
                for c in range(count):
                    rows = acc[g, c * prompt_rows : (c + 1) * prompt_rows, :]
                    send_ref[c, at : at + dim, :] = (rows * scale).T.astype(jnp.bfloat16)
                own_ref[at : at + dim, :] = (acc[g, count * prompt_rows :, :] * scale).T
        for k in range(1, count):
            send(k).start()

    @pl.when(i == tiles)
    def _():
        line.step(tiles * slots)
        kv_dim = kv_heads * dim

        def finish(flat, cosine, sine):
            pieces = []
            for at in range(0, kv_dim, dim):
                first, second = flat[at : at + half], flat[at + half : at + dim]
                pieces += [first * cosine + second * sine, second * cosine - first * sine]
            pieces.append(flat[kv_dim:])
            return jnp.concatenate(pieces, axis=0).T.astype(jnp.bfloat16)

        cosine, sine = cos_own_ref[...], sin_own_ref[...]
        gkv_ref[prompt_rows:, :] = finish(
            own_ref[...], cosine[:, prompt_rows:], sine[:, prompt_rows:]
        )
        total = send_ref[context].astype(jnp.float32)
        for k in range(1, count):
            send(k).wait()
            total += got[k].astype(jnp.float32)
        gkv_ref[:prompt_rows, :] = finish(
            total, cosine[:, :prompt_rows], sine[:, :prompt_rows]
        )

    @pl.when(i >= tiles)
    def _():
        n = i - tiles
        later = pl.num_programs(0) - tiles
        rest = line.blocks - tiles * slots - 1
        q_cols = gq_ref.shape[1]
        wide = up_grads_ref.shape[1]
        here = pl.ds(pl.multiple_of(n * SIZE, SIZE), SIZE)
        grads_ref[:, :wide] = up_grads_ref[...]
        grads_ref[:, wide : wide + q_cols] = contract_first(gm[:, here], att_ref[...]).astype(
            jnp.bfloat16
        )
        grads_ref[:, wide + q_cols : wide + 2 * q_cols] = contract_first(
            normed_ref[...], gq_ref[...]
        ).astype(jnp.bfloat16)
        grads_ref[:, wide + 2 * q_cols :] = contract_first(normed_ref[...], gkv_ref[...]).astype(
            jnp.bfloat16
        )
        low = tiles * slots + 1 + lax.div(n * rest, later)
        high = tiles * slots + 1 + lax.div((n + 1) * rest, later)

        @pl.loop(low, high)
        def _(t):
            line.step(t)

        @pl.when(n == later - 1)
        def _():
            line.drain()


def window(
    q_t,
    prompt_all,
    kvt_cont,
    bias,
    attended,
    lse,
    back,
    cot,
    x,
    attn_sum,
    gain,
    packed_full,
    cos_t,
    sin_t,
    normed,
    up_grads,
    mlp_part,
    q_heads,
    kv_heads,
    cid,
):
    dim = HEAD_SIZE
    count, kv2, prompt_rows, cont_rows, chunk = attend_shape(prompt_all, kvt_cont)
    rows, width = cot.shape
    q_cols = q_heads * dim
    keys_all = bias.shape[0]
    tile = 128
    whole = pl.BlockSpec(memory_space=pltpu.VMEM)
    anywhere = pl.BlockSpec(memory_space=pl.ANY)
    tiles, later = rows // tile, width // SIZE
    grad_cols = up_grads.shape[1] + 2 * q_cols + kv2
    early = lambda i: jnp.minimum(i, tiles - 1)
    late = lambda i: jnp.maximum(i - tiles, 0)
    by_col = lambda i: (0, early(i))
    by_row = lambda i: (early(i), 0)
    fixed = lambda i: (0, 0)
    return pl.pallas_call(
        functools.partial(
            window_kernel, (count, prompt_rows, chunk), dim, kv_heads, q_heads // kv_heads, tile
        ),
        grid=(tiles + later,),
        in_specs=[
            pl.BlockSpec((q_cols, tile), by_col),
            whole,
            whole,
            pl.BlockSpec((keys_all, tile), by_col),
            pl.BlockSpec((tile, q_cols), by_row),
            pl.BlockSpec((q_heads, tile), by_col),
            pl.BlockSpec((tile, width), by_row),
            pl.BlockSpec((tile, width), by_row),
            pl.BlockSpec((tile, width), by_row),
            pl.BlockSpec((tile, width), by_row),
            pl.BlockSpec((1, width), fixed),
            pl.BlockSpec((width, q_cols), fixed, pipeline_mode=pl.Buffered(1)),
            pl.BlockSpec((dim // 2, tile), by_col),
            pl.BlockSpec((dim // 2, tile), by_col),
            whole,
            whole,
            pl.BlockSpec((rows, SIZE), lambda i: (0, late(i))),
            whole,
            pl.BlockSpec((SIZE, up_grads.shape[1]), lambda i: (late(i), 0)),
            anywhere,
        ],
        out_specs=[
            pl.BlockSpec((tile, q_cols), by_row),
            pl.BlockSpec((rows, kv2), fixed),
            pl.BlockSpec((tile, width), by_row),
            pl.BlockSpec((SIZE, grad_cols), lambda i: (late(i), 0)),
            anywhere,
        ],
        out_shape=[
            jax.ShapeDtypeStruct((rows, q_cols), jnp.bfloat16),
            jax.ShapeDtypeStruct((rows, kv2), jnp.bfloat16),
            jax.ShapeDtypeStruct((rows, width), jnp.bfloat16),
            jax.ShapeDtypeStruct((width, grad_cols), jnp.bfloat16),
            jax.ShapeDtypeStruct((rows, width), jnp.bfloat16),
        ],
        scratch_shapes=[
            pltpu.VMEM((kv_heads, keys_all, dim), jnp.bfloat16),
            pltpu.VMEM((kv_heads, keys_all, dim), jnp.bfloat16),
            pltpu.VMEM((keys_all // chunk, kv2, chunk), jnp.bfloat16),
            pltpu.VMEM((kv_heads, keys_all, dim), jnp.float32),
            pltpu.VMEM((kv_heads, keys_all, dim), jnp.float32),
            pltpu.VMEM((rows, width), jnp.bfloat16),
            pltpu.VMEM((rows, q_cols), jnp.bfloat16),
            pltpu.VMEM((count, kv2, prompt_rows), jnp.bfloat16),
            pltpu.VMEM((count, kv2, prompt_rows), jnp.bfloat16),
            pltpu.VMEM((kv2, cont_rows), jnp.float32),
            pltpu.SemaphoreType.DMA((2, count)),
            *line_scratch(mlp_part.shape),
        ],
        compiler_params=pltpu.CompilerParams(
            collective_id=cid, has_side_effects=True, vmem_limit_bytes=60 << 20
        ),
        cost_estimate=pl.CostEstimate(
            flops=120_000_000_000, bytes_accessed=200 << 20, transcendentals=0
        ),
    )(
        q_t,
        prompt_all,
        kvt_cont,
        bias,
        attended,
        lse,
        back,
        cot,
        x,
        attn_sum,
        gain,
        packed_full,
        cos_t,
        sin_t,
        cos_t,
        sin_t,
        normed,
        attended,
        up_grads,
        mlp_part,
    )


def product_kernel(cut, spans, lhs_refs, w_ref, sum_ref, part, recv, out, sems, sink_sems):
    n = pl.program_id(0)
    per = sum_ref.shape[0] // cut
    line = Line(part, recv, out, sum_ref, sems, sink_sems)
    term = sum(
        contract_last(ref[...], w_ref[:, low:high]) for ref, (low, high) in zip(lhs_refs, spans)
    ).astype(jnp.bfloat16)
    for r in range(per):
        part[n * per + r] = term[r * cut : (r + 1) * cut]

    @pl.when(n == 0)
    def _():
        line.greet()

    line.start(n * per, per)
    for r in range(per):
        line.step(n * per + r)

    @pl.when(n == pl.num_programs(0) - 1)
    def _():
        line.drain()


def product_sum(lhs, spans, weights, cid):
    rows = lhs[0].shape[0]
    width, cols = weights.shape
    cut = math.gcd(rows, 128)
    tiles = width // SIZE
    blocks = (tiles * rows // cut, cut, SIZE)

    def body(*refs):
        product_kernel(cut, spans, refs[: len(lhs)], *refs[len(lhs) :])

    return pl.pallas_call(
        body,
        grid=(tiles,),
        in_specs=[pl.BlockSpec(memory_space=pltpu.VMEM)] * len(lhs)
        + [pl.BlockSpec((SIZE, cols), lambda n: (n, 0))],
        out_specs=pl.BlockSpec(memory_space=pl.ANY),
        out_shape=jax.ShapeDtypeStruct((rows, width), jnp.bfloat16),
        scratch_shapes=line_scratch(blocks),
        compiler_params=pltpu.CompilerParams(
            collective_id=cid, has_side_effects=True, vmem_limit_bytes=60 << 20
        ),
        cost_estimate=pl.CostEstimate(
            flops=120_000_000_000, bytes_accessed=40 << 20, transcendentals=0
        ),
    )(*lhs, weights)


def feed_tile(normed, cot, wd, wg, wu):
    gate = jnp.dot(normed, wg, preferred_element_type=jnp.float32)
    up = jnp.dot(normed, wu, preferred_element_type=jnp.float32)
    grad_hidden = jnp.dot(cot, wd, preferred_element_type=jnp.float32)
    sigmoid = 1.0 / (1.0 + jnp.exp(-gate))
    silu = gate * sigmoid
    return (
        (silu * up).astype(jnp.bfloat16),
        (grad_hidden * up * sigmoid * (1.0 + gate * (1.0 - sigmoid))).astype(jnp.bfloat16),
        (grad_hidden * silu).astype(jnp.bfloat16),
    )


def feed_kernel(normed_ref, cot_ref, wd_ref, wg_ref, wu_ref, hidden_ref, gate_ref, up_ref):
    hidden_ref[...], gate_ref[...], up_ref[...] = feed_tile(
        normed_ref[...], cot_ref[...], wd_ref[...], wg_ref[...], wu_ref[...]
    )


def feed(normed, cot, mlp_full, rows):
    width = cot.shape[1]
    wide = mlp_full.shape[1] // 3
    tiles = wide // SIZE
    tile = pl.BlockSpec((rows, SIZE), lambda n: (0, n))
    return pl.pallas_call(
        feed_kernel,
        grid=(tiles,),
        in_specs=[pl.BlockSpec((rows, width), lambda n: (0, 0), pipeline_mode=pl.Buffered(1))] * 2
        + [pl.BlockSpec((width, SIZE), lambda n, k=k: (0, k * tiles + n)) for k in range(3)],
        out_specs=[
            tile,
            tile,
            tile,
        ],
        out_shape=[jax.ShapeDtypeStruct((rows, wide), jnp.bfloat16)] * 3,
        compiler_params=pltpu.CompilerParams(vmem_limit_bytes=58 << 20),
        cost_estimate=pl.CostEstimate(
            flops=6 * rows * width * wide, bytes_accessed=60 << 20, transcendentals=rows * wide
        ),
    )(normed, cot, mlp_full, mlp_full, mlp_full)


def finish_kernel(
    prompt_tiles, x_ref, attn_ref, mlp_ref, gm_ref, back_ref, gain_ref, po_ref, co_ref, pg_ref, cg_ref
):
    i = pl.program_id(0)
    x = x_ref[...].astype(jnp.float32)
    result = (x + attn_ref[...].astype(jnp.float32)) + mlp_ref[...].astype(jnp.float32)
    result = result.astype(jnp.bfloat16)
    unit, inverse = normalize(x)
    grad = gm_ref[...].astype(jnp.float32) + norm_back(back_ref[...].astype(jnp.float32) * gain_ref[...], unit, inverse)

    @pl.when(i < prompt_tiles)
    def _():
        po_ref[...] = result
        pg_ref[...] = grad

    @pl.when(i >= prompt_tiles)
    def _():
        co_ref[...] = result
        cg_ref[...] = grad


def finish(x, attn_sum, mlp_sum, grad_middle, back, gain, prompt_rows):
    rows, width = x.shape
    tile = 128
    prompt_tiles = prompt_rows // tile
    every = pl.BlockSpec((tile, width), lambda i: (i, 0))
    first = pl.BlockSpec((tile, width), lambda i: (jnp.minimum(i, prompt_tiles - 1), 0))
    second = pl.BlockSpec((tile, width), lambda i: (jnp.maximum(i - prompt_tiles, 0), 0))
    shapes = [(prompt_rows, width), (rows - prompt_rows, width)]
    return pl.pallas_call(
        functools.partial(finish_kernel, prompt_tiles),
        grid=(rows // tile,),
        in_specs=[every] * 5 + [pl.BlockSpec((1, width), lambda i: (0, 0))],
        out_specs=[first, second, first, second],
        out_shape=[jax.ShapeDtypeStruct(shape, jnp.bfloat16) for shape in shapes]
        + [jax.ShapeDtypeStruct(shape, jnp.float32) for shape in shapes],
        compiler_params=pltpu.CompilerParams(vmem_limit_bytes=60 << 20),
        cost_estimate=pl.CostEstimate(
            flops=20 * x.size, bytes_accessed=20 * x.size, transcendentals=0
        ),
    )(x, attn_sum, mlp_sum, grad_middle, back, gain)


def per_device(
    prompt_x,
    cont_x,
    prompt_len,
    cont_seg,
    attn_gain,
    q_weight,
    key_matrix,
    value_matrix,
    o_weight,
    mlp_gain,
    gate_weight,
    up_weight,
    down_weight,
    prompt_cot,
    cont_cot,
):
    head_dim = HEAD_SIZE
    data = ("dp", "context")
    prompt_rows = prompt_x.shape[0]
    cont_rows = cont_x.shape[0]
    prompt_total = prompt_rows * lax.axis_size("context")
    q_cols = q_weight.shape[1]
    kv_cols = key_matrix.shape[1]
    q_heads = q_cols // head_dim
    kv_heads = kv_cols // head_dim
    qkv_cols = q_cols + 2 * kv_cols
    qkv_wide = qkv_cols + 2 + -(qkv_cols + 2) % 128
    hidden_cols = gate_weight.shape[1]
    wide = hidden_cols + -hidden_cols % 256
    context_pos = lax.axis_index("context")
    prompt_pos = context_pos * prompt_rows + jnp.arange(prompt_rows, dtype=jnp.int32)
    segment = cont_seg[0]
    earlier = jnp.sum((segment[None, :] < segment[:, None]).astype(jnp.int32), axis=1)
    local_index = jnp.arange(cont_rows, dtype=jnp.int32)
    length = prompt_len[0]
    cont_pos = length + local_index - earlier
    position = jnp.concatenate([prompt_pos, cont_pos]).astype(jnp.float32)
    inv_freq = THETA ** (-jnp.arange(head_dim // 2, dtype=jnp.float32) * 2.0 / head_dim)
    angle_table = inv_freq[:, None] * position[None, :]
    cosine = jnp.cos(angle_table)
    sine_table = jnp.sin(angle_table)
    shards = (down_weight, gate_weight, up_weight)
    attn_shards = (o_weight, q_weight, key_matrix, value_matrix)
    if lax.axis_size("dp") == 4 and lax.axis_size("context") == 2:
        info = jnp.stack([earlier, jnp.broadcast_to(length, earlier.shape)])
        packed_full, mlp_shard, x_all, grad_out, bias = plane_gather(
            attn_shards,
            (attn_gain, mlp_gain),
            info,
            shards,
            wide,
            q_cols + qkv_wide,
            prompt_x,
            cont_x,
            prompt_cot,
            cont_cot,
            6,
        )
    else:
        packed = jnp.concatenate([*attn_shards, attn_gain[:, None], mlp_gain[:, None]], axis=1)
        packed = jnp.pad(packed, ((0, 0), (0, q_cols + qkv_wide - packed.shape[1])))
        packed_full = lax.all_gather(packed, data, axis=0, tiled=True)
        fill = ((0, 0), (0, wide - hidden_cols))
        mlp_shard = jnp.concatenate([jnp.pad(w, fill) for w in shards], axis=1)
        x_all = jnp.concatenate([prompt_x, cont_x], axis=0)
        grad_out = jnp.concatenate([prompt_cot, cont_cot], axis=0)
        key_index = jnp.arange(prompt_total, dtype=jnp.int32)
        prompt_mask = jnp.concatenate(
            [
                key_index[:, None] <= prompt_pos[None, :],
                jnp.zeros((cont_rows, prompt_rows), jnp.bool_),
            ],
            axis=0,
        )
        own_mask = (segment[:, None] == segment[None, :]) & (
            local_index[:, None] <= local_index[None, :]
        )
        reach_mask = jnp.broadcast_to(key_index[:, None] < length, (prompt_total, cont_rows))
        allowed = jnp.concatenate(
            [prompt_mask, jnp.concatenate([reach_mask, own_mask], axis=0)], axis=1
        )
        bias = jnp.where(allowed, 0.0, NEGATIVE).astype(jnp.bfloat16)
    first_normed, q_t, cont_kv, gains, prompt_all = project_rope(
        x_all, packed_full, cosine, sine_table, q_heads, kv_heads, prompt_rows, 4
    )
    gain_one, gain_two = gains[0:1], gains[1:2]
    prompt_all, mlp_shard = lax.optimization_barrier((prompt_all, mlp_shard))
    mlp_full = lax.all_gather(mlp_shard, data, axis=0, tiled=True)
    attn_out, lse, attn_sum, normed_two = attend(
        q_t, prompt_all, cont_kv, bias, packed_full, x_all, gains, q_heads, kv_heads, 0
    )
    rows = prompt_rows + cont_rows
    early_rows = rows // 2 if rows % 1024 == 0 else rows - rows // 5
    hidden, grad_gate, grad_up = feed(normed_two, grad_out, mlp_full, early_rows)
    mlp_grads, up_grads, mlp_part, back_two = feed_back(
        hidden, grad_gate, grad_up, mlp_full, grad_out, normed_two, 1
    )

    def scatter(values):
        return lax.psum_scatter(values, data, scatter_dimension=0, tiled=True)

    cut = math.gcd(prompt_rows + cont_rows, SIZE // 2)
    grad_q, grad_kv, grad_middle, grad_rest, mlp_sum = window(
        q_t,
        prompt_all,
        cont_kv,
        bias,
        attn_out,
        lse,
        back_two,
        grad_out,
        x_all,
        attn_sum,
        gain_two,
        packed_full,
        cosine,
        sine_table,
        first_normed,
        up_grads,
        mlp_part.reshape(-1, cut, SIZE),
        q_heads,
        kv_heads,
        3,
    )
    mlp_own = scatter(mlp_grads)
    grad_q, grad_rest, mlp_own = lax.optimization_barrier((grad_q, grad_rest, mlp_own))
    back_one = product_sum(
        [grad_q, grad_kv], [(q_cols, 2 * q_cols), (2 * q_cols, q_cols + qkv_cols)], packed_full, 2
    )
    back_one, mlp_own = lax.optimization_barrier((back_one, mlp_own))
    outs = finish(x_all, attn_sum, mlp_sum, grad_middle, back_one, gain_one, prompt_rows)
    down_own = mlp_own[:, :hidden_cols].astype(jnp.float32)
    gate_own = mlp_own[:, wide : wide + hidden_cols].astype(jnp.float32)
    rest_own = scatter(grad_rest)
    up_own = rest_own[:, :hidden_cols].astype(jnp.float32)
    o_own = rest_own[:, wide : wide + q_cols].astype(jnp.float32)
    q_own = rest_own[:, wide + q_cols : wide + 2 * q_cols].astype(jnp.float32)
    k_own = rest_own[:, wide + 2 * q_cols : wide + 2 * q_cols + kv_cols].astype(jnp.float32)
    v_own = rest_own[:, wide + 2 * q_cols + kv_cols :].astype(jnp.float32)

    def row_dot(weight, grad):
        return jnp.sum(weight.astype(jnp.float32) * grad, axis=1)

    gain_rows = jnp.stack(
        [
            (row_dot(q_weight, q_own) + row_dot(key_matrix, k_own) + row_dot(value_matrix, v_own))
            / attn_gain.astype(jnp.float32),
            (row_dot(gate_weight, gate_own) + row_dot(up_weight, up_own))
            / mlp_gain.astype(jnp.float32),
        ]
    )
    gain_rows = tensor_total(gain_rows, 5)
    owned = (gain_rows[0], q_own, k_own, v_own, o_own, gain_rows[1], gate_own, up_own, down_own)
    return (*outs, *owned)


def solution(mesh):
    in_specs = (
        P(("dp", "context"), None),
        P(("dp", "context"), None),
        P("dp"),
        P(("dp", "context"), None),
        P(("dp", "context")),
        P(("dp", "context"), "tensor"),
        P(("dp", "context"), "tensor"),
        P(("dp", "context"), "tensor"),
        P(("dp", "context"), "tensor"),
        P(("dp", "context")),
        P(("dp", "context"), "tensor"),
        P(("dp", "context"), "tensor"),
        P(("dp", "context"), "tensor"),
        P(("dp", "context"), None),
        P(("dp", "context"), None),
    )
    out_specs = (
        P(("dp", "context"), None),
        P(("dp", "context"), None),
        P(("dp", "context"), None),
        P(("dp", "context"), None),
        P(("dp", "context")),
        P(("dp", "context"), "tensor"),
        P(("dp", "context"), "tensor"),
        P(("dp", "context"), "tensor"),
        P(("dp", "context"), "tensor"),
        P(("dp", "context")),
        P(("dp", "context"), "tensor"),
        P(("dp", "context"), "tensor"),
        P(("dp", "context"), "tensor"),
    )
    return jax.shard_map(
        per_device, mesh=mesh, in_specs=in_specs, out_specs=out_specs, check_vma=False
    )
```

```python
import functools
import math

import jax
import jax.numpy as jnp
from jax import lax
from jax.experimental import pallas as pl
from jax.experimental.pallas import tpu as pltpu
from jax.sharding import PartitionSpec as P

HEAD_SIZE = 80


EPS = 1e-05
THETA = 10000.0
NEGATIVE = -1e30
LOG2E = math.log2(math.e)
MESH = pl.DeviceIdType.MESH
AXIS = "tensor"
LAG = 3
SIZE = 256
FEED_STEPS = 10
SLOTS = 6


def normalize(values):
    inverse = lax.rsqrt(jnp.mean(values * values, axis=-1, keepdims=True) + EPS)
    return (values * inverse, inverse)


def norm_back(grad_unit, unit_rows, inverse):
    inner_sum = jnp.mean(grad_unit * unit_rows, axis=-1, keepdims=True)
    return inverse * (grad_unit - unit_rows * inner_sum)


def contract_last(left_side, right_side):
    return lax.dot_general(
        left_side, right_side, (((1,), (1,)), ((), ())), preferred_element_type=jnp.float32
    )


def contract_first(left_side, right_side):
    return lax.dot_general(
        left_side, right_side, (((0,), (0,)), ((), ())), preferred_element_type=jnp.float32
    )


def greet(axis, count):
    me = lax.axis_index(axis)
    barrier = pltpu.get_barrier_semaphore()
    for k in range(1, count):
        peer = lax.rem(me + k, count)
        pl.semaphore_signal(barrier, inc=1, device_id={axis: peer}, device_id_type=MESH)
    pl.semaphore_wait(barrier, count - 1)


def rope_kernel(
    q_heads,
    kv_heads,
    dim,
    prompt_steps,
    x_ref,
    w_ref,
    cos_ref,
    sin_ref,
    normed_ref,
    qt_ref,
    kvt_ref,
    gains_ref,
    all_ref,
    own,
    send,
    recv,
    local,
):
    i = pl.program_id(0)
    count = all_ref.shape[0]
    me = lax.axis_index("context")
    last = (q_heads + 2 * kv_heads + q_heads) * dim

    @pl.when(i == 0)
    def _():
        greet("context", count)
        low = last - last % 128
        turned = w_ref[:, low:].astype(jnp.float32).T
        gains_ref[...] = turned[last - low : last - low + 8]

    rows = x_ref[...].astype(jnp.float32)
    inverse = lax.rsqrt(jnp.mean(rows * rows, axis=-1, keepdims=True) + EPS)
    normed = (rows * inverse * gains_ref[0:1, :]).astype(jnp.bfloat16)
    normed_ref[...] = normed
    flat = jnp.dot(
        normed, w_ref[:, q_heads * dim :], preferred_element_type=jnp.float32
    ).T
    cosine, sine = cos_ref[...], sin_ref[...]
    half = dim // 2
    pieces = []
    for head in range(q_heads + kv_heads):
        first = flat[head * dim : head * dim + half]
        second = flat[head * dim + half : (head + 1) * dim]
        turned = jnp.concatenate(
            [first * cosine - second * sine, second * cosine + first * sine], axis=0
        ).astype(jnp.bfloat16)
        if head < q_heads:
            qt_ref[head * dim : (head + 1) * dim, :] = turned
        else:
            pieces.append(turned)
    at = (q_heads + kv_heads) * dim
    pieces.append(flat[at : at + kv_heads * dim].astype(jnp.bfloat16))
    low = 0
    for piece in pieces:
        kvt_ref[low : low + piece.shape[0], :] = piece
        low += piece.shape[0]
    step = x_ref.shape[0]
    for k in range(prompt_steps):

        @pl.when(i == k)
        def _():
            own[:, k * step : (k + 1) * step] = kvt_ref[...]

    def exchange(k):
        peer = lax.rem(me + k, count)
        return pltpu.make_async_remote_copy(
            own,
            all_ref.at[me],
            send.at[k],
            recv.at[k],
            device_id={"context": peer},
            device_id_type=MESH,
        )

    keep = pltpu.make_async_copy(own, all_ref.at[me], local)

    @pl.when(i == prompt_steps - 1)
    def _():
        for k in range(1, count):
            exchange(k).start()
        keep.start()

    @pl.when(i == pl.num_programs(0) - 1)
    def _():
        for k in range(1, count):
            exchange(k).wait()
        keep.wait()


def project_rope(x, packed_full, cos_t, sin_t, q_heads, kv_heads, prompt_rows, cid):
    rows, width = x.shape
    dim = HEAD_SIZE
    count = lax.axis_size("context")
    step = math.gcd(math.gcd(rows, prompt_rows), 256)
    cols_wide = packed_full.shape[1]
    kv2 = 2 * kv_heads * dim
    by_row = lambda i: (i, 0)
    by_col = lambda i: (0, i)
    fixed = lambda i: (0, 0)
    return pl.pallas_call(
        functools.partial(rope_kernel, q_heads, kv_heads, dim, prompt_rows // step),
        grid=(rows // step,),
        in_specs=[
            pl.BlockSpec((step, width), by_row),
            pl.BlockSpec(packed_full.shape, fixed, pipeline_mode=pl.Buffered(1)),
            pl.BlockSpec((dim // 2, step), by_col),
            pl.BlockSpec((dim // 2, step), by_col),
        ],
        out_specs=[
            pl.BlockSpec((step, width), by_row),
            pl.BlockSpec((q_heads * dim, step), by_col),
            pl.BlockSpec((kv2, step), by_col),
            pl.BlockSpec((8, width), fixed),
            pl.BlockSpec(memory_space=pltpu.HBM),
        ],
        out_shape=[
            jax.ShapeDtypeStruct((rows, width), jnp.bfloat16),
            jax.ShapeDtypeStruct((q_heads * dim, rows), jnp.bfloat16),
            jax.ShapeDtypeStruct((kv2, rows), jnp.bfloat16),
            jax.ShapeDtypeStruct((8, width), jnp.float32),
            jax.ShapeDtypeStruct((count, kv2, prompt_rows), jnp.bfloat16),
        ],
        scratch_shapes=[
            pltpu.VMEM((kv2, prompt_rows), jnp.bfloat16),
            pltpu.SemaphoreType.DMA((count,)),
            pltpu.SemaphoreType.DMA((count,)),
            pltpu.SemaphoreType.DMA,
        ],
        compiler_params=pltpu.CompilerParams(
            collective_id=cid, has_side_effects=True, vmem_limit_bytes=48 << 20
        ),
        cost_estimate=pl.CostEstimate(
            flops=2 * rows * width * cols_wide,
            bytes_accessed=4 * x.size + 2 * width * cols_wide,
            transcendentals=0,
        ),
    )(x, packed_full, cos_t, sin_t)


def attend_shape(prompt_all, kvt_cont):
    count, kv2, prompt_rows = prompt_all.shape
    cont_rows = kvt_cont.shape[1] - prompt_rows
    chunk = math.gcd(math.gcd(prompt_rows, cont_rows), 256)
    return count, kv2, prompt_rows, cont_rows, chunk


def total_kernel(count, part_ref, out_ref, got, send, recv):
    greet(AXIS, count)
    me = lax.axis_index(AXIS)
    copies = []
    for k in range(1, count):
        peer = lax.rem(me + k, count)
        copy = pltpu.make_async_remote_copy(
            part_ref,
            got.at[me],
            send.at[k],
            recv.at[k],
            device_id={AXIS: peer},
            device_id_type=MESH,
        )
        copy.start()
        copies.append(copy)
    got[me] = part_ref[...]
    for copy in copies:
        copy.wait()
    total = got[0]
    for k in range(1, count):
        total += got[k]
    out_ref[...] = total


def tensor_total(part, cid):
    count = lax.axis_size(AXIS)
    return pl.pallas_call(
        functools.partial(total_kernel, count),
        out_shape=jax.ShapeDtypeStruct(part.shape, part.dtype),
        in_specs=[pl.BlockSpec(memory_space=pltpu.VMEM)],
        out_specs=pl.BlockSpec(memory_space=pltpu.VMEM),
        scratch_shapes=[
            pltpu.VMEM((count, *part.shape), part.dtype),
            pltpu.SemaphoreType.DMA((count,)),
            pltpu.SemaphoreType.DMA((count,)),
        ],
        compiler_params=pltpu.CompilerParams(collective_id=cid, has_side_effects=True),
        cost_estimate=pl.CostEstimate(flops=0, bytes_accessed=4 << 20, transcendentals=0),
    )(part)


def plane_kernel(
    prompt_total,
    o_ref,
    q_ref,
    kt_ref,
    vt_ref,
    again_ref,
    mgain_ref,
    info_ref,
    w0_ref,
    w1_ref,
    w2_ref,
    px_ref,
    cx_ref,
    pc_ref,
    cc_ref,
    all_ref,
    shard_ref,
    x_ref,
    cot_ref,
    bias_ref,
    own_ref,
    stage,
    send,
    recv,
    local,
):
    dp, context = lax.axis_index("dp"), lax.axis_index("context")
    side = {"context": 1 - context}
    along = {"dp": lax.rem(dp + 2, 4)}
    twin_dp = dp + 1 - 2 * lax.rem(dp, 2)
    twin = {"dp": twin_dp}
    barrier = pltpu.get_barrier_semaphore()
    for peer in (side, along, twin):
        pl.semaphore_signal(barrier, inc=1, device_id=peer, device_id_type=MESH)
    pl.semaphore_wait(barrier, 3)
    rows = own_ref.shape[0]
    q_cols = q_ref.shape[1]
    own_ref[:, :q_cols] = o_ref[...]
    own_ref[:, q_cols : 2 * q_cols] = q_ref[...]
    small = [kt_ref[...], vt_ref[...], again_ref[...], mgain_ref[...]]
    rest = own_ref.shape[1] - 2 * q_cols
    used = sum(part.shape[0] for part in small)
    small.append(jnp.zeros((rest - used, rows), jnp.bfloat16))
    own_ref[:, 2 * q_cols :] = (
        jnp.concatenate([part.astype(jnp.float32) for part in small], axis=0).T
    ).astype(jnp.bfloat16)
    half = rows // 2
    mine = 2 * dp + context
    from_side = 2 * dp + 1 - context
    from_along = 2 * lax.rem(dp + 2, 4) + context
    from_far = 2 * lax.rem(dp + 2, 4) + 1 - context

    def spot(block, h):
        return pl.ds(pl.multiple_of(block * rows + h * half, half), half)

    def copy(k, block, h, peer, first=False):
        source = own_ref.at[pl.ds(h * half, half)] if first else all_ref.at[spot(block, h)]
        return pltpu.make_async_remote_copy(
            source,
            all_ref.at[spot(block, h)],
            send.at[k],
            recv.at[k],
            device_id=peer,
            device_id_type=MESH,
        )

    def land(k, block, h):
        return pltpu.make_async_remote_copy(
            own_ref.at[pl.ds(h * half, half)],
            all_ref.at[spot(block, h)],
            send.at[k],
            recv.at[k],
            device_id=side,
            device_id_type=MESH,
        )

    started = []

    def go(*args, **kwargs):
        one = copy(*args, **kwargs)
        one.start()
        started.append(one)

    go(0, mine, 0, side, first=True)
    go(2, mine, 1, along, first=True)
    go(1, mine, 1, side, first=True)
    go(3, mine, 0, along, first=True)
    go(6, mine, 0, twin, first=True)
    go(7, mine, 1, twin, first=True)
    prompt_rows = px_ref.shape[0]
    moves = [
        pltpu.make_async_copy(own_ref, all_ref.at[pl.ds(pl.multiple_of(mine * rows, rows), rows)], local.at[0]),
    ]
    moves[0].start()
    joins = []
    for k, (source, target, low) in enumerate(
        (
            (px_ref, x_ref, 0),
            (cx_ref, x_ref, prompt_rows),
            (pc_ref, cot_ref, 0),
            (cc_ref, cot_ref, prompt_rows),
        )
    ):
        rows_at = pl.ds((k % 2) * prompt_rows, source.shape[0])
        load = pltpu.make_async_copy(source, stage.at[k // 2, rows_at], local.at[1 + k])
        load.start()
        joins.append(
            (
                load,
                pltpu.make_async_copy(
                    stage.at[k // 2, rows_at],
                    target.at[pl.ds(low, source.shape[0])],
                    local.at[5 + k],
                ),
            )
        )
    cols = w0_ref.shape[1]
    wide = shard_ref.shape[1] // 3
    for k, ref in enumerate((w0_ref, w1_ref, w2_ref)):
        shard_ref[:, k * wide : k * wide + cols] = ref[...]
        shard_ref[:, k * wide + cols : (k + 1) * wide] = jnp.zeros(
            (rows, wide - cols), jnp.bfloat16
        )
    cont_rows = cx_ref.shape[0]
    block = 128

    def fill_bias(low, count, at, columns, rule):
        @pl.loop(0, count // block)
        def _(c):
            key = lax.broadcasted_iota(jnp.int32, (block, columns), 0) + c * block
            query = lax.broadcasted_iota(jnp.int32, (block, columns), 1)
            rows_at = pl.ds(pl.multiple_of(low + c * block, block), block)
            bias_ref[rows_at, at : at + columns] = jnp.where(
                rule(key, query), 0.0, NEGATIVE
            ).astype(jnp.bfloat16)

    first = context * prompt_rows
    earlier, length = info_ref[0:1, :], info_ref[1:2, :]
    fill_bias(0, prompt_total, 0, prompt_rows, lambda k, q: k <= q + first)
    fill_bias(prompt_total, cont_rows, 0, prompt_rows, lambda k, q: k < 0)
    fill_bias(0, prompt_total, prompt_rows, cont_rows, lambda k, q: k < length)
    fill_bias(
        prompt_total, cont_rows, prompt_rows, cont_rows, lambda k, q: (k >= earlier) & (k <= q)
    )
    for load, save in joins:
        load.wait()
        save.start()
        moves.append(save)
    land(0, from_side, 0).wait_recv()
    go(4, from_side, 0, along)
    go(8, from_side, 0, twin)
    land(2, from_along, 1).wait_recv()
    go(5, from_along, 1, side)
    go(9, from_along, 1, twin)
    land(1, from_side, 1).wait_recv()
    go(10, from_side, 1, twin)
    land(3, from_along, 0).wait_recv()
    go(11, from_along, 0, twin)
    land(4, from_far, 0).wait_recv()
    go(12, from_far, 0, twin)
    land(5, from_far, 1).wait_recv()
    go(13, from_far, 1, twin)
    base = 2 * twin_dp
    other = 2 * lax.rem(twin_dp + 2, 4)
    for k, block, h in (
        (6, base + context, 0),
        (7, base + context, 1),
        (8, base + 1 - context, 0),
        (9, other + context, 1),
        (10, base + 1 - context, 1),
        (11, other + context, 0),
        (12, other + 1 - context, 0),
        (13, other + 1 - context, 1),
    ):
        land(k, block, h).wait_recv()
    for one in started:
        one.wait_send()
    for move in moves:
        move.wait()


def plane_gather(
    attn, gains, info, weights, wide, attn_wide, prompt_x, cont_x, prompt_cot, cont_cot, cid
):
    o_weight, q_weight, key_matrix, value_matrix = attn
    rows = q_weight.shape[0]
    count = lax.axis_size("dp") * lax.axis_size("context")
    prompt_rows, width = prompt_x.shape
    total = prompt_rows + cont_x.shape[0]
    prompt_total = prompt_rows * lax.axis_size("context")
    hbm = pl.BlockSpec(memory_space=pltpu.HBM)
    vmem = pl.BlockSpec(memory_space=pltpu.VMEM)
    both = jax.ShapeDtypeStruct((total, width), jnp.bfloat16)
    return pl.pallas_call(
        functools.partial(plane_kernel, prompt_total),
        out_shape=[
            jax.ShapeDtypeStruct((count * rows, attn_wide), jnp.bfloat16),
            jax.ShapeDtypeStruct((rows, 3 * wide), jnp.bfloat16),
            both,
            both,
            jax.ShapeDtypeStruct((prompt_total + cont_x.shape[0], total), jnp.bfloat16),
        ],
        in_specs=[vmem] * 10 + [hbm] * 4,
        out_specs=[hbm, vmem, hbm, hbm, vmem],
        scratch_shapes=[
            pltpu.VMEM((rows, attn_wide), jnp.bfloat16),
            pltpu.VMEM((2, total, width), jnp.bfloat16),
            pltpu.SemaphoreType.DMA((14,)),
            pltpu.SemaphoreType.DMA((14,)),
            pltpu.SemaphoreType.DMA((9,)),
        ],
        compiler_params=pltpu.CompilerParams(
            collective_id=cid, has_side_effects=True, vmem_limit_bytes=60 << 20
        ),
        cost_estimate=pl.CostEstimate(
            flops=30_000_000_000, bytes_accessed=40 << 20, transcendentals=0
        ),
    )(
        o_weight,
        q_weight,
        key_matrix.T,
        value_matrix.T,
        gains[0][None, :],
        gains[1][None, :],
        info,
        *weights,
        prompt_x,
        cont_x,
        prompt_cot,
        cont_cot,
    )


def fill_keys(chunk, dim, kv_heads, all_ref, cont_ref, rows_of, chunks_ref):
    count, _, prompt_rows = all_ref.shape
    per = prompt_rows // chunk
    total = count * per + (cont_ref.shape[1] - prompt_rows) // chunk
    for c in range(total):
        if c < count * per:
            block = all_ref[c // per, :, (c % per) * chunk : (c % per + 1) * chunk]
        else:
            at = prompt_rows + (c - count * per) * chunk
            block = cont_ref[:, at : at + chunk]
        chunks_ref[c] = block
        for n, target in enumerate(rows_of):
            for g in range(kv_heads):
                at = (n * kv_heads + g) * dim
                target[g, c * chunk : (c + 1) * chunk, :] = (
                    block[at : at + dim].astype(jnp.float32).T.astype(jnp.bfloat16)
                )


def trip_count(tile, chunk, i, prompt_rows, count):
    me = lax.axis_index("context")
    prompt_tiles = prompt_rows // tile
    n_prompt = lax.div(me * prompt_rows + (i + 1) * tile + chunk - 1, chunk)
    n_own = lax.div((i - prompt_tiles + 1) * tile + chunk - 1, chunk)
    return i < prompt_tiles, n_prompt, count * prompt_rows // chunk, n_own


class Line:
    def __init__(self, part, recv, out, sink, sems, sink_sems, ready=None, place=None):
        self.ready, self.place = ready, place
        self.part, self.recv, self.out, self.sink = part, recv, out, sink
        self.per = sink.shape[0] // out.shape[1]
        self.sems, self.sink_sems = sems, sink_sems
        self.blocks = out.shape[0]
        me, n = lax.axis_index(AXIS), lax.axis_size(AXIS)
        self.outer = (me == 0) | (me == n - 1)
        self.inner = jnp.logical_not(self.outer)
        self.mate = jnp.where(me < n // 2, 1 - me, 2 * n - 3 - me)
        self.across = n - 1 - me

    def copy(self, k, source, target, peer, b):
        return pltpu.make_async_remote_copy(
            source.at[b],
            target.at[b],
            self.sems.at[2 * k, b],
            self.sems.at[2 * k + 1, b],
            device_id={AXIS: peer},
            device_id_type=MESH,
        )

    def up(self, b):
        return self.copy(0, self.part, self.recv, self.mate, b)

    def mid(self, b):
        return self.copy(1, self.part, self.out, self.across, b)

    def down(self, b):
        return self.copy(2, self.out, self.out, self.mate, b)

    def keep(self, b):
        _, rows, cols = self.out.shape
        row, col = lax.rem(b, self.per), lax.div(b, self.per)
        if self.place is not None:
            row, col = self.place(b)
        at = (
            pl.ds(pl.multiple_of(row * rows, rows), rows),
            pl.ds(pl.multiple_of(col * cols, cols), cols),
        )
        return pltpu.make_async_copy(self.out.at[b], self.sink.at[at], self.sink_sems.at[b])

    def greet(self, axis=None, count=1):
        barrier = pltpu.get_barrier_semaphore()
        pl.semaphore_signal(barrier, inc=1, device_id={AXIS: self.mate}, device_id_type=MESH)
        for k in range(1, count):
            peer = lax.rem(lax.axis_index(axis) + k, count)
            pl.semaphore_signal(barrier, inc=1, device_id={axis: peer}, device_id_type=MESH)

        @pl.when(self.inner)
        def _():
            pl.semaphore_signal(barrier, inc=1, device_id={AXIS: self.across}, device_id_type=MESH)
            pl.semaphore_wait(barrier, 1 + count)

        @pl.when(self.outer)
        def _():
            pl.semaphore_wait(barrier, count)

    def start(self, first, count):
        @pl.when(self.outer)
        def _():
            @pl.loop(0, count)
            def _(k):
                self.up(first + k).start()

    def step(self, t):
        @pl.when(self.inner & (t >= 0) & (t < self.blocks))
        def _():
            self.up(t).wait_recv()
            self.part[t] = (
                self.part[t].astype(jnp.float32) + self.recv[t].astype(jnp.float32)
            ).astype(jnp.bfloat16)
            self.mid(t).start()

        @pl.when(self.inner & (t >= LAG) & (t < self.blocks + LAG))
        def _():
            b = t - LAG
            self.mid(b).wait_recv()
            self.out[b] = (
                self.part[b].astype(jnp.float32) + self.out[b].astype(jnp.float32)
            ).astype(jnp.bfloat16)
            self.down(b).start()
            self.keep(b).start()
            if self.ready is not None:
                self.ready(b)

    def drain(self):
        for k in range(LAG):
            self.step(self.blocks + k)

        @pl.when(self.outer)
        def _():
            @pl.loop(0, self.blocks)
            def _(b):
                self.down(b).wait_recv()
                self.keep(b).start()
                if self.ready is not None:
                    self.ready(b)
                self.up(b).wait_send()

        @pl.when(self.inner)
        def _():
            @pl.loop(0, self.blocks)
            def _(b):
                self.mid(b).wait_send()
                self.down(b).wait_send()

        @pl.loop(0, self.blocks)
        def _(b):
            self.keep(b).wait()


def line_scratch(shape):
    return [pltpu.VMEM(shape, jnp.bfloat16)] * 3 + [
        pltpu.SemaphoreType.DMA((6, shape[0])),
        pltpu.SemaphoreType.DMA((shape[0],)),
    ]


def attend_kernel(
    shape,
    dim,
    kv_heads,
    per,
    tile,
    cut,
    q_ref,
    all_ref,
    cont_ref,
    bias_ref,
    wo_ref,
    x_ref,
    gains_ref,
    out_ref,
    lse_ref,
    sum_ref,
    normed_ref,
    keys,
    chunks,
    norm_buf,
    norm_sems,
    part,
    recv,
    out,
    sems,
    sink_sems,
):
    count, prompt_rows, chunk = shape
    i = pl.program_id(0)

    def norm_out(b):
        at = pl.ds(pl.multiple_of(b * cut, cut), cut)
        return pltpu.make_async_copy(norm_buf.at[b], normed_ref.at[at], norm_sems.at[b])

    def ready(b):
        at = pl.ds(pl.multiple_of(b * cut, cut), cut)
        unit, _ = normalize(x_ref[at, :].astype(jnp.float32) + out[b].astype(jnp.float32))
        norm_buf[b] = (unit * gains_ref[1:2, :]).astype(jnp.bfloat16)
        norm_out(b).start()

    line = Line(part, recv, out, sum_ref, sems, sink_sems, ready)
    blocks = tile // cut

    @pl.when(i == 0)
    def _():
        fill_keys(chunk, dim, kv_heads, all_ref, cont_ref, [keys], chunks)
        line.greet()

    is_prompt, n_prompt, base, n_own = trip_count(tile, chunk, i, prompt_rows, count)
    wide = per * tile
    factor = dim ** (-0.5) * LOG2E
    outs, sums = [], []
    for g in range(kv_heads):
        q = jnp.concatenate(
            [q_ref[(g * per + h) * dim : (g * per + h + 1) * dim, :] for h in range(per)], axis=1
        )

        def body(c, state):
            top, total, acc = state
            at = pl.ds(pl.multiple_of(c * chunk, chunk), chunk)
            s = jnp.dot(keys[g, at, :], q, preferred_element_type=jnp.float32)
            t = s * factor + jnp.concatenate([bias_ref[at, :].astype(jnp.float32)] * per, axis=1)
            new = jnp.maximum(top, jnp.max(t, axis=0, keepdims=True))
            p = jnp.exp2(t - new)
            scale = jnp.exp2(top - new)
            total = total * scale + jnp.sum(p, axis=0, keepdims=True)
            v = chunks[c, (kv_heads + g) * dim : (kv_heads + g + 1) * dim, :]
            acc = acc * scale + jnp.dot(
                v, p.astype(jnp.bfloat16), preferred_element_type=jnp.float32
            )
            return new, total, acc

        start = (
            jnp.full((1, wide), NEGATIVE, jnp.float32),
            jnp.zeros((1, wide), jnp.float32),
            jnp.zeros((dim, wide), jnp.float32),
        )
        state = lax.fori_loop(0, jnp.where(is_prompt, n_prompt, base), body, start)
        top, total, acc = lax.fori_loop(base, base + jnp.where(is_prompt, 0, n_own), body, state)
        acc = acc / total
        top = top + jnp.log2(total)
        outs += [acc[:, h * tile : (h + 1) * tile] for h in range(per)]
        sums += [top[:, h * tile : (h + 1) * tile] for h in range(per)]
        if g < kv_heads - 1:
            for r in range(blocks // 2):
                line.step((i - 1) * blocks + r)
    attended = jnp.concatenate(outs, axis=0).T.astype(jnp.bfloat16)
    out_ref[...] = attended
    lse_ref[...] = jnp.concatenate(sums, axis=0)
    term = contract_last(attended, wo_ref[...]).astype(jnp.bfloat16)
    for r in range(blocks):
        part[i * blocks + r] = term[r * cut : (r + 1) * cut]

    line.start(i * blocks, blocks)
    for r in range(blocks // 2, blocks):
        line.step((i - 1) * blocks + r)

    @pl.when(i == pl.num_programs(0) - 1)
    def _():
        @pl.loop(0, blocks)
        def _(r):
            line.step(i * blocks + r)

        line.drain()

        @pl.loop(0, line.blocks)
        def _(b):
            norm_out(b).wait()


def attend(q_t, prompt_all, kvt_cont, bias, packed_full, x, gains, q_heads, kv_heads, cid):
    dim = HEAD_SIZE
    count, kv2, prompt_rows, cont_rows, chunk = attend_shape(prompt_all, kvt_cont)
    q_cols, rows = q_t.shape
    width = packed_full.shape[0]
    keys_all = bias.shape[0]
    tile, cut = 128, 16
    whole = pl.BlockSpec(memory_space=pltpu.VMEM)
    by_col = lambda i: (0, i)
    return pl.pallas_call(
        functools.partial(
            attend_kernel,
            (count, prompt_rows, chunk),
            dim,
            kv_heads,
            q_heads // kv_heads,
            tile,
            cut,
        ),
        grid=(rows // tile,),
        in_specs=[
            pl.BlockSpec((q_cols, tile), by_col),
            whole,
            whole,
            pl.BlockSpec((keys_all, tile), by_col),
            pl.BlockSpec((width, q_cols), lambda i: (0, 0), pipeline_mode=pl.Buffered(1)),
            whole,
            whole,
        ],
        out_specs=[
            pl.BlockSpec((tile, q_cols), lambda i: (i, 0)),
            pl.BlockSpec((q_heads, tile), by_col),
            pl.BlockSpec(memory_space=pl.ANY),
            pl.BlockSpec(memory_space=pl.ANY),
        ],
        out_shape=[
            jax.ShapeDtypeStruct((rows, q_cols), jnp.bfloat16),
            jax.ShapeDtypeStruct((q_heads, rows), jnp.float32),
            jax.ShapeDtypeStruct((rows, width), jnp.bfloat16),
            jax.ShapeDtypeStruct((rows, width), jnp.bfloat16),
        ],
        scratch_shapes=[
            pltpu.VMEM((kv_heads, keys_all, dim), jnp.bfloat16),
            pltpu.VMEM((keys_all // chunk, kv2, chunk), jnp.bfloat16),
            pltpu.VMEM((rows // cut, cut, width), jnp.bfloat16),
            pltpu.SemaphoreType.DMA((rows // cut,)),
            *line_scratch((rows // cut, cut, width)),
        ],
        compiler_params=pltpu.CompilerParams(
            collective_id=cid, has_side_effects=True, vmem_limit_bytes=56 << 20
        ),
        cost_estimate=pl.CostEstimate(
            flops=120_000_000_000, bytes_accessed=40 << 20, transcendentals=0
        ),
    )(q_t, prompt_all, kvt_cont, bias, packed_full, x, gains)


def feed_back_kernel(
    cut,
    hidden_in,
    gate_in,
    up_in,
    normed_late,
    cot_late,
    fd_ref,
    fg_ref,
    fu_ref,
    wd_ref,
    wg_ref,
    wu_ref,
    cot_ref,
    normed_ref,
    grads_ref,
    up_grads_ref,
    mlp_ref,
    sum_ref,
    hidden,
    gate,
    up,
    late_sems,
    part,
    recv,
    out,
    sems,
    sink_sems,
):
    i = pl.program_id(0)
    rows, wide = gate.shape
    first = hidden_in.shape[0]
    tiles = sum_ref.shape[1] // SIZE
    feeds = wide // SIZE
    low, high = first // cut, (rows - first) // cut
    split = tiles * low

    def place(b):
        early = b < split
        c = b - split
        row = jnp.where(early, lax.rem(b, low), low + lax.rem(c, high))
        return row, jnp.where(early, lax.div(b, low), lax.div(c, high))

    line = Line(part, recv, out, sum_ref, sems, sink_sems, place=place)

    def loads():
        return [
            pltpu.make_async_copy(source, target.at[pl.ds(0, first)], late_sems.at[k])
            for k, (source, target) in enumerate(((gate_in, gate), (up_in, up), (hidden_in, hidden)))
        ]

    def produce(at, block, count):
        back = contract_last(gate[at, :], wg_ref[...]) + contract_last(up[at, :], wu_ref[...])
        back = back.astype(jnp.bfloat16)
        for r in range(count):
            part[block + r] = back[r * cut : (r + 1) * cut]
        line.start(block, count)

    def steps(start, stop):
        @pl.loop(start, stop)
        def _(t):
            line.step(t)

    @pl.when(i == 0)
    def _():
        for load in loads():
            load.start()
        line.greet()
        for load in loads():
            load.wait()

    @pl.when(i < tiles)
    def _():
        produce(slice(0, first), i * low, low)

    beside = min(split, FEED_STEPS)

    @pl.when((i >= tiles) & (i < tiles + feeds))
    def _():
        m = i - tiles
        here = pl.ds(pl.multiple_of(m * SIZE, SIZE), SIZE)
        hidden[first:, here], gate[first:, here], up[first:, here] = feed_tile(
            normed_late[...], cot_late[...], fd_ref[...], fg_ref[...], fu_ref[...]
        )
        steps(lax.div(m * beside, feeds), lax.div((m + 1) * beside, feeds))

    @pl.when(i >= tiles + feeds)
    def _():
        n = i - tiles - feeds
        produce(slice(first, rows), split + n * high, high)
        rest = line.blocks - beside
        spots = 4

        def step(k):
            start = beside + lax.div((n * spots + k) * rest, tiles * spots)
            steps(start, beside + lax.div((n * spots + k + 1) * rest, tiles * spots))

        step(0)
        grads_ref[:, :wide] = contract_first(cot_ref[...], hidden[...]).astype(jnp.bfloat16)
        step(1)
        grads_ref[:, wide:] = contract_first(normed_ref[...], gate[...]).astype(jnp.bfloat16)
        step(2)
        up_grads_ref[...] = contract_first(normed_ref[...], up[...]).astype(jnp.bfloat16)
        step(3)
        mlp_ref[0] = contract_last(hidden[...], wd_ref[...]).astype(jnp.bfloat16)

        @pl.when(n == tiles - 1)
        def _():
            line.drain()


def feed_back(hidden, grad_gate, grad_up, mlp_full, cot, normed, cid):
    first, wide = hidden.shape
    rows, width = cot.shape
    cut = math.gcd(math.gcd(rows, first), SIZE)
    tiles, feeds = width // SIZE, wide // SIZE
    blocks = (tiles * rows // cut, cut, SIZE)
    anywhere = pl.BlockSpec(memory_space=pltpu.HBM)
    second = lambda i: (first // (rows - first), 0)
    late = lambda i: jnp.maximum(i - tiles - feeds, 0)
    back = lambda i: jnp.where(i < tiles, i, late(i))
    ahead = lambda i: jnp.clip(i - tiles, 0, feeds - 1)
    return pl.pallas_call(
        functools.partial(feed_back_kernel, cut),
        grid=(2 * tiles + feeds,),
        in_specs=[anywhere] * 3
        + [pl.BlockSpec((rows - first, width), second, pipeline_mode=pl.Buffered(1))] * 2
        + [pl.BlockSpec((width, SIZE), lambda i, k=k: (0, k * feeds + ahead(i))) for k in range(3)]
        + [pl.BlockSpec((SIZE, wide), lambda i: (late(i), 0))]
        + [pl.BlockSpec((SIZE, wide), lambda i, k=k: (back(i), k)) for k in (1, 2)]
        + [pl.BlockSpec((rows, SIZE), lambda i: (0, late(i)))] * 2,
        out_specs=[
            pl.BlockSpec((SIZE, 2 * wide), lambda i: (late(i), 0)),
            pl.BlockSpec((SIZE, wide), lambda i: (late(i), 0)),
            pl.BlockSpec((1, rows, SIZE), lambda i: (late(i), 0, 0)),
            pl.BlockSpec(memory_space=pl.ANY),
        ],
        out_shape=[
            jax.ShapeDtypeStruct((width, 2 * wide), jnp.bfloat16),
            jax.ShapeDtypeStruct((width, wide), jnp.bfloat16),
            jax.ShapeDtypeStruct((tiles, rows, SIZE), jnp.bfloat16),
            jax.ShapeDtypeStruct((rows, width), jnp.bfloat16),
        ],
        scratch_shapes=[
            pltpu.VMEM((rows, wide), jnp.bfloat16),
            pltpu.VMEM((rows, wide), jnp.bfloat16),
            pltpu.VMEM((rows, wide), jnp.bfloat16),
            pltpu.SemaphoreType.DMA((3,)),
            *line_scratch(blocks),
        ],
        compiler_params=pltpu.CompilerParams(
            collective_id=cid, has_side_effects=True, vmem_limit_bytes=61 << 20
        ),
        cost_estimate=pl.CostEstimate(
            flops=12 * rows * wide * width, bytes_accessed=200 << 20, transcendentals=0
        ),
    )(
        hidden,
        grad_gate,
        grad_up,
        normed,
        cot,
        mlp_full,
        mlp_full,
        mlp_full,
        mlp_full,
        mlp_full,
        mlp_full,
        cot,
        normed,
    )


def window_kernel(
    shape,
    dim,
    kv_heads,
    per,
    tile,
    q_ref,
    all_ref,
    cont_ref,
    bias_ref,
    out_ref,
    lse_ref,
    back_ref,
    cot_ref,
    x_ref,
    attn_ref,
    gain_ref,
    wo_ref,
    cos_ref,
    sin_ref,
    cos_own_ref,
    sin_own_ref,
    normed_ref,
    att_ref,
    up_grads_ref,
    mlp_ref,
    gq_out_ref,
    gkv_ref,
    gm_ref,
    grads_ref,
    sum_ref,
    keys,
    values,
    chunks,
    gk,
    gv,
    gm,
    gq_ref,
    send_ref,
    got,
    own_ref,
    kv_sems,
    part,
    recv,
    out,
    sems,
    sink_sems,
):
    count, prompt_rows, chunk = shape
    i = pl.program_id(0)
    line = Line(part, recv, out, sum_ref, sems, sink_sems)
    context = lax.axis_index("context")
    prompt_tiles = prompt_rows // tile
    tiles = gq_ref.shape[0] // tile
    slots = SLOTS
    spots = 2 + kv_heads

    def step(k):
        for s in range(k * slots // spots, (k + 1) * slots // spots):
            line.step(i * slots + s)

    def send(k):
        peer = lax.rem(context + k, count)
        return pltpu.make_async_remote_copy(
            send_ref.at[peer],
            got.at[k],
            kv_sems.at[0, k],
            kv_sems.at[1, k],
            device_id={"context": peer},
            device_id_type=MESH,
        )

    root = dim ** (-0.5)
    half = dim // 2

    @pl.when(i == 0)
    def _():
        load = pltpu.make_async_copy(mlp_ref, part, sink_sems.at[0])
        load.start()
        fill_keys(chunk, dim, kv_heads, all_ref, cont_ref, [keys, values], chunks)
        gk[...] = jnp.zeros_like(gk)
        gv[...] = jnp.zeros_like(gv)
        line.greet("context", count)
        load.wait()
        line.start(0, line.blocks)

    @pl.when(i < tiles)
    def _():
        middle = x_ref[...].astype(jnp.float32) + attn_ref[...].astype(jnp.float32)
        inverse = lax.rsqrt(jnp.mean(middle * middle, axis=-1, keepdims=True) + EPS)
        unit = middle * inverse
        grad_unit = back_ref[...].astype(jnp.float32) * gain_ref[...]
        grad_middle = cot_ref[...].astype(jnp.float32) + norm_back(grad_unit, unit, inverse)
        gm_ref[...] = grad_middle.astype(jnp.bfloat16)
        grad_b = grad_middle.astype(jnp.bfloat16)
        step(0)
        grad_t = (
            jnp.dot(grad_b, wo_ref[...], preferred_element_type=jnp.float32).astype(jnp.bfloat16)
        ).astype(jnp.float32).T
        gm[pl.ds(pl.multiple_of(i * tile, tile), tile), :] = grad_b
        step(1)

        is_prompt, n_prompt, base, n_own = trip_count(tile, chunk, i, prompt_rows, count)
        factor = root * LOG2E
        prod = grad_t * out_ref[...].astype(jnp.float32).T
        grad_t = grad_t.astype(jnp.bfloat16)
        cosine, sine = cos_ref[...], sin_ref[...]
        pieces = []
        for g in range(kv_heads):
            heads = [g * per + h for h in range(per)]
            q = jnp.concatenate([q_ref[h * dim : (h + 1) * dim, :] for h in heads], axis=1)
            grad = jnp.concatenate([grad_t[h * dim : (h + 1) * dim] for h in heads], axis=1)
            inner = jnp.concatenate(
                [jnp.sum(prod[h * dim : (h + 1) * dim], axis=0, keepdims=True) for h in heads], axis=1
            )
            lse = jnp.concatenate([lse_ref[h : h + 1, :] for h in heads], axis=1)

            def body(c, acc):
                at = pl.ds(pl.multiple_of(c * chunk, chunk), chunk)
                s = jnp.dot(keys[g, at, :], q, preferred_element_type=jnp.float32)
                b = bias_ref[at, :].astype(jnp.float32)
                p = jnp.exp2(s * factor + (jnp.concatenate([b] * per, axis=1) - lse))
                dp = jnp.dot(values[g, at, :], grad, preferred_element_type=jnp.float32)
                ds = (p * (dp - inner)).astype(jnp.bfloat16)
                gv[g, at, :] += contract_last(p.astype(jnp.bfloat16), grad)
                gk[g, at, :] += contract_last(ds, q)
                k_t = chunks[c, g * dim : (g + 1) * dim, :]
                return acc + jnp.dot(k_t, ds, preferred_element_type=jnp.float32)

            acc = jnp.zeros((dim, per * tile), jnp.float32)
            acc = lax.fori_loop(0, jnp.where(is_prompt, n_prompt, base), body, acc)
            acc = lax.fori_loop(base, base + jnp.where(is_prompt, 0, n_own), body, acc)
            acc = acc * root
            for h in range(per):
                first = acc[:half, h * tile : (h + 1) * tile]
                second = acc[half:, h * tile : (h + 1) * tile]
                pieces += [first * cosine + second * sine, second * cosine - first * sine]
            step(2 + g)
        rows_q = jnp.concatenate(pieces, axis=0).T.astype(jnp.bfloat16)
        gq_ref[pl.ds(pl.multiple_of(i * tile, tile), tile), :] = rows_q
        gq_out_ref[...] = rows_q

    @pl.when(i == tiles - 1)
    def _():
        for g in range(kv_heads):
            for n, (acc, scale) in enumerate(((gk, root), (gv, 1.0))):
                at = (n * kv_heads + g) * dim
                for c in range(count):
                    rows = acc[g, c * prompt_rows : (c + 1) * prompt_rows, :]
                    send_ref[c, at : at + dim, :] = (rows * scale).T.astype(jnp.bfloat16)
                own_ref[at : at + dim, :] = (acc[g, count * prompt_rows :, :] * scale).T
        for k in range(1, count):
            send(k).start()

    @pl.when(i == tiles)
    def _():
        line.step(tiles * slots)
        kv_dim = kv_heads * dim

        def finish(flat, cosine, sine):
            pieces = []
            for at in range(0, kv_dim, dim):
                first, second = flat[at : at + half], flat[at + half : at + dim]
                pieces += [first * cosine + second * sine, second * cosine - first * sine]
            pieces.append(flat[kv_dim:])
            return jnp.concatenate(pieces, axis=0).T.astype(jnp.bfloat16)

        cosine, sine = cos_own_ref[...], sin_own_ref[...]
        gkv_ref[prompt_rows:, :] = finish(
            own_ref[...], cosine[:, prompt_rows:], sine[:, prompt_rows:]
        )
        total = send_ref[context].astype(jnp.float32)
        for k in range(1, count):
            send(k).wait()
            total += got[k].astype(jnp.float32)
        gkv_ref[:prompt_rows, :] = finish(
            total, cosine[:, :prompt_rows], sine[:, :prompt_rows]
        )

    @pl.when(i >= tiles)
    def _():
        n = i - tiles
        later = pl.num_programs(0) - tiles
        rest = line.blocks - tiles * slots - 1
        q_cols = gq_ref.shape[1]
        wide = up_grads_ref.shape[1]
        here = pl.ds(pl.multiple_of(n * SIZE, SIZE), SIZE)
        grads_ref[:, :wide] = up_grads_ref[...]
        grads_ref[:, wide : wide + q_cols] = contract_first(gm[:, here], att_ref[...]).astype(
            jnp.bfloat16
        )
        grads_ref[:, wide + q_cols : wide + 2 * q_cols] = contract_first(
            normed_ref[...], gq_ref[...]
        ).astype(jnp.bfloat16)
        grads_ref[:, wide + 2 * q_cols :] = contract_first(normed_ref[...], gkv_ref[...]).astype(
            jnp.bfloat16
        )
        low = tiles * slots + 1 + lax.div(n * rest, later)
        high = tiles * slots + 1 + lax.div((n + 1) * rest, later)

        @pl.loop(low, high)
        def _(t):
            line.step(t)

        @pl.when(n == later - 1)
        def _():
            line.drain()


def window(
    q_t,
    prompt_all,
    kvt_cont,
    bias,
    attended,
    lse,
    back,
    cot,
    x,
    attn_sum,
    gain,
    packed_full,
    cos_t,
    sin_t,
    normed,
    up_grads,
    mlp_part,
    q_heads,
    kv_heads,
    cid,
):
    dim = HEAD_SIZE
    count, kv2, prompt_rows, cont_rows, chunk = attend_shape(prompt_all, kvt_cont)
    rows, width = cot.shape
    q_cols = q_heads * dim
    keys_all = bias.shape[0]
    tile = 128
    whole = pl.BlockSpec(memory_space=pltpu.VMEM)
    anywhere = pl.BlockSpec(memory_space=pl.ANY)
    tiles, later = rows // tile, width // SIZE
    grad_cols = up_grads.shape[1] + 2 * q_cols + kv2
    early = lambda i: jnp.minimum(i, tiles - 1)
    late = lambda i: jnp.maximum(i - tiles, 0)
    by_col = lambda i: (0, early(i))
    by_row = lambda i: (early(i), 0)
    fixed = lambda i: (0, 0)
    return pl.pallas_call(
        functools.partial(
            window_kernel, (count, prompt_rows, chunk), dim, kv_heads, q_heads // kv_heads, tile
        ),
        grid=(tiles + later,),
        in_specs=[
            pl.BlockSpec((q_cols, tile), by_col),
            whole,
            whole,
            pl.BlockSpec((keys_all, tile), by_col),
            pl.BlockSpec((tile, q_cols), by_row),
            pl.BlockSpec((q_heads, tile), by_col),
            pl.BlockSpec((tile, width), by_row),
            pl.BlockSpec((tile, width), by_row),
            pl.BlockSpec((tile, width), by_row),
            pl.BlockSpec((tile, width), by_row),
            pl.BlockSpec((1, width), fixed),
            pl.BlockSpec((width, q_cols), fixed, pipeline_mode=pl.Buffered(1)),
            pl.BlockSpec((dim // 2, tile), by_col),
            pl.BlockSpec((dim // 2, tile), by_col),
            whole,
            whole,
            pl.BlockSpec((rows, SIZE), lambda i: (0, late(i))),
            whole,
            pl.BlockSpec((SIZE, up_grads.shape[1]), lambda i: (late(i), 0)),
            anywhere,
        ],
        out_specs=[
            pl.BlockSpec((tile, q_cols), by_row),
            pl.BlockSpec((rows, kv2), fixed),
            pl.BlockSpec((tile, width), by_row),
            pl.BlockSpec((SIZE, grad_cols), lambda i: (late(i), 0)),
            anywhere,
        ],
        out_shape=[
            jax.ShapeDtypeStruct((rows, q_cols), jnp.bfloat16),
            jax.ShapeDtypeStruct((rows, kv2), jnp.bfloat16),
            jax.ShapeDtypeStruct((rows, width), jnp.bfloat16),
            jax.ShapeDtypeStruct((width, grad_cols), jnp.bfloat16),
            jax.ShapeDtypeStruct((rows, width), jnp.bfloat16),
        ],
        scratch_shapes=[
            pltpu.VMEM((kv_heads, keys_all, dim), jnp.bfloat16),
            pltpu.VMEM((kv_heads, keys_all, dim), jnp.bfloat16),
            pltpu.VMEM((keys_all // chunk, kv2, chunk), jnp.bfloat16),
            pltpu.VMEM((kv_heads, keys_all, dim), jnp.float32),
            pltpu.VMEM((kv_heads, keys_all, dim), jnp.float32),
            pltpu.VMEM((rows, width), jnp.bfloat16),
            pltpu.VMEM((rows, q_cols), jnp.bfloat16),
            pltpu.VMEM((count, kv2, prompt_rows), jnp.bfloat16),
            pltpu.VMEM((count, kv2, prompt_rows), jnp.bfloat16),
            pltpu.VMEM((kv2, cont_rows), jnp.float32),
            pltpu.SemaphoreType.DMA((2, count)),
            *line_scratch(mlp_part.shape),
        ],
        compiler_params=pltpu.CompilerParams(
            collective_id=cid, has_side_effects=True, vmem_limit_bytes=60 << 20
        ),
        cost_estimate=pl.CostEstimate(
            flops=120_000_000_000, bytes_accessed=200 << 20, transcendentals=0
        ),
    )(
        q_t,
        prompt_all,
        kvt_cont,
        bias,
        attended,
        lse,
        back,
        cot,
        x,
        attn_sum,
        gain,
        packed_full,
        cos_t,
        sin_t,
        cos_t,
        sin_t,
        normed,
        attended,
        up_grads,
        mlp_part,
    )


def product_kernel(cut, spans, lhs_refs, w_ref, sum_ref, part, recv, out, sems, sink_sems):
    n = pl.program_id(0)
    per = sum_ref.shape[0] // cut
    line = Line(part, recv, out, sum_ref, sems, sink_sems)
    term = sum(
        contract_last(ref[...], w_ref[:, low:high]) for ref, (low, high) in zip(lhs_refs, spans)
    ).astype(jnp.bfloat16)
    for r in range(per):
        part[n * per + r] = term[r * cut : (r + 1) * cut]

    @pl.when(n == 0)
    def _():
        line.greet()

    line.start(n * per, per)
    for r in range(per):
        line.step(n * per + r)

    @pl.when(n == pl.num_programs(0) - 1)
    def _():
        line.drain()


def product_sum(lhs, spans, weights, cid):
    rows = lhs[0].shape[0]
    width, cols = weights.shape
    cut = math.gcd(rows, 128)
    tiles = width // SIZE
    blocks = (tiles * rows // cut, cut, SIZE)

    def body(*refs):
        product_kernel(cut, spans, refs[: len(lhs)], *refs[len(lhs) :])

    return pl.pallas_call(
        body,
        grid=(tiles,),
        in_specs=[pl.BlockSpec(memory_space=pltpu.VMEM)] * len(lhs)
        + [pl.BlockSpec((SIZE, cols), lambda n: (n, 0))],
        out_specs=pl.BlockSpec(memory_space=pl.ANY),
        out_shape=jax.ShapeDtypeStruct((rows, width), jnp.bfloat16),
        scratch_shapes=line_scratch(blocks),
        compiler_params=pltpu.CompilerParams(
            collective_id=cid, has_side_effects=True, vmem_limit_bytes=40 << 20
        ),
        cost_estimate=pl.CostEstimate(
            flops=120_000_000_000, bytes_accessed=40 << 20, transcendentals=0
        ),
    )(*lhs, weights)


def feed_tile(normed, cot, wd, wg, wu):
    gate = jnp.dot(normed, wg, preferred_element_type=jnp.float32)
    up = jnp.dot(normed, wu, preferred_element_type=jnp.float32)
    grad_hidden = jnp.dot(cot, wd, preferred_element_type=jnp.float32)
    sigmoid = 1.0 / (1.0 + jnp.exp(-gate))
    silu = gate * sigmoid
    return (
        (silu * up).astype(jnp.bfloat16),
        (grad_hidden * up * sigmoid * (1.0 + gate * (1.0 - sigmoid))).astype(jnp.bfloat16),
        (grad_hidden * silu).astype(jnp.bfloat16),
    )


def feed_kernel(normed_ref, cot_ref, wd_ref, wg_ref, wu_ref, hidden_ref, gate_ref, up_ref):
    hidden_ref[...], gate_ref[...], up_ref[...] = feed_tile(
        normed_ref[...], cot_ref[...], wd_ref[...], wg_ref[...], wu_ref[...]
    )


def feed(normed, cot, mlp_full, rows):
    width = cot.shape[1]
    wide = mlp_full.shape[1] // 3
    tiles = wide // SIZE
    tile = pl.BlockSpec((rows, SIZE), lambda n: (0, n))
    return pl.pallas_call(
        feed_kernel,
        grid=(tiles,),
        in_specs=[pl.BlockSpec((rows, width), lambda n: (0, 0), pipeline_mode=pl.Buffered(1))] * 2
        + [pl.BlockSpec((width, SIZE), lambda n, k=k: (0, k * tiles + n)) for k in range(3)],
        out_specs=[
            tile,
            tile,
            tile,
        ],
        out_shape=[jax.ShapeDtypeStruct((rows, wide), jnp.bfloat16)] * 3,
        compiler_params=pltpu.CompilerParams(vmem_limit_bytes=58 << 20),
        cost_estimate=pl.CostEstimate(
            flops=6 * rows * width * wide, bytes_accessed=60 << 20, transcendentals=rows * wide
        ),
    )(normed, cot, mlp_full, mlp_full, mlp_full)


def finish_kernel(
    prompt_tiles, x_ref, attn_ref, mlp_ref, gm_ref, back_ref, gain_ref, po_ref, co_ref, pg_ref, cg_ref
):
    i = pl.program_id(0)
    x = x_ref[...].astype(jnp.float32)
    result = (x + attn_ref[...].astype(jnp.float32)) + mlp_ref[...].astype(jnp.float32)
    result = result.astype(jnp.bfloat16)
    unit, inverse = normalize(x)
    grad = gm_ref[...].astype(jnp.float32) + norm_back(back_ref[...].astype(jnp.float32) * gain_ref[...], unit, inverse)

    @pl.when(i < prompt_tiles)
    def _():
        po_ref[...] = result
        pg_ref[...] = grad

    @pl.when(i >= prompt_tiles)
    def _():
        co_ref[...] = result
        cg_ref[...] = grad


def finish(x, attn_sum, mlp_sum, grad_middle, back, gain, prompt_rows):
    rows, width = x.shape
    tile = 128
    prompt_tiles = prompt_rows // tile
    every = pl.BlockSpec((tile, width), lambda i: (i, 0))
    first = pl.BlockSpec((tile, width), lambda i: (jnp.minimum(i, prompt_tiles - 1), 0))
    second = pl.BlockSpec((tile, width), lambda i: (jnp.maximum(i - prompt_tiles, 0), 0))
    shapes = [(prompt_rows, width), (rows - prompt_rows, width)]
    return pl.pallas_call(
        functools.partial(finish_kernel, prompt_tiles),
        grid=(rows // tile,),
        in_specs=[every] * 5 + [pl.BlockSpec((1, width), lambda i: (0, 0))],
        out_specs=[first, second, first, second],
        out_shape=[jax.ShapeDtypeStruct(shape, jnp.bfloat16) for shape in shapes]
        + [jax.ShapeDtypeStruct(shape, jnp.float32) for shape in shapes],
        compiler_params=pltpu.CompilerParams(vmem_limit_bytes=40 << 20),
        cost_estimate=pl.CostEstimate(
            flops=20 * x.size, bytes_accessed=20 * x.size, transcendentals=0
        ),
    )(x, attn_sum, mlp_sum, grad_middle, back, gain)


def per_device(
    prompt_x,
    cont_x,
    prompt_len,
    cont_seg,
    attn_gain,
    q_weight,
    key_matrix,
    value_matrix,
    o_weight,
    mlp_gain,
    gate_weight,
    up_weight,
    down_weight,
    prompt_cot,
    cont_cot,
):
    head_dim = HEAD_SIZE
    data = ("dp", "context")
    prompt_rows = prompt_x.shape[0]
    cont_rows = cont_x.shape[0]
    prompt_total = prompt_rows * lax.axis_size("context")
    q_cols = q_weight.shape[1]
    kv_cols = key_matrix.shape[1]
    q_heads = q_cols // head_dim
    kv_heads = kv_cols // head_dim
    qkv_cols = q_cols + 2 * kv_cols
    qkv_wide = qkv_cols + 2 + -(qkv_cols + 2) % 128
    hidden_cols = gate_weight.shape[1]
    wide = hidden_cols + -hidden_cols % 256
    context_pos = lax.axis_index("context")
    prompt_pos = context_pos * prompt_rows + jnp.arange(prompt_rows, dtype=jnp.int32)
    segment = cont_seg[0]
    earlier = jnp.sum((segment[None, :] < segment[:, None]).astype(jnp.int32), axis=1)
    local_index = jnp.arange(cont_rows, dtype=jnp.int32)
    length = prompt_len[0]
    cont_pos = length + local_index - earlier
    position = jnp.concatenate([prompt_pos, cont_pos]).astype(jnp.float32)
    inv_freq = THETA ** (-jnp.arange(head_dim // 2, dtype=jnp.float32) * 2.0 / head_dim)
    angle_table = inv_freq[:, None] * position[None, :]
    cosine = jnp.cos(angle_table)
    sine_table = jnp.sin(angle_table)
    shards = (down_weight, gate_weight, up_weight)
    attn_shards = (o_weight, q_weight, key_matrix, value_matrix)
    if lax.axis_size("dp") == 4 and lax.axis_size("context") == 2:
        info = jnp.stack([earlier, jnp.broadcast_to(length, earlier.shape)])
        packed_full, mlp_shard, x_all, grad_out, bias = plane_gather(
            attn_shards,
            (attn_gain, mlp_gain),
            info,
            shards,
            wide,
            q_cols + qkv_wide,
            prompt_x,
            cont_x,
            prompt_cot,
            cont_cot,
            6,
        )
    else:
        packed = jnp.concatenate([*attn_shards, attn_gain[:, None], mlp_gain[:, None]], axis=1)
        packed = jnp.pad(packed, ((0, 0), (0, q_cols + qkv_wide - packed.shape[1])))
        packed_full = lax.all_gather(packed, data, axis=0, tiled=True)
        fill = ((0, 0), (0, wide - hidden_cols))
        mlp_shard = jnp.concatenate([jnp.pad(w, fill) for w in shards], axis=1)
        x_all = jnp.concatenate([prompt_x, cont_x], axis=0)
        grad_out = jnp.concatenate([prompt_cot, cont_cot], axis=0)
        key_index = jnp.arange(prompt_total, dtype=jnp.int32)
        prompt_mask = jnp.concatenate(
            [
                key_index[:, None] <= prompt_pos[None, :],
                jnp.zeros((cont_rows, prompt_rows), jnp.bool_),
            ],
            axis=0,
        )
        own_mask = (segment[:, None] == segment[None, :]) & (
            local_index[:, None] <= local_index[None, :]
        )
        reach_mask = jnp.broadcast_to(key_index[:, None] < length, (prompt_total, cont_rows))
        allowed = jnp.concatenate(
            [prompt_mask, jnp.concatenate([reach_mask, own_mask], axis=0)], axis=1
        )
        bias = jnp.where(allowed, 0.0, NEGATIVE).astype(jnp.bfloat16)
    first_normed, q_t, cont_kv, gains, prompt_all = project_rope(
        x_all, packed_full, cosine, sine_table, q_heads, kv_heads, prompt_rows, 4
    )
    gain_one, gain_two = gains[0:1], gains[1:2]
    prompt_all, mlp_shard = lax.optimization_barrier((prompt_all, mlp_shard))
    mlp_full = lax.all_gather(mlp_shard, data, axis=0, tiled=True)
    attn_out, lse, attn_sum, normed_two = attend(
        q_t, prompt_all, cont_kv, bias, packed_full, x_all, gains, q_heads, kv_heads, 0
    )
    rows = prompt_rows + cont_rows
    early_rows = rows // 2 if rows % 1024 == 0 else rows - rows // 5
    hidden, grad_gate, grad_up = feed(normed_two, grad_out, mlp_full, early_rows)
    mlp_grads, up_grads, mlp_part, back_two = feed_back(
        hidden, grad_gate, grad_up, mlp_full, grad_out, normed_two, 1
    )

    def scatter(values):
        return lax.psum_scatter(values, data, scatter_dimension=0, tiled=True)

    cut = math.gcd(prompt_rows + cont_rows, SIZE // 2)
    grad_q, grad_kv, grad_middle, grad_rest, mlp_sum = window(
        q_t,
        prompt_all,
        cont_kv,
        bias,
        attn_out,
        lse,
        back_two,
        grad_out,
        x_all,
        attn_sum,
        gain_two,
        packed_full,
        cosine,
        sine_table,
        first_normed,
        up_grads,
        mlp_part.reshape(-1, cut, SIZE),
        q_heads,
        kv_heads,
        3,
    )
    mlp_own = scatter(mlp_grads)
    grad_q, grad_rest, mlp_own = lax.optimization_barrier((grad_q, grad_rest, mlp_own))
    back_one = product_sum(
        [grad_q, grad_kv], [(q_cols, 2 * q_cols), (2 * q_cols, q_cols + qkv_cols)], packed_full, 2
    )
    back_one, mlp_own = lax.optimization_barrier((back_one, mlp_own))
    outs = finish(x_all, attn_sum, mlp_sum, grad_middle, back_one, gain_one, prompt_rows)
    down_own = mlp_own[:, :hidden_cols].astype(jnp.float32)
    gate_own = mlp_own[:, wide : wide + hidden_cols].astype(jnp.float32)
    rest_own = scatter(grad_rest)
    up_own = rest_own[:, :hidden_cols].astype(jnp.float32)
    o_own = rest_own[:, wide : wide + q_cols].astype(jnp.float32)
    q_own = rest_own[:, wide + q_cols : wide + 2 * q_cols].astype(jnp.float32)
    k_own = rest_own[:, wide + 2 * q_cols : wide + 2 * q_cols + kv_cols].astype(jnp.float32)
    v_own = rest_own[:, wide + 2 * q_cols + kv_cols :].astype(jnp.float32)

    def row_dot(weight, grad):
        return jnp.sum(weight.astype(jnp.float32) * grad, axis=1)

    gain_rows = jnp.stack(
        [
            (row_dot(q_weight, q_own) + row_dot(key_matrix, k_own) + row_dot(value_matrix, v_own))
            / attn_gain.astype(jnp.float32),
            (row_dot(gate_weight, gate_own) + row_dot(up_weight, up_own))
            / mlp_gain.astype(jnp.float32),
        ]
    )
    gain_rows = tensor_total(gain_rows, 5)
    owned = (gain_rows[0], q_own, k_own, v_own, o_own, gain_rows[1], gate_own, up_own, down_own)
    return (*outs, *owned)


def solution(mesh):
    in_specs = (
        P(("dp", "context"), None),
        P(("dp", "context"), None),
        P("dp"),
        P(("dp", "context"), None),
        P(("dp", "context")),
        P(("dp", "context"), "tensor"),
        P(("dp", "context"), "tensor"),
        P(("dp", "context"), "tensor"),
        P(("dp", "context"), "tensor"),
        P(("dp", "context")),
        P(("dp", "context"), "tensor"),
        P(("dp", "context"), "tensor"),
        P(("dp", "context"), "tensor"),
        P(("dp", "context"), None),
        P(("dp", "context"), None),
    )
    out_specs = (
        P(("dp", "context"), None),
        P(("dp", "context"), None),
        P(("dp", "context"), None),
        P(("dp", "context"), None),
        P(("dp", "context")),
        P(("dp", "context"), "tensor"),
        P(("dp", "context"), "tensor"),
        P(("dp", "context"), "tensor"),
        P(("dp", "context"), "tensor"),
        P(("dp", "context")),
        P(("dp", "context"), "tensor"),
        P(("dp", "context"), "tensor"),
        P(("dp", "context"), "tensor"),
    )
    return jax.shard_map(
        per_device, mesh=mesh, in_specs=in_specs, out_specs=out_specs, check_vma=False
    )
```
